32 devices in a mesh: batch: 4 (over z), seq: 8 (over y, x, core).
Axes of the slice: x: 2, y: 2, z: 4, core: 2. Of those that a mesh axis runs over, the one named last changes fastest.
Arguments:
- inputs: float32 [8, 1024, 768], P('batch', 'seq'), may hold values from -6 to 6
- cotangent: float32 [8, 1024, 768], P('batch', 'seq'), may hold values from -6 to 6
- lengths: int32 [8], P('batch'), may hold values from 256 to 1024, as said below
- joint_weight: bfloat16 [768, 2304], P(('batch', 'seq')), may hold values from -0.3125 to 0.3125
- output_weight: bfloat16 [768, 768], P(('batch', 'seq')), may hold values from -1.25 to 1.25
- vectors: bfloat16 [8, 768], P(None, ('batch', 'seq')), may hold values from -2 to 2
- expand_weight: bfloat16 [768, 3072], P(('batch', 'seq')), may hold values from -0.21875 to 0.21875
- expand_bias: bfloat16 [3072], P(('batch', 'seq')), may hold values from -1.1953125 to 1.1953125
- reduce_weight: bfloat16 [3072, 768], P(('batch', 'seq')), may hold values from -0.15625 to 0.15625
Outputs:
- result: float32 [8, 1024, 768], P('batch', 'seq')
- grad_inputs: float32 [8, 1024, 768], P('batch', 'seq')
- grad_joint: float32 [768, 2304], P(('batch', 'seq'))
- grad_output: float32 [768, 768], P(('batch', 'seq'))
- grad_vectors: float32 [8, 768], P(None, ('batch', 'seq'))
- grad_expand: float32 [768, 3072], P(('batch', 'seq'))
- grad_expand_bias: float32 [3072], P(('batch', 'seq'))
- grad_reduce: float32 [3072, 768], P(('batch', 'seq'))
The draws below stay inside these ranges and needn't reach their ends.
Inputs may be any that keep to these rules, and one draw needn't show every extreme that they name: `lengths`: some sequence is full (1024 valid tokens) in every draw.
All inputs are finite; a program needn't handle non-finite values.
Results may differ from the reference program's by a relative error of at most 0.018.
The reference program's roundings to bfloat16 on the way count: a program that leaves them out, or rounds other values in their place, can miss the bound.
Values may be sent and summed in bfloat16 or wider, within the bound.
A program may use at most 192 MiB of HBM per device.

```python
import math
import jax
import jax.numpy as jnp
from jax import lax

D = 768
HEADS = 12
HEAD_DIM = 64
FF = 3072
LEN = 1024
SEQS = 8


def draw_lengths(key, part):
    lengths_drawn = jax.random.randint(jax.random.fold_in(key, 11), (SEQS,), LEN // 4, LEN + 1)
    full_index = jax.random.randint(jax.random.fold_in(key, 12), (), 0, SEQS)
    return jnp.where(jnp.arange(SEQS) == full_index, LEN, lengths_drawn).astype(jnp.int32)


def draw_vectors(key, part):
    normal_draw = jnp.clip(jax.random.normal(jax.random.fold_in(key, 21), (8, D), jnp.float32), -4.0, 4.0)
    row_index = jnp.arange(8)[:, None]
    gain_rows = (row_index == 0) | (row_index == 5)
    return jnp.where(gain_rows, 1.0 + 0.15 * normal_draw, 0.3 * normal_draw).astype(jnp.bfloat16)


def levels(rng, shape, shards, least, top_value):
    loudness = 1.0
    for dim, shards_of in shards:
        heights = jax.random.uniform(jax.random.fold_in(jax.random.fold_in(rng, 6), dim), (shards_of,), jnp.float32, least / len(shards), top_value / len(shards))
        loudness = loudness * jnp.repeat(jnp.exp(heights), shape[dim] // shards_of).reshape((-1,) + (1,) * (len(shape) - 1 - dim))
    return loudness


def scatter_about(key, extent, deviation, reach, pieces=(), held_as=jnp.bfloat16):
    level = levels(key, extent, pieces, -0.22, 0.18) if pieces else 1.0
    entries = jax.random.normal(key, extent, jnp.float32) * deviation * level
    return jnp.minimum(jnp.maximum(entries, -reach), reach).astype(held_as)


def setup_inputs(seed: int = 0) -> dict:
    splits = jax.random.split(jax.random.key(seed), 10)
    inputs = scatter_about(splits[0], (SEQS, LEN, D), 1.0, 6.0, ((0, 4), (1, 8)), jnp.float32)
    cotangent = scatter_about(splits[1], (SEQS, LEN, D), 1.0, 6.0, ((0, 4), (1, 8)), jnp.float32)
    lengths = draw_lengths(jax.random.fold_in(splits[9], 71), 0)
    joint_weight = scatter_about(splits[3], (D, 3 * D), (D // 2) ** -0.5, 0.3125, ((0, 32),))
    output_weight = scatter_about(splits[4], (D, D), (max(4, D // 32)) ** -0.5, 1.25, ((0, 32),))
    vectors = draw_vectors(jax.random.fold_in(splits[9], 71), 0)
    expand_weight = scatter_about(splits[6], (D, FF), D ** -0.5, 0.21875, ((0, 32),))
    expand_bias = scatter_about(splits[7], (FF,), 0.3, 1.1953125, ((0, 32),))
    reduce_weight = scatter_about(splits[8], (FF, D), (FF // 2) ** -0.5, 0.15625, ((0, 32),))
    return {"inputs": inputs, "cotangent": cotangent, "lengths": lengths, "joint_weight": joint_weight, "output_weight": output_weight, "vectors": vectors, "expand_weight": expand_weight, "expand_bias": expand_bias, "reduce_weight": reduce_weight}


EPSILON = 1e-12
SCORE_SCALE = 0.125
NEG_FILL = -1e+30
query_limit = 512

@jax.custom_vjp
def low(v):
    return lax.optimization_barrier(v.astype(jnp.bfloat16)).astype(jnp.float32)

@jax.custom_vjp
def low_back(v):
    return v

def low_keep(v):
    return (low(v), None)

def low_pass(kept, grad):
    return (grad,)

def back_keep(v):
    return (v, None)

def back_low(kept, grad):
    return (low(grad),)
low.defvjp(low_keep, low_pass)
low_back.defvjp(back_keep, back_low)

def highest_dot(left_matrix, right_matrix):
    return jnp.dot(left_matrix, right_matrix, preferred_element_type=jnp.float32, precision=lax.Precision.HIGHEST)

def layer_norm(residual, norm_gain, norm_shift):
    centered = residual - lax.optimization_barrier(jnp.mean(residual, axis=-1, keepdims=True))
    inverse = lax.rsqrt(lax.optimization_barrier(jnp.mean(centered * centered, axis=-1, keepdims=True)) + EPSILON)
    return centered * inverse * norm_gain + norm_shift

def gelu_value(before_gelu):
    return 0.5 * before_gelu * (1.0 + lax.erf(before_gelu * 0.7071067811865476))

def attention(query_low, key_low, value_low, key_valid):
    model_width = HEADS * HEAD_DIM
    key_heads = key_low.reshape(LEN, HEADS, HEAD_DIM)
    value_heads = value_low.reshape(LEN, HEADS, HEAD_DIM)

    def query_block_fn(query_block):
        query_heads = query_block.reshape(-1, HEADS, HEAD_DIM)
        scores = jnp.einsum('qhd,khd->hqk', query_heads, key_heads, precision=lax.Precision.HIGHEST) * SCORE_SCALE
        scores = low_back(scores)
        scores = jnp.where(key_valid[None, None, :], scores, NEG_FILL)
        attention_weights = low(jax.nn.softmax(scores, axis=-1))
        mixed_heads = jnp.einsum('hqk,khd->qhd', attention_weights, value_heads, precision=lax.Precision.HIGHEST)
        return mixed_heads.reshape(-1, model_width)
    block_size = math.gcd(LEN, query_limit)
    outputs = lax.map(jax.checkpoint(query_block_fn), query_low.reshape(LEN // block_size, block_size, model_width))
    return outputs.reshape(LEN, model_width)

def encoder_layer(inputs_row, joint_weight, output_weight, vectors, expand_weight, expand_bias, reduce_weight, key_valid):
    model_width = HEADS * HEAD_DIM
    input_low = low(inputs_row)
    projected = highest_dot(input_low, joint_weight)
    query_low = low(low_back(projected[:, :model_width] + vectors[2]))
    key_low = low(low_back(projected[:, model_width:2 * model_width]))
    value_low = low(low_back(projected[:, 2 * model_width:] + vectors[3]))
    attended = attention(query_low, key_low, value_low, key_valid)
    context = low(low_back(attended))
    branch = low_back(highest_dot(context, output_weight) + vectors[4])
    first = layer_norm(inputs_row + branch, vectors[0], vectors[1])
    first_low = low(first)
    before_gelu = low_back(highest_dot(first_low, expand_weight) + expand_bias)
    hidden_low = low(gelu_value(before_gelu))
    feed = low_back(highest_dot(hidden_low, reduce_weight) + vectors[7])
    return layer_norm(first + feed, vectors[5], vectors[6])

def reference(inputs, cotangent, lengths, joint_weight, output_weight, vectors, expand_weight, expand_bias, reduce_weight):
    weights = (joint_weight.astype(jnp.float32), output_weight.astype(jnp.float32), vectors.astype(jnp.float32), expand_weight.astype(jnp.float32), expand_bias.astype(jnp.float32), reduce_weight.astype(jnp.float32))
    places = jnp.arange(LEN, dtype=jnp.int32)

    def sequence_step(totals, sequence_item):
        inputs_row, cotangent_row, length_row = sequence_item
        key_valid = places < length_row

        def forward_fn(inputs_arg, *weight_args):
            return encoder_layer(inputs_arg, *weight_args, key_valid)
        result_row, pullback = jax.vjp(forward_fn, inputs_row, *weights)
        gradients = pullback(jnp.where(key_valid[:, None], cotangent_row, 0.0))
        totals = tuple((older + newer for older, newer in zip(totals, gradients[1:])))
        return (totals, (result_row, gradients[0]))
    zero_grads = tuple((jnp.zeros_like(weight_item) for weight_item in weights))
    totals, (result, grad_inputs) = lax.scan(sequence_step, zero_grads, (inputs, cotangent, lengths))
    return (result, grad_inputs, totals[0], totals[1], totals[2], totals[3], totals[4], totals[5])
```

```python
import math

import jax
import jax.numpy as jnp
from jax import lax
from jax.experimental import pallas as pl
from jax.experimental.pallas import tpu as pltpu
from jax.sharding import PartitionSpec as P

HEADS = 12
HEAD_DIM = 64


EPSILON = 1e-12
SCORE_SCALE = 0.125
NEG_FILL = -1e30
HALF_ROOT = 0.7071067811865476
INV_ROOT_TAU = 0.3989422804014327
block_limit = 256


def layer_norm(residual, norm_gain, norm_shift):
    centered = residual - jnp.mean(residual, axis=-1, keepdims=True)
    inverse = lax.rsqrt(jnp.mean(centered * centered, axis=-1, keepdims=True) + EPSILON)
    normed = centered * inverse
    return (normed * norm_gain + norm_shift, normed, inverse)


def norm_back(grad_out, normed, inverse, norm_gain):
    grad_normed = grad_out * norm_gain
    mean_grad = jnp.mean(grad_normed, axis=-1, keepdims=True)
    mean_proj = jnp.mean(grad_normed * normed, axis=-1, keepdims=True)
    grad_in = inverse * (grad_normed - mean_grad - normed * mean_proj)
    return (grad_in, jnp.sum(grad_out * normed, axis=0), jnp.sum(grad_out, axis=0))


def gelu_value(before_gelu):
    return 0.5 * before_gelu * (1.0 + lax.erf(before_gelu * HALF_ROOT))


def gelu_slope(before_gelu):
    return (
        0.5 * (1.0 + lax.erf(before_gelu * HALF_ROOT))
        + before_gelu * jnp.exp(-0.5 * before_gelu * before_gelu) * INV_ROOT_TAU
    )


def over_blocks(piece_rows, block_fn, carried):
    block_size = math.gcd(piece_rows, block_limit)

    def run_block(block_index, current):
        return block_fn(current, block_index * block_size, block_size)

    return lax.fori_loop(0, piece_rows // block_size, run_block, carried)


def head_scores(left_heads, right_heads, right_places, lengths):
    scores = (
        jnp.einsum("sqhd,skhd->shqk", left_heads, right_heads, preferred_element_type=jnp.float32)
        * SCORE_SCALE
    )
    allowed = right_places[None, :] < lengths[:, None]
    return jnp.where(allowed[:, None, None, :], scores, NEG_FILL)


def cut_heads(gathered_piece, offset, block_size, head_count):
    sliced = lax.dynamic_slice_in_dim(gathered_piece, offset, block_size, 1)
    return sliced.reshape(sliced.shape[0], block_size, head_count, -1)


def gather_attention(joint_weight, output_weight, vectors):
    return (
        lax.all_gather(joint_weight, ("batch", "seq"), axis=0, tiled=True),
        lax.all_gather(output_weight, ("batch", "seq"), axis=0, tiled=True),
        lax.all_gather(vectors, ("batch", "seq"), axis=1, tiled=True),
    )


def gather_feed(expand_weight, reduce_weight, expand_bias):
    return (
        lax.all_gather(expand_weight, ("batch", "seq"), axis=0, tiled=True),
        lax.all_gather(reduce_weight, ("batch", "seq"), axis=0, tiled=True),
        lax.all_gather(expand_bias, ("batch", "seq"), axis=0, tiled=True),
    )


def general_on_device(
    inputs,
    cotangent,
    lengths,
    joint_weight,
    output_weight,
    vectors,
    expand_weight,
    expand_bias,
    reduce_weight,
):
    seq_count, row_count, model_width = inputs.shape
    head_count = HEADS
    head_size = HEAD_DIM
    tokens = seq_count * row_count
    head_shape = (seq_count, row_count, head_count, head_size)
    own_places = lax.axis_index("seq") * row_count + jnp.arange(row_count, dtype=jnp.int32)
    row_valid = own_places[None, :] < lengths[:, None]
    row_mask = row_valid.reshape(tokens, 1).astype(jnp.float32)
    full_joint, full_output, full_vectors = gather_attention(joint_weight, output_weight, vectors)
    vector_rows = full_vectors.astype(jnp.float32)
    flat_inputs = inputs.reshape(tokens, model_width)
    input_low = flat_inputs.astype(jnp.bfloat16)
    projected = jnp.dot(input_low, full_joint, preferred_element_type=jnp.float32)
    query_low = (projected[:, :model_width] + vector_rows[2]).astype(jnp.bfloat16)
    key_low = projected[:, model_width : 2 * model_width].astype(jnp.bfloat16)
    value_low = (projected[:, 2 * model_width :] + vector_rows[3]).astype(jnp.bfloat16)
    query_heads = query_low.reshape(head_shape)
    key_rows = key_low.reshape(seq_count, row_count, model_width)
    value_rows = value_low.reshape(seq_count, row_count, model_width)
    start_state = (
        jnp.full((seq_count, head_count, row_count), NEG_FILL, jnp.float32),
        jnp.zeros((seq_count, head_count, row_count), jnp.float32),
        jnp.zeros(head_shape, jnp.float32),
    )
    key_piece = lax.all_gather(key_rows, "seq", axis=1, tiled=True)
    value_piece = lax.all_gather(value_rows, "seq", axis=1, tiled=True)

    def forward_score_block(current, offset, block_size):
        running_max, running_sum, summed = current
        key_heads = cut_heads(key_piece, offset, block_size, head_count)
        value_heads = cut_heads(value_piece, offset, block_size, head_count)
        key_places = offset + jnp.arange(block_size, dtype=jnp.int32)
        scores = head_scores(query_heads, key_heads, key_places, lengths)
        new_max = jnp.maximum(running_max, jnp.max(scores, axis=-1))
        factor = jnp.exp(running_max - new_max)
        exp_scores = jnp.exp(scores - new_max[..., None])
        running_sum = running_sum * factor + jnp.sum(exp_scores, axis=-1)
        update = jnp.einsum(
            "shqk,skhd->sqhd",
            exp_scores.astype(jnp.bfloat16),
            value_heads,
            preferred_element_type=jnp.float32,
        )
        summed = summed * jnp.transpose(factor, (0, 2, 1))[..., None] + update
        return (new_max, running_sum, summed)

    running_max, running_sum, summed = over_blocks(
        key_piece.shape[1], forward_score_block, start_state
    )
    attended = summed / jnp.transpose(running_sum, (0, 2, 1))[..., None]
    log_total = jnp.transpose(running_max + jnp.log(running_sum), (0, 2, 1))
    context_low = attended.reshape(tokens, model_width).astype(jnp.bfloat16)
    branch = jnp.dot(context_low, full_output, preferred_element_type=jnp.float32) + vector_rows[4]
    first, first_normed, first_inverse = layer_norm(
        flat_inputs + branch, vector_rows[0], vector_rows[1]
    )
    first_low = first.astype(jnp.bfloat16)
    full_expand, full_reduce, full_bias = gather_feed(expand_weight, reduce_weight, expand_bias)
    before_gelu = jnp.dot(
        first_low, full_expand, preferred_element_type=jnp.float32
    ) + full_bias.astype(jnp.float32)
    hidden_low = gelu_value(before_gelu).astype(jnp.bfloat16)
    feed = jnp.dot(hidden_low, full_reduce, preferred_element_type=jnp.float32) + vector_rows[7]
    result, second_normed, second_inverse = layer_norm(first + feed, vector_rows[5], vector_rows[6])
    full_expand, full_reduce, full_bias = gather_feed(expand_weight, reduce_weight, expand_bias)
    full_joint, full_output, full_vectors = gather_attention(joint_weight, output_weight, vectors)
    grad_res = cotangent.reshape(tokens, model_width) * row_mask
    grad_second, grad_gain_two, grad_shift_two = norm_back(
        grad_res, second_normed, second_inverse, vector_rows[5]
    )
    grad_feed_low = grad_second.astype(jnp.bfloat16)
    grad_reduce_local = jnp.dot(hidden_low.T, grad_feed_low, preferred_element_type=jnp.float32)
    grad_hidden = jnp.dot(
        grad_feed_low, full_reduce.T, preferred_element_type=jnp.float32
    ) * gelu_slope(before_gelu)
    grad_hidden_low = grad_hidden.astype(jnp.bfloat16)
    grad_expand_local = jnp.dot(first_low.T, grad_hidden_low, preferred_element_type=jnp.float32)
    grad_bias_local = jnp.sum(grad_hidden_low.astype(jnp.float32), axis=0)
    grad_first = grad_second + jnp.dot(
        grad_hidden_low, full_expand.T, preferred_element_type=jnp.float32
    )
    grad_resid, grad_gain_one, grad_shift_one = norm_back(
        grad_first, first_normed, first_inverse, vector_rows[0]
    )
    grad_branch_low = grad_resid.astype(jnp.bfloat16)
    grad_output_local = jnp.dot(context_low.T, grad_branch_low, preferred_element_type=jnp.float32)
    grad_context_low = jnp.dot(
        grad_branch_low, full_output.T, preferred_element_type=jnp.float32
    ).astype(jnp.bfloat16)
    grad_context_heads = grad_context_low.reshape(head_shape)
    row_delta = jnp.sum(grad_context_heads.astype(jnp.float32) * attended, axis=-1)
    log_heads = jnp.transpose(log_total, (0, 2, 1))
    delta_heads = jnp.transpose(row_delta, (0, 2, 1))
    query_key_piece = lax.all_gather(key_rows, "seq", axis=1, tiled=True)
    query_value_piece = lax.all_gather(value_rows, "seq", axis=1, tiled=True)

    def query_score_block(current, offset, block_size):
        key_heads = cut_heads(query_key_piece, offset, block_size, head_count)
        value_heads = cut_heads(query_value_piece, offset, block_size, head_count)
        key_places = offset + jnp.arange(block_size, dtype=jnp.int32)
        scores = head_scores(query_heads, key_heads, key_places, lengths)
        softmax_rows = jnp.exp(scores - log_heads[..., None])
        grad_probs = jnp.einsum(
            "sqhd,skhd->shqk", grad_context_heads, value_heads, preferred_element_type=jnp.float32
        )
        grad_scores = (softmax_rows * (grad_probs - delta_heads[..., None])).astype(jnp.bfloat16)
        return (
            current
            + jnp.einsum(
                "shqk,skhd->sqhd", grad_scores, key_heads, preferred_element_type=jnp.float32
            )
            * SCORE_SCALE
        )

    grad_query = over_blocks(
        query_key_piece.shape[1], query_score_block, jnp.zeros(head_shape, jnp.float32)
    )
    own_keys = key_low.reshape(head_shape)
    own_values = value_low.reshape(head_shape)
    query_rows = query_low.reshape(seq_count, row_count, model_width)
    grad_context_rows = grad_context_low.reshape(seq_count, row_count, model_width)
    zero_heads = jnp.zeros(head_shape, jnp.float32)
    query_piece = lax.all_gather(query_rows.astype(jnp.float32), "seq", axis=1, tiled=True).astype(
        jnp.bfloat16
    )
    grad_piece = lax.all_gather(
        grad_context_rows.astype(jnp.float32), "seq", axis=1, tiled=True
    ).astype(jnp.bfloat16)
    log_piece = lax.all_gather(log_total, "seq", axis=1, tiled=True)
    delta_piece = lax.all_gather(row_delta, "seq", axis=1, tiled=True)

    def key_score_block(current, offset, block_size):
        grad_key, grad_value = current
        query_block = cut_heads(query_piece, offset, block_size, head_count)
        grad_block = cut_heads(grad_piece, offset, block_size, head_count)
        log_block = jnp.transpose(
            lax.dynamic_slice_in_dim(log_piece, offset, block_size, 1), (0, 2, 1)
        )
        delta_block = jnp.transpose(
            lax.dynamic_slice_in_dim(delta_piece, offset, block_size, 1), (0, 2, 1)
        )
        scores = head_scores(query_block, own_keys, own_places, lengths)
        softmax_rows = jnp.exp(scores - log_block[..., None])
        grad_value = grad_value + jnp.einsum(
            "shqk,sqhd->skhd",
            softmax_rows.astype(jnp.bfloat16),
            grad_block,
            preferred_element_type=jnp.float32,
        )
        grad_probs = jnp.einsum(
            "sqhd,skhd->shqk", grad_block, own_values, preferred_element_type=jnp.float32
        )
        grad_scores = (softmax_rows * (grad_probs - delta_block[..., None])).astype(jnp.bfloat16)
        grad_key = (
            grad_key
            + jnp.einsum(
                "shqk,sqhd->skhd", grad_scores, query_block, preferred_element_type=jnp.float32
            )
            * SCORE_SCALE
        )
        return (grad_key, grad_value)

    grad_key, grad_value = over_blocks(
        query_piece.shape[1], key_score_block, (zero_heads, zero_heads)
    )
    grad_query_low = grad_query.reshape(tokens, model_width).astype(jnp.bfloat16)
    grad_key_low = grad_key.reshape(tokens, model_width).astype(jnp.bfloat16)
    grad_value_low = grad_value.reshape(tokens, model_width).astype(jnp.bfloat16)
    grad_projected = jnp.concatenate([grad_query_low, grad_key_low, grad_value_low], axis=1)
    grad_joint_local = jnp.dot(input_low.T, grad_projected, preferred_element_type=jnp.float32)
    grad_inputs = grad_resid + jnp.dot(
        grad_projected, full_joint.T, preferred_element_type=jnp.float32
    )
    grad_vector_local = jnp.stack(
        [
            grad_gain_one,
            grad_shift_one,
            jnp.sum(grad_query_low.astype(jnp.float32), axis=0),
            jnp.sum(grad_value_low.astype(jnp.float32), axis=0),
            jnp.sum(grad_branch_low.astype(jnp.float32), axis=0),
            grad_gain_two,
            grad_shift_two,
            jnp.sum(grad_feed_low.astype(jnp.float32), axis=0),
        ],
        axis=0,
    )
    every_grad = (
        lax.psum_scatter(grad_joint_local, ("batch", "seq"), scatter_dimension=0, tiled=True),
        lax.psum_scatter(grad_output_local, ("batch", "seq"), scatter_dimension=0, tiled=True),
        lax.psum_scatter(grad_vector_local, ("batch", "seq"), scatter_dimension=1, tiled=True),
        lax.psum_scatter(grad_expand_local, ("batch", "seq"), scatter_dimension=0, tiled=True),
        lax.psum_scatter(grad_reduce_local, ("batch", "seq"), scatter_dimension=0, tiled=True),
        lax.psum_scatter(grad_bias_local, ("batch", "seq"), scatter_dimension=0, tiled=True),
    )
    summed_grads = (
        every_grad[0],
        every_grad[1],
        every_grad[2],
        every_grad[3],
        every_grad[5],
        every_grad[4],
    )
    return (
        result.reshape(seq_count, row_count, model_width),
        grad_inputs.reshape(seq_count, row_count, model_width),
        summed_grads[0],
        summed_grads[1],
        summed_grads[2],
        summed_grads[3],
        summed_grads[4],
        summed_grads[5],
    )


MESH = pl.DeviceIdType.MESH
ANY = pl.BlockSpec(memory_space=pl.ANY)
VM = pl.BlockSpec(memory_space=pltpu.VMEM)
SM = pl.BlockSpec(memory_space=pltpu.SMEM)
DMA = pltpu.SemaphoreType.DMA
VMEM_LIMIT = 60 << 20
F32 = jnp.float32
BF16 = jnp.bfloat16


def send(src, dst, send_sem, recv_sem, device):
    return pltpu.make_async_remote_copy(
        src_ref=src,
        dst_ref=dst,
        send_sem=send_sem,
        recv_sem=recv_sem,
        device_id=device,
        device_id_type=MESH,
    )


class Place:
    def __init__(self, nb):
        self.nb = nb
        self.b = lax.axis_index("batch")
        self.s = lax.axis_index("seq")
        self.c = self.s % 2
        self.p = self.s // 2
        x, y = self.p % 2, self.p // 2
        self.px = 2 * y + (1 - x)
        self.py = 2 * (1 - y) + x
        self.pd = 2 * (1 - y) + (1 - x)
        self.sib = (self.b, 2 * self.p + 1 - self.c)
        self.xn = (self.b, 2 * self.px + self.c)
        self.yn = (self.b, 2 * self.py + self.c)

    def chip(self, step):
        return (self.p, self.px, self.py, self.pd)[step]

    def up(self, step):
        return (self.b + step) % self.nb

    def down(self, step):
        return (self.b + self.nb - step) % self.nb


def greet(devices):
    barrier = pltpu.get_barrier_semaphore()
    for device in devices:
        pl.semaphore_signal(barrier, inc=1, device_id=device, device_id_type=MESH)
    pl.semaphore_wait(barrier, len(devices))


def same_core(pos):
    return [
        (pos.up(d), 2 * pos.chip(k) + pos.c)
        for d in range(pos.nb)
        for k in range(4)
        if d or k
    ]


def plane_others(pos):
    return [
        (pos.b, 2 * pos.chip(k) + (pos.c if j == 0 else 1 - pos.c))
        for k in range(4)
        for j in range(2)
        if k or j
    ]


class Gather:
    SEMS = 6

    def __init__(self, pos, shard, out, halves, sems):
        self.pos, self.shard, self.out, self.halves = pos, shard, out, halves
        self.zs, self.xs, self.ys, self.f0, self.f1, self.sb = sems[:6]
        self.started = []

    @staticmethod
    def scratch(nb):
        return [DMA((2, nb)) for _ in range(6)]

    def src(self, k):
        pos = self.pos
        return self.shard if k == 0 else self.out.at[pos.down(k), pos.p, pos.c]

    def z_copy(self, k):
        pos = self.pos
        return send(
            self.shard,
            self.out.at[pos.b, pos.p, pos.c],
            self.zs.at[0, k],
            self.zs.at[1, k],
            (pos.up(k), pos.s),
        )

    def z_land(self, k):
        pos = self.pos
        land = self.out.at[pos.down(k), pos.p, pos.c]
        return send(land, land, self.zs.at[0, k], self.zs.at[1, k], (pos.up(k), pos.s))

    def go(self, copy):
        copy.start()
        self.started.append(copy)

    def own(self, local_sem):
        pos = self.pos
        for k in range(1, pos.nb):
            self.go(self.z_copy(k))
        self.local = pltpu.make_async_copy(
            self.shard, self.out.at[pos.b, pos.p, pos.c], local_sem
        )
        self.local.start()

    def plane(self, k):
        pos = self.pos
        if k:
            self.z_land(k).wait_recv()
        src, there = self.src(k), self.out.at[pos.down(k), pos.p, pos.c]
        self.go(send(src, there, self.xs.at[0, k], self.xs.at[1, k], pos.xn))
        self.go(send(src, there, self.ys.at[0, k], self.ys.at[1, k], pos.yn))

    def land(self, sems, k, chip, half=None):
        pos = self.pos
        ref = self.out.at[pos.down(k), chip, pos.c]
        if half is not None:
            ref = ref.at[half]
        return send(ref, ref, sems.at[0, k], sems.at[1, k], pos.xn)

    def forward(self, k):
        pos = self.pos
        h0, h1 = self.halves
        self.land(self.xs, k, pos.px).wait_recv()
        ref = self.out.at[pos.down(k), pos.px, pos.c].at[h0]
        self.go(send(ref, ref, self.f0.at[0, k], self.f0.at[1, k], pos.yn))
        self.land(self.ys, k, pos.py).wait_recv()
        if h1 is not None:
            ref = self.out.at[pos.down(k), pos.py, pos.c].at[h1]
            self.go(send(ref, ref, self.f1.at[0, k], self.f1.at[1, k], pos.xn))

    def sibling(self, k):
        pos = self.pos
        h0, h1 = self.halves
        self.land(self.f0, k, pos.pd, h0).wait_recv()
        if h1 is not None:
            self.land(self.f1, k, pos.pd, h1).wait_recv()
        if k == 0:
            self.local.wait()
        ref = self.out.at[pos.down(k), :, pos.c]
        self.go(send(ref, ref, self.sb.at[0, k], self.sb.at[1, k], pos.sib))

    def finish(self):
        pos = self.pos
        for k in range(pos.nb):
            ref = self.out.at[pos.down(k), :, 1 - pos.c]
            send(ref, ref, self.sb.at[0, k], self.sb.at[1, k], pos.sib).wait_recv()
        for copy in self.started:
            copy.wait_send()


class InputExchange:
    def __init__(self, pos, rows, out, sems):
        self.pos, self.rows, self.out, self.sems = pos, rows, out, sems
        self.started = []

    @staticmethod
    def scratch():
        return [DMA((2, 2)), DMA((2, 2)), DMA((2, 2)), DMA((2,)), DMA]

    def go(self, copy):
        copy.start()
        self.started.append(copy)

    def start(self):
        pos, (xs, ys, _, sb, local) = self.pos, self.sems
        there = self.out.at[pos.p, pos.c]
        for sems, chip in ((xs, pos.px), (ys, pos.py)):
            for j in range(2):
                self.go(
                    send(
                        self.rows.at[j],
                        there,
                        sems.at[0, j],
                        sems.at[1, pos.c],
                        (pos.b, 2 * chip + j),
                    )
                )
        self.go(send(self.rows.at[1 - pos.c], there, sb.at[0], sb.at[1], pos.sib))
        self.local = pltpu.make_async_copy(self.rows.at[pos.c], there, local)
        self.local.start()

    def landed(self, sems, j, chip):
        ref = self.out.at[chip, j]
        send(ref, ref, sems.at[0, j], sems.at[1, j], self.pos.xn).wait_recv()

    def forward(self):
        pos, (xs, ys, fs, _, _) = self.pos, self.sems
        self.landed(xs, 0, pos.px)
        ref = self.out.at[pos.px, 0]
        self.go(send(ref, ref, fs.at[0, 0], fs.at[1, 0], pos.yn))
        self.landed(ys, 1, pos.py)
        ref = self.out.at[pos.py, 1]
        self.go(send(ref, ref, fs.at[0, 1], fs.at[1, 1], pos.xn))

    def finish(self):
        pos, (xs, ys, fs, sb, _) = self.pos, self.sems
        self.landed(xs, 1, pos.px)
        self.landed(ys, 0, pos.py)
        self.landed(fs, 0, pos.pd)
        self.landed(fs, 1, pos.pd)
        ref = self.out.at[pos.p, 1 - pos.c]
        send(ref, ref, sb.at[0], sb.at[1], pos.sib).wait_recv()
        self.local.wait()

    def drain(self):
        for copy in self.started:
            copy.wait_send()


class JointGather:
    def __init__(self, pos, parts, out, sems):
        self.pos, self.parts, self.out = pos, parts, out
        self.direct, self.sb, self.local_sem = sems
        self.started = []

    @staticmethod
    def scratch(nb):
        return [DMA((2, nb, 4)), DMA((2,)), DMA]

    def start(self):
        pos = self.pos
        there = self.out.at[pos.b, pos.p, pos.c]
        for d in range(pos.nb):
            for k in range(4):
                if d or k:
                    chip = pos.chip(k)
                    copy = send(
                        self.parts.at[chip],
                        there,
                        self.direct.at[0, d, k],
                        self.direct.at[1, d, k],
                        (pos.up(d), 2 * chip + pos.c),
                    )
                    copy.start()
                    self.started.append(copy)
        self.local = pltpu.make_async_copy(self.parts.at[pos.p], there, self.local_sem)
        self.local.start()

    def sibling(self):
        pos = self.pos
        for d in range(pos.nb):
            for k in range(4):
                if d or k:
                    ref = self.out.at[pos.down(d), pos.chip(k), pos.c]
                    send(
                        ref, ref, self.direct.at[0, d, k], self.direct.at[1, d, k], pos.sib
                    ).wait_recv()
        self.local.wait()
        ref = self.out.at[:, :, pos.c]
        copy = send(ref, ref, self.sb.at[0], self.sb.at[1], pos.sib)
        copy.start()
        self.started.append(copy)

    def finish(self):
        pos = self.pos
        ref = self.out.at[:, :, 1 - pos.c]
        send(ref, ref, self.sb.at[0], self.sb.at[1], pos.sib).wait_recv()

    def drain(self):
        for copy in self.started:
            copy.wait_send()


def gather_all(rows, joint, small, output, expand, reduce, nb):
    def body(
        rows_ref, joint_ref, small_ref, output_ref, expand_ref, reduce_ref,
        rows_out, joint_out, small_out, output_out, expand_out, reduce_out,
        *scratch,
    ):
        pos = Place(nb)
        scratch = list(scratch)

        def take(n):
            got = scratch[:n]
            del scratch[:n]
            return got

        exchange = InputExchange(pos, rows_ref, rows_out, take(5))
        joints = JointGather(pos, joint_ref, joint_out, take(3))
        gathers = []
        for shard, out in (
            (small_ref, small_out),
            (output_ref, output_out),
            (expand_ref, expand_out),
            (reduce_ref, reduce_out),
        ):
            gathers.append(Gather(pos, shard, out, halves_of(shard.shape), take(6)))
        local_sems = take(1)[0]
        greet(
            same_core(pos)
            + [
                pos.sib,
                (pos.b, 2 * pos.px + 1 - pos.c),
                (pos.b, 2 * pos.py + 1 - pos.c),
            ]
        )
        exchange.start()
        joints.start()
        for i, gather in enumerate(gathers):
            gather.own(local_sems.at[i])
        for gather in gathers:
            gather.plane(0)
        exchange.forward()
        for k in range(nb):
            if k:
                for gather in gathers:
                    gather.plane(k)
                for gather in gathers:
                    gather.forward(k - 1)
        for gather in gathers:
            gather.forward(nb - 1)
        joints.sibling()
        for k in range(nb):
            for gather in gathers:
                gather.sibling(k)
        exchange.finish()
        joints.finish()
        for gather in gathers:
            gather.finish()
        exchange.drain()
        joints.drain()

    def shape(shard):
        return jax.ShapeDtypeStruct((nb, 4, 2) + shard.shape, shard.dtype)

    arrays = (rows, joint, small, output, expand, reduce)
    return pl.pallas_call(
        body,
        out_shape=(
            jax.ShapeDtypeStruct((4, 2) + rows.shape[1:], rows.dtype),
            jax.ShapeDtypeStruct((nb, 4, 2) + joint.shape[1:], joint.dtype),
            shape(small),
            shape(output),
            shape(expand),
            shape(reduce),
        ),
        in_specs=[ANY] * 6,
        out_specs=(ANY,) * 6,
        scratch_shapes=InputExchange.scratch()
        + JointGather.scratch(nb)
        + Gather.scratch(nb) * 4
        + [DMA((4,))],
        name="gather_all",
        compiler_params=pltpu.CompilerParams(
            collective_id=1, has_side_effects=True, vmem_limit_bytes=8 << 20
        ),
    )(*arrays)


def halves_of(shape):
    rows, columns = shape
    if columns % 256 == 0 and columns >= 1024:
        return (
            (slice(None), pl.ds(0, columns // 2)),
            (slice(None), pl.ds(columns // 2, columns // 2)),
        )
    if rows % 32 == 0:
        return (
            (pl.ds(0, rows // 2), slice(None)),
            (pl.ds(rows // 2, rows // 2), slice(None)),
        )
    if columns % 256 == 0:
        return (
            (slice(None), pl.ds(0, columns // 2)),
            (slice(None), pl.ds(columns // 2, columns // 2)),
        )
    return ((slice(None), slice(None)), None)


def plane_exchange(parts, collective_id, name):
    def body(parts_ref, out_ref, sems, local_sem):
        pos = Place(1)
        greet(plane_others(pos))
        copies = []
        there = out_ref.at[pos.p, pos.c]
        for k in range(4):
            for j in range(2):
                chip = pos.chip(k)
                core = pos.c if j == 0 else 1 - pos.c
                if k or j:
                    copies.append(
                        send(
                            parts_ref.at[chip, core],
                            there,
                            sems.at[0, 2 * k + j],
                            sems.at[1, 2 * k + j],
                            (pos.b, 2 * chip + core),
                        )
                    )
        for copy in copies:
            copy.start()
        local = pltpu.make_async_copy(parts_ref.at[pos.p, pos.c], there, local_sem)
        local.start()
        for k in range(4):
            for j in range(2):
                if k or j:
                    ref = out_ref.at[pos.chip(k), pos.c if j == 0 else 1 - pos.c]
                    send(
                        ref, ref, sems.at[0, 2 * k + j], sems.at[1, 2 * k + j], pos.sib
                    ).wait_recv()
        local.wait()
        for copy in copies:
            copy.wait_send()

    return pl.pallas_call(
        body,
        out_shape=jax.ShapeDtypeStruct(parts.shape, parts.dtype),
        in_specs=[ANY],
        out_specs=ANY,
        scratch_shapes=[DMA((2, 8)), DMA],
        name=name,
        compiler_params=pltpu.CompilerParams(
            collective_id=collective_id, has_side_effects=True, vmem_limit_bytes=8 << 20
        ),
    )(parts)


def attend(length, rows, weight, bias, heads):
    size, _ = rows.shape
    width = weight.shape[1] // 3
    step = math.gcd(size, 256)

    def body(length_ref, rows_ref, weight_ref, bias_ref, context_ref, qkv_ref, log_ref):
        limit = length_ref[0]

        def project(i, _):
            at = pl.ds(pl.multiple_of(i * step, step), step)
            qkv_ref[at, :] = (
                jnp.dot(rows_ref[at, :], weight_ref[...], preferred_element_type=F32)
                + bias_ref[...]
            ).astype(BF16)
            return 0

        lax.fori_loop(0, size // step, project, 0)

        def block(i, _):
            at = pl.ds(pl.multiple_of(i * step, step), step)
            allowed = lax.broadcasted_iota(jnp.int32, (1, size), 1) < limit
            lanes = lax.broadcasted_iota(jnp.int32, (step, 128), 1)
            parts, logs = [], jnp.zeros((step, 128), F32)
            for h in range(heads):
                query = qkv_ref[at, h * HEAD_DIM : (h + 1) * HEAD_DIM]
                key = qkv_ref[:, width + h * HEAD_DIM : width + (h + 1) * HEAD_DIM]
                value = qkv_ref[:, 2 * width + h * HEAD_DIM : 2 * width + (h + 1) * HEAD_DIM]
                scores = (
                    lax.dot_general(
                        query, key, (((1,), (1,)), ((), ())), preferred_element_type=F32
                    )
                    * SCORE_SCALE
                )
                scores = jnp.where(allowed, scores, NEG_FILL)
                top = jnp.max(scores, axis=-1, keepdims=True)
                exps = jnp.exp(scores - top)
                total = jnp.sum(exps, axis=-1, keepdims=True)
                mixed = jnp.dot(exps.astype(BF16), value, preferred_element_type=F32)
                parts.append(mixed / total)
                logs = jnp.where(lanes == h, top + jnp.log(total), logs)
            context_ref[at, :] = jnp.concatenate(parts, axis=1).astype(BF16)
            log_ref[at, :] = logs
            return 0

        lax.fori_loop(0, size // step, block, 0)

    return pl.pallas_call(
        body,
        out_shape=(
            jax.ShapeDtypeStruct((size, width), BF16),
            jax.ShapeDtypeStruct((size, 3 * width), BF16),
            jax.ShapeDtypeStruct((size, 128), F32),
        ),
        in_specs=[SM, VM, VM, VM],
        out_specs=(VM, VM, VM),
        name="attend",
        compiler_params=pltpu.CompilerParams(vmem_limit_bytes=48 << 20),
    )(length, rows, weight, bias)


def attend_back(length, rows, weight, qkv, logs, grad_context, heads):
    size, model_width = rows.shape
    width = weight.shape[1] // 3
    step = math.gcd(size, 256)

    def body(
        length_ref, rows_ref, weight_ref, qkv_ref, log_ref, grad_ref,
        grad_rows_ref, grad_weight_ref, sums_ref,
        grad_qkv, grad_key, grad_value,
    ):
        limit = length_ref[0]
        grad_key[...] = jnp.zeros_like(grad_key)
        grad_value[...] = jnp.zeros_like(grad_value)

        def block(i, _):
            at = pl.ds(pl.multiple_of(i * step, step), step)
            allowed = lax.broadcasted_iota(jnp.int32, (1, size), 1) < limit
            parts = []
            for h in range(heads):
                query = qkv_ref[at, h * HEAD_DIM : (h + 1) * HEAD_DIM]
                key = qkv_ref[:, width + h * HEAD_DIM : width + (h + 1) * HEAD_DIM]
                value = qkv_ref[:, 2 * width + h * HEAD_DIM : 2 * width + (h + 1) * HEAD_DIM]
                grad_out = grad_ref[at, h * HEAD_DIM : (h + 1) * HEAD_DIM]
                scores = (
                    lax.dot_general(
                        query, key, (((1,), (1,)), ((), ())), preferred_element_type=F32
                    )
                    * SCORE_SCALE
                )
                probs = jnp.where(
                    allowed, jnp.exp(scores - log_ref[at, h : h + 1]), 0.0
                )
                grad_probs = lax.dot_general(
                    grad_out, value, (((1,), (1,)), ((), ())), preferred_element_type=F32
                )
                delta = jnp.sum(probs * grad_probs, axis=-1, keepdims=True)
                grad_scores = (probs * (grad_probs - delta)).astype(BF16)
                parts.append(
                    jnp.dot(grad_scores, key, preferred_element_type=F32) * SCORE_SCALE
                )
                grad_key[h] += lax.dot_general(
                    grad_scores, query, (((0,), (0,)), ((), ())), preferred_element_type=F32
                )
                grad_value[h] += lax.dot_general(
                    probs.astype(BF16),
                    grad_out,
                    (((0,), (0,)), ((), ())),
                    preferred_element_type=F32,
                )
            grad_qkv[at, :width] = jnp.concatenate(parts, axis=1).astype(BF16)
            return 0

        lax.fori_loop(0, size // step, block, 0)
        grad_qkv[:, width : 2 * width] = (
            jnp.concatenate([grad_key[h] for h in range(heads)], axis=1) * SCORE_SCALE
        ).astype(BF16)
        grad_qkv[:, 2 * width :] = jnp.concatenate(
            [grad_value[h] for h in range(heads)], axis=1
        ).astype(BF16)
        sums_ref[...] = jnp.sum(grad_qkv[...].astype(F32), axis=0, keepdims=True)

        def spread(i, _):
            at = pl.ds(pl.multiple_of(i * step, step), step)
            grad_rows_ref[at, :] = lax.dot_general(
                grad_qkv[at, :],
                weight_ref[...],
                (((1,), (1,)), ((), ())),
                preferred_element_type=F32,
            ).astype(BF16)
            return 0

        lax.fori_loop(0, size // step, spread, 0)
        grad_weight_ref[...] = lax.dot_general(
            rows_ref[...], grad_qkv[...], (((0,), (0,)), ((), ())), preferred_element_type=F32
        ).astype(BF16)

    return pl.pallas_call(
        body,
        out_shape=(
            jax.ShapeDtypeStruct((size, model_width), BF16),
            jax.ShapeDtypeStruct((model_width, 3 * width), BF16),
            jax.ShapeDtypeStruct((1, 3 * width), F32),
        ),
        in_specs=[SM, VM, VM, VM, VM, VM],
        out_specs=(VM, VM, VM),
        scratch_shapes=[
            pltpu.VMEM((size, 3 * width), BF16),
            pltpu.VMEM((heads, size, HEAD_DIM), F32),
            pltpu.VMEM((heads, size, HEAD_DIM), F32),
        ],
        name="attend_back",
        compiler_params=pltpu.CompilerParams(vmem_limit_bytes=48 << 20),
    )(length, rows, weight, qkv, logs, grad_context)


class Scatter:
    def __init__(self, pos, partial, halves, bufs, sems):
        self.pos, self.partial, self.halves = pos, partial, halves
        (self.mine, self.theirs, self.a0, self.a1, self.bx, self.by, self.tz, self.z) = bufs
        (self.sb, self.s0, self.s1, self.dx, self.dy, self.cx, self.cy, self.zs, self.ld) = sems
        self.started = []

    @staticmethod
    def scratch(nb, shape, dtype, halves):
        rows, columns = shape
        first, second = half_shapes(shape, halves)
        return [
            pltpu.VMEM((nb, 4) + shape, dtype),
            pltpu.VMEM((nb, 4) + shape, dtype),
            pltpu.VMEM((nb,) + first, dtype),
            pltpu.VMEM((nb,) + second, dtype),
            pltpu.VMEM((nb,) + shape, dtype),
            pltpu.VMEM((nb,) + shape, dtype),
            pltpu.VMEM((nb,) + shape, dtype),
            pltpu.VMEM((nb,) + shape, dtype),
        ]

    @staticmethod
    def sem_scratch(nb):
        return [DMA((2,))] + [DMA((2, nb)) for _ in range(7)] + [DMA]

    def go(self, copy):
        copy.start()
        self.started.append(copy)

    def begin(self):
        pos = self.pos
        self.go(
            send(
                self.partial.at[:, :, 1 - pos.c],
                self.theirs,
                self.sb.at[0],
                self.sb.at[1],
                pos.sib,
            )
        )
        self.local = pltpu.make_async_copy(
            self.partial.at[:, :, pos.c], self.mine, self.ld
        )
        self.local.start()

    def joined(self):
        self.local.wait()
        pos = self.pos
        send(self.theirs, self.theirs, self.sb.at[0], self.sb.at[1], pos.sib).wait_recv()

    def first(self, k):
        pos, mine = self.pos, self.mine
        h0, h1 = self.halves
        z = pos.up(k)
        for j in range(4):
            chip = pos.chip(j)
            mine[z, chip] = (
                mine[z, chip].astype(F32) + self.theirs[z, chip].astype(F32)
            ).astype(mine.dtype)
        there = mine.at[z, pos.pd]
        self.go(send(there.at[h0], self.a0.at[k], self.s0.at[0, k], self.s0.at[1, k], pos.xn))
        if h1 is not None:
            self.go(
                send(there.at[h1], self.a1.at[k], self.s1.at[0, k], self.s1.at[1, k], pos.yn)
            )
        self.go(
            send(
                mine.at[z, pos.px].at[h0],
                self.bx.at[k].at[h0],
                self.dx.at[0, k],
                self.dx.at[1, k],
                pos.xn,
            )
        )
        if h1 is not None:
            self.go(
                send(
                    mine.at[z, pos.py].at[h1],
                    self.by.at[k].at[h1],
                    self.dy.at[0, k],
                    self.dy.at[1, k],
                    pos.yn,
                )
            )

    def landed(self, ref, sems, k):
        send(ref, ref, sems.at[0, k], sems.at[1, k], self.pos.xn).wait_recv()

    def second(self, k):
        pos, mine = self.pos, self.mine
        h0, h1 = self.halves
        z = pos.up(k)
        self.landed(self.a0.at[k], self.s0, k)
        ref = mine.at[z, pos.py]
        ref[h0] = (ref[h0].astype(F32) + self.a0[k].astype(F32)).astype(mine.dtype)
        self.go(
            send(
                ref.at[h0], self.by.at[k].at[h0], self.cy.at[0, k], self.cy.at[1, k], pos.yn
            )
        )
        if h1 is not None:
            self.landed(self.a1.at[k], self.s1, k)
            ref = mine.at[z, pos.px]
            ref[h1] = (ref[h1].astype(F32) + self.a1[k].astype(F32)).astype(mine.dtype)
            self.go(
                send(
                    ref.at[h1], self.bx.at[k].at[h1], self.cx.at[0, k], self.cx.at[1, k], pos.xn
                )
            )

    def third(self, k, total):
        pos = self.pos
        h0, h1 = self.halves
        z = pos.up(k)
        self.landed(self.bx.at[k].at[h0], self.dx, k)
        self.landed(self.by.at[k].at[h0], self.cy, k)
        if h1 is not None:
            self.landed(self.by.at[k].at[h1], self.dy, k)
            self.landed(self.bx.at[k].at[h1], self.cx, k)
        value = (
            self.mine[z, pos.p].astype(F32)
            + self.bx[k].astype(F32)
            + self.by[k].astype(F32)
        )
        if k:
            self.tz[k] = value.astype(self.tz.dtype)
            self.go(
                send(
                    self.tz.at[k],
                    self.z.at[k],
                    self.zs.at[0, k],
                    self.zs.at[1, k],
                    (pos.up(k), pos.s),
                )
            )
        else:
            total[...] = value

    def last(self, total):
        pos = self.pos
        value = total[...]
        for k in range(1, pos.nb):
            self.landed(self.z.at[k], self.zs, k)
            value = value + self.z[k].astype(F32)
        total[...] = value

    def drain(self):
        for copy in self.started:
            copy.wait_send()


def half_shapes(shape, halves):
    def cut(half):
        return tuple(n if h == slice(None) else h.size for n, h in zip(shape, half))

    first = cut(halves[0])
    return first, (first if halves[1] is None else cut(halves[1]))


class RowScatter:
    def __init__(self, pos, partial, out, bufs, sems):
        self.pos, self.partial, self.out = pos, partial, out
        self.mine, self.a0, self.a1, self.bx, self.by, self.far = bufs
        self.sm, self.ld = sems
        self.started = []

    @staticmethod
    def scratch(rows, columns):
        return [
            pltpu.VMEM((4, 2, rows, columns), BF16),
            pltpu.VMEM((rows, columns), BF16),
            pltpu.VMEM((rows, columns), BF16),
            pltpu.VMEM((2, rows, columns), BF16),
            pltpu.VMEM((2, rows, columns), BF16),
            pltpu.VMEM((rows, columns), F32),
            DMA((2, 7)),
            DMA,
        ]

    def go(self, i, src, dst, device):
        copy = send(src, dst, self.sm.at[0, i], self.sm.at[1, i], device)
        copy.start()
        self.started.append(copy)

    def landed(self, i, ref):
        send(ref, ref, self.sm.at[0, i], self.sm.at[1, i], self.pos.xn).wait_recv()

    def begin(self):
        self.local = pltpu.make_async_copy(self.partial, self.mine, self.ld)
        self.local.start()

    def first(self):
        pos, mine = self.pos, self.mine
        self.local.wait()
        self.go(0, mine.at[pos.pd, 0], self.a0, pos.xn)
        self.go(1, mine.at[pos.pd, 1], self.a1, pos.yn)
        self.go(2, mine.at[pos.px, 0], self.bx.at[0], pos.xn)
        self.go(3, mine.at[pos.py, 1], self.by.at[1], pos.yn)

    def second(self):
        pos, mine = self.pos, self.mine
        self.landed(0, self.a0)
        mine[pos.py, 0] = (mine[pos.py, 0].astype(F32) + self.a0[...].astype(F32)).astype(BF16)
        self.go(4, mine.at[pos.py, 0], self.by.at[0], pos.yn)
        self.landed(1, self.a1)
        mine[pos.px, 1] = (mine[pos.px, 1].astype(F32) + self.a1[...].astype(F32)).astype(BF16)
        self.go(5, mine.at[pos.px, 1], self.bx.at[1], pos.xn)

    def third(self):
        pos = self.pos
        self.landed(2, self.bx.at[0])
        self.landed(3, self.by.at[1])
        self.landed(4, self.by.at[0])
        self.landed(5, self.bx.at[1])

        def total(core):
            return (
                self.mine[pos.p, core].astype(F32)
                + self.bx[core].astype(F32)
                + self.by[core].astype(F32)
            )

        self.far[...] = total(1 - pos.c)
        self.go(6, self.far, self.out.at[pos.c], pos.sib)
        self.out[pos.c] = total(pos.c)

    def last(self):
        pos = self.pos
        self.landed(6, self.out.at[1 - pos.c])
        for copy in self.started:
            copy.wait_send()


class JointScatter:
    def __init__(self, pos, partial, bufs, sems):
        self.pos, self.partial = pos, partial
        self.mine, self.theirs, self.got = bufs
        self.sb, self.direct, self.ld = sems
        self.started = []

    @staticmethod
    def scratch(nb, shape):
        return [pltpu.VMEM((nb, 4) + shape, BF16) for _ in range(3)]

    @staticmethod
    def sem_scratch(nb):
        return [DMA((2,)), DMA((2, nb, 4)), DMA]

    def begin(self):
        pos = self.pos
        copy = send(
            self.partial.at[:, :, 1 - pos.c], self.theirs, self.sb.at[0], self.sb.at[1], pos.sib
        )
        copy.start()
        self.started.append(copy)
        self.local = pltpu.make_async_copy(
            self.partial.at[:, :, pos.c], self.mine, self.ld
        )
        self.local.start()

    def first(self):
        pos, mine = self.pos, self.mine
        self.local.wait()
        send(self.theirs, self.theirs, self.sb.at[0], self.sb.at[1], pos.sib).wait_recv()
        mine[...] = (mine[...].astype(F32) + self.theirs[...].astype(F32)).astype(BF16)
        for d in range(pos.nb):
            for k in range(4):
                if d or k:
                    chip = pos.chip(k)
                    copy = send(
                        mine.at[pos.up(d), chip],
                        self.got.at[d, k],
                        self.direct.at[0, d, k],
                        self.direct.at[1, d, k],
                        (pos.up(d), 2 * chip + pos.c),
                    )
                    copy.start()
                    self.started.append(copy)

    def last(self, out):
        pos = self.pos
        for k in range(4):
            value = None
            for d in range(pos.nb):
                if d or k:
                    ref = self.got.at[d, k]
                    send(
                        ref, ref, self.direct.at[0, d, k], self.direct.at[1, d, k], pos.sib
                    ).wait_recv()
                    term = self.got[d, k].astype(F32)
                else:
                    term = self.mine[pos.b, pos.p].astype(F32)
                value = term if value is None else value + term
            out[pos.chip(k)] = value
        for copy in self.started:
            copy.wait_send()


def scatter_all(grad_rows, joint, small, output, expand, reduce, nb):
    arrays = (small, output, expand, reduce)
    shapes = [a.shape[3:] for a in arrays]
    row_shape = grad_rows.shape[2:]
    joint_shape = joint.shape[3:]

    def body(
        rows_ref, joint_ref, small_ref, output_ref, expand_ref, reduce_ref,
        rows_out, joint_out, small_out, output_out, expand_out, reduce_out,
        *scratch,
    ):
        pos = Place(nb)
        scratch = list(scratch)

        def take(n):
            got = scratch[:n]
            del scratch[:n]
            return got

        rows = RowScatter(pos, rows_ref, rows_out, take(6), take(2))
        joints = JointScatter(pos, joint_ref, take(3), take(3))
        outs = (small_out, output_out, expand_out, reduce_out)
        scatters = [
            Scatter(pos, ref, halves_of(ref.shape[3:]), take(8), take(9))
            for ref in (small_ref, output_ref, expand_ref, reduce_ref)
        ]
        greet(same_core(pos) + [pos.sib])
        rows.begin()
        for scatter in scatters:
            scatter.begin()
        joints.begin()
        rows.first()
        order = [k for k in range(1, nb)] + [0]
        for scatter in scatters:
            scatter.joined()
        for k in order:
            for scatter in scatters:
                scatter.first(k)
            if k == order[0]:
                joints.first()
                rows.second()
        for k in order:
            for scatter in scatters:
                scatter.second(k)
        rows.third()
        for k in order:
            for scatter, out in zip(scatters, outs):
                scatter.third(k, out)
        joints.last(joint_out)
        for scatter, out in zip(scatters, outs):
            scatter.last(out)
            scatter.drain()
        rows.last()

    scratch = RowScatter.scratch(*row_shape) + JointScatter.scratch(nb, joint_shape)
    scratch += JointScatter.sem_scratch(nb)
    for array, shape in zip(arrays, shapes):
        scratch += Scatter.scratch(nb, shape, array.dtype, halves_of(shape))
        scratch += Scatter.sem_scratch(nb)
    return pl.pallas_call(
        body,
        out_shape=(
            jax.ShapeDtypeStruct((2,) + row_shape, F32),
            jax.ShapeDtypeStruct((4,) + joint_shape, F32),
        )
        + tuple(jax.ShapeDtypeStruct(shape, F32) for shape in shapes),
        in_specs=[ANY] * 6,
        out_specs=(VM,) * 6,
        scratch_shapes=scratch,
        name="scatter_all",
        compiler_params=pltpu.CompilerParams(
            collective_id=4, has_side_effects=True, vmem_limit_bytes=VMEM_LIMIT
        ),
    )(grad_rows, joint, small, output, expand, reduce)


def plane_on_device(
    inputs,
    cotangent,
    lengths,
    joint_weight,
    output_weight,
    vectors,
    expand_weight,
    expand_bias,
    reduce_weight,
):
    nb = lax.axis_size("batch")
    seq_count, row_count, model_width = inputs.shape
    tokens = seq_count * row_count
    hidden_width = expand_weight.shape[1]
    place = lax.axis_index("seq")
    core, chip = place % 2, place // 2
    width = model_width // 4
    heads = width // HEAD_DIM
    vec = vectors.shape[1]
    per_row = expand_bias.shape[0] // 8
    owners = 8 * nb

    flat_inputs = inputs.reshape(tokens, model_width)
    joint_parts = joint_weight.reshape(-1, 3, 4, width).transpose(2, 0, 1, 3)
    joint_parts = joint_parts.reshape(4, -1, 3 * width)
    small = jnp.concatenate(
        [
            vectors.astype(F32),
            expand_bias.reshape(8, per_row).astype(F32),
            jnp.zeros((8, 128 - vec - per_row), F32),
        ],
        axis=1,
    )
    rows_all, joint_all, small_all, output_all, expand_all, reduce_all = gather_all(
        inputs.astype(BF16), joint_parts, small, output_weight, expand_weight, reduce_weight, nb
    )
    rows_all = rows_all.reshape(8 * row_count, model_width)
    joint_all = joint_all.reshape(model_width, 3 * width)
    full_output = output_all.reshape(model_width, model_width)
    full_expand = expand_all.reshape(model_width, hidden_width)
    full_reduce = reduce_all.reshape(hidden_width, model_width)
    small_all = small_all.reshape(owners, 8, 128)
    vector_rows = small_all[:, :, :vec].transpose(1, 0, 2).reshape(8, model_width)
    full_bias = small_all[:, :, vec : vec + per_row].reshape(hidden_width)

    own_bias = lax.dynamic_slice_in_dim(vector_rows[2:4], chip * width, width, 1)
    bias = jnp.concatenate([own_bias[0], jnp.zeros((width,), F32), own_bias[1]])[None]
    length = lax.dynamic_slice_in_dim(lengths, core, 1)
    context, qkv, logs = attend(length, rows_all, joint_all, bias, heads)
    mixed = plane_exchange(context.reshape(4, 2, row_count, width), 2, "context_exchange")
    context_low = mixed.transpose(1, 2, 0, 3).reshape(tokens, model_width)

    branch = jnp.dot(context_low, full_output, preferred_element_type=F32) + vector_rows[4]
    first, first_normed, first_inverse = layer_norm(
        flat_inputs + branch, vector_rows[0], vector_rows[1]
    )
    first_low = first.astype(BF16)
    before_gelu = jnp.dot(first_low, full_expand, preferred_element_type=F32) + full_bias
    hidden_low = gelu_value(before_gelu).astype(BF16)
    feed = jnp.dot(hidden_low, full_reduce, preferred_element_type=F32) + vector_rows[7]
    result, second_normed, second_inverse = layer_norm(first + feed, vector_rows[5], vector_rows[6])

    own_places = place * row_count + jnp.arange(row_count, dtype=jnp.int32)
    row_mask = (own_places[None, :] < lengths[:, None]).reshape(tokens, 1).astype(F32)
    grad_res = cotangent.reshape(tokens, model_width) * row_mask
    grad_second, grad_gain_two, grad_shift_two = norm_back(
        grad_res, second_normed, second_inverse, vector_rows[5]
    )
    grad_feed_low = grad_second.astype(BF16)
    grad_reduce = jnp.dot(hidden_low.T, grad_feed_low, preferred_element_type=F32)
    grad_hidden = jnp.dot(
        grad_feed_low, full_reduce.T, preferred_element_type=F32
    ) * gelu_slope(before_gelu)
    grad_hidden_low = grad_hidden.astype(BF16)
    grad_expand = jnp.dot(first_low.T, grad_hidden_low, preferred_element_type=F32)
    grad_bias = jnp.sum(grad_hidden_low.astype(F32), axis=0)
    grad_first = grad_second + jnp.dot(
        grad_hidden_low, full_expand.T, preferred_element_type=F32
    )
    grad_resid, grad_gain_one, grad_shift_one = norm_back(
        grad_first, first_normed, first_inverse, vector_rows[0]
    )
    grad_branch_low = grad_resid.astype(BF16)
    grad_output = jnp.dot(context_low.T, grad_branch_low, preferred_element_type=F32)
    grad_context_low = jnp.dot(
        grad_branch_low, full_output.T, preferred_element_type=F32
    ).astype(BF16)

    parts = grad_context_low.reshape(seq_count, row_count, 4, width).transpose(2, 0, 1, 3)
    grad_context = plane_exchange(parts, 3, "gradient_exchange").reshape(8 * row_count, width)
    grad_rows, grad_joint, sums = attend_back(
        length, rows_all, joint_all, qkv, logs, grad_context, heads
    )

    def spread(own):
        return lax.dynamic_update_slice_in_dim(
            jnp.zeros((model_width,), F32), own, chip * width, 0
        )

    grad_vectors = jnp.stack(
        [
            grad_gain_one,
            grad_shift_one,
            spread(sums[0, :width]),
            spread(sums[0, 2 * width :]),
            jnp.sum(grad_branch_low.astype(F32), axis=0),
            grad_gain_two,
            grad_shift_two,
            jnp.sum(grad_feed_low.astype(F32), axis=0),
        ]
    )
    grad_small = jnp.concatenate(
        [
            grad_vectors.reshape(8, owners, vec).transpose(1, 0, 2),
            grad_bias.reshape(owners, 8, per_row),
            jnp.zeros((owners, 8, 128 - vec - per_row), F32),
        ],
        axis=2,
    )

    def split(partial):
        return partial.reshape((nb, 4, 2, partial.shape[0] // owners) + partial.shape[1:])

    rows_sum, joint_sum, small_sum, output_sum, expand_sum, reduce_sum = scatter_all(
        grad_rows.reshape(4, 2, row_count, model_width),
        split(grad_joint),
        grad_small.reshape(nb, 4, 2, 8, 128),
        split(grad_output.astype(BF16)),
        split(grad_expand.astype(BF16)),
        split(grad_reduce.astype(BF16)),
        nb,
    )
    joint_sum = joint_sum.reshape(4, -1, 3, width).transpose(1, 2, 0, 3)
    return (
        result.reshape(seq_count, row_count, model_width),
        grad_resid.reshape(seq_count, row_count, model_width) + rows_sum,
        joint_sum.reshape(-1, 3 * model_width),
        output_sum,
        small_sum[:, :vec],
        expand_sum,
        small_sum[:, vec : vec + per_row].reshape(-1),
        reduce_sum,
    )


def plane_fits(mesh, inputs, expand_bias, expand_weight):
    return (
        mesh.shape["seq"] == 8
        and inputs[0] == 2 * mesh.shape["batch"]
        and HEADS % 4 == 0
        and inputs[2] == HEADS * HEAD_DIM
        and inputs[1] % (8 * 16) == 0
        and expand_weight[0] % (8 * mesh.shape["seq"] * mesh.shape["batch"]) == 0
        and expand_bias[0] % (8 * mesh.shape["seq"] * mesh.shape["batch"]) == 0
        and (expand_weight[0] + expand_bias[0] // 8) <= 128 * mesh.shape["seq"] * mesh.shape["batch"]
    )


def solution(mesh):
    def program(*args):
        fits = plane_fits(mesh, args[0].shape, args[7].shape, args[6].shape)
        return jax.shard_map(
            plane_on_device if fits else general_on_device,
            mesh=mesh,
            in_specs=(
                P("batch", "seq", None),
                P("batch", "seq", None),
                P("batch"),
                P(("batch", "seq"), None),
                P(("batch", "seq"), None),
                P(None, ("batch", "seq")),
                P(("batch", "seq"), None),
                P(("batch", "seq")),
                P(("batch", "seq"), None),
            ),
            out_specs=(
                P("batch", "seq", None),
                P("batch", "seq", None),
                P(("batch", "seq"), None),
                P(("batch", "seq"), None),
                P(None, ("batch", "seq")),
                P(("batch", "seq"), None),
                P(("batch", "seq")),
                P(("batch", "seq"), None),
            ),
            check_vma=False,
        )(*args)

    return program
```

```python
import math

import jax
import jax.numpy as jnp
from jax import lax
from jax.experimental import pallas as pl
from jax.experimental.pallas import tpu as pltpu
from jax.sharding import PartitionSpec as P

HEADS = 12
HEAD_DIM = 64


EPSILON = 1e-12
SCORE_SCALE = 0.125
NEG_FILL = -1e30
HALF_ROOT = 0.7071067811865476
INV_ROOT_TAU = 0.3989422804014327
block_limit = 256


def layer_norm(residual, norm_gain, norm_shift):
    centered = residual - jnp.mean(residual, axis=-1, keepdims=True)
    inverse = lax.rsqrt(jnp.mean(centered * centered, axis=-1, keepdims=True) + EPSILON)
    normed = centered * inverse
    return (normed * norm_gain + norm_shift, normed, inverse)


def norm_back(grad_out, normed, inverse, norm_gain):
    grad_normed = grad_out * norm_gain
    mean_grad = jnp.mean(grad_normed, axis=-1, keepdims=True)
    mean_proj = jnp.mean(grad_normed * normed, axis=-1, keepdims=True)
    grad_in = inverse * (grad_normed - mean_grad - normed * mean_proj)
    return (grad_in, jnp.sum(grad_out * normed, axis=0), jnp.sum(grad_out, axis=0))


def gelu_value(before_gelu):
    return 0.5 * before_gelu * (1.0 + lax.erf(before_gelu * HALF_ROOT))


def gelu_slope(before_gelu):
    return (
        0.5 * (1.0 + lax.erf(before_gelu * HALF_ROOT))
        + before_gelu * jnp.exp(-0.5 * before_gelu * before_gelu) * INV_ROOT_TAU
    )


def over_blocks(piece_rows, block_fn, carried):
    block_size = math.gcd(piece_rows, block_limit)

    def run_block(block_index, current):
        return block_fn(current, block_index * block_size, block_size)

    return lax.fori_loop(0, piece_rows // block_size, run_block, carried)


def head_scores(left_heads, right_heads, right_places, lengths):
    scores = (
        jnp.einsum("sqhd,skhd->shqk", left_heads, right_heads, preferred_element_type=jnp.float32)
        * SCORE_SCALE
    )
    allowed = right_places[None, :] < lengths[:, None]
    return jnp.where(allowed[:, None, None, :], scores, NEG_FILL)


def cut_heads(gathered_piece, offset, block_size, head_count):
    sliced = lax.dynamic_slice_in_dim(gathered_piece, offset, block_size, 1)
    return sliced.reshape(sliced.shape[0], block_size, head_count, -1)


def gather_attention(joint_weight, output_weight, vectors):
    return (
        lax.all_gather(joint_weight, ("batch", "seq"), axis=0, tiled=True),
        lax.all_gather(output_weight, ("batch", "seq"), axis=0, tiled=True),
        lax.all_gather(vectors, ("batch", "seq"), axis=1, tiled=True),
    )


def gather_feed(expand_weight, reduce_weight, expand_bias):
    return (
        lax.all_gather(expand_weight, ("batch", "seq"), axis=0, tiled=True),
        lax.all_gather(reduce_weight, ("batch", "seq"), axis=0, tiled=True),
        lax.all_gather(expand_bias, ("batch", "seq"), axis=0, tiled=True),
    )


def general_on_device(
    inputs,
    cotangent,
    lengths,
    joint_weight,
    output_weight,
    vectors,
    expand_weight,
    expand_bias,
    reduce_weight,
):
    seq_count, row_count, model_width = inputs.shape
    head_count = HEADS
    head_size = HEAD_DIM
    tokens = seq_count * row_count
    head_shape = (seq_count, row_count, head_count, head_size)
    own_places = lax.axis_index("seq") * row_count + jnp.arange(row_count, dtype=jnp.int32)
    row_valid = own_places[None, :] < lengths[:, None]
    row_mask = row_valid.reshape(tokens, 1).astype(jnp.float32)
    full_joint, full_output, full_vectors = gather_attention(joint_weight, output_weight, vectors)
    vector_rows = full_vectors.astype(jnp.float32)
    flat_inputs = inputs.reshape(tokens, model_width)
    input_low = flat_inputs.astype(jnp.bfloat16)
    projected = jnp.dot(input_low, full_joint, preferred_element_type=jnp.float32)
    query_low = (projected[:, :model_width] + vector_rows[2]).astype(jnp.bfloat16)
    key_low = projected[:, model_width : 2 * model_width].astype(jnp.bfloat16)
    value_low = (projected[:, 2 * model_width :] + vector_rows[3]).astype(jnp.bfloat16)
    query_heads = query_low.reshape(head_shape)
    key_rows = key_low.reshape(seq_count, row_count, model_width)
    value_rows = value_low.reshape(seq_count, row_count, model_width)
    start_state = (
        jnp.full((seq_count, head_count, row_count), NEG_FILL, jnp.float32),
        jnp.zeros((seq_count, head_count, row_count), jnp.float32),
        jnp.zeros(head_shape, jnp.float32),
    )
    key_piece = lax.all_gather(key_rows, "seq", axis=1, tiled=True)
    value_piece = lax.all_gather(value_rows, "seq", axis=1, tiled=True)

    def forward_score_block(current, offset, block_size):
        running_max, running_sum, summed = current
        key_heads = cut_heads(key_piece, offset, block_size, head_count)
        value_heads = cut_heads(value_piece, offset, block_size, head_count)
        key_places = offset + jnp.arange(block_size, dtype=jnp.int32)
        scores = head_scores(query_heads, key_heads, key_places, lengths)
        new_max = jnp.maximum(running_max, jnp.max(scores, axis=-1))
        factor = jnp.exp(running_max - new_max)
        exp_scores = jnp.exp(scores - new_max[..., None])
        running_sum = running_sum * factor + jnp.sum(exp_scores, axis=-1)
        update = jnp.einsum(
            "shqk,skhd->sqhd",
            exp_scores.astype(jnp.bfloat16),
            value_heads,
            preferred_element_type=jnp.float32,
        )
        summed = summed * jnp.transpose(factor, (0, 2, 1))[..., None] + update
        return (new_max, running_sum, summed)

    running_max, running_sum, summed = over_blocks(
        key_piece.shape[1], forward_score_block, start_state
    )
    attended = summed / jnp.transpose(running_sum, (0, 2, 1))[..., None]
    log_total = jnp.transpose(running_max + jnp.log(running_sum), (0, 2, 1))
    context_low = attended.reshape(tokens, model_width).astype(jnp.bfloat16)
    branch = jnp.dot(context_low, full_output, preferred_element_type=jnp.float32) + vector_rows[4]
    first, first_normed, first_inverse = layer_norm(
        flat_inputs + branch, vector_rows[0], vector_rows[1]
    )
    first_low = first.astype(jnp.bfloat16)
    full_expand, full_reduce, full_bias = gather_feed(expand_weight, reduce_weight, expand_bias)
    before_gelu = jnp.dot(
        first_low, full_expand, preferred_element_type=jnp.float32
    ) + full_bias.astype(jnp.float32)
    hidden_low = gelu_value(before_gelu).astype(jnp.bfloat16)
    feed = jnp.dot(hidden_low, full_reduce, preferred_element_type=jnp.float32) + vector_rows[7]
    result, second_normed, second_inverse = layer_norm(first + feed, vector_rows[5], vector_rows[6])
    full_expand, full_reduce, full_bias = gather_feed(expand_weight, reduce_weight, expand_bias)
    full_joint, full_output, full_vectors = gather_attention(joint_weight, output_weight, vectors)
    grad_res = cotangent.reshape(tokens, model_width) * row_mask
    grad_second, grad_gain_two, grad_shift_two = norm_back(
        grad_res, second_normed, second_inverse, vector_rows[5]
    )
    grad_feed_low = grad_second.astype(jnp.bfloat16)
    grad_reduce_local = jnp.dot(hidden_low.T, grad_feed_low, preferred_element_type=jnp.float32)
    grad_hidden = jnp.dot(
        grad_feed_low, full_reduce.T, preferred_element_type=jnp.float32
    ) * gelu_slope(before_gelu)
    grad_hidden_low = grad_hidden.astype(jnp.bfloat16)
    grad_expand_local = jnp.dot(first_low.T, grad_hidden_low, preferred_element_type=jnp.float32)
    grad_bias_local = jnp.sum(grad_hidden_low.astype(jnp.float32), axis=0)
    grad_first = grad_second + jnp.dot(
        grad_hidden_low, full_expand.T, preferred_element_type=jnp.float32
    )
    grad_resid, grad_gain_one, grad_shift_one = norm_back(
        grad_first, first_normed, first_inverse, vector_rows[0]
    )
    grad_branch_low = grad_resid.astype(jnp.bfloat16)
    grad_output_local = jnp.dot(context_low.T, grad_branch_low, preferred_element_type=jnp.float32)
    grad_context_low = jnp.dot(
        grad_branch_low, full_output.T, preferred_element_type=jnp.float32
    ).astype(jnp.bfloat16)
    grad_context_heads = grad_context_low.reshape(head_shape)
    row_delta = jnp.sum(grad_context_heads.astype(jnp.float32) * attended, axis=-1)
    log_heads = jnp.transpose(log_total, (0, 2, 1))
    delta_heads = jnp.transpose(row_delta, (0, 2, 1))
    query_key_piece = lax.all_gather(key_rows, "seq", axis=1, tiled=True)
    query_value_piece = lax.all_gather(value_rows, "seq", axis=1, tiled=True)

    def query_score_block(current, offset, block_size):
        key_heads = cut_heads(query_key_piece, offset, block_size, head_count)
        value_heads = cut_heads(query_value_piece, offset, block_size, head_count)
        key_places = offset + jnp.arange(block_size, dtype=jnp.int32)
        scores = head_scores(query_heads, key_heads, key_places, lengths)
        softmax_rows = jnp.exp(scores - log_heads[..., None])
        grad_probs = jnp.einsum(
            "sqhd,skhd->shqk", grad_context_heads, value_heads, preferred_element_type=jnp.float32
        )
        grad_scores = (softmax_rows * (grad_probs - delta_heads[..., None])).astype(jnp.bfloat16)
        return (
            current
            + jnp.einsum(
                "shqk,skhd->sqhd", grad_scores, key_heads, preferred_element_type=jnp.float32
            )
            * SCORE_SCALE
        )

    grad_query = over_blocks(
        query_key_piece.shape[1], query_score_block, jnp.zeros(head_shape, jnp.float32)
    )
    own_keys = key_low.reshape(head_shape)
    own_values = value_low.reshape(head_shape)
    query_rows = query_low.reshape(seq_count, row_count, model_width)
    grad_context_rows = grad_context_low.reshape(seq_count, row_count, model_width)
    zero_heads = jnp.zeros(head_shape, jnp.float32)
    query_piece = lax.all_gather(query_rows.astype(jnp.float32), "seq", axis=1, tiled=True).astype(
        jnp.bfloat16
    )
    grad_piece = lax.all_gather(
        grad_context_rows.astype(jnp.float32), "seq", axis=1, tiled=True
    ).astype(jnp.bfloat16)
    log_piece = lax.all_gather(log_total, "seq", axis=1, tiled=True)
    delta_piece = lax.all_gather(row_delta, "seq", axis=1, tiled=True)

    def key_score_block(current, offset, block_size):
        grad_key, grad_value = current
        query_block = cut_heads(query_piece, offset, block_size, head_count)
        grad_block = cut_heads(grad_piece, offset, block_size, head_count)
        log_block = jnp.transpose(
            lax.dynamic_slice_in_dim(log_piece, offset, block_size, 1), (0, 2, 1)
        )
        delta_block = jnp.transpose(
            lax.dynamic_slice_in_dim(delta_piece, offset, block_size, 1), (0, 2, 1)
        )
        scores = head_scores(query_block, own_keys, own_places, lengths)
        softmax_rows = jnp.exp(scores - log_block[..., None])
        grad_value = grad_value + jnp.einsum(
            "shqk,sqhd->skhd",
            softmax_rows.astype(jnp.bfloat16),
            grad_block,
            preferred_element_type=jnp.float32,
        )
        grad_probs = jnp.einsum(
            "sqhd,skhd->shqk", grad_block, own_values, preferred_element_type=jnp.float32
        )
        grad_scores = (softmax_rows * (grad_probs - delta_block[..., None])).astype(jnp.bfloat16)
        grad_key = (
            grad_key
            + jnp.einsum(
                "shqk,sqhd->skhd", grad_scores, query_block, preferred_element_type=jnp.float32
            )
            * SCORE_SCALE
        )
        return (grad_key, grad_value)

    grad_key, grad_value = over_blocks(
        query_piece.shape[1], key_score_block, (zero_heads, zero_heads)
    )
    grad_query_low = grad_query.reshape(tokens, model_width).astype(jnp.bfloat16)
    grad_key_low = grad_key.reshape(tokens, model_width).astype(jnp.bfloat16)
    grad_value_low = grad_value.reshape(tokens, model_width).astype(jnp.bfloat16)
    grad_projected = jnp.concatenate([grad_query_low, grad_key_low, grad_value_low], axis=1)
    grad_joint_local = jnp.dot(input_low.T, grad_projected, preferred_element_type=jnp.float32)
    grad_inputs = grad_resid + jnp.dot(
        grad_projected, full_joint.T, preferred_element_type=jnp.float32
    )
    grad_vector_local = jnp.stack(
        [
            grad_gain_one,
            grad_shift_one,
            jnp.sum(grad_query_low.astype(jnp.float32), axis=0),
            jnp.sum(grad_value_low.astype(jnp.float32), axis=0),
            jnp.sum(grad_branch_low.astype(jnp.float32), axis=0),
            grad_gain_two,
            grad_shift_two,
            jnp.sum(grad_feed_low.astype(jnp.float32), axis=0),
        ],
        axis=0,
    )
    every_grad = (
        lax.psum_scatter(grad_joint_local, ("batch", "seq"), scatter_dimension=0, tiled=True),
        lax.psum_scatter(grad_output_local, ("batch", "seq"), scatter_dimension=0, tiled=True),
        lax.psum_scatter(grad_vector_local, ("batch", "seq"), scatter_dimension=1, tiled=True),
        lax.psum_scatter(grad_expand_local, ("batch", "seq"), scatter_dimension=0, tiled=True),
        lax.psum_scatter(grad_reduce_local, ("batch", "seq"), scatter_dimension=0, tiled=True),
        lax.psum_scatter(grad_bias_local, ("batch", "seq"), scatter_dimension=0, tiled=True),
    )
    summed_grads = (
        every_grad[0],
        every_grad[1],
        every_grad[2],
        every_grad[3],
        every_grad[5],
        every_grad[4],
    )
    return (
        result.reshape(seq_count, row_count, model_width),
        grad_inputs.reshape(seq_count, row_count, model_width),
        summed_grads[0],
        summed_grads[1],
        summed_grads[2],
        summed_grads[3],
        summed_grads[4],
        summed_grads[5],
    )


MESH = pl.DeviceIdType.MESH
ANY = pl.BlockSpec(memory_space=pl.ANY)
VM = pl.BlockSpec(memory_space=pltpu.VMEM)
SM = pl.BlockSpec(memory_space=pltpu.SMEM)
DMA = pltpu.SemaphoreType.DMA
VMEM_LIMIT = 60 << 20
F32 = jnp.float32
BF16 = jnp.bfloat16


def send(src, dst, send_sem, recv_sem, device):
    return pltpu.make_async_remote_copy(
        src_ref=src,
        dst_ref=dst,
        send_sem=send_sem,
        recv_sem=recv_sem,
        device_id=device,
        device_id_type=MESH,
    )


AHEAD = 3


class Place:
    def __init__(self, nb):
        self.nb = nb
        self.b = lax.axis_index("batch")
        self.s = lax.axis_index("seq")
        self.c = self.s % 2
        self.p = self.s // 2
        x, y = self.p % 2, self.p // 2
        self.px = 2 * y + (1 - x)
        self.py = 2 * (1 - y) + x
        self.pd = 2 * (1 - y) + (1 - x)
        self.sib = (self.b, 2 * self.p + 1 - self.c)
        self.xn = (self.b, 2 * self.px + self.c)
        self.yn = (self.b, 2 * self.py + self.c)

    def chip(self, step):
        return (self.p, self.px, self.py, self.pd)[step]

    def up(self, step):
        return (self.b + step) % self.nb

    def down(self, step):
        return (self.b + self.nb - step) % self.nb


def greet(devices):
    barrier = pltpu.get_barrier_semaphore()
    for device in devices:
        pl.semaphore_signal(barrier, inc=1, device_id=device, device_id_type=MESH)
    pl.semaphore_wait(barrier, len(devices))


def greet_near(pos):
    barrier = pltpu.get_barrier_semaphore()

    def signal(device):
        pl.semaphore_signal(barrier, inc=1, device_id=device, device_id_type=MESH)

    for device in plane_others(pos):
        signal(device)
    last = pos.nb - 1
    guarded(pos.b < last, lambda: signal(((pos.b + 1) % pos.nb, pos.s)))
    guarded(pos.b > 0, lambda: signal(((pos.b + last) % pos.nb, pos.s)))
    beside = jnp.where(pos.b < last, 1, 0) + jnp.where(pos.b > 0, 1, 0)
    pl.semaphore_wait(barrier, 7 + beside)


def same_core(pos):
    return [
        (pos.up(d), 2 * pos.chip(k) + pos.c)
        for d in range(pos.nb)
        for k in range(4)
        if d or k
    ]


def plane_others(pos):
    return [
        (pos.b, 2 * pos.chip(k) + (pos.c if j == 0 else 1 - pos.c))
        for k in range(4)
        for j in range(2)
        if k or j
    ]


def guarded(condition, action):
    pl.when(condition)(action)


class Chain:
    def __init__(self, pos, mine, spot, sems):
        self.pos, self.mine, self.spot = pos, mine, spot
        self.up, self.down = sems

    @staticmethod
    def scratch(nb):
        return [DMA((2, nb)), DMA((2, nb))]

    def copy(self, src, z, sems, hop, there):
        pos = self.pos
        return send(src, self.spot(z), sems.at[0, hop], sems.at[1, hop], (there, pos.s))

    def moves(self, hop):
        pos = self.pos
        last = pos.nb - 1
        low, high = (pos.b - hop + 1 + pos.nb) % pos.nb, (pos.b + hop - 1) % pos.nb
        above, below = (pos.b + 1) % pos.nb, (pos.b + last) % pos.nb
        own = hop == 1
        return (
            (
                (pos.b >= hop - 1) & (pos.b < last),
                self.copy(self.mine if own else self.spot(low), low, self.up, hop, above),
            ),
            (
                (pos.b + hop - 1 < pos.nb) & (pos.b > 0),
                self.copy(self.mine if own else self.spot(high), high, self.down, hop, below),
            ),
        )

    def start(self, hop=1):
        for made, copy in self.moves(hop):
            guarded(made, copy.start)

    def hop(self, hop):
        pos = self.pos
        low, high = (pos.b - hop + pos.nb) % pos.nb, (pos.b + hop) % pos.nb
        for made, z, sems in (
            (pos.b >= hop, low, self.up),
            (pos.b + hop < pos.nb, high, self.down),
        ):
            guarded(made, self.copy(self.spot(z), z, sems, hop, pos.b).wait_recv)
        if hop < pos.nb - 1:
            self.start(hop + 1)

    def drain(self):
        for hop in range(1, self.pos.nb):
            for made, copy in self.moves(hop):
                guarded(made, copy.wait_send)


class Gather:
    def __init__(self, pos, shard, out, halves, sems):
        self.pos, self.shard, self.out, self.halves = pos, shard, out, halves
        self.xs, self.ys, self.f0, self.f1, self.sb, self.local_sem = sems[:6]
        self.chain = Chain(pos, shard, lambda z: out.at[z, pos.p, pos.c], sems[6:])
        self.started = []

    @staticmethod
    def scratch(nb):
        return [DMA((2, nb)) for _ in range(5)] + [DMA] + Chain.scratch(nb)

    def z(self, k):
        return jnp.where(k <= self.pos.b, self.pos.b - k, k)

    def go(self, copy):
        copy.start()
        self.started.append(copy)

    def own(self):
        pos = self.pos
        self.local = pltpu.make_async_copy(
            self.shard, self.out.at[pos.b, pos.p, pos.c], self.local_sem
        )
        self.local.start()

    def plane(self, k):
        pos = self.pos
        there = self.out.at[self.z(k), pos.p, pos.c]
        src = there if k else self.shard
        self.go(send(src, there, self.xs.at[0, k], self.xs.at[1, k], pos.xn))
        self.go(send(src, there, self.ys.at[0, k], self.ys.at[1, k], pos.yn))

    def land(self, sems, k, chip, half=None):
        pos = self.pos
        ref = self.out.at[self.z(k), chip, pos.c]
        if half is not None:
            ref = ref.at[half]
        return send(ref, ref, sems.at[0, k], sems.at[1, k], pos.xn)

    def forward(self, k):
        pos = self.pos
        h0, h1 = self.halves
        self.land(self.xs, k, pos.px).wait_recv()
        ref = self.out.at[self.z(k), pos.px, pos.c].at[h0]
        self.go(send(ref, ref, self.f0.at[0, k], self.f0.at[1, k], pos.yn))
        self.land(self.ys, k, pos.py).wait_recv()
        if h1 is not None:
            ref = self.out.at[self.z(k), pos.py, pos.c].at[h1]
            self.go(send(ref, ref, self.f1.at[0, k], self.f1.at[1, k], pos.xn))

    def sibling(self, k):
        pos = self.pos
        h0, h1 = self.halves
        self.land(self.f0, k, pos.pd, h0).wait_recv()
        if h1 is not None:
            self.land(self.f1, k, pos.pd, h1).wait_recv()
        if k == 0:
            self.local.wait()
        ref = self.out.at[self.z(k), :, pos.c]
        self.go(send(ref, ref, self.sb.at[0, k], self.sb.at[1, k], pos.sib))

    def finish(self):
        pos = self.pos
        for k in range(pos.nb):
            ref = self.out.at[self.z(k), :, 1 - pos.c]
            send(ref, ref, self.sb.at[0, k], self.sb.at[1, k], pos.sib).wait_recv()
        for copy in self.started:
            copy.wait_send()
        self.chain.drain()


class InputExchange:
    def __init__(self, pos, rows, out, sems):
        self.pos, self.rows, self.out, self.sems = pos, rows, out, sems
        self.started = []

    @staticmethod
    def scratch():
        return [DMA((2, 2)), DMA((2, 2)), DMA((2, 2)), DMA((2,)), DMA]

    def go(self, copy):
        copy.start()
        self.started.append(copy)

    def start(self):
        pos, (xs, ys, _, sb, local) = self.pos, self.sems
        there = self.out.at[pos.p, pos.c]
        for sems, chip in ((xs, pos.px), (ys, pos.py)):
            for j in range(2):
                self.go(
                    send(
                        self.rows.at[j],
                        there,
                        sems.at[0, j],
                        sems.at[1, pos.c],
                        (pos.b, 2 * chip + j),
                    )
                )
        self.go(send(self.rows.at[1 - pos.c], there, sb.at[0], sb.at[1], pos.sib))
        self.local = pltpu.make_async_copy(self.rows.at[pos.c], there, local)
        self.local.start()

    def landed(self, sems, j, chip):
        ref = self.out.at[chip, j]
        send(ref, ref, sems.at[0, j], sems.at[1, j], self.pos.xn).wait_recv()

    def forward(self):
        pos, (xs, ys, fs, _, _) = self.pos, self.sems
        self.landed(xs, 0, pos.px)
        ref = self.out.at[pos.px, 0]
        self.go(send(ref, ref, fs.at[0, 0], fs.at[1, 0], pos.yn))
        self.landed(ys, 1, pos.py)
        ref = self.out.at[pos.py, 1]
        self.go(send(ref, ref, fs.at[0, 1], fs.at[1, 1], pos.xn))

    def finish(self):
        pos, (xs, ys, fs, sb, _) = self.pos, self.sems
        self.landed(xs, 1, pos.px)
        self.landed(ys, 0, pos.py)
        self.landed(fs, 0, pos.pd)
        self.landed(fs, 1, pos.pd)
        ref = self.out.at[pos.p, 1 - pos.c]
        send(ref, ref, sb.at[0], sb.at[1], pos.sib).wait_recv()
        self.local.wait()

    def drain(self):
        for copy in self.started:
            copy.wait_send()


class JointGather:
    def __init__(self, pos, parts, out, sems):
        self.pos, self.parts, self.out = pos, parts, out
        self.direct, self.sb, self.local_sem = sems[:3]
        self.chain = Chain(
            pos, out.at[pos.b, :, pos.c], lambda z: out.at[z, :, pos.c], sems[3:]
        )

    @staticmethod
    def scratch(nb):
        return [DMA((2, 4)), DMA((2,)), DMA] + Chain.scratch(nb)

    def start(self):
        pos = self.pos
        there = self.out.at[pos.b, pos.p, pos.c]
        self.started = [
            send(
                self.parts.at[pos.chip(k)],
                there,
                self.direct.at[0, k],
                self.direct.at[1, k],
                (pos.b, 2 * pos.chip(k) + pos.c),
            )
            for k in range(1, 4)
        ]
        for copy in self.started:
            copy.start()
        self.local = pltpu.make_async_copy(self.parts.at[pos.p], there, self.local_sem)
        self.local.start()

    def own(self):
        pos = self.pos
        for k in range(1, 4):
            ref = self.out.at[pos.b, pos.chip(k), pos.c]
            send(ref, ref, self.direct.at[0, k], self.direct.at[1, k], pos.sib).wait_recv()
        self.local.wait()
        self.chain.start()

    def sibling(self):
        pos = self.pos
        ref = self.out.at[:, :, pos.c]
        copy = send(ref, ref, self.sb.at[0], self.sb.at[1], pos.sib)
        copy.start()
        self.started.append(copy)

    def finish(self):
        pos = self.pos
        ref = self.out.at[:, :, 1 - pos.c]
        send(ref, ref, self.sb.at[0], self.sb.at[1], pos.sib).wait_recv()

    def drain(self):
        for copy in self.started:
            copy.wait_send()
        self.chain.drain()


class ContextExchange:
    def __init__(self, pos, parts, out, sems):
        self.pos, self.parts, self.out = pos, parts, out
        self.sems, self.local_sem = sems

    @staticmethod
    def scratch():
        return [DMA((2, 8)), DMA]

    def pairs(self):
        pos = self.pos
        for k in range(4):
            for j in range(2):
                if k or j:
                    yield 2 * k + j, pos.chip(k), pos.c if j == 0 else 1 - pos.c

    def start(self):
        pos, sems = self.pos, self.sems
        there = self.out.at[pos.p, pos.c]
        self.copies = [
            send(
                self.parts.at[chip, core],
                there,
                sems.at[0, i],
                sems.at[1, i],
                (pos.b, 2 * chip + core),
            )
            for i, chip, core in self.pairs()
        ]
        for copy in self.copies:
            copy.start()
        self.local = pltpu.make_async_copy(
            self.parts.at[pos.p, pos.c], there, self.local_sem
        )
        self.local.start()

    def arrive(self):
        for i, chip, core in self.pairs():
            ref = self.out.at[chip, core]
            send(ref, ref, self.sems.at[0, i], self.sems.at[1, i], self.pos.sib).wait_recv()
        self.local.wait()

    def drain(self):
        for copy in self.copies:
            copy.wait_send()


def gather_attend(length, rows, joint, small, output, expand, reduce, nb, model_width, heads):
    _, count, _ = rows.shape
    shard = model_width // (8 * nb)
    width = heads * HEAD_DIM
    size = 8 * count

    def body(
        length_ref, rows_ref, joint_ref, small_ref, output_ref, expand_ref, reduce_ref,
        rows_out, weight_out, qkv_out, log_out, context_out,
        small_out, output_out, expand_out, reduce_out,
        joint_all, context,
        *scratch,
    ):
        pos = Place(nb)
        scratch = list(scratch)

        def take(n):
            got = scratch[:n]
            del scratch[:n]
            return got

        exchange = InputExchange(pos, rows_ref, rows_out, take(5))
        joints = JointGather(pos, joint_ref, joint_all, take(5))
        mixing = ContextExchange(pos, context, context_out, take(2))
        outputs, expands, reduces, smalls = (
            Gather(pos, part, out, halves_of(part.shape), take(8))
            for part, out in (
                (output_ref, output_out),
                (expand_ref, expand_out),
                (reduce_ref, reduce_out),
                (small_ref, small_out),
            )
        )
        gathers = (outputs, expands, reduces, smalls)
        units = [
            (unit, k)
            for k in range(nb)
            for unit in ((expands,), (reduces,), (outputs, smalls))
        ]

        def plane(n):
            if n < len(units):
                unit, k = units[n]
                for gather in unit:
                    gather.plane(k)

        def forward(n):
            unit, k = units[n]
            for gather in unit:
                gather.forward(k)

        def sibling(n):
            if 0 <= n < len(units):
                unit, k = units[n]
                for gather in unit:
                    gather.sibling(k)

        def hop(t):
            if t < nb:
                for gather in gathers:
                    gather.chain.hop(t)

        def step(n):
            if (n + AHEAD) % 3 == 0 and n + AHEAD > 3:
                hop((n + AHEAD) // 3)
            forward(n)
            plane(n + AHEAD)
            sibling(n - 2)

        greet_near(pos)
        exchange.start()
        joints.start()
        for gather in gathers:
            gather.own()
            gather.chain.start()
        joints.own()
        exchange.forward()
        for n in range(AHEAD):
            plane(n)
        hop(1)
        for n in range(nb - 1):
            step(n)
            joints.chain.hop(n + 1)
        joints.sibling()
        step(nb - 1)
        exchange.finish()
        joints.finish()

        parts = joint_all[...]
        weight_out[...] = parts[:, :, :, :shard].reshape(model_width, 3 * width)
        bias = jnp.sum(
            parts[:, :, :, shard:].astype(F32).reshape(-1, 3 * width), axis=0, keepdims=True
        )

        def project(i, _):
            at = pl.ds(pl.multiple_of(i * 2 * count, 2 * count), 2 * count)
            qkv_out[at, :] = (
                jnp.dot(
                    rows_out[i].reshape(2 * count, model_width),
                    weight_out[...],
                    preferred_element_type=F32,
                )
                + bias
            ).astype(BF16)
            return 0

        lax.fori_loop(0, 4, project, 0)
        attend = attend_block(length_ref[0], qkv_out, log_out, context, heads, count)
        for i in range(4):
            step(nb + i)
            attend(i)
        mixing.start()
        for n in range(nb + 4, len(units) + 2):
            if n < len(units):
                step(n)
            else:
                sibling(n - 2)
        mixing.arrive()
        for gather in gathers:
            gather.finish()
        exchange.drain()
        joints.drain()
        mixing.drain()

    def shape(part):
        return jax.ShapeDtypeStruct((nb, 4, 2) + part.shape, part.dtype)

    return pl.pallas_call(
        body,
        out_shape=(
            jax.ShapeDtypeStruct((4, 2) + rows.shape[1:], BF16),
            jax.ShapeDtypeStruct((model_width, 3 * width), BF16),
            jax.ShapeDtypeStruct((size, 3 * width), BF16),
            jax.ShapeDtypeStruct((size, 128), F32),
            jax.ShapeDtypeStruct((4, 2, count, width), BF16),
            shape(small),
            shape(output),
            shape(expand),
            shape(reduce),
        ),
        in_specs=[SM] + [ANY] * 6,
        out_specs=(VM,) * 4 + (ANY,) * 5,
        scratch_shapes=[
            pltpu.VMEM((nb, 4, 2) + joint.shape[1:], BF16),
            pltpu.VMEM((4, 2, count, width), BF16),
        ]
        + InputExchange.scratch()
        + JointGather.scratch(nb)
        + ContextExchange.scratch()
        + Gather.scratch(nb) * 4,
        name="gather_attend",
        compiler_params=pltpu.CompilerParams(
            collective_id=1, has_side_effects=True, vmem_limit_bytes=VMEM_LIMIT
        ),
    )(length, rows, joint, small, output, expand, reduce)


def halves_of(shape):
    rows, columns = shape
    if columns % 256 == 0 and columns >= 1024:
        return (
            (slice(None), pl.ds(0, columns // 2)),
            (slice(None), pl.ds(columns // 2, columns // 2)),
        )
    if rows % 32 == 0:
        return (
            (pl.ds(0, rows // 2), slice(None)),
            (pl.ds(rows // 2, rows // 2), slice(None)),
        )
    if columns % 256 == 0:
        return (
            (slice(None), pl.ds(0, columns // 2)),
            (slice(None), pl.ds(columns // 2, columns // 2)),
        )
    return ((slice(None), slice(None)), None)


def attend_block(limit, qkv_ref, log_ref, context_ref, heads, count):
    width = heads * HEAD_DIM
    size, step = 8 * count, 2 * count

    def block(i):
        at = pl.ds(i * step, step)
        allowed = lax.broadcasted_iota(jnp.int32, (1, size), 1) < limit
        lanes = lax.broadcasted_iota(jnp.int32, (step, 128), 1)
        parts, logs = [], jnp.zeros((step, 128), F32)
        for h in range(heads):
            query = qkv_ref[at, h * HEAD_DIM : (h + 1) * HEAD_DIM]
            key = qkv_ref[:, width + h * HEAD_DIM : width + (h + 1) * HEAD_DIM]
            value = qkv_ref[:, 2 * width + h * HEAD_DIM : 2 * width + (h + 1) * HEAD_DIM]
            scores = (
                lax.dot_general(
                    query, key, (((1,), (1,)), ((), ())), preferred_element_type=F32
                )
                * SCORE_SCALE
            )
            scores = jnp.where(allowed, scores, NEG_FILL)
            top = jnp.max(scores, axis=-1, keepdims=True)
            exps = jnp.exp(scores - top)
            total = jnp.sum(exps, axis=-1, keepdims=True)
            mixed = jnp.dot(exps.astype(BF16), value, preferred_element_type=F32)
            parts.append(mixed / total)
            logs = jnp.where(lanes == h, top + jnp.log(total), logs)
        context_ref[i] = (
            jnp.concatenate(parts, axis=1).astype(BF16).reshape(2, count, width)
        )
        log_ref[at, :] = logs

    return block


def attend_back_block(limit, qkv_ref, log_ref, grad_ref, grad_qkv, grad_key, grad_value, heads, count):
    width = heads * HEAD_DIM
    size, step = 8 * count, 2 * count
    along_keys = (((1,), (1,)), ((), ()))
    along_rows = (((0,), (0,)), ((), ()))

    def block(i):
        at = pl.ds(i * step, step)
        allowed = lax.broadcasted_iota(jnp.int32, (1, size), 1) < limit
        grads = grad_ref[i].reshape(step, width)
        parts = []
        for h in range(heads):
            query = qkv_ref[at, h * HEAD_DIM : (h + 1) * HEAD_DIM]
            key = qkv_ref[:, width + h * HEAD_DIM : width + (h + 1) * HEAD_DIM]
            value = qkv_ref[:, 2 * width + h * HEAD_DIM : 2 * width + (h + 1) * HEAD_DIM]
            grad_out = grads[:, h * HEAD_DIM : (h + 1) * HEAD_DIM]
            scores = (
                lax.dot_general(query, key, along_keys, preferred_element_type=F32)
                * SCORE_SCALE
            )
            probs = jnp.where(allowed, jnp.exp(scores - log_ref[at, h : h + 1]), 0.0)
            grad_probs = lax.dot_general(
                grad_out, value, along_keys, preferred_element_type=F32
            )
            delta = jnp.sum(probs * grad_probs, axis=-1, keepdims=True)
            grad_scores = (probs * (grad_probs - delta)).astype(BF16)
            parts.append(
                jnp.dot(grad_scores, key, preferred_element_type=F32) * SCORE_SCALE
            )
            key_part = lax.dot_general(
                grad_scores, query, along_rows, preferred_element_type=F32
            )
            value_part = lax.dot_general(
                probs.astype(BF16), grad_out, along_rows, preferred_element_type=F32
            )
            if i:
                grad_key[h] += key_part
                grad_value[h] += value_part
            else:
                grad_key[h] = key_part
                grad_value[h] = value_part
        grad_qkv[at, :width] = jnp.concatenate(parts, axis=1).astype(BF16)

    return block


class Scatter:
    def __init__(self, pos, partial, halves, bufs, sems):
        self.pos, self.partial, self.halves = pos, partial, halves
        (self.mine, self.theirs, self.a0, self.a1, self.bx, self.by, self.tz, self.z) = bufs
        (self.sb, self.s0, self.s1, self.dx, self.dy, self.cx, self.cy, self.zs, self.ld) = sems
        self.started = []

    @staticmethod
    def scratch(nb, shape, dtype, halves):
        rows, columns = shape
        first, second = half_shapes(shape, halves)
        return [
            pltpu.VMEM((nb, 4) + shape, dtype),
            pltpu.VMEM((nb, 4) + shape, dtype),
            pltpu.VMEM((nb,) + first, dtype),
            pltpu.VMEM((nb,) + second, dtype),
            pltpu.VMEM((nb,) + shape, dtype),
            pltpu.VMEM((nb,) + shape, dtype),
            pltpu.VMEM((nb,) + shape, dtype),
            pltpu.VMEM((nb,) + shape, dtype),
        ]

    @staticmethod
    def sem_scratch(nb):
        return [DMA((2,))] + [DMA((2, nb)) for _ in range(7)] + [DMA]

    def go(self, copy):
        copy.start()
        self.started.append(copy)

    def begin(self):
        pos = self.pos
        self.go(
            send(
                self.partial.at[:, :, 1 - pos.c],
                self.theirs,
                self.sb.at[0],
                self.sb.at[1],
                pos.sib,
            )
        )
        self.local = pltpu.make_async_copy(
            self.partial.at[:, :, pos.c], self.mine, self.ld
        )
        self.local.start()

    def joined(self):
        self.local.wait()
        pos = self.pos
        send(self.theirs, self.theirs, self.sb.at[0], self.sb.at[1], pos.sib).wait_recv()

    def first(self, k):
        pos, mine = self.pos, self.mine
        h0, h1 = self.halves
        z = pos.up(k)
        for j in range(4):
            chip = pos.chip(j)
            mine[z, chip] = (
                mine[z, chip].astype(F32) + self.theirs[z, chip].astype(F32)
            ).astype(mine.dtype)
        there = mine.at[z, pos.pd]
        self.go(send(there.at[h0], self.a0.at[k], self.s0.at[0, k], self.s0.at[1, k], pos.xn))
        if h1 is not None:
            self.go(
                send(there.at[h1], self.a1.at[k], self.s1.at[0, k], self.s1.at[1, k], pos.yn)
            )
        self.go(
            send(
                mine.at[z, pos.px].at[h0],
                self.bx.at[k].at[h0],
                self.dx.at[0, k],
                self.dx.at[1, k],
                pos.xn,
            )
        )
        if h1 is not None:
            self.go(
                send(
                    mine.at[z, pos.py].at[h1],
                    self.by.at[k].at[h1],
                    self.dy.at[0, k],
                    self.dy.at[1, k],
                    pos.yn,
                )
            )

    def landed(self, ref, sems, k):
        send(ref, ref, sems.at[0, k], sems.at[1, k], self.pos.xn).wait_recv()

    def second(self, k):
        pos, mine = self.pos, self.mine
        h0, h1 = self.halves
        z = pos.up(k)
        self.landed(self.a0.at[k], self.s0, k)
        ref = mine.at[z, pos.py]
        ref[h0] = (ref[h0].astype(F32) + self.a0[k].astype(F32)).astype(mine.dtype)
        self.go(
            send(
                ref.at[h0], self.by.at[k].at[h0], self.cy.at[0, k], self.cy.at[1, k], pos.yn
            )
        )
        if h1 is not None:
            self.landed(self.a1.at[k], self.s1, k)
            ref = mine.at[z, pos.px]
            ref[h1] = (ref[h1].astype(F32) + self.a1[k].astype(F32)).astype(mine.dtype)
            self.go(
                send(
                    ref.at[h1], self.bx.at[k].at[h1], self.cx.at[0, k], self.cx.at[1, k], pos.xn
                )
            )

    def third(self, k, total):
        pos = self.pos
        h0, h1 = self.halves
        z = pos.up(k)
        self.landed(self.bx.at[k].at[h0], self.dx, k)
        self.landed(self.by.at[k].at[h0], self.cy, k)
        if h1 is not None:
            self.landed(self.by.at[k].at[h1], self.dy, k)
            self.landed(self.bx.at[k].at[h1], self.cx, k)
        value = (
            self.mine[z, pos.p].astype(F32)
            + self.bx[k].astype(F32)
            + self.by[k].astype(F32)
        )
        if k:
            self.tz[k] = value.astype(self.tz.dtype)
            self.go(
                send(
                    self.tz.at[k],
                    self.z.at[k],
                    self.zs.at[0, k],
                    self.zs.at[1, k],
                    (pos.up(k), pos.s),
                )
            )
        else:
            total[...] = value

    def last(self, total):
        pos = self.pos
        value = total[...]
        for k in range(1, pos.nb):
            self.landed(self.z.at[k], self.zs, k)
            value = value + self.z[k].astype(F32)
        total[...] = value

    def drain(self):
        for copy in self.started:
            copy.wait_send()


def half_shapes(shape, halves):
    def cut(half):
        return tuple(n if h == slice(None) else h.size for n, h in zip(shape, half))

    first = cut(halves[0])
    return first, (first if halves[1] is None else cut(halves[1]))


class RowScatter:
    def __init__(self, pos, out, bufs, sems):
        self.pos, self.out = pos, out
        self.mine, self.a0, self.a1, self.bx, self.by, self.far = bufs
        (self.sm,) = sems
        self.started = []

    @staticmethod
    def scratch(rows, columns):
        return [
            pltpu.VMEM((4, 2, rows, columns), BF16),
            pltpu.VMEM((rows, columns), BF16),
            pltpu.VMEM((rows, columns), BF16),
            pltpu.VMEM((2, rows, columns), BF16),
            pltpu.VMEM((2, rows, columns), BF16),
            pltpu.VMEM((rows, columns), F32),
            DMA((2, 7)),
        ]

    def go(self, i, src, dst, device):
        copy = send(src, dst, self.sm.at[0, i], self.sm.at[1, i], device)
        copy.start()
        self.started.append(copy)

    def landed(self, i, ref):
        send(ref, ref, self.sm.at[0, i], self.sm.at[1, i], self.pos.xn).wait_recv()

    def first(self):
        pos, mine = self.pos, self.mine
        self.go(0, mine.at[pos.pd, 0], self.a0, pos.xn)
        self.go(1, mine.at[pos.pd, 1], self.a1, pos.yn)
        self.go(2, mine.at[pos.px, 0], self.bx.at[0], pos.xn)
        self.go(3, mine.at[pos.py, 1], self.by.at[1], pos.yn)

    def second(self):
        pos, mine = self.pos, self.mine
        self.landed(0, self.a0)
        mine[pos.py, 0] = (mine[pos.py, 0].astype(F32) + self.a0[...].astype(F32)).astype(BF16)
        self.go(4, mine.at[pos.py, 0], self.by.at[0], pos.yn)
        self.landed(1, self.a1)
        mine[pos.px, 1] = (mine[pos.px, 1].astype(F32) + self.a1[...].astype(F32)).astype(BF16)
        self.go(5, mine.at[pos.px, 1], self.bx.at[1], pos.xn)

    def third(self):
        pos = self.pos
        self.landed(2, self.bx.at[0])
        self.landed(3, self.by.at[1])
        self.landed(4, self.by.at[0])
        self.landed(5, self.bx.at[1])

        def total(core):
            return (
                self.mine[pos.p, core].astype(F32)
                + self.bx[core].astype(F32)
                + self.by[core].astype(F32)
            )

        self.far[...] = total(1 - pos.c)
        self.go(6, self.far, self.out.at[pos.c], pos.sib)
        self.out[pos.c] = total(pos.c)

    def last(self):
        pos = self.pos
        self.landed(6, self.out.at[1 - pos.c])
        for copy in self.started:
            copy.wait_send()


class JointScatter:
    def __init__(self, pos, bufs, sems):
        self.pos = pos
        self.partial, self.mine, self.theirs, self.zbuf, self.sums, self.got = bufs
        self.sb, self.zs, self.ps = sems
        self.started = []

    @staticmethod
    def scratch(nb, shape):
        return [
            pltpu.VMEM((nb, 4, 2) + shape, BF16),
            pltpu.VMEM((nb, 4) + shape, BF16),
            pltpu.VMEM((nb, 4) + shape, BF16),
            pltpu.VMEM((nb, 4) + shape, BF16),
            pltpu.VMEM((4,) + shape, BF16),
            pltpu.VMEM((4,) + shape, BF16),
        ]

    @staticmethod
    def sem_scratch(nb):
        return [DMA((2,)), DMA((2, nb)), DMA((2, 4))]

    def go(self, src, dst, sems, k, device):
        copy = send(src, dst, sems.at[0, k], sems.at[1, k], device)
        copy.start()
        self.started.append(copy)

    def begin(self):
        pos = self.pos
        copy = send(
            self.partial.at[:, :, 1 - pos.c], self.theirs, self.sb.at[0], self.sb.at[1], pos.sib
        )
        copy.start()
        self.started.append(copy)

    def first(self):
        pos, mine = self.pos, self.mine
        send(self.theirs, self.theirs, self.sb.at[0], self.sb.at[1], pos.sib).wait_recv()
        for d in range(pos.nb):
            z = pos.up(d)
            mine[z] = (
                self.partial[z, :, pos.c].astype(F32) + self.theirs[z].astype(F32)
            ).astype(BF16)
        for d in range(1, pos.nb):
            self.go(mine.at[pos.up(d)], self.zbuf.at[d], self.zs, d, (pos.up(d), pos.s))

    def second(self):
        pos = self.pos
        value = self.mine[pos.b].astype(F32)
        for d in range(1, pos.nb):
            ref = self.zbuf.at[d]
            send(ref, ref, self.zs.at[0, d], self.zs.at[1, d], pos.sib).wait_recv()
            value = value + self.zbuf[d].astype(F32)
        self.sums[...] = value.astype(BF16)
        for k in range(1, 4):
            chip = pos.chip(k)
            self.go(
                self.sums.at[chip], self.got.at[k], self.ps, k, (pos.b, 2 * chip + pos.c)
            )

    def last(self, out):
        pos = self.pos
        out[pos.p] = self.sums[pos.p].astype(F32)
        for k in range(1, 4):
            ref = self.got.at[k]
            send(ref, ref, self.ps.at[0, k], self.ps.at[1, k], pos.sib).wait_recv()
            out[pos.chip(k)] = self.got[k].astype(F32)
        for copy in self.started:
            copy.wait_send()


def back_scatter(
    length, rows, weight, qkv, logs, grad_parts, small, output, expand, reduce, nb, heads
):
    arrays = (small, output, expand, reduce)
    shapes = [a.shape[3:] for a in arrays]
    _, _, count, model_width = rows.shape
    width = heads * HEAD_DIM
    size = 8 * count
    shard = model_width // (8 * nb)
    joint_shape = (-(-(shard + 8) // 16) * 16, 3 * width)

    def body(
        length_ref, rows_ref, weight_ref, qkv_ref, log_ref, parts_ref,
        small_ref, output_ref, expand_ref, reduce_ref,
        rows_out, joint_out, small_out, output_out, expand_out, reduce_out,
        grad_context, grad_qkv, grad_key, grad_value,
        *scratch,
    ):
        pos = Place(nb)
        scratch = list(scratch)

        def take(n):
            got = scratch[:n]
            del scratch[:n]
            return got

        mixing = ContextExchange(pos, parts_ref, grad_context, take(2))
        row_sums = RowScatter(pos, rows_out, take(6), take(1))
        joints = JointScatter(pos, take(6), take(3))
        smalls, outputs, expands, reduces = (
            Scatter(pos, ref, halves_of(ref.shape[3:]), take(8), take(9))
            for ref in (small_ref, output_ref, expand_ref, reduce_ref)
        )
        totals = {smalls: small_out, outputs: output_out, expands: expand_out, reduces: reduce_out}
        order = ([2] if nb > 2 else []) + [k for k in range(1, nb) if k != 2] + [0]
        units = [
            (unit, k)
            for k in order
            for unit in ((expands,), (reduces,), (outputs, smalls))
        ]

        def first(n):
            if n < len(units):
                unit, k = units[n]
                for scatter in unit:
                    if k == order[0]:
                        scatter.joined()
                    scatter.first(k)

        def third(n):
            if 0 <= n < len(units):
                unit, k = units[n]
                for scatter in unit:
                    scatter.third(k, totals[scatter])

        def step(n):
            unit, k = units[n]
            for scatter in unit:
                scatter.second(k)
            first(n + AHEAD)
            third(n - 2)

        greet([(pos.up(d), pos.s) for d in range(1, nb)] + plane_others(pos))
        mixing.start()
        for scatter in (expands, reduces, outputs, smalls):
            scatter.begin()
        for n in range(AHEAD):
            first(n)
        mixing.arrive()
        back = attend_back_block(
            length_ref[0], qkv_ref, log_ref, grad_context, grad_qkv, grad_key, grad_value,
            heads, count,
        )
        for i in range(4):
            back(i)
            step(i)
        grad_qkv[:, width : 2 * width] = (
            jnp.concatenate([grad_key[h] for h in range(heads)], axis=1) * SCORE_SCALE
        ).astype(BF16)
        grad_qkv[:, 2 * width :] = jnp.concatenate(
            [grad_value[h] for h in range(heads)], axis=1
        ).astype(BF16)

        def spread(i, _):
            at = pl.ds(pl.multiple_of(i * 2 * count, 2 * count), 2 * count)
            row_sums.mine[i] = (
                lax.dot_general(
                    grad_qkv[at, :],
                    weight_ref[...],
                    (((1,), (1,)), ((), ())),
                    preferred_element_type=F32,
                )
                .astype(BF16)
                .reshape(2, count, model_width)
            )
            return 0

        lax.fori_loop(0, 4, spread, 0)
        row_sums.first()
        step(4)
        grad_joint = lax.dot_general(
            rows_ref[...].reshape(size, model_width),
            grad_qkv[...],
            (((0,), (0,)), ((), ())),
            preferred_element_type=F32,
        )
        joints.partial[:, :, :, :shard] = grad_joint.reshape(nb, 4, 2, shard, 3 * width).astype(
            BF16
        )
        sums = jnp.sum(grad_qkv[...].astype(F32), axis=0, keepdims=True)
        joints.partial[:, :, :, shard:] = jnp.broadcast_to(
            sums.astype(BF16), (nb, 4, 2, joint_shape[0] - shard, 3 * width)
        )
        joints.begin()
        step(5)
        joints.first()
        row_sums.second()
        step(6)
        joints.second()
        for n in range(7, len(units)):
            step(n)
            if n == 8:
                row_sums.third()
        for n in range(len(units) - 2, len(units)):
            third(n)
        joints.last(joint_out)
        for scatter in (expands, reduces, outputs, smalls):
            scatter.last(totals[scatter])
            scatter.drain()
        row_sums.last()
        mixing.drain()

    scratch = [
        pltpu.VMEM((4, 2, count, width), BF16),
        pltpu.VMEM((size, 3 * width), BF16),
        pltpu.VMEM((heads, size, HEAD_DIM), F32),
        pltpu.VMEM((heads, size, HEAD_DIM), F32),
    ]
    scratch += ContextExchange.scratch() + RowScatter.scratch(count, model_width)
    scratch += JointScatter.scratch(nb, joint_shape) + JointScatter.sem_scratch(nb)
    for array, shape in zip(arrays, shapes):
        scratch += Scatter.scratch(nb, shape, array.dtype, halves_of(shape))
        scratch += Scatter.sem_scratch(nb)
    return pl.pallas_call(
        body,
        out_shape=(
            jax.ShapeDtypeStruct((2, count, model_width), F32),
            jax.ShapeDtypeStruct((4,) + joint_shape, F32),
        )
        + tuple(jax.ShapeDtypeStruct(shape, F32) for shape in shapes),
        in_specs=[SM] + [VM] * 4 + [ANY] * 5,
        out_specs=(VM,) * 6,
        scratch_shapes=scratch,
        name="back_scatter",
        compiler_params=pltpu.CompilerParams(
            collective_id=4, has_side_effects=True, vmem_limit_bytes=VMEM_LIMIT
        ),
    )(length, rows, weight, qkv, logs, grad_parts, small, output, expand, reduce)


def plane_on_device(
    inputs,
    cotangent,
    lengths,
    joint_weight,
    output_weight,
    vectors,
    expand_weight,
    expand_bias,
    reduce_weight,
):
    nb = lax.axis_size("batch")
    seq_count, row_count, model_width = inputs.shape
    tokens = seq_count * row_count
    hidden_width = expand_weight.shape[1]
    place = lax.axis_index("seq")
    core, chip = place % 2, place // 2
    width = model_width // 4
    heads = width // HEAD_DIM
    vec = vectors.shape[1]
    per_row = expand_bias.shape[0] // 8
    owners = 8 * nb

    flat_inputs = inputs.reshape(tokens, model_width)
    shard = joint_weight.shape[0]
    pad = -(shard + 8) % 16 + 8
    joint_parts = joint_weight.reshape(shard, 3, 4, width).transpose(2, 0, 1, 3)
    joint_parts = joint_parts.reshape(4, shard, 3 * width)
    first_column = vec * (8 * lax.axis_index("batch") + place)
    spot = lax.dynamic_update_slice_in_dim(
        jnp.zeros((2, model_width), BF16), vectors[2:4], first_column, 1
    ).reshape(2, 4, width)
    spot = jnp.concatenate([spot[0], jnp.zeros_like(spot[0]), spot[1]], axis=1)
    spot = jnp.pad(spot[:, None], ((0, 0), (0, pad - 1), (0, 0)))
    joint_parts = jnp.concatenate([joint_parts, spot], axis=1)
    small = jnp.concatenate(
        [
            vectors.astype(F32),
            expand_bias.reshape(8, per_row).astype(F32),
            jnp.zeros((8, 128 - vec - per_row), F32),
        ],
        axis=1,
    )
    length = lax.dynamic_slice_in_dim(lengths, core, 1)
    (
        rows_all, joint_all, qkv, logs, mixed,
        small_all, output_all, expand_all, reduce_all,
    ) = gather_attend(
        length,
        inputs.astype(BF16),
        joint_parts,
        small,
        output_weight,
        expand_weight,
        reduce_weight,
        nb,
        model_width,
        heads,
    )
    full_output = output_all.reshape(model_width, model_width)
    full_expand = expand_all.reshape(model_width, hidden_width)
    full_reduce = reduce_all.reshape(hidden_width, model_width)
    small_all = small_all.reshape(owners, 8, 128)
    vector_rows = small_all[:, :, :vec].transpose(1, 0, 2).reshape(8, model_width)
    full_bias = small_all[:, :, vec : vec + per_row].reshape(hidden_width)

    context_low = mixed.transpose(1, 2, 0, 3).reshape(tokens, model_width)

    branch = jnp.dot(context_low, full_output, preferred_element_type=F32) + vector_rows[4]
    first, first_normed, first_inverse = layer_norm(
        flat_inputs + branch, vector_rows[0], vector_rows[1]
    )
    first_low = first.astype(BF16)
    before_gelu = jnp.dot(first_low, full_expand, preferred_element_type=F32) + full_bias
    hidden_low = gelu_value(before_gelu).astype(BF16)
    feed = jnp.dot(hidden_low, full_reduce, preferred_element_type=F32) + vector_rows[7]
    result, second_normed, second_inverse = layer_norm(first + feed, vector_rows[5], vector_rows[6])

    own_places = place * row_count + jnp.arange(row_count, dtype=jnp.int32)
    row_mask = (own_places[None, :] < lengths[:, None]).reshape(tokens, 1).astype(F32)
    grad_res = cotangent.reshape(tokens, model_width) * row_mask
    grad_second, grad_gain_two, grad_shift_two = norm_back(
        grad_res, second_normed, second_inverse, vector_rows[5]
    )
    grad_feed_low = grad_second.astype(BF16)
    grad_reduce = jnp.dot(hidden_low.T, grad_feed_low, preferred_element_type=F32)
    grad_hidden = jnp.dot(
        grad_feed_low, full_reduce.T, preferred_element_type=F32
    ) * gelu_slope(before_gelu)
    grad_hidden_low = grad_hidden.astype(BF16)
    grad_expand = jnp.dot(first_low.T, grad_hidden_low, preferred_element_type=F32)
    grad_bias = jnp.sum(grad_hidden_low.astype(F32), axis=0)
    grad_first = grad_second + jnp.dot(
        grad_hidden_low, full_expand.T, preferred_element_type=F32
    )
    grad_resid, grad_gain_one, grad_shift_one = norm_back(
        grad_first, first_normed, first_inverse, vector_rows[0]
    )
    grad_branch_low = grad_resid.astype(BF16)
    grad_output = jnp.dot(context_low.T, grad_branch_low, preferred_element_type=F32)
    grad_context_low = jnp.dot(
        grad_branch_low, full_output.T, preferred_element_type=F32
    ).astype(BF16)

    parts = grad_context_low.reshape(seq_count, row_count, 4, width).transpose(2, 0, 1, 3)
    grad_vectors = jnp.stack(
        [
            grad_gain_one,
            grad_shift_one,
            jnp.zeros((model_width,), F32),
            jnp.zeros((model_width,), F32),
            jnp.sum(grad_branch_low.astype(F32), axis=0),
            grad_gain_two,
            grad_shift_two,
            jnp.sum(grad_feed_low.astype(F32), axis=0),
        ]
    )
    grad_small = jnp.concatenate(
        [
            grad_vectors.reshape(8, owners, vec).transpose(1, 0, 2),
            grad_bias.reshape(owners, 8, per_row),
            jnp.zeros((owners, 8, 128 - vec - per_row), F32),
        ],
        axis=2,
    )

    def split(partial):
        return partial.reshape((nb, 4, 2, partial.shape[0] // owners) + partial.shape[1:])

    rows_sum, joint_sum, small_sum, output_sum, expand_sum, reduce_sum = back_scatter(
        length,
        rows_all,
        joint_all,
        qkv,
        logs,
        parts,
        grad_small.reshape(nb, 4, 2, 8, 128),
        split(grad_output.astype(BF16)),
        split(grad_expand.astype(BF16)),
        split(grad_reduce.astype(BF16)),
        nb,
        heads,
    )
    sums = lax.dynamic_slice(
        joint_sum[:, shard].reshape(4, 3, width),
        (first_column // width, 0, first_column % width),
        (1, 3, vec),
    )[0]
    vectors_sum = jnp.concatenate(
        [small_sum[:2, :vec], sums[0:1], sums[2:3], small_sum[4:, :vec]], axis=0
    )
    joint_sum = joint_sum[:, :shard].reshape(4, shard, 3, width).transpose(1, 2, 0, 3)
    return (
        result.reshape(seq_count, row_count, model_width),
        grad_resid.reshape(seq_count, row_count, model_width) + rows_sum,
        joint_sum.reshape(shard, 3 * model_width),
        output_sum,
        vectors_sum,
        expand_sum,
        small_sum[:, vec : vec + per_row].reshape(-1),
        reduce_sum,
    )


def plane_fits(mesh, inputs, expand_bias, expand_weight):
    return (
        mesh.shape["seq"] == 8
        and inputs[0] == 2 * mesh.shape["batch"]
        and HEADS % 4 == 0
        and inputs[2] == HEADS * HEAD_DIM
        and inputs[1] % (8 * 16) == 0
        and expand_weight[0] % (8 * mesh.shape["seq"] * mesh.shape["batch"]) == 0
        and expand_bias[0] % (8 * mesh.shape["seq"] * mesh.shape["batch"]) == 0
        and (expand_weight[0] + expand_bias[0] // 8) <= 128 * mesh.shape["seq"] * mesh.shape["batch"]
    )


def solution(mesh):
    def program(*args):
        fits = plane_fits(mesh, args[0].shape, args[7].shape, args[6].shape)
        return jax.shard_map(
            plane_on_device if fits else general_on_device,
            mesh=mesh,
            in_specs=(
                P("batch", "seq", None),
                P("batch", "seq", None),
                P("batch"),
                P(("batch", "seq"), None),
                P(("batch", "seq"), None),
                P(None, ("batch", "seq")),
                P(("batch", "seq"), None),
                P(("batch", "seq")),
                P(("batch", "seq"), None),
            ),
            out_specs=(
                P("batch", "seq", None),
                P("batch", "seq", None),
                P(("batch", "seq"), None),
                P(("batch", "seq"), None),
                P(None, ("batch", "seq")),
                P(("batch", "seq"), None),
                P(("batch", "seq")),
                P(("batch", "seq"), None),
            ),
            check_vma=False,
        )(*args)

    return program
```

```python
import functools
import math

import jax
import jax.numpy as jnp
from jax import lax
from jax.experimental import pallas as pl
from jax.experimental.pallas import tpu as pltpu
from jax.sharding import PartitionSpec as P

HEADS = 12
HEAD_DIM = 64


EPSILON = 1e-12
SCORE_SCALE = 0.125
NEG_FILL = -1e30
HALF_ROOT = 0.7071067811865476
INV_ROOT_TAU = 0.3989422804014327
block_limit = 256


def layer_norm(residual, norm_gain, norm_shift):
    centered = residual - jnp.mean(residual, axis=-1, keepdims=True)
    inverse = lax.rsqrt(jnp.mean(centered * centered, axis=-1, keepdims=True) + EPSILON)
    normed = centered * inverse
    return (normed * norm_gain + norm_shift, normed, inverse)


def norm_back(grad_out, normed, inverse, norm_gain):
    grad_normed = grad_out * norm_gain
    mean_grad = jnp.mean(grad_normed, axis=-1, keepdims=True)
    mean_proj = jnp.mean(grad_normed * normed, axis=-1, keepdims=True)
    grad_in = inverse * (grad_normed - mean_grad - normed * mean_proj)
    return (grad_in, jnp.sum(grad_out * normed, axis=0), jnp.sum(grad_out, axis=0))


def gelu_value(before_gelu):
    return 0.5 * before_gelu * (1.0 + lax.erf(before_gelu * HALF_ROOT))


def gelu_slope(before_gelu):
    return (
        0.5 * (1.0 + lax.erf(before_gelu * HALF_ROOT))
        + before_gelu * jnp.exp(-0.5 * before_gelu * before_gelu) * INV_ROOT_TAU
    )


def over_blocks(piece_rows, block_fn, carried):
    block_size = math.gcd(piece_rows, block_limit)

    def run_block(block_index, current):
        return block_fn(current, block_index * block_size, block_size)

    return lax.fori_loop(0, piece_rows // block_size, run_block, carried)


def head_scores(left_heads, right_heads, right_places, lengths):
    scores = (
        jnp.einsum("sqhd,skhd->shqk", left_heads, right_heads, preferred_element_type=jnp.float32)
        * SCORE_SCALE
    )
    allowed = right_places[None, :] < lengths[:, None]
    return jnp.where(allowed[:, None, None, :], scores, NEG_FILL)


def cut_heads(gathered_piece, offset, block_size, head_count):
    sliced = lax.dynamic_slice_in_dim(gathered_piece, offset, block_size, 1)
    return sliced.reshape(sliced.shape[0], block_size, head_count, -1)


def gather_attention(joint_weight, output_weight, vectors):
    return (
        lax.all_gather(joint_weight, ("batch", "seq"), axis=0, tiled=True),
        lax.all_gather(output_weight, ("batch", "seq"), axis=0, tiled=True),
        lax.all_gather(vectors, ("batch", "seq"), axis=1, tiled=True),
    )


def gather_feed(expand_weight, reduce_weight, expand_bias):
    return (
        lax.all_gather(expand_weight, ("batch", "seq"), axis=0, tiled=True),
        lax.all_gather(reduce_weight, ("batch", "seq"), axis=0, tiled=True),
        lax.all_gather(expand_bias, ("batch", "seq"), axis=0, tiled=True),
    )


def general_on_device(
    inputs,
    cotangent,
    lengths,
    joint_weight,
    output_weight,
    vectors,
    expand_weight,
    expand_bias,
    reduce_weight,
):
    seq_count, row_count, model_width = inputs.shape
    head_count = HEADS
    head_size = HEAD_DIM
    tokens = seq_count * row_count
    head_shape = (seq_count, row_count, head_count, head_size)
    own_places = lax.axis_index("seq") * row_count + jnp.arange(row_count, dtype=jnp.int32)
    row_valid = own_places[None, :] < lengths[:, None]
    row_mask = row_valid.reshape(tokens, 1).astype(jnp.float32)
    full_joint, full_output, full_vectors = gather_attention(joint_weight, output_weight, vectors)
    vector_rows = full_vectors.astype(jnp.float32)
    flat_inputs = inputs.reshape(tokens, model_width)
    input_low = flat_inputs.astype(jnp.bfloat16)
    projected = jnp.dot(input_low, full_joint, preferred_element_type=jnp.float32)
    query_low = (projected[:, :model_width] + vector_rows[2]).astype(jnp.bfloat16)
    key_low = projected[:, model_width : 2 * model_width].astype(jnp.bfloat16)
    value_low = (projected[:, 2 * model_width :] + vector_rows[3]).astype(jnp.bfloat16)
    query_heads = query_low.reshape(head_shape)
    key_rows = key_low.reshape(seq_count, row_count, model_width)
    value_rows = value_low.reshape(seq_count, row_count, model_width)
    start_state = (
        jnp.full((seq_count, head_count, row_count), NEG_FILL, jnp.float32),
        jnp.zeros((seq_count, head_count, row_count), jnp.float32),
        jnp.zeros(head_shape, jnp.float32),
    )
    key_piece = lax.all_gather(key_rows, "seq", axis=1, tiled=True)
    value_piece = lax.all_gather(value_rows, "seq", axis=1, tiled=True)

    def forward_score_block(current, offset, block_size):
        running_max, running_sum, summed = current
        key_heads = cut_heads(key_piece, offset, block_size, head_count)
        value_heads = cut_heads(value_piece, offset, block_size, head_count)
        key_places = offset + jnp.arange(block_size, dtype=jnp.int32)
        scores = head_scores(query_heads, key_heads, key_places, lengths)
        new_max = jnp.maximum(running_max, jnp.max(scores, axis=-1))
        factor = jnp.exp(running_max - new_max)
        exp_scores = jnp.exp(scores - new_max[..., None])
        running_sum = running_sum * factor + jnp.sum(exp_scores, axis=-1)
        update = jnp.einsum(
            "shqk,skhd->sqhd",
            exp_scores.astype(jnp.bfloat16),
            value_heads,
            preferred_element_type=jnp.float32,
        )
        summed = summed * jnp.transpose(factor, (0, 2, 1))[..., None] + update
        return (new_max, running_sum, summed)

    running_max, running_sum, summed = over_blocks(
        key_piece.shape[1], forward_score_block, start_state
    )
    attended = summed / jnp.transpose(running_sum, (0, 2, 1))[..., None]
    log_total = jnp.transpose(running_max + jnp.log(running_sum), (0, 2, 1))
    context_low = attended.reshape(tokens, model_width).astype(jnp.bfloat16)
    branch = jnp.dot(context_low, full_output, preferred_element_type=jnp.float32) + vector_rows[4]
    first, first_normed, first_inverse = layer_norm(
        flat_inputs + branch, vector_rows[0], vector_rows[1]
    )
    first_low = first.astype(jnp.bfloat16)
    full_expand, full_reduce, full_bias = gather_feed(expand_weight, reduce_weight, expand_bias)
    before_gelu = jnp.dot(
        first_low, full_expand, preferred_element_type=jnp.float32
    ) + full_bias.astype(jnp.float32)
    hidden_low = gelu_value(before_gelu).astype(jnp.bfloat16)
    feed = jnp.dot(hidden_low, full_reduce, preferred_element_type=jnp.float32) + vector_rows[7]
    result, second_normed, second_inverse = layer_norm(first + feed, vector_rows[5], vector_rows[6])
    full_expand, full_reduce, full_bias = gather_feed(expand_weight, reduce_weight, expand_bias)
    full_joint, full_output, full_vectors = gather_attention(joint_weight, output_weight, vectors)
    grad_res = cotangent.reshape(tokens, model_width) * row_mask
    grad_second, grad_gain_two, grad_shift_two = norm_back(
        grad_res, second_normed, second_inverse, vector_rows[5]
    )
    grad_feed_low = grad_second.astype(jnp.bfloat16)
    grad_reduce_local = jnp.dot(hidden_low.T, grad_feed_low, preferred_element_type=jnp.float32)
    grad_hidden = jnp.dot(
        grad_feed_low, full_reduce.T, preferred_element_type=jnp.float32
    ) * gelu_slope(before_gelu)
    grad_hidden_low = grad_hidden.astype(jnp.bfloat16)
    grad_expand_local = jnp.dot(first_low.T, grad_hidden_low, preferred_element_type=jnp.float32)
    grad_bias_local = jnp.sum(grad_hidden_low.astype(jnp.float32), axis=0)
    grad_first = grad_second + jnp.dot(
        grad_hidden_low, full_expand.T, preferred_element_type=jnp.float32
    )
    grad_resid, grad_gain_one, grad_shift_one = norm_back(
        grad_first, first_normed, first_inverse, vector_rows[0]
    )
    grad_branch_low = grad_resid.astype(jnp.bfloat16)
    grad_output_local = jnp.dot(context_low.T, grad_branch_low, preferred_element_type=jnp.float32)
    grad_context_low = jnp.dot(
        grad_branch_low, full_output.T, preferred_element_type=jnp.float32
    ).astype(jnp.bfloat16)
    grad_context_heads = grad_context_low.reshape(head_shape)
    row_delta = jnp.sum(grad_context_heads.astype(jnp.float32) * attended, axis=-1)
    log_heads = jnp.transpose(log_total, (0, 2, 1))
    delta_heads = jnp.transpose(row_delta, (0, 2, 1))
    query_key_piece = lax.all_gather(key_rows, "seq", axis=1, tiled=True)
    query_value_piece = lax.all_gather(value_rows, "seq", axis=1, tiled=True)

    def query_score_block(current, offset, block_size):
        key_heads = cut_heads(query_key_piece, offset, block_size, head_count)
        value_heads = cut_heads(query_value_piece, offset, block_size, head_count)
        key_places = offset + jnp.arange(block_size, dtype=jnp.int32)
        scores = head_scores(query_heads, key_heads, key_places, lengths)
        softmax_rows = jnp.exp(scores - log_heads[..., None])
        grad_probs = jnp.einsum(
            "sqhd,skhd->shqk", grad_context_heads, value_heads, preferred_element_type=jnp.float32
        )
        grad_scores = (softmax_rows * (grad_probs - delta_heads[..., None])).astype(jnp.bfloat16)
        return (
            current
            + jnp.einsum(
                "shqk,skhd->sqhd", grad_scores, key_heads, preferred_element_type=jnp.float32
            )
            * SCORE_SCALE
        )

    grad_query = over_blocks(
        query_key_piece.shape[1], query_score_block, jnp.zeros(head_shape, jnp.float32)
    )
    own_keys = key_low.reshape(head_shape)
    own_values = value_low.reshape(head_shape)
    query_rows = query_low.reshape(seq_count, row_count, model_width)
    grad_context_rows = grad_context_low.reshape(seq_count, row_count, model_width)
    zero_heads = jnp.zeros(head_shape, jnp.float32)
    query_piece = lax.all_gather(query_rows.astype(jnp.float32), "seq", axis=1, tiled=True).astype(
        jnp.bfloat16
    )
    grad_piece = lax.all_gather(
        grad_context_rows.astype(jnp.float32), "seq", axis=1, tiled=True
    ).astype(jnp.bfloat16)
    log_piece = lax.all_gather(log_total, "seq", axis=1, tiled=True)
    delta_piece = lax.all_gather(row_delta, "seq", axis=1, tiled=True)

    def key_score_block(current, offset, block_size):
        grad_key, grad_value = current
        query_block = cut_heads(query_piece, offset, block_size, head_count)
        grad_block = cut_heads(grad_piece, offset, block_size, head_count)
        log_block = jnp.transpose(
            lax.dynamic_slice_in_dim(log_piece, offset, block_size, 1), (0, 2, 1)
        )
        delta_block = jnp.transpose(
            lax.dynamic_slice_in_dim(delta_piece, offset, block_size, 1), (0, 2, 1)
        )
        scores = head_scores(query_block, own_keys, own_places, lengths)
        softmax_rows = jnp.exp(scores - log_block[..., None])
        grad_value = grad_value + jnp.einsum(
            "shqk,sqhd->skhd",
            softmax_rows.astype(jnp.bfloat16),
            grad_block,
            preferred_element_type=jnp.float32,
        )
        grad_probs = jnp.einsum(
            "sqhd,skhd->shqk", grad_block, own_values, preferred_element_type=jnp.float32
        )
        grad_scores = (softmax_rows * (grad_probs - delta_block[..., None])).astype(jnp.bfloat16)
        grad_key = (
            grad_key
            + jnp.einsum(
                "shqk,sqhd->skhd", grad_scores, query_block, preferred_element_type=jnp.float32
            )
            * SCORE_SCALE
        )
        return (grad_key, grad_value)

    grad_key, grad_value = over_blocks(
        query_piece.shape[1], key_score_block, (zero_heads, zero_heads)
    )
    grad_query_low = grad_query.reshape(tokens, model_width).astype(jnp.bfloat16)
    grad_key_low = grad_key.reshape(tokens, model_width).astype(jnp.bfloat16)
    grad_value_low = grad_value.reshape(tokens, model_width).astype(jnp.bfloat16)
    grad_projected = jnp.concatenate([grad_query_low, grad_key_low, grad_value_low], axis=1)
    grad_joint_local = jnp.dot(input_low.T, grad_projected, preferred_element_type=jnp.float32)
    grad_inputs = grad_resid + jnp.dot(
        grad_projected, full_joint.T, preferred_element_type=jnp.float32
    )
    grad_vector_local = jnp.stack(
        [
            grad_gain_one,
            grad_shift_one,
            jnp.sum(grad_query_low.astype(jnp.float32), axis=0),
            jnp.sum(grad_value_low.astype(jnp.float32), axis=0),
            jnp.sum(grad_branch_low.astype(jnp.float32), axis=0),
            grad_gain_two,
            grad_shift_two,
            jnp.sum(grad_feed_low.astype(jnp.float32), axis=0),
        ],
        axis=0,
    )
    every_grad = (
        lax.psum_scatter(grad_joint_local, ("batch", "seq"), scatter_dimension=0, tiled=True),
        lax.psum_scatter(grad_output_local, ("batch", "seq"), scatter_dimension=0, tiled=True),
        lax.psum_scatter(grad_vector_local, ("batch", "seq"), scatter_dimension=1, tiled=True),
        lax.psum_scatter(grad_expand_local, ("batch", "seq"), scatter_dimension=0, tiled=True),
        lax.psum_scatter(grad_reduce_local, ("batch", "seq"), scatter_dimension=0, tiled=True),
        lax.psum_scatter(grad_bias_local, ("batch", "seq"), scatter_dimension=0, tiled=True),
    )
    summed_grads = (
        every_grad[0],
        every_grad[1],
        every_grad[2],
        every_grad[3],
        every_grad[5],
        every_grad[4],
    )
    return (
        result.reshape(seq_count, row_count, model_width),
        grad_inputs.reshape(seq_count, row_count, model_width),
        summed_grads[0],
        summed_grads[1],
        summed_grads[2],
        summed_grads[3],
        summed_grads[4],
        summed_grads[5],
    )


MESH = pl.DeviceIdType.MESH
ANY = pl.BlockSpec(memory_space=pl.ANY)
VM = pl.BlockSpec(memory_space=pltpu.VMEM)
SM = pl.BlockSpec(memory_space=pltpu.SMEM)
DMA = pltpu.SemaphoreType.DMA
VMEM_LIMIT = 60 << 20
F32 = jnp.float32
BF16 = jnp.bfloat16


def send(src, dst, send_sem, recv_sem, device):
    return pltpu.make_async_remote_copy(
        src_ref=src,
        dst_ref=dst,
        send_sem=send_sem,
        recv_sem=recv_sem,
        device_id=device,
        device_id_type=MESH,
    )


class Place:
    def __init__(self, nb):
        self.nb = nb
        self.b = lax.axis_index("batch")
        self.s = lax.axis_index("seq")
        self.c = self.s % 2
        self.p = self.s // 2
        x, y = self.p % 2, self.p // 2
        self.px = 2 * y + (1 - x)
        self.py = 2 * (1 - y) + x
        self.pd = 2 * (1 - y) + (1 - x)
        self.sib = (self.b, 2 * self.p + 1 - self.c)
        self.xn = (self.b, 2 * self.px + self.c)
        self.yn = (self.b, 2 * self.py + self.c)

    def chip(self, step):
        return (self.p, self.px, self.py, self.pd)[step]

    def up(self, step):
        return (self.b + step) % self.nb

    def down(self, step):
        return (self.b + self.nb - step) % self.nb


def greet(devices):
    barrier = pltpu.get_barrier_semaphore()
    for device in devices:
        pl.semaphore_signal(barrier, inc=1, device_id=device, device_id_type=MESH)
    pl.semaphore_wait(barrier, len(devices))


def greet_near(pos):
    barrier = pltpu.get_barrier_semaphore()

    def signal(device):
        pl.semaphore_signal(barrier, inc=1, device_id=device, device_id_type=MESH)

    for device in plane_others(pos):
        signal(device)
    last = pos.nb - 1
    guarded(pos.b < last, lambda: signal(((pos.b + 1) % pos.nb, pos.s)))
    guarded(pos.b > 0, lambda: signal(((pos.b + last) % pos.nb, pos.s)))
    beside = jnp.where(pos.b < last, 1, 0) + jnp.where(pos.b > 0, 1, 0)
    pl.semaphore_wait(barrier, 7 + beside)


def same_core(pos):
    return [
        (pos.up(d), 2 * pos.chip(k) + pos.c)
        for d in range(pos.nb)
        for k in range(4)
        if d or k
    ]


def plane_others(pos):
    return [
        (pos.b, 2 * pos.chip(k) + (pos.c if j == 0 else 1 - pos.c))
        for k in range(4)
        for j in range(2)
        if k or j
    ]


def guarded(condition, action):
    if isinstance(condition, bool):
        if condition:
            action()
    else:

        @pl.when(condition)
        def _():
            action()


class Chain:
    def __init__(self, pos, mine, spot, sems):
        self.pos, self.mine, self.spot = pos, mine, spot
        self.up, self.down = sems

    @staticmethod
    def scratch(nb):
        return [DMA((2, nb)), DMA((2, nb))]

    def copy(self, src, z, sems, hop, there):
        pos = self.pos
        return send(src, self.spot(z), sems.at[0, hop], sems.at[1, hop], (there, pos.s))

    def moves(self, hop):
        pos = self.pos
        last = pos.nb - 1
        low, high = (pos.b - hop + 1 + pos.nb) % pos.nb, (pos.b + hop - 1) % pos.nb
        above, below = (pos.b + 1) % pos.nb, (pos.b + last) % pos.nb
        own = isinstance(hop, int) and hop == 1
        return (
            (
                (pos.b >= hop - 1) & (pos.b < last),
                self.copy(self.mine if own else self.spot(low), low, self.up, hop, above),
            ),
            (
                (pos.b + hop - 1 < pos.nb) & (pos.b > 0),
                self.copy(self.mine if own else self.spot(high), high, self.down, hop, below),
            ),
        )

    def start(self, hop=1):
        for made, copy in self.moves(hop):
            guarded(made, copy.start)

    def hop(self, hop):
        pos = self.pos
        low, high = (pos.b - hop + pos.nb) % pos.nb, (pos.b + hop) % pos.nb
        for made, z, sems in (
            (pos.b >= hop, low, self.up),
            (pos.b + hop < pos.nb, high, self.down),
        ):
            guarded(made, self.copy(self.spot(z), z, sems, hop, pos.b).wait_recv)
        guarded(hop < pos.nb - 1, lambda: self.start(hop + 1))

    def drain(self):
        for hop in range(1, self.pos.nb):
            for made, copy in self.moves(hop):
                guarded(made, copy.wait_send)


class Gather:
    def __init__(self, pos, shard, out, halves, sems):
        self.pos, self.shard, self.out, self.halves = pos, shard, out, halves
        self.xs, self.ys, self.f0, self.f1, self.sb, self.local_sem = sems[:6]
        self.chain = Chain(pos, shard, lambda z: out.at[z, pos.p, pos.c], sems[6:])

    @staticmethod
    def scratch(nb):
        return [DMA((2, nb)) for _ in range(5)] + [DMA] + Chain.scratch(nb)

    def z(self, k):
        return jnp.where(k <= self.pos.b, self.pos.b - k, k)

    def own(self):
        pos = self.pos
        self.local = pltpu.make_async_copy(
            self.shard, self.out.at[pos.b, pos.p, pos.c], self.local_sem
        )
        self.local.start()

    def x_copy(self, k, src=None):
        pos = self.pos
        there = self.out.at[self.z(k), pos.p, pos.c]
        src = there if src is None else src
        return send(src, there, self.xs.at[0, k], self.xs.at[1, k], pos.xn)

    def y_copy(self, k, src=None):
        pos = self.pos
        there = self.out.at[self.z(k), pos.p, pos.c]
        src = there if src is None else src
        return send(src, there, self.ys.at[0, k], self.ys.at[1, k], pos.yn)

    def plane(self, k, src=None):
        self.x_copy(k, src).start()
        self.y_copy(k, src).start()

    def land(self, sems, k, chip, half=None):
        pos = self.pos
        ref = self.out.at[self.z(k), chip, pos.c]
        if half is not None:
            ref = ref.at[half]
        return send(ref, ref, sems.at[0, k], sems.at[1, k], pos.xn)

    def y_forward(self, k):
        pos = self.pos
        ref = self.out.at[self.z(k), pos.px, pos.c].at[self.halves[0]]
        return send(ref, ref, self.f0.at[0, k], self.f0.at[1, k], pos.yn)

    def x_forward(self, k):
        pos = self.pos
        ref = self.out.at[self.z(k), pos.py, pos.c].at[self.halves[1]]
        return send(ref, ref, self.f1.at[0, k], self.f1.at[1, k], pos.xn)

    def forward(self, k):
        pos = self.pos
        self.land(self.xs, k, pos.px).wait_recv()
        self.y_forward(k).start()
        self.land(self.ys, k, pos.py).wait_recv()
        if self.halves[1] is not None:
            self.x_forward(k).start()

    def sibling_copy(self, k):
        pos = self.pos
        ref = self.out.at[self.z(k), :, pos.c]
        return send(ref, ref, self.sb.at[0, k], self.sb.at[1, k], pos.sib)

    def sibling(self, k):
        pos = self.pos
        h0, h1 = self.halves
        self.land(self.f0, k, pos.pd, h0).wait_recv()
        if h1 is not None:
            self.land(self.f1, k, pos.pd, h1).wait_recv()
        self.sibling_copy(k).start()

    def finish(self, k):
        pos = self.pos
        ref = self.out.at[self.z(k), :, 1 - pos.c]
        send(ref, ref, self.sb.at[0, k], self.sb.at[1, k], pos.sib).wait_recv()
        self.x_copy(k).wait_send()
        self.y_copy(k).wait_send()
        self.y_forward(k).wait_send()
        if self.halves[1] is not None:
            self.x_forward(k).wait_send()
        self.sibling_copy(k).wait_send()


class InputExchange:
    def __init__(self, pos, rows, out, sems):
        self.pos, self.rows, self.out, self.sems = pos, rows, out, sems
        self.started = []

    @staticmethod
    def scratch():
        return [DMA((2, 2)), DMA((2, 2)), DMA((2, 2)), DMA((2,)), DMA]

    def go(self, copy):
        copy.start()
        self.started.append(copy)

    def start(self):
        pos, (xs, ys, _, sb, local) = self.pos, self.sems
        there = self.out.at[pos.p, pos.c]
        for sems, chip in ((xs, pos.px), (ys, pos.py)):
            for j in range(2):
                self.go(
                    send(
                        self.rows.at[j],
                        there,
                        sems.at[0, j],
                        sems.at[1, pos.c],
                        (pos.b, 2 * chip + j),
                    )
                )
        self.go(send(self.rows.at[1 - pos.c], there, sb.at[0], sb.at[1], pos.sib))
        self.local = pltpu.make_async_copy(self.rows.at[pos.c], there, local)
        self.local.start()

    def landed(self, sems, j, chip):
        ref = self.out.at[chip, j]
        send(ref, ref, sems.at[0, j], sems.at[1, j], self.pos.xn).wait_recv()

    def forward(self):
        pos, (xs, ys, fs, _, _) = self.pos, self.sems
        self.landed(xs, 0, pos.px)
        ref = self.out.at[pos.px, 0]
        self.go(send(ref, ref, fs.at[0, 0], fs.at[1, 0], pos.yn))
        self.landed(ys, 1, pos.py)
        ref = self.out.at[pos.py, 1]
        self.go(send(ref, ref, fs.at[0, 1], fs.at[1, 1], pos.xn))

    def finish(self):
        pos, (xs, ys, fs, sb, _) = self.pos, self.sems
        self.landed(xs, 1, pos.px)
        self.landed(ys, 0, pos.py)
        self.landed(fs, 0, pos.pd)
        self.landed(fs, 1, pos.pd)
        ref = self.out.at[pos.p, 1 - pos.c]
        send(ref, ref, sb.at[0], sb.at[1], pos.sib).wait_recv()
        self.local.wait()

    def drain(self):
        for copy in self.started:
            copy.wait_send()


class JointGather:
    def __init__(self, pos, parts, out, sems):
        self.pos, self.parts, self.out = pos, parts, out
        self.direct, self.sb, self.local_sem = sems[:3]
        self.chain = Chain(
            pos, out.at[pos.b, :, pos.c], lambda z: out.at[z, :, pos.c], sems[3:]
        )

    @staticmethod
    def scratch(nb):
        return [DMA((2, 4)), DMA((2,)), DMA] + Chain.scratch(nb)

    def start(self):
        pos = self.pos
        there = self.out.at[pos.b, pos.p, pos.c]
        self.started = [
            send(
                self.parts.at[pos.chip(k)],
                there,
                self.direct.at[0, k],
                self.direct.at[1, k],
                (pos.b, 2 * pos.chip(k) + pos.c),
            )
            for k in range(1, 4)
        ]
        for copy in self.started:
            copy.start()
        self.local = pltpu.make_async_copy(self.parts.at[pos.p], there, self.local_sem)
        self.local.start()

    def own(self):
        pos = self.pos
        for k in range(1, 4):
            ref = self.out.at[pos.b, pos.chip(k), pos.c]
            send(ref, ref, self.direct.at[0, k], self.direct.at[1, k], pos.sib).wait_recv()
        self.local.wait()
        self.chain.start()

    def sibling(self):
        pos = self.pos
        ref = self.out.at[:, :, pos.c]
        send(ref, ref, self.sb.at[0], self.sb.at[1], pos.sib).start()

    def finish(self):
        pos = self.pos
        ref = self.out.at[:, :, 1 - pos.c]
        send(ref, ref, self.sb.at[0], self.sb.at[1], pos.sib).wait_recv()

    def drain(self):
        for copy in self.started:
            copy.wait_send()
        ref = self.out.at[:, :, self.pos.c]
        send(ref, ref, self.sb.at[0], self.sb.at[1], self.pos.sib).wait_send()
        self.chain.drain()


class ContextExchange:
    def __init__(self, pos, parts, out, sems):
        self.pos, self.parts, self.out = pos, parts, out
        self.sems, self.local_sem = sems

    @staticmethod
    def scratch():
        return [DMA((2, 8)), DMA]

    def pairs(self):
        pos = self.pos
        for k in range(4):
            for j in range(2):
                if k or j:
                    yield 2 * k + j, pos.chip(k), pos.c if j == 0 else 1 - pos.c

    def copies(self):
        pos, sems = self.pos, self.sems
        there = self.out.at[pos.p, pos.c]
        return [
            send(
                self.parts.at[chip, core],
                there,
                sems.at[0, i],
                sems.at[1, i],
                (pos.b, 2 * chip + core),
            )
            for i, chip, core in self.pairs()
        ]

    def local(self):
        pos = self.pos
        return pltpu.make_async_copy(
            self.parts.at[pos.p, pos.c], self.out.at[pos.p, pos.c], self.local_sem
        )

    def start(self):
        for copy in self.copies():
            copy.start()
        self.local().start()

    def arrive(self):
        for i, chip, core in self.pairs():
            ref = self.out.at[chip, core]
            send(ref, ref, self.sems.at[0, i], self.sems.at[1, i], self.pos.sib).wait_recv()
        self.local().wait()

    def drain(self):
        for copy in self.copies():
            copy.wait_send()


def gather_attend(length, rows, joint, small, output, expand, reduce, nb, model_width, heads):
    _, count, _ = rows.shape
    shard = vec = model_width // (8 * nb)
    per = reduce.shape[0]
    width = heads * HEAD_DIM
    size = 8 * count

    def body(
        length_ref, rows_ref, joint_ref, small_ref, output_ref, expand_ref, reduce_ref,
        rows_out, weight_out, qkv_out, log_out, vectors_out, hidden_out,
        context_out, output_out, expand_out, reduce_out,
        joint_all, context, small_all, bias_ref,
        *scratch,
    ):
        pos = Place(nb)
        scratch = list(scratch)

        def take(n):
            got = scratch[:n]
            del scratch[:n]
            return got

        exchange = InputExchange(pos, rows_ref, rows_out, take(5))
        joints = JointGather(pos, joint_ref, joint_all, take(5))
        mixing = ContextExchange(pos, context, context_out, take(2))
        outputs, expands, reduces, smalls = (
            Gather(pos, part, out, halves_of(part.shape), take(8))
            for part, out in (
                (output_ref, output_out),
                (expand_ref, expand_out),
                (reduce_ref, reduce_out),
                (small_ref, small_all),
            )
        )
        gathers = (outputs, expands, reduces, smalls)
        units = ((expands, smalls), (reduces,), (outputs,))
        hops = list(range(1, nb))

        def project(i, _):
            at = pl.ds(pl.multiple_of(i * 2 * count, 2 * count), 2 * count)
            qkv_out[at, :] = (
                jnp.dot(
                    rows_out[i].reshape(2 * count, model_width),
                    weight_out[...],
                    preferred_element_type=F32,
                )
                + bias_ref[...]
            ).astype(BF16)
            return 0

        def prepare():
            exchange.finish()
            joints.finish()
            for z in range(nb):
                parts = joint_all[z]
                weight_out[z * 8 * shard : (z + 1) * 8 * shard, :] = parts[:, :, :shard].reshape(
                    8 * shard, 3 * width
                )
            bias_ref[...] = jnp.sum(
                joint_all[:, :, :, shard:].astype(F32).reshape(-1, 3 * width),
                axis=0,
                keepdims=True,
            )
            lax.fori_loop(0, 4, project, 0)

        attend = attend_block(length_ref[0], qkv_out, log_out, context, heads, count)

        def slot(i, _):
            def more(n):
                for gather in units[n]:
                    gather.plane(i + 1)

            guarded(i + 1 < nb, lambda: [gather.chain.hop(i + 1) for gather in gathers])
            for j in range(3):
                for gather in units[j]:
                    gather.forward(i)
                guarded(i + 1 < nb, functools.partial(more, j))
                if j == 2:
                    for gather in units[0]:
                        gather.sibling(i)
                else:
                    guarded(
                        i > 0,
                        lambda j=j: [gather.sibling(i - 1) for gather in units[j + 1]],
                    )
                if len(hops) >= 3 - j:
                    guarded(i == 0, lambda j=j: joints.chain.hop(hops[j - 3]))
                if j == 2:
                    guarded(i == 0, joints.sibling)
                if j == 0:
                    guarded(i == 1, prepare)
                turn = 3 * (i - 1) + j
                guarded((turn >= 0) & (turn < 4), lambda turn=turn: attend(turn))
                if j == 0:
                    guarded(i == 2, mixing.start)
            return 0

        greet_near(pos)
        exchange.start()
        joints.start()
        for gather in gathers:
            gather.own()
            gather.chain.start()
        joints.own()
        for t in hops[:-3]:
            joints.chain.hop(t)
        exchange.forward()
        for unit in units:
            for gather in unit:
                gather.plane(0, gather.shard)
        for gather in gathers:
            gather.local.wait()
        lax.fori_loop(0, nb, slot, 0)
        for unit in units[1:]:
            for gather in unit:
                gather.sibling(nb - 1)

        def finish(k, _):
            for gather in gathers:
                gather.finish(k)
            return 0

        lax.fori_loop(0, nb, finish, 0)
        for owner in range(8 * nb):
            part = small_all[owner // 8, owner % 8 // 2, owner % 2].astype(F32)
            vectors_out[:, owner * vec : (owner + 1) * vec] = part[:8, :vec]
            hidden_out[:, owner * per : (owner + 1) * per] = part[8:9, :per]
        mixing.arrive()
        for gather in gathers:
            gather.chain.drain()
        exchange.drain()
        joints.drain()
        mixing.drain()

    def shape(part):
        return jax.ShapeDtypeStruct((nb, 4, 2) + part.shape, part.dtype)

    return pl.pallas_call(
        body,
        out_shape=(
            jax.ShapeDtypeStruct((4, 2) + rows.shape[1:], BF16),
            jax.ShapeDtypeStruct((model_width, 3 * width), BF16),
            jax.ShapeDtypeStruct((size, 3 * width), BF16),
            jax.ShapeDtypeStruct((size, 128), F32),
            jax.ShapeDtypeStruct((8, model_width), F32),
            jax.ShapeDtypeStruct((1, 8 * nb * per), F32),
            jax.ShapeDtypeStruct((4, 2, count, width), BF16),
            shape(output),
            shape(expand),
            shape(reduce),
        ),
        in_specs=[SM] + [ANY] * 6,
        out_specs=(VM,) * 6 + (ANY,) * 4,
        scratch_shapes=[
            pltpu.VMEM((nb, 4, 2) + joint.shape[1:], BF16),
            pltpu.VMEM((4, 2, count, width), BF16),
            pltpu.VMEM((nb, 4, 2) + small.shape, small.dtype),
            pltpu.VMEM((1, 3 * width), F32),
        ]
        + InputExchange.scratch()
        + JointGather.scratch(nb)
        + ContextExchange.scratch()
        + Gather.scratch(nb) * 4,
        name="gather_attend",
        compiler_params=pltpu.CompilerParams(
            collective_id=1, has_side_effects=True, vmem_limit_bytes=VMEM_LIMIT
        ),
    )(length, rows, joint, small, output, expand, reduce)


def halves_of(shape):
    rows, columns = shape
    if columns % 256 == 0 and columns >= 1024:
        return (
            (slice(None), pl.ds(0, columns // 2)),
            (slice(None), pl.ds(columns // 2, columns // 2)),
        )
    if rows % 32 == 0:
        return (
            (pl.ds(0, rows // 2), slice(None)),
            (pl.ds(rows // 2, rows // 2), slice(None)),
        )
    if columns % 256 == 0:
        return (
            (slice(None), pl.ds(0, columns // 2)),
            (slice(None), pl.ds(columns // 2, columns // 2)),
        )
    return ((slice(None), slice(None)), None)


def attend_block(limit, qkv_ref, log_ref, context_ref, heads, count):
    width = heads * HEAD_DIM
    size = 8 * count

    def part(n, _):
        at = pl.ds(pl.multiple_of(n * count, count), count)
        allowed = lax.broadcasted_iota(jnp.int32, (1, size), 1) < limit
        lanes = lax.broadcasted_iota(jnp.int32, (count, 128), 1)
        parts, logs = [], jnp.zeros((count, 128), F32)
        for h in range(heads):
            query = qkv_ref[at, h * HEAD_DIM : (h + 1) * HEAD_DIM]
            key = qkv_ref[:, width + h * HEAD_DIM : width + (h + 1) * HEAD_DIM]
            value = qkv_ref[:, 2 * width + h * HEAD_DIM : 2 * width + (h + 1) * HEAD_DIM]
            scores = (
                lax.dot_general(
                    query, key, (((1,), (1,)), ((), ())), preferred_element_type=F32
                )
                * SCORE_SCALE
            )
            scores = jnp.where(allowed, scores, NEG_FILL)
            top = jnp.max(scores, axis=-1, keepdims=True)
            exps = jnp.exp(scores - top)
            total = jnp.sum(exps, axis=-1, keepdims=True)
            mixed = jnp.dot(exps.astype(BF16), value, preferred_element_type=F32)
            parts.append(mixed / total)
            logs = jnp.where(lanes == h, top + jnp.log(total), logs)
        context_ref[n // 2, n % 2] = jnp.concatenate(parts, axis=1).astype(BF16)
        log_ref[at, :] = logs
        return 0

    def block(i):
        lax.fori_loop(2 * i, 2 * i + 2, part, 0)

    return block


def attend_back_block(limit, qkv_ref, log_ref, grad_ref, grad_qkv, grad_key, grad_value, heads, count):
    width = heads * HEAD_DIM
    size = 8 * count
    along_keys = (((1,), (1,)), ((), ()))
    along_rows = (((0,), (0,)), ((), ()))

    def part(n, _):
        at = pl.ds(pl.multiple_of(n * count, count), count)
        allowed = lax.broadcasted_iota(jnp.int32, (1, size), 1) < limit
        grads = grad_ref[n // 2, n % 2]
        parts = []
        for h in range(heads):
            query = qkv_ref[at, h * HEAD_DIM : (h + 1) * HEAD_DIM]
            key = qkv_ref[:, width + h * HEAD_DIM : width + (h + 1) * HEAD_DIM]
            value = qkv_ref[:, 2 * width + h * HEAD_DIM : 2 * width + (h + 1) * HEAD_DIM]
            grad_out = grads[:, h * HEAD_DIM : (h + 1) * HEAD_DIM]
            scores = (
                lax.dot_general(query, key, along_keys, preferred_element_type=F32)
                * SCORE_SCALE
            )
            probs = jnp.where(allowed, jnp.exp(scores - log_ref[at, h : h + 1]), 0.0)
            grad_probs = lax.dot_general(
                grad_out, value, along_keys, preferred_element_type=F32
            )
            delta = jnp.sum(probs * grad_probs, axis=-1, keepdims=True)
            grad_scores = (probs * (grad_probs - delta)).astype(BF16)
            parts.append(
                jnp.dot(grad_scores, key, preferred_element_type=F32) * SCORE_SCALE
            )
            key_part = lax.dot_general(
                grad_scores, query, along_rows, preferred_element_type=F32
            )
            value_part = lax.dot_general(
                probs.astype(BF16), grad_out, along_rows, preferred_element_type=F32
            )
            grad_key[h] += key_part
            grad_value[h] += value_part
        grad_qkv[at, :width] = jnp.concatenate(parts, axis=1).astype(BF16)
        return 0

    def block(i):
        lax.fori_loop(2 * i, 2 * i + 2, part, 0)

    return block


class Scatter:
    def __init__(self, pos, partial, halves, bufs, sems):
        self.pos, self.partial, self.halves = pos, partial, halves
        (self.mine, self.theirs, self.a0, self.a1, self.bx, self.by, self.tz, self.z) = bufs
        (self.sb, self.s0, self.s1, self.dx, self.dy, self.cx, self.cy, self.zs, self.ld) = sems

    @staticmethod
    def scratch(nb, shape, dtype, halves):
        rows, columns = shape
        first, second = half_shapes(shape, halves)
        return [
            pltpu.VMEM((nb, 4) + shape, dtype),
            pltpu.VMEM((nb, 4) + shape, dtype),
            pltpu.VMEM((nb,) + first, dtype),
            pltpu.VMEM((nb,) + second, dtype),
            pltpu.VMEM((nb,) + shape, dtype),
            pltpu.VMEM((nb,) + shape, dtype),
            pltpu.VMEM((nb,) + shape, dtype),
            pltpu.VMEM((nb,) + shape, dtype),
        ]

    @staticmethod
    def sem_scratch(nb):
        return [DMA((2,))] + [DMA((2, nb)) for _ in range(7)] + [DMA]

    def sibling_copy(self):
        pos = self.pos
        return send(
            self.partial.at[:, :, 1 - pos.c], self.theirs, self.sb.at[0], self.sb.at[1], pos.sib
        )

    def begin(self):
        pos = self.pos
        self.sibling_copy().start()
        self.local = pltpu.make_async_copy(
            self.partial.at[:, :, pos.c], self.mine, self.ld
        )
        self.local.start()

    def joined(self):
        self.local.wait()
        self.sibling_copy().wait_recv()

    def copies(self, k):
        pos, mine = self.pos, self.mine
        h0, h1 = self.halves
        z = pos.up(k)

        def copy(src, dst, sems, there):
            return send(src, dst, sems.at[0, k], sems.at[1, k], there)

        first = [
            copy(mine.at[z, pos.pd].at[h0], self.a0.at[k], self.s0, pos.xn),
            copy(mine.at[z, pos.px].at[h0], self.bx.at[k].at[h0], self.dx, pos.xn),
        ]
        second = [copy(mine.at[z, pos.py].at[h0], self.by.at[k].at[h0], self.cy, pos.yn)]
        if h1 is not None:
            first += [
                copy(mine.at[z, pos.pd].at[h1], self.a1.at[k], self.s1, pos.yn),
                copy(mine.at[z, pos.py].at[h1], self.by.at[k].at[h1], self.dy, pos.yn),
            ]
            second.append(
                copy(mine.at[z, pos.px].at[h1], self.bx.at[k].at[h1], self.cx, pos.xn)
            )
        return first, second

    def first(self, k):
        pos, mine = self.pos, self.mine
        z = pos.up(k)
        for j in range(4):
            chip = pos.chip(3 - j)
            mine[z, chip] = (
                mine[z, chip].astype(F32) + self.theirs[z, chip].astype(F32)
            ).astype(mine.dtype)
        for copy in self.copies(k)[0]:
            copy.start()

    def landed(self, ref, sems, k):
        send(ref, ref, sems.at[0, k], sems.at[1, k], self.pos.xn).wait_recv()

    def second(self, k):
        pos, mine = self.pos, self.mine
        h0, h1 = self.halves
        z = pos.up(k)
        copies = self.copies(k)[1]
        self.landed(self.a0.at[k], self.s0, k)
        ref = mine.at[z, pos.py]
        ref[h0] = (ref[h0].astype(F32) + self.a0[k].astype(F32)).astype(mine.dtype)
        copies[0].start()
        if h1 is not None:
            self.landed(self.a1.at[k], self.s1, k)
            ref = mine.at[z, pos.px]
            ref[h1] = (ref[h1].astype(F32) + self.a1[k].astype(F32)).astype(mine.dtype)
            copies[1].start()

    def z_copy(self, k):
        pos = self.pos
        return send(
            self.tz.at[k], self.z.at[k], self.zs.at[0, k], self.zs.at[1, k], (pos.up(k), pos.s)
        )

    def third(self, k, total):
        pos = self.pos
        h0, h1 = self.halves
        z = pos.up(k)
        self.landed(self.bx.at[k].at[h0], self.dx, k)
        self.landed(self.by.at[k].at[h0], self.cy, k)
        if h1 is not None:
            self.landed(self.by.at[k].at[h1], self.dy, k)
            self.landed(self.bx.at[k].at[h1], self.cx, k)
        total[...] = (
            self.mine[z, pos.p].astype(F32)
            + self.bx[k].astype(F32)
            + self.by[k].astype(F32)
        )

        def on():
            self.tz[k] = total[...].astype(self.tz.dtype)
            self.z_copy(k).start()

        guarded(k != 0, on)

    def last(self, total):
        value = total[...]
        for k in range(1, self.pos.nb):
            self.landed(self.z.at[k], self.zs, k)
            value = value + self.z[k].astype(F32)
        total[...] = value

    def drain(self):
        self.sibling_copy().wait_send()

        def done(k, _):
            first, second = self.copies(k)
            for copy in first + second:
                copy.wait_send()
            guarded(k != 0, self.z_copy(k).wait_send)
            return 0

        lax.fori_loop(0, self.pos.nb, done, 0)


def half_shapes(shape, halves):
    def cut(half):
        return tuple(n if h == slice(None) else h.size for n, h in zip(shape, half))

    first = cut(halves[0])
    return first, (first if halves[1] is None else cut(halves[1]))


class RowScatter:
    def __init__(self, pos, out, bufs, sems):
        self.pos, self.out = pos, out
        self.mine, self.a0, self.a1, self.bx, self.by, self.far = bufs
        (self.sm,) = sems

    @staticmethod
    def scratch(rows, columns):
        return [
            pltpu.VMEM((4, 2, rows, columns), BF16),
            pltpu.VMEM((rows, columns), BF16),
            pltpu.VMEM((rows, columns), BF16),
            pltpu.VMEM((2, rows, columns), BF16),
            pltpu.VMEM((2, rows, columns), BF16),
            pltpu.VMEM((rows, columns), F32),
            DMA((2, 7)),
        ]

    def copy(self, i):
        pos, mine = self.pos, self.mine
        src, dst, there = (
            (mine.at[pos.pd, 0], self.a0, pos.xn),
            (mine.at[pos.pd, 1], self.a1, pos.yn),
            (mine.at[pos.px, 0], self.bx.at[0], pos.xn),
            (mine.at[pos.py, 1], self.by.at[1], pos.yn),
            (mine.at[pos.py, 0], self.by.at[0], pos.yn),
            (mine.at[pos.px, 1], self.bx.at[1], pos.xn),
            (self.far, self.out.at[pos.c], pos.sib),
        )[i]
        return send(src, dst, self.sm.at[0, i], self.sm.at[1, i], there)

    def landed(self, i, ref):
        send(ref, ref, self.sm.at[0, i], self.sm.at[1, i], self.pos.xn).wait_recv()

    def first(self):
        for i in range(4):
            self.copy(i).start()

    def second(self):
        pos, mine = self.pos, self.mine
        self.landed(0, self.a0)
        mine[pos.py, 0] = (mine[pos.py, 0].astype(F32) + self.a0[...].astype(F32)).astype(BF16)
        self.copy(4).start()
        self.landed(1, self.a1)
        mine[pos.px, 1] = (mine[pos.px, 1].astype(F32) + self.a1[...].astype(F32)).astype(BF16)
        self.copy(5).start()

    def third(self):
        pos = self.pos
        self.landed(2, self.bx.at[0])
        self.landed(3, self.by.at[1])
        self.landed(4, self.by.at[0])
        self.landed(5, self.bx.at[1])

        def total(core):
            return (
                self.mine[pos.p, core].astype(F32)
                + self.bx[core].astype(F32)
                + self.by[core].astype(F32)
            )

        self.far[...] = total(1 - pos.c)
        self.copy(6).start()
        self.out[pos.c] = total(pos.c)

    def last(self):
        pos = self.pos
        self.landed(6, self.out.at[1 - pos.c])
        for i in range(7):
            self.copy(i).wait_send()


class JointScatter:
    def __init__(self, pos, bufs, sems):
        self.pos = pos
        self.partial, self.mine, self.theirs, self.zbuf, self.sums, self.got = bufs
        self.sb, self.zs, self.ps = sems

    @staticmethod
    def scratch(nb, shape):
        return [
            pltpu.VMEM((nb, 4, 2) + shape, BF16),
            pltpu.VMEM((nb, 4) + shape, BF16),
            pltpu.VMEM((nb, 4) + shape, BF16),
            pltpu.VMEM((nb, 4) + shape, BF16),
            pltpu.VMEM((4,) + shape, BF16),
            pltpu.VMEM((4,) + shape, BF16),
        ]

    @staticmethod
    def sem_scratch(nb):
        return [DMA((2,)), DMA((2, nb)), DMA((2, 4))]

    def sibling_copy(self):
        pos = self.pos
        return send(
            self.partial.at[:, :, 1 - pos.c], self.theirs, self.sb.at[0], self.sb.at[1], pos.sib
        )

    def z_copy(self, d):
        pos = self.pos
        return send(
            self.mine.at[pos.up(d)],
            self.zbuf.at[d],
            self.zs.at[0, d],
            self.zs.at[1, d],
            (pos.up(d), pos.s),
        )

    def plane_copy(self, k):
        pos = self.pos
        chip = pos.chip(k)
        return send(
            self.sums.at[chip],
            self.got.at[k],
            self.ps.at[0, k],
            self.ps.at[1, k],
            (pos.b, 2 * chip + pos.c),
        )

    def begin(self):
        self.sibling_copy().start()

    def first(self):
        pos, mine = self.pos, self.mine
        self.sibling_copy().wait_recv()
        for d in (*range(1, pos.nb), 0):
            z = pos.up(d)
            mine[z] = (
                self.partial[z, :, pos.c].astype(F32) + self.theirs[z].astype(F32)
            ).astype(BF16)
            if d:
                self.z_copy(d).start()

    def second(self):
        pos = self.pos
        value = self.mine[pos.b].astype(F32)
        for d in range(1, pos.nb):
            self.z_copy(d).wait_recv()
            value = value + self.zbuf[d].astype(F32)
        self.sums[...] = value.astype(BF16)
        for k in range(1, 4):
            self.plane_copy(k).start()

    def last(self, out):
        pos = self.pos
        out[pos.p] = self.sums[pos.p].astype(F32)
        for k in range(1, 4):
            self.plane_copy(k).wait_recv()
            out[pos.chip(k)] = self.got[k].astype(F32)
        self.sibling_copy().wait_send()
        for d in range(1, pos.nb):
            self.z_copy(d).wait_send()
        for k in range(1, 4):
            self.plane_copy(k).wait_send()


def back_scatter(
    length, rows, weight, qkv, logs, grad_parts, small, output, expand, reduce, nb, heads
):
    arrays = (small, output, expand, reduce)
    shapes = [a.shape[3:] for a in arrays]
    _, _, count, model_width = rows.shape
    width = heads * HEAD_DIM
    size = 8 * count
    shard = model_width // (8 * nb)
    joint_shape = (-(-(shard + 8) // 16) * 16, 3 * width)

    def body(
        length_ref, rows_ref, weight_ref, qkv_ref, log_ref, parts_ref,
        small_ref, output_ref, expand_ref, reduce_ref,
        rows_out, joint_out, small_out, output_out, expand_out, reduce_out,
        grad_context, grad_qkv, grad_key, grad_value,
        *scratch,
    ):
        pos = Place(nb)
        scratch = list(scratch)

        def take(n):
            got = scratch[:n]
            del scratch[:n]
            return got

        mixing = ContextExchange(pos, parts_ref, grad_context, take(2))
        row_sums = RowScatter(pos, rows_out, take(6), take(1))
        joints = JointScatter(pos, take(6), take(3))
        smalls, outputs, expands, reduces = (
            Scatter(pos, ref, halves_of(ref.shape[3:]), take(8), take(9))
            for ref in (small_ref, output_ref, expand_ref, reduce_ref)
        )
        totals = {smalls: small_out, outputs: output_out, expands: expand_out, reduces: reduce_out}
        units = ((expands, smalls), (reduces,), (outputs,))
        scatters = (expands, smalls, reduces, outputs)
        back = attend_back_block(
            length_ref[0], qkv_ref, log_ref, grad_context, grad_qkv, grad_key, grad_value,
            heads, count,
        )

        def turn(i):
            return (i + 1) % nb

        def third(n, i):
            for scatter in units[n]:
                scatter.third(turn(i), totals[scatter])

        def spread(i, _):
            at = pl.ds(pl.multiple_of(i * 2 * count, 2 * count), 2 * count)
            row_sums.mine[i] = (
                lax.dot_general(
                    grad_qkv[at, :],
                    weight_ref[...],
                    (((1,), (1,)), ((), ())),
                    preferred_element_type=F32,
                )
                .astype(BF16)
                .reshape(2, count, model_width)
            )
            return 0

        def to_rows():
            grad_qkv[:, width : 2 * width] = (
                jnp.concatenate([grad_key[h] for h in range(heads)], axis=1) * SCORE_SCALE
            ).astype(BF16)
            grad_qkv[:, 2 * width :] = jnp.concatenate(
                [grad_value[h] for h in range(heads)], axis=1
            ).astype(BF16)
            lax.fori_loop(0, 4, spread, 0)
            row_sums.first()

        def to_weight():
            for z in range(nb):
                grad_joint = lax.dot_general(
                    rows_ref[:, :, :, z * 8 * shard : (z + 1) * 8 * shard].reshape(
                        size, 8 * shard
                    ),
                    grad_qkv[...],
                    (((0,), (0,)), ((), ())),
                    preferred_element_type=F32,
                )
                joints.partial[z, :, :, :shard] = grad_joint.reshape(
                    4, 2, shard, 3 * width
                ).astype(BF16)
            sums = jnp.sum(grad_qkv[...].astype(F32), axis=0, keepdims=True)
            joints.partial[:, :, :, shard:] = jnp.broadcast_to(
                sums.astype(BF16), (nb, 4, 2, joint_shape[0] - shard, 3 * width)
            )
            joints.begin()

        events = {
            (1, 1): to_rows,
            (1, 2): to_weight,
            (2, 0): joints.first,
            (2, 1): row_sums.second,
            (2, 2): joints.second,
            (3, 0): row_sums.third,
        }

        def slot(i, _):
            for j in range(3):
                if j == 0:
                    guarded(i < 2, lambda: back(3 * i))
                else:
                    guarded(i == 0, lambda j=j: back(j))
                for scatter in units[j]:
                    scatter.second(turn(i))
                guarded(
                    i + 1 < nb,
                    lambda j=j: [scatter.first(turn(i + 1)) for scatter in units[j]],
                )
                if j == 2:
                    third(0, i)
                else:
                    guarded(i > 0, lambda j=j: third(j + 1, i - 1))
                for (when, place), event in events.items():
                    if place == j:
                        guarded(i == when, event)
            return 0

        greet([(pos.up(d), pos.s) for d in range(1, nb)] + plane_others(pos))
        mixing.start()
        for scatter in scatters:
            scatter.begin()
        grad_key[...] = jnp.zeros_like(grad_key)
        grad_value[...] = jnp.zeros_like(grad_value)
        for unit in units:
            for scatter in unit:
                scatter.joined()
                scatter.first(turn(0))
        mixing.arrive()
        lax.fori_loop(0, nb, slot, 0)
        third(1, nb - 1)
        third(2, nb - 1)
        joints.last(joint_out)
        for scatter in scatters:
            scatter.last(totals[scatter])
            scatter.drain()
        row_sums.last()
        mixing.drain()

    scratch = [
        pltpu.VMEM((4, 2, count, width), BF16),
        pltpu.VMEM((size, 3 * width), BF16),
        pltpu.VMEM((heads, size, HEAD_DIM), F32),
        pltpu.VMEM((heads, size, HEAD_DIM), F32),
    ]
    scratch += ContextExchange.scratch() + RowScatter.scratch(count, model_width)
    scratch += JointScatter.scratch(nb, joint_shape) + JointScatter.sem_scratch(nb)
    for array, shape in zip(arrays, shapes):
        scratch += Scatter.scratch(nb, shape, array.dtype, halves_of(shape))
        scratch += Scatter.sem_scratch(nb)
    return pl.pallas_call(
        body,
        out_shape=(
            jax.ShapeDtypeStruct((2, count, model_width), F32),
            jax.ShapeDtypeStruct((4,) + joint_shape, F32),
        )
        + tuple(jax.ShapeDtypeStruct(shape, F32) for shape in shapes),
        in_specs=[SM] + [VM] * 4 + [ANY] * 5,
        out_specs=(VM,) * 6,
        scratch_shapes=scratch,
        name="back_scatter",
        compiler_params=pltpu.CompilerParams(
            collective_id=4, has_side_effects=True, vmem_limit_bytes=VMEM_LIMIT
        ),
    )(length, rows, weight, qkv, logs, grad_parts, small, output, expand, reduce)


def plane_on_device(
    inputs,
    cotangent,
    lengths,
    joint_weight,
    output_weight,
    vectors,
    expand_weight,
    expand_bias,
    reduce_weight,
):
    nb = lax.axis_size("batch")
    seq_count, row_count, model_width = inputs.shape
    tokens = seq_count * row_count
    hidden_width = expand_weight.shape[1]
    place = lax.axis_index("seq")
    core, chip = place % 2, place // 2
    width = model_width // 4
    heads = width // HEAD_DIM
    vec = vectors.shape[1]
    per = expand_bias.shape[0]
    owners = 8 * nb

    flat_inputs = inputs.reshape(tokens, model_width)
    shard = joint_weight.shape[0]
    pad = -(shard + 8) % 16 + 8
    joint_parts = joint_weight.reshape(shard, 3, 4, width).transpose(2, 0, 1, 3)
    joint_parts = joint_parts.reshape(4, shard, 3 * width)
    first_column = vec * (8 * lax.axis_index("batch") + place)
    spot = lax.dynamic_update_slice_in_dim(
        jnp.zeros((2, model_width), BF16), vectors[2:4], first_column, 1
    ).reshape(2, 4, width)
    spot = jnp.concatenate([spot[0], jnp.zeros_like(spot[0]), spot[1]], axis=1)
    spot = jnp.pad(spot[:, None], ((0, 0), (0, pad - 1), (0, 0)))
    joint_parts = jnp.concatenate([joint_parts, spot], axis=1)
    small = jnp.concatenate(
        [
            jnp.pad(vectors, ((0, 0), (0, 128 - vec))),
            jnp.pad(expand_bias[None], ((0, 7), (0, 128 - per))),
        ]
    )
    length = lax.dynamic_slice_in_dim(lengths, core, 1)
    (
        rows_all, joint_all, qkv, logs, vector_rows, full_bias,
        mixed, output_all, expand_all, reduce_all,
    ) = gather_attend(
        length,
        inputs.astype(BF16),
        joint_parts,
        small,
        output_weight,
        expand_weight,
        reduce_weight,
        nb,
        model_width,
        heads,
    )
    full_output = output_all.reshape(model_width, model_width)
    full_expand = expand_all.reshape(model_width, hidden_width)
    full_reduce = reduce_all.reshape(hidden_width, model_width)

    context_low = mixed.transpose(1, 2, 0, 3).reshape(tokens, model_width)

    branch = jnp.dot(context_low, full_output, preferred_element_type=F32) + vector_rows[4]
    first, first_normed, first_inverse = layer_norm(
        flat_inputs + branch, vector_rows[0], vector_rows[1]
    )
    first_low = first.astype(BF16)
    before_gelu = jnp.dot(first_low, full_expand, preferred_element_type=F32) + full_bias
    hidden_low = gelu_value(before_gelu).astype(BF16)
    feed = jnp.dot(hidden_low, full_reduce, preferred_element_type=F32) + vector_rows[7]
    result, second_normed, second_inverse = layer_norm(first + feed, vector_rows[5], vector_rows[6])

    own_places = place * row_count + jnp.arange(row_count, dtype=jnp.int32)
    row_mask = (own_places[None, :] < lengths[:, None]).reshape(tokens, 1).astype(F32)
    grad_res = cotangent.reshape(tokens, model_width) * row_mask
    grad_second, grad_gain_two, grad_shift_two = norm_back(
        grad_res, second_normed, second_inverse, vector_rows[5]
    )
    grad_feed_low = grad_second.astype(BF16)
    grad_reduce = jnp.dot(hidden_low.T, grad_feed_low, preferred_element_type=F32)
    grad_hidden = jnp.dot(
        grad_feed_low, full_reduce.T, preferred_element_type=F32
    ) * gelu_slope(before_gelu)
    grad_hidden_low = grad_hidden.astype(BF16)
    grad_expand = jnp.dot(first_low.T, grad_hidden_low, preferred_element_type=F32)
    grad_bias = jnp.sum(grad_hidden_low.astype(F32), axis=0)
    grad_first = grad_second + jnp.dot(
        grad_hidden_low, full_expand.T, preferred_element_type=F32
    )
    grad_resid, grad_gain_one, grad_shift_one = norm_back(
        grad_first, first_normed, first_inverse, vector_rows[0]
    )
    grad_branch_low = grad_resid.astype(BF16)
    grad_output = jnp.dot(context_low.T, grad_branch_low, preferred_element_type=F32)
    grad_context_low = jnp.dot(
        grad_branch_low, full_output.T, preferred_element_type=F32
    ).astype(BF16)

    parts = grad_context_low.reshape(seq_count, row_count, 4, width).transpose(2, 0, 1, 3)
    grad_vectors = jnp.stack(
        [
            grad_gain_one,
            grad_shift_one,
            jnp.zeros((model_width,), F32),
            jnp.zeros((model_width,), F32),
            jnp.sum(grad_branch_low.astype(F32), axis=0),
            grad_gain_two,
            grad_shift_two,
            jnp.sum(grad_feed_low.astype(F32), axis=0),
        ]
    )
    grad_small = jnp.concatenate(
        [
            jnp.pad(
                grad_vectors.reshape(8, owners, vec).transpose(1, 0, 2),
                ((0, 0), (0, 0), (0, 128 - vec)),
            ),
            jnp.pad(grad_bias.reshape(owners, 1, per), ((0, 0), (0, 7), (0, 128 - per))),
        ],
        axis=1,
    )

    def split(partial):
        return partial.reshape((nb, 4, 2, partial.shape[0] // owners) + partial.shape[1:])

    rows_sum, joint_sum, small_sum, output_sum, expand_sum, reduce_sum = back_scatter(
        length,
        rows_all,
        joint_all,
        qkv,
        logs,
        parts,
        grad_small.reshape(nb, 4, 2, 16, 128),
        split(grad_output.astype(BF16)),
        split(grad_expand.astype(BF16)),
        split(grad_reduce.astype(BF16)),
        nb,
        heads,
    )
    sums = lax.dynamic_slice(
        joint_sum[:, shard].reshape(4, 3, width),
        (first_column // width, 0, first_column % width),
        (1, 3, vec),
    )[0]
    vectors_sum = jnp.concatenate(
        [small_sum[:2, :vec], sums[0:1], sums[2:3], small_sum[4:8, :vec]], axis=0
    )
    joint_sum = joint_sum[:, :shard].reshape(4, shard, 3, width).transpose(1, 2, 0, 3)
    return (
        result.reshape(seq_count, row_count, model_width),
        grad_resid.reshape(seq_count, row_count, model_width) + rows_sum,
        joint_sum.reshape(shard, 3 * model_width),
        output_sum,
        vectors_sum,
        expand_sum,
        small_sum[8, :per],
        reduce_sum,
    )


def plane_fits(mesh, inputs, expand_bias, expand_weight):
    return (
        mesh.shape["seq"] == 8
        and mesh.shape["batch"] == 4
        and inputs[0] == 2 * mesh.shape["batch"]
        and HEADS % 4 == 0
        and inputs[2] == HEADS * HEAD_DIM
        and inputs[1] % (8 * 16) == 0
        and inputs[2] % 256 == 0
        and expand_weight[0] % (8 * 32) == 0
        and expand_weight[1] % (16 * 32) == 0
        and expand_bias[0] <= 128 * 32
    )


def solution(mesh):
    def program(*args):
        fits = plane_fits(mesh, args[0].shape, args[7].shape, args[6].shape)
        return jax.shard_map(
            plane_on_device if fits else general_on_device,
            mesh=mesh,
            in_specs=(
                P("batch", "seq", None),
                P("batch", "seq", None),
                P("batch"),
                P(("batch", "seq"), None),
                P(("batch", "seq"), None),
                P(None, ("batch", "seq")),
                P(("batch", "seq"), None),
                P(("batch", "seq")),
                P(("batch", "seq"), None),
            ),
            out_specs=(
                P("batch", "seq", None),
                P("batch", "seq", None),
                P(("batch", "seq"), None),
                P(("batch", "seq"), None),
                P(None, ("batch", "seq")),
                P(("batch", "seq"), None),
                P(("batch", "seq")),
                P(("batch", "seq"), None),
            ),
            check_vma=False,
        )(*args)

    return program
```

```python
import functools
import math

import jax
import jax.numpy as jnp
from jax import lax
from jax.experimental import pallas as pl
from jax.experimental.pallas import tpu as pltpu
from jax.sharding import PartitionSpec as P

HEADS = 12
HEAD_DIM = 64


EPSILON = 1e-12
SCORE_SCALE = 0.125
NEG_FILL = -1e30
HALF_ROOT = 0.7071067811865476
INV_ROOT_TAU = 0.3989422804014327
block_limit = 256


def layer_norm(residual, norm_gain, norm_shift):
    centered = residual - jnp.mean(residual, axis=-1, keepdims=True)
    inverse = lax.rsqrt(jnp.mean(centered * centered, axis=-1, keepdims=True) + EPSILON)
    normed = centered * inverse
    return (normed * norm_gain + norm_shift, normed, inverse)


def norm_back(grad_out, normed, inverse, norm_gain):
    grad_normed = grad_out * norm_gain
    mean_grad = jnp.mean(grad_normed, axis=-1, keepdims=True)
    mean_proj = jnp.mean(grad_normed * normed, axis=-1, keepdims=True)
    grad_in = inverse * (grad_normed - mean_grad - normed * mean_proj)
    return (grad_in, jnp.sum(grad_out * normed, axis=0), jnp.sum(grad_out, axis=0))


def gelu_value(before_gelu):
    return 0.5 * before_gelu * (1.0 + lax.erf(before_gelu * HALF_ROOT))


def gelu_slope(before_gelu):
    return (
        0.5 * (1.0 + lax.erf(before_gelu * HALF_ROOT))
        + before_gelu * jnp.exp(-0.5 * before_gelu * before_gelu) * INV_ROOT_TAU
    )


def over_blocks(piece_rows, block_fn, carried):
    block_size = math.gcd(piece_rows, block_limit)

    def run_block(block_index, current):
        return block_fn(current, block_index * block_size, block_size)

    return lax.fori_loop(0, piece_rows // block_size, run_block, carried)


def head_scores(left_heads, right_heads, right_places, lengths):
    scores = (
        jnp.einsum("sqhd,skhd->shqk", left_heads, right_heads, preferred_element_type=jnp.float32)
        * SCORE_SCALE
    )
    allowed = right_places[None, :] < lengths[:, None]
    return jnp.where(allowed[:, None, None, :], scores, NEG_FILL)


def cut_heads(gathered_piece, offset, block_size, head_count):
    sliced = lax.dynamic_slice_in_dim(gathered_piece, offset, block_size, 1)
    return sliced.reshape(sliced.shape[0], block_size, head_count, -1)


def gather_attention(joint_weight, output_weight, vectors):
    return (
        lax.all_gather(joint_weight, ("batch", "seq"), axis=0, tiled=True),
        lax.all_gather(output_weight, ("batch", "seq"), axis=0, tiled=True),
        lax.all_gather(vectors, ("batch", "seq"), axis=1, tiled=True),
    )


def gather_feed(expand_weight, reduce_weight, expand_bias):
    return (
        lax.all_gather(expand_weight, ("batch", "seq"), axis=0, tiled=True),
        lax.all_gather(reduce_weight, ("batch", "seq"), axis=0, tiled=True),
        lax.all_gather(expand_bias, ("batch", "seq"), axis=0, tiled=True),
    )


def general_on_device(
    inputs,
    cotangent,
    lengths,
    joint_weight,
    output_weight,
    vectors,
    expand_weight,
    expand_bias,
    reduce_weight,
):
    seq_count, row_count, model_width = inputs.shape
    head_count = HEADS
    head_size = HEAD_DIM
    tokens = seq_count * row_count
    head_shape = (seq_count, row_count, head_count, head_size)
    own_places = lax.axis_index("seq") * row_count + jnp.arange(row_count, dtype=jnp.int32)
    row_valid = own_places[None, :] < lengths[:, None]
    row_mask = row_valid.reshape(tokens, 1).astype(jnp.float32)
    full_joint, full_output, full_vectors = gather_attention(joint_weight, output_weight, vectors)
    vector_rows = full_vectors.astype(jnp.float32)
    flat_inputs = inputs.reshape(tokens, model_width)
    input_low = flat_inputs.astype(jnp.bfloat16)
    projected = jnp.dot(input_low, full_joint, preferred_element_type=jnp.float32)
    query_low = (projected[:, :model_width] + vector_rows[2]).astype(jnp.bfloat16)
    key_low = projected[:, model_width : 2 * model_width].astype(jnp.bfloat16)
    value_low = (projected[:, 2 * model_width :] + vector_rows[3]).astype(jnp.bfloat16)
    query_heads = query_low.reshape(head_shape)
    key_rows = key_low.reshape(seq_count, row_count, model_width)
    value_rows = value_low.reshape(seq_count, row_count, model_width)
    start_state = (
        jnp.full((seq_count, head_count, row_count), NEG_FILL, jnp.float32),
        jnp.zeros((seq_count, head_count, row_count), jnp.float32),
        jnp.zeros(head_shape, jnp.float32),
    )
    key_piece = lax.all_gather(key_rows, "seq", axis=1, tiled=True)
    value_piece = lax.all_gather(value_rows, "seq", axis=1, tiled=True)

    def forward_score_block(current, offset, block_size):
        running_max, running_sum, summed = current
        key_heads = cut_heads(key_piece, offset, block_size, head_count)
        value_heads = cut_heads(value_piece, offset, block_size, head_count)
        key_places = offset + jnp.arange(block_size, dtype=jnp.int32)
        scores = head_scores(query_heads, key_heads, key_places, lengths)
        new_max = jnp.maximum(running_max, jnp.max(scores, axis=-1))
        factor = jnp.exp(running_max - new_max)
        exp_scores = jnp.exp(scores - new_max[..., None])
        running_sum = running_sum * factor + jnp.sum(exp_scores, axis=-1)
        update = jnp.einsum(
            "shqk,skhd->sqhd",
            exp_scores.astype(jnp.bfloat16),
            value_heads,
            preferred_element_type=jnp.float32,
        )
        summed = summed * jnp.transpose(factor, (0, 2, 1))[..., None] + update
        return (new_max, running_sum, summed)

    running_max, running_sum, summed = over_blocks(
        key_piece.shape[1], forward_score_block, start_state
    )
    attended = summed / jnp.transpose(running_sum, (0, 2, 1))[..., None]
    log_total = jnp.transpose(running_max + jnp.log(running_sum), (0, 2, 1))
    context_low = attended.reshape(tokens, model_width).astype(jnp.bfloat16)
    branch = jnp.dot(context_low, full_output, preferred_element_type=jnp.float32) + vector_rows[4]
    first, first_normed, first_inverse = layer_norm(
        flat_inputs + branch, vector_rows[0], vector_rows[1]
    )
    first_low = first.astype(jnp.bfloat16)
    full_expand, full_reduce, full_bias = gather_feed(expand_weight, reduce_weight, expand_bias)
    before_gelu = jnp.dot(
        first_low, full_expand, preferred_element_type=jnp.float32
    ) + full_bias.astype(jnp.float32)
    hidden_low = gelu_value(before_gelu).astype(jnp.bfloat16)
    feed = jnp.dot(hidden_low, full_reduce, preferred_element_type=jnp.float32) + vector_rows[7]
    result, second_normed, second_inverse = layer_norm(first + feed, vector_rows[5], vector_rows[6])
    full_expand, full_reduce, full_bias = gather_feed(expand_weight, reduce_weight, expand_bias)
    full_joint, full_output, full_vectors = gather_attention(joint_weight, output_weight, vectors)
    grad_res = cotangent.reshape(tokens, model_width) * row_mask
    grad_second, grad_gain_two, grad_shift_two = norm_back(
        grad_res, second_normed, second_inverse, vector_rows[5]
    )
    grad_feed_low = grad_second.astype(jnp.bfloat16)
    grad_reduce_local = jnp.dot(hidden_low.T, grad_feed_low, preferred_element_type=jnp.float32)
    grad_hidden = jnp.dot(
        grad_feed_low, full_reduce.T, preferred_element_type=jnp.float32
    ) * gelu_slope(before_gelu)
    grad_hidden_low = grad_hidden.astype(jnp.bfloat16)
    grad_expand_local = jnp.dot(first_low.T, grad_hidden_low, preferred_element_type=jnp.float32)
    grad_bias_local = jnp.sum(grad_hidden_low.astype(jnp.float32), axis=0)
    grad_first = grad_second + jnp.dot(
        grad_hidden_low, full_expand.T, preferred_element_type=jnp.float32
    )
    grad_resid, grad_gain_one, grad_shift_one = norm_back(
        grad_first, first_normed, first_inverse, vector_rows[0]
    )
    grad_branch_low = grad_resid.astype(jnp.bfloat16)
    grad_output_local = jnp.dot(context_low.T, grad_branch_low, preferred_element_type=jnp.float32)
    grad_context_low = jnp.dot(
        grad_branch_low, full_output.T, preferred_element_type=jnp.float32
    ).astype(jnp.bfloat16)
    grad_context_heads = grad_context_low.reshape(head_shape)
    row_delta = jnp.sum(grad_context_heads.astype(jnp.float32) * attended, axis=-1)
    log_heads = jnp.transpose(log_total, (0, 2, 1))
    delta_heads = jnp.transpose(row_delta, (0, 2, 1))
    query_key_piece = lax.all_gather(key_rows, "seq", axis=1, tiled=True)
    query_value_piece = lax.all_gather(value_rows, "seq", axis=1, tiled=True)

    def query_score_block(current, offset, block_size):
        key_heads = cut_heads(query_key_piece, offset, block_size, head_count)
        value_heads = cut_heads(query_value_piece, offset, block_size, head_count)
        key_places = offset + jnp.arange(block_size, dtype=jnp.int32)
        scores = head_scores(query_heads, key_heads, key_places, lengths)
        softmax_rows = jnp.exp(scores - log_heads[..., None])
        grad_probs = jnp.einsum(
            "sqhd,skhd->shqk", grad_context_heads, value_heads, preferred_element_type=jnp.float32
        )
        grad_scores = (softmax_rows * (grad_probs - delta_heads[..., None])).astype(jnp.bfloat16)
        return (
            current
            + jnp.einsum(
                "shqk,skhd->sqhd", grad_scores, key_heads, preferred_element_type=jnp.float32
            )
            * SCORE_SCALE
        )

    grad_query = over_blocks(
        query_key_piece.shape[1], query_score_block, jnp.zeros(head_shape, jnp.float32)
    )
    own_keys = key_low.reshape(head_shape)
    own_values = value_low.reshape(head_shape)
    query_rows = query_low.reshape(seq_count, row_count, model_width)
    grad_context_rows = grad_context_low.reshape(seq_count, row_count, model_width)
    zero_heads = jnp.zeros(head_shape, jnp.float32)
    query_piece = lax.all_gather(query_rows.astype(jnp.float32), "seq", axis=1, tiled=True).astype(
        jnp.bfloat16
    )
    grad_piece = lax.all_gather(
        grad_context_rows.astype(jnp.float32), "seq", axis=1, tiled=True
    ).astype(jnp.bfloat16)
    log_piece = lax.all_gather(log_total, "seq", axis=1, tiled=True)
    delta_piece = lax.all_gather(row_delta, "seq", axis=1, tiled=True)

    def key_score_block(current, offset, block_size):
        grad_key, grad_value = current
        query_block = cut_heads(query_piece, offset, block_size, head_count)
        grad_block = cut_heads(grad_piece, offset, block_size, head_count)
        log_block = jnp.transpose(
            lax.dynamic_slice_in_dim(log_piece, offset, block_size, 1), (0, 2, 1)
        )
        delta_block = jnp.transpose(
            lax.dynamic_slice_in_dim(delta_piece, offset, block_size, 1), (0, 2, 1)
        )
        scores = head_scores(query_block, own_keys, own_places, lengths)
        softmax_rows = jnp.exp(scores - log_block[..., None])
        grad_value = grad_value + jnp.einsum(
            "shqk,sqhd->skhd",
            softmax_rows.astype(jnp.bfloat16),
            grad_block,
            preferred_element_type=jnp.float32,
        )
        grad_probs = jnp.einsum(
            "sqhd,skhd->shqk", grad_block, own_values, preferred_element_type=jnp.float32
        )
        grad_scores = (softmax_rows * (grad_probs - delta_block[..., None])).astype(jnp.bfloat16)
        grad_key = (
            grad_key
            + jnp.einsum(
                "shqk,sqhd->skhd", grad_scores, query_block, preferred_element_type=jnp.float32
            )
            * SCORE_SCALE
        )
        return (grad_key, grad_value)

    grad_key, grad_value = over_blocks(
        query_piece.shape[1], key_score_block, (zero_heads, zero_heads)
    )
    grad_query_low = grad_query.reshape(tokens, model_width).astype(jnp.bfloat16)
    grad_key_low = grad_key.reshape(tokens, model_width).astype(jnp.bfloat16)
    grad_value_low = grad_value.reshape(tokens, model_width).astype(jnp.bfloat16)
    grad_projected = jnp.concatenate([grad_query_low, grad_key_low, grad_value_low], axis=1)
    grad_joint_local = jnp.dot(input_low.T, grad_projected, preferred_element_type=jnp.float32)
    grad_inputs = grad_resid + jnp.dot(
        grad_projected, full_joint.T, preferred_element_type=jnp.float32
    )
    grad_vector_local = jnp.stack(
        [
            grad_gain_one,
            grad_shift_one,
            jnp.sum(grad_query_low.astype(jnp.float32), axis=0),
            jnp.sum(grad_value_low.astype(jnp.float32), axis=0),
            jnp.sum(grad_branch_low.astype(jnp.float32), axis=0),
            grad_gain_two,
            grad_shift_two,
            jnp.sum(grad_feed_low.astype(jnp.float32), axis=0),
        ],
        axis=0,
    )
    every_grad = (
        lax.psum_scatter(grad_joint_local, ("batch", "seq"), scatter_dimension=0, tiled=True),
        lax.psum_scatter(grad_output_local, ("batch", "seq"), scatter_dimension=0, tiled=True),
        lax.psum_scatter(grad_vector_local, ("batch", "seq"), scatter_dimension=1, tiled=True),
        lax.psum_scatter(grad_expand_local, ("batch", "seq"), scatter_dimension=0, tiled=True),
        lax.psum_scatter(grad_reduce_local, ("batch", "seq"), scatter_dimension=0, tiled=True),
        lax.psum_scatter(grad_bias_local, ("batch", "seq"), scatter_dimension=0, tiled=True),
    )
    summed_grads = (
        every_grad[0],
        every_grad[1],
        every_grad[2],
        every_grad[3],
        every_grad[5],
        every_grad[4],
    )
    return (
        result.reshape(seq_count, row_count, model_width),
        grad_inputs.reshape(seq_count, row_count, model_width),
        summed_grads[0],
        summed_grads[1],
        summed_grads[2],
        summed_grads[3],
        summed_grads[4],
        summed_grads[5],
    )


MESH = pl.DeviceIdType.MESH
ANY = pl.BlockSpec(memory_space=pl.ANY)
VM = pl.BlockSpec(memory_space=pltpu.VMEM)
SM = pl.BlockSpec(memory_space=pltpu.SMEM)
DMA = pltpu.SemaphoreType.DMA
VMEM_LIMIT = 60 << 20
F32 = jnp.float32
BF16 = jnp.bfloat16


def send(src, dst, send_sem, recv_sem, device):
    return pltpu.make_async_remote_copy(
        src_ref=src,
        dst_ref=dst,
        send_sem=send_sem,
        recv_sem=recv_sem,
        device_id=device,
        device_id_type=MESH,
    )


class Place:
    def __init__(self, nb):
        self.nb = nb
        self.b = lax.axis_index("batch")
        self.s = lax.axis_index("seq")
        self.c = self.s % 2
        self.p = self.s // 2
        x, y = self.p % 2, self.p // 2
        self.px = 2 * y + (1 - x)
        self.py = 2 * (1 - y) + x
        self.pd = 2 * (1 - y) + (1 - x)
        self.sib = (self.b, 2 * self.p + 1 - self.c)
        self.xn = (self.b, 2 * self.px + self.c)
        self.yn = (self.b, 2 * self.py + self.c)

    def chip(self, step):
        return (self.p, self.px, self.py, self.pd)[step]

    def up(self, step):
        return (self.b + step) % self.nb

    def down(self, step):
        return (self.b + self.nb - step) % self.nb


def greet_near(pos):
    barrier = pltpu.get_barrier_semaphore()

    def signal(device):
        pl.semaphore_signal(barrier, inc=1, device_id=device, device_id_type=MESH)

    for device in plane_others(pos):
        signal(device)
    last = pos.nb - 1
    guarded(pos.b < last, lambda: signal(((pos.b + 1) % pos.nb, pos.s)))
    guarded(pos.b > 0, lambda: signal(((pos.b + last) % pos.nb, pos.s)))
    beside = jnp.where(pos.b < last, 1, 0) + jnp.where(pos.b > 0, 1, 0)
    pl.semaphore_wait(barrier, 7 + beside)


def same_core(pos):
    return [
        (pos.up(d), 2 * pos.chip(k) + pos.c)
        for d in range(pos.nb)
        for k in range(4)
        if d or k
    ]


def plane_others(pos):
    return [
        (pos.b, 2 * pos.chip(k) + (pos.c if j == 0 else 1 - pos.c))
        for k in range(4)
        for j in range(2)
        if k or j
    ]


def guarded(condition, action):
    if isinstance(condition, bool):
        if condition:
            action()
    else:

        @pl.when(condition)
        def _():
            action()


class Chain:
    def __init__(self, pos, mine, spot, sems):
        self.pos, self.mine, self.spot = pos, mine, spot
        self.up, self.down = sems

    @staticmethod
    def scratch(nb):
        return [DMA((2, nb)), DMA((2, nb))]

    def copy(self, src, z, sems, hop, there):
        pos = self.pos
        return send(src, self.spot(z), sems.at[0, hop], sems.at[1, hop], (there, pos.s))

    def moves(self, hop):
        pos = self.pos
        last = pos.nb - 1
        low, high = (pos.b - hop + 1 + pos.nb) % pos.nb, (pos.b + hop - 1) % pos.nb
        above, below = (pos.b + 1) % pos.nb, (pos.b + last) % pos.nb
        own = isinstance(hop, int) and hop == 1
        return (
            (
                (pos.b >= hop - 1) & (pos.b < last),
                self.copy(self.mine if own else self.spot(low), low, self.up, hop, above),
            ),
            (
                (pos.b + hop - 1 < pos.nb) & (pos.b > 0),
                self.copy(self.mine if own else self.spot(high), high, self.down, hop, below),
            ),
        )

    def start(self, hop=1):
        for made, copy in self.moves(hop):
            guarded(made, copy.start)

    def hop(self, hop):
        pos = self.pos
        low, high = (pos.b - hop + pos.nb) % pos.nb, (pos.b + hop) % pos.nb
        for made, z, sems in (
            (pos.b >= hop, low, self.up),
            (pos.b + hop < pos.nb, high, self.down),
        ):
            guarded(made, self.copy(self.spot(z), z, sems, hop, pos.b).wait_recv)
        guarded(hop < pos.nb - 1, lambda: self.start(hop + 1))

    def drain(self):
        for hop in range(1, self.pos.nb):
            for made, copy in self.moves(hop):
                guarded(made, copy.wait_send)


class Gather:
    def __init__(self, pos, shard, out, halves, tall, sems):
        self.tall = tall
        self.pos, self.shard, self.out, self.halves = pos, shard, out, halves
        self.xs, self.ys, self.f0, self.f1, self.sb, self.local_sem = sems[:6]
        self.chain = Chain(pos, shard, lambda z: out.at[z, pos.p, pos.c], sems[6:8])
        self.across = Chain(
            pos, out.at[pos.b, pos.pd, pos.c], lambda z: out.at[z, pos.pd, pos.c], sems[8:]
        )

    @staticmethod
    def scratch(nb):
        return [DMA((2, nb))] * 5 + [DMA] + Chain.scratch(nb) * 2

    def z(self, k):
        return jnp.where(k <= self.pos.b, self.pos.b - k, k)

    def own(self):
        pos = self.pos
        self.local = pltpu.make_async_copy(
            self.shard, self.out.at[pos.b, pos.p, pos.c], self.local_sem
        )
        self.local.start()

    def x_copy(self, k, src=None):
        pos = self.pos
        there = self.out.at[self.z(k), pos.p, pos.c]
        src = there if src is None else src
        return send(src, there, self.xs.at[0, k], self.xs.at[1, k], pos.xn)

    def y_copy(self, k, src=None):
        pos = self.pos
        there = self.out.at[self.z(k), pos.p, pos.c]
        src = there if src is None else src
        return send(src, there, self.ys.at[0, k], self.ys.at[1, k], pos.yn)

    def plane(self, k, src=None):
        self.x_copy(k, src).start()
        self.y_copy(k, src).start()

    def landed(self, sems, k, chip):
        pos = self.pos
        ref = self.out.at[self.z(k), chip, pos.c]
        send(ref, ref, sems.at[0, k], sems.at[1, k], pos.xn).wait_recv()

    def y_forward(self, k):
        pos = self.pos
        ref = self.out.at[self.z(k), pos.px, pos.c].at[self.halves[0]]
        return send(ref, ref, self.f0.at[0, k], self.f0.at[1, k], pos.yn)

    def x_forward(self, k):
        pos = self.pos
        ref = self.out.at[self.z(k), pos.py, pos.c].at[self.halves[1]]
        return send(ref, ref, self.f1.at[0, k], self.f1.at[1, k], pos.xn)

    def two_ways(self, k):
        return True if not self.tall else k == 0

    def forward(self, k):
        pos = self.pos
        self.landed(self.xs, k, pos.px)
        guarded(self.two_ways(k), lambda: self.y_forward(k).start())
        self.landed(self.ys, k, pos.py)
        if self.halves[1] is not None:
            guarded(self.two_ways(k), lambda: self.x_forward(k).start())

    def crossed(self, k):
        pos = self.pos
        across = self.out.at[self.z(k), pos.pd, pos.c]
        for half, sems in zip(self.halves, (self.f0, self.f1)):
            if half is not None:
                ref = across.at[half]
                send(ref, ref, sems.at[0, k], sems.at[1, k], pos.xn).wait_recv()

    def complete(self, k):
        if not self.tall:
            self.crossed(k)
        elif isinstance(k, int) and k == 0:
            self.crossed(k)
            self.across.start()
        else:
            self.across.hop(k)

    def sibling_copy(self, k):
        pos = self.pos
        ref = self.out.at[self.z(k), :, pos.c]
        return send(ref, ref, self.sb.at[0, k], self.sb.at[1, k], pos.sib)

    def sibling(self, k):
        self.sibling_copy(k).start()

    def finish(self, k):
        pos = self.pos
        ref = self.out.at[self.z(k), :, 1 - pos.c]
        send(ref, ref, self.sb.at[0, k], self.sb.at[1, k], pos.sib).wait_recv()
        self.x_copy(k).wait_send()
        self.y_copy(k).wait_send()
        self.sibling_copy(k).wait_send()
        guarded(self.two_ways(k), lambda: self.y_forward(k).wait_send())
        if self.halves[1] is not None:
            guarded(self.two_ways(k), lambda: self.x_forward(k).wait_send())

    def drain(self):
        self.chain.drain()
        if self.tall:
            self.across.drain()


class InputExchange:
    def __init__(self, pos, rows, out, sems):
        self.pos, self.rows, self.out, self.sems = pos, rows, out, sems
        self.started = []

    @staticmethod
    def scratch():
        return [DMA((2, 2)), DMA((2, 2)), DMA((2, 2)), DMA((2,)), DMA]

    def go(self, copy):
        copy.start()
        self.started.append(copy)

    def start(self):
        pos, (xs, ys, _, sb, local) = self.pos, self.sems
        there = self.out.at[pos.p, pos.c]
        for sems, chip in ((xs, pos.px), (ys, pos.py)):
            for j in range(2):
                self.go(
                    send(
                        self.rows.at[j],
                        there,
                        sems.at[0, j],
                        sems.at[1, pos.c],
                        (pos.b, 2 * chip + j),
                    )
                )
        self.go(send(self.rows.at[1 - pos.c], there, sb.at[0], sb.at[1], pos.sib))
        self.local = pltpu.make_async_copy(self.rows.at[pos.c], there, local)
        self.local.start()

    def landed(self, sems, j, chip):
        ref = self.out.at[chip, j]
        send(ref, ref, sems.at[0, j], sems.at[1, j], self.pos.xn).wait_recv()

    def forward(self):
        pos, (xs, ys, fs, _, _) = self.pos, self.sems
        self.landed(xs, 0, pos.px)
        ref = self.out.at[pos.px, 0]
        self.go(send(ref, ref, fs.at[0, 0], fs.at[1, 0], pos.yn))
        self.landed(ys, 1, pos.py)
        ref = self.out.at[pos.py, 1]
        self.go(send(ref, ref, fs.at[0, 1], fs.at[1, 1], pos.xn))

    def finish(self):
        pos, (xs, ys, fs, sb, _) = self.pos, self.sems
        self.landed(xs, 1, pos.px)
        self.landed(ys, 0, pos.py)
        self.landed(fs, 0, pos.pd)
        self.landed(fs, 1, pos.pd)
        ref = self.out.at[pos.p, 1 - pos.c]
        send(ref, ref, sb.at[0], sb.at[1], pos.sib).wait_recv()
        self.local.wait()

    def drain(self):
        for copy in self.started:
            copy.wait_send()


class JointGather:
    def __init__(self, pos, parts, out, sems):
        self.pos, self.parts, self.out = pos, parts, out
        self.direct, self.sb, self.local_sem = sems[:3]
        self.chain = Chain(
            pos, out.at[pos.b, :, pos.c], lambda z: out.at[z, :, pos.c], sems[3:]
        )

    @staticmethod
    def scratch(nb):
        return [DMA((2, 4)), DMA((2,)), DMA] + Chain.scratch(nb)

    def start(self):
        pos = self.pos
        there = self.out.at[pos.b, pos.p, pos.c]
        self.started = [
            send(
                self.parts.at[pos.chip(k)],
                there,
                self.direct.at[0, k],
                self.direct.at[1, k],
                (pos.b, 2 * pos.chip(k) + pos.c),
            )
            for k in range(1, 4)
        ]
        for copy in self.started:
            copy.start()
        self.local = pltpu.make_async_copy(self.parts.at[pos.p], there, self.local_sem)
        self.local.start()

    def own(self):
        pos = self.pos
        for k in range(1, 4):
            ref = self.out.at[pos.b, pos.chip(k), pos.c]
            send(ref, ref, self.direct.at[0, k], self.direct.at[1, k], pos.sib).wait_recv()
        self.local.wait()
        self.chain.start()

    def sibling(self):
        pos = self.pos
        ref = self.out.at[:, :, pos.c]
        send(ref, ref, self.sb.at[0], self.sb.at[1], pos.sib).start()

    def finish(self):
        pos = self.pos
        ref = self.out.at[:, :, 1 - pos.c]
        send(ref, ref, self.sb.at[0], self.sb.at[1], pos.sib).wait_recv()

    def drain(self):
        for copy in self.started:
            copy.wait_send()
        ref = self.out.at[:, :, self.pos.c]
        send(ref, ref, self.sb.at[0], self.sb.at[1], self.pos.sib).wait_send()
        self.chain.drain()


class ContextExchange:
    def __init__(self, pos, parts, out, sems):
        self.pos, self.parts, self.out = pos, parts, out
        self.sems, self.local_sem = sems

    @staticmethod
    def scratch():
        return [DMA((2, 8)), DMA]

    def pairs(self):
        pos = self.pos
        for k in range(4):
            for j in range(2):
                if k or j:
                    yield 2 * k + j, pos.chip(k), pos.c if j == 0 else 1 - pos.c

    def copies(self):
        pos, sems = self.pos, self.sems
        there = self.out.at[pos.p, pos.c]
        return [
            send(
                self.parts.at[chip, core],
                there,
                sems.at[0, i],
                sems.at[1, i],
                (pos.b, 2 * chip + core),
            )
            for i, chip, core in self.pairs()
        ]

    def local(self):
        pos = self.pos
        return pltpu.make_async_copy(
            self.parts.at[pos.p, pos.c], self.out.at[pos.p, pos.c], self.local_sem
        )

    def start(self):
        for copy in self.copies():
            copy.start()
        self.local().start()

    def arrive(self):
        for i, chip, core in self.pairs():
            ref = self.out.at[chip, core]
            send(ref, ref, self.sems.at[0, i], self.sems.at[1, i], self.pos.sib).wait_recv()
        self.local().wait()

    def drain(self):
        for copy in self.copies():
            copy.wait_send()


def gather_attend(
    lengths, inputs, joint, vectors, hidden_bias, output, expand, reduce, nb, heads
):
    _, count, model_width = inputs.shape
    shard = vec = model_width // (8 * nb)
    per = reduce.shape[0]
    width = heads * HEAD_DIM
    size = 8 * count
    joint_shape = (4, shard, 3 * width + 64)
    small_shape = (16, 128)

    def body(
        lengths_ref, inputs_ref, joint_weight_ref, own_vectors_ref, own_bias_ref,
        output_ref, expand_ref, reduce_ref,
        vectors_out, hidden_out, rows_any, weight_any, qkv_any, log_any,
        context_out, output_out, expand_out, reduce_out,
        rows_out, weight_out, qkv_out, log_out, stores,
        joint_all, context, small_all, bias_ref, rows_ref, joint_ref, small_ref,
        *scratch,
    ):
        pos = Place(nb)
        scratch = list(scratch)

        def take(n):
            got = scratch[:n]
            del scratch[:n]
            return got

        exchange = InputExchange(pos, rows_ref, rows_out, take(5))
        joints = JointGather(pos, joint_ref, joint_all, take(5))
        mixing = ContextExchange(pos, context, context_out, take(2))
        outputs, expands, reduces, smalls = (
            Gather(pos, part, out, halves_of(part.shape), tall, take(10))
            for part, out, tall in (
                (output_ref, output_out, True),
                (expand_ref, expand_out, True),
                (reduce_ref, reduce_out, True),
                (small_ref, small_all, True),
            )
        )
        gathers = (expands, smalls, reduces, outputs)
        units = ((expands, smalls), (reduces,), (outputs,))

        saves = [
            pltpu.make_async_copy(src, dst, stores.at[n])
            for n, (src, dst) in enumerate(
                (
                    (rows_out, rows_any),
                    (weight_out, weight_any),
                    (qkv_out, qkv_any),
                    (log_out, log_any),
                )
            )
        ]

        def project(i, _):
            at = pl.ds(pl.multiple_of(i * 2 * count, 2 * count), 2 * count)
            qkv_out[at, :] = (
                jnp.dot(
                    rows_out[i].reshape(2 * count, model_width),
                    weight_out[...],
                    preferred_element_type=F32,
                )
                + bias_ref[...]
            ).astype(BF16)
            return 0

        def prepare():
            joints.finish()
            for z in range(nb):
                weight_out[z * 8 * shard : (z + 1) * 8 * shard, :] = joint_all[
                    z, :, :, :, : 3 * width
                ].reshape(8 * shard, 3 * width)
            bias_ref[...] = jnp.zeros_like(bias_ref)
            for s in range(8):
                spot = joint_all[pos.p, s // 2, s % 2, :, 3 * width :].astype(F32)
                bias_ref[:, s * vec : (s + 1) * vec] = spot[0:1, :vec]
                bias_ref[:, 2 * width + s * vec : 2 * width + (s + 1) * vec] = spot[1:2, :vec]
            lax.fori_loop(0, 4, project, 0)
            for copy in saves[:3]:
                copy.start()

        def hop(k):
            for gather in gathers:
                gather.chain.hop(k)

        def hand_on(k, some):
            for gather in some:
                gather.complete(k)
            for gather in some:
                if k:
                    gather.forward(k)
                gather.sibling(k)

        attend = attend_block(lengths_ref[pos.c], qkv_out, log_out, context, heads, count)

        def spread(k):
            for gather in gathers:
                gather.plane(k)

        weight = joint_weight_ref[...]
        spot = jnp.pad(
            own_vectors_ref[2:4, :].astype(F32), ((0, shard - 2), (0, 64 - vec))
        ).astype(BF16)
        for chip in range(4):
            at = slice(chip * width, (chip + 1) * width)
            joint_ref[chip] = jnp.concatenate(
                [weight[:, n * model_width :][:, at] for n in range(3)] + [spot], axis=1
            )
        small_ref[...] = jnp.concatenate(
            [
                jnp.pad(own_vectors_ref[...].astype(F32), ((0, 0), (0, 128 - vec))),
                jnp.pad(own_bias_ref[...].astype(F32), ((0, 7), (0, 128 - per))),
            ]
        ).astype(BF16)
        rows_ref[...] = inputs_ref[...].astype(BF16)
        greet_near(pos)
        joints.start()
        for gather in gathers:
            gather.own()
            gather.chain.start()
            gather.plane(0, gather.shard)
        joints.own()
        for n, gather in enumerate(gathers):
            gather.local.wait()
            gather.forward(0)
            if n == 1:
                exchange.start()
        hop(1)
        joints.chain.hop(1)
        hand_on(0, gathers)
        spread(1)
        joints.chain.hop(2)
        hop(2)
        exchange.forward()
        joints.chain.hop(3)
        joints.sibling()
        hop(3)
        for gather in units[0]:
            gather.plane(2)
        exchange.finish()
        for unit in units[1:]:
            for gather in unit:
                gather.plane(2)
        spread(3)
        prepare()
        hand_on(1, gathers)
        for i in range(3):
            attend(i)
        hand_on(2, gathers)
        attend(3)
        mixing.start()
        saves[3].start()
        hand_on(nb - 1, (smalls,))

        def finish(some):
            def done(k, _):
                for gather in some:
                    gather.finish(k)
                return 0

            return done

        lax.fori_loop(0, nb, finish((smalls,)), 0)
        for owner in range(8 * nb):
            part = small_all[owner // 8, owner % 8 // 2, owner % 2].astype(F32)
            vectors_out[:, owner * vec : (owner + 1) * vec] = part[:8, :vec]
            hidden_out[:, owner * per : (owner + 1) * per] = part[8:9, :per]
        large = (expands, reduces, outputs)
        lax.fori_loop(0, nb - 1, finish(large), 0)
        smalls.drain()
        mixing.arrive()
        exchange.drain()
        joints.drain()
        mixing.drain()
        hand_on(nb - 1, large)
        for gather in large:
            gather.drain()
        finish(large)(nb - 1, 0)
        for copy in saves:
            copy.wait()

    kept = (
        ((4, 2) + inputs.shape[1:], BF16),
        ((model_width, 3 * width), BF16),
        ((size, 3 * width), BF16),
        ((size, 128), F32),
    )

    def shape(part):
        return jax.ShapeDtypeStruct((nb, 4, 2) + part.shape, part.dtype)

    return pl.pallas_call(
        body,
        out_shape=(
            jax.ShapeDtypeStruct((8, model_width), F32),
            jax.ShapeDtypeStruct((1, 8 * nb * per), F32),
            *(jax.ShapeDtypeStruct(shape, dtype) for shape, dtype in kept),
            jax.ShapeDtypeStruct((4, 2, count, width), BF16),
            shape(output),
            shape(expand),
            shape(reduce),
        ),
        in_specs=[SM] + [VM] * 7,
        out_specs=(VM,) * 2 + (ANY,) * 8,
        scratch_shapes=[pltpu.VMEM(shape, dtype) for shape, dtype in kept]
        + [DMA((4,))]
        + [
            pltpu.VMEM((nb, 4, 2) + joint_shape[1:], BF16),
            pltpu.VMEM((4, 2, count, width), BF16),
            pltpu.VMEM((nb, 4, 2) + small_shape, BF16),
            pltpu.VMEM((1, 3 * width), F32),
            pltpu.VMEM(inputs.shape, BF16),
            pltpu.VMEM(joint_shape, BF16),
            pltpu.VMEM(small_shape, BF16),
        ]
        + InputExchange.scratch()
        + JointGather.scratch(nb)
        + ContextExchange.scratch()
        + Gather.scratch(nb) * 4,
        name="gather_attend",
        compiler_params=pltpu.CompilerParams(
            collective_id=1, has_side_effects=True, vmem_limit_bytes=VMEM_LIMIT
        ),
    )(lengths, inputs, joint, vectors, hidden_bias, output, expand, reduce)


def halves_of(shape):
    rows, columns = shape
    if columns % 256 == 0 and columns >= 1024:
        return (
            (slice(None), pl.ds(0, columns // 2)),
            (slice(None), pl.ds(columns // 2, columns // 2)),
        )
    if rows % 32 == 0:
        return (
            (pl.ds(0, rows // 2), slice(None)),
            (pl.ds(rows // 2, rows // 2), slice(None)),
        )
    if columns % 256 == 0:
        return (
            (slice(None), pl.ds(0, columns // 2)),
            (slice(None), pl.ds(columns // 2, columns // 2)),
        )
    return ((slice(None), slice(None)), None)


def attend_block(limit, qkv_ref, log_ref, context_ref, heads, count):
    width = heads * HEAD_DIM
    size = 8 * count

    def part(n, _):
        at = pl.ds(pl.multiple_of(n * count, count), count)
        allowed = lax.broadcasted_iota(jnp.int32, (1, size), 1) < limit
        lanes = lax.broadcasted_iota(jnp.int32, (count, 128), 1)
        parts, logs = [], jnp.zeros((count, 128), F32)
        for h in range(heads):
            query = qkv_ref[at, h * HEAD_DIM : (h + 1) * HEAD_DIM]
            key = qkv_ref[:, width + h * HEAD_DIM : width + (h + 1) * HEAD_DIM]
            value = qkv_ref[:, 2 * width + h * HEAD_DIM : 2 * width + (h + 1) * HEAD_DIM]
            scores = (
                lax.dot_general(
                    query, key, (((1,), (1,)), ((), ())), preferred_element_type=F32
                )
                * SCORE_SCALE
            )
            scores = jnp.where(allowed, scores, NEG_FILL)
            top = jnp.max(scores, axis=-1, keepdims=True)
            exps = jnp.exp(scores - top)
            total = jnp.sum(exps, axis=-1, keepdims=True)
            mixed = jnp.dot(exps.astype(BF16), value, preferred_element_type=F32)
            parts.append(mixed / total)
            logs = jnp.where(lanes == h, top + jnp.log(total), logs)
        context_ref[n // 2, n % 2] = jnp.concatenate(parts, axis=1).astype(BF16)
        log_ref[at, :] = logs
        return 0

    def block(i):
        lax.fori_loop(2 * i, 2 * i + 2, part, 0)

    return block


def attend_back_block(limit, qkv_ref, log_ref, grad_ref, grad_qkv, grad_key, grad_value, heads, count):
    width = heads * HEAD_DIM
    size = 8 * count
    along_keys = (((1,), (1,)), ((), ()))
    along_rows = (((0,), (0,)), ((), ()))

    def part(n, _):
        at = pl.ds(pl.multiple_of(n * count, count), count)
        allowed = lax.broadcasted_iota(jnp.int32, (1, size), 1) < limit
        grads = grad_ref[n // 2, n % 2]
        parts = []
        for h in range(heads):
            query = qkv_ref[at, h * HEAD_DIM : (h + 1) * HEAD_DIM]
            key = qkv_ref[:, width + h * HEAD_DIM : width + (h + 1) * HEAD_DIM]
            value = qkv_ref[:, 2 * width + h * HEAD_DIM : 2 * width + (h + 1) * HEAD_DIM]
            grad_out = grads[:, h * HEAD_DIM : (h + 1) * HEAD_DIM]
            scores = (
                lax.dot_general(query, key, along_keys, preferred_element_type=F32)
                * SCORE_SCALE
            )
            probs = jnp.where(allowed, jnp.exp(scores - log_ref[at, h : h + 1]), 0.0)
            grad_probs = lax.dot_general(
                grad_out, value, along_keys, preferred_element_type=F32
            )
            delta = jnp.sum(probs * grad_probs, axis=-1, keepdims=True)
            grad_scores = (probs * (grad_probs - delta)).astype(BF16)
            parts.append(
                jnp.dot(grad_scores, key, preferred_element_type=F32) * SCORE_SCALE
            )
            key_part = lax.dot_general(
                grad_scores, query, along_rows, preferred_element_type=F32
            )
            value_part = lax.dot_general(
                probs.astype(BF16), grad_out, along_rows, preferred_element_type=F32
            )
            own = slice(h * HEAD_DIM, (h + 1) * HEAD_DIM)
            grad_key[:, own] += key_part
            grad_value[:, own] += value_part
        grad_qkv[at, :width] = jnp.concatenate(parts, axis=1).astype(BF16)
        return 0

    def block(i):
        lax.fori_loop(2 * i, 2 * i + 2, part, 0)

    return block


class Scatter:
    def __init__(self, pos, halves, bufs, sems):
        self.pos, self.halves = pos, halves
        (self.partial, self.theirs, self.a0, self.a1, self.bx, self.by, self.z) = bufs
        (self.sb, self.s0, self.s1, self.dx, self.dy, self.cx, self.cy, self.zs) = sems

    @staticmethod
    def scratch(nb, shape, dtype, halves):
        first, second = half_shapes(shape, halves)
        return [
            pltpu.VMEM((nb, 4, 2) + shape, dtype),
            pltpu.VMEM((nb, 4) + shape, dtype),
            pltpu.VMEM((nb,) + first, dtype),
            pltpu.VMEM((nb,) + second, dtype),
            pltpu.VMEM((nb,) + shape, dtype),
            pltpu.VMEM((nb,) + shape, dtype),
            pltpu.VMEM((nb,) + shape, dtype),
        ]

    @staticmethod
    def sem_scratch(nb):
        return [DMA((2, nb)) for _ in range(8)]

    def mine(self, k, chip):
        return self.partial.at[self.pos.up(k), chip, self.pos.c]

    def sibling_copy(self, k):
        pos = self.pos
        z = pos.up(k)
        return send(
            self.partial.at[z, :, 1 - pos.c],
            self.theirs.at[z],
            self.sb.at[0, k],
            self.sb.at[1, k],
            pos.sib,
        )

    def begin(self, k):
        self.sibling_copy(k).start()

    def copy(self, k, src, dst, sems, there):
        return send(src, dst, sems.at[0, k], sems.at[1, k], there)

    def first_copies(self, k):
        pos = self.pos
        h0, h1 = self.halves
        copies = [
            self.copy(k, self.mine(k, pos.pd).at[h0], self.a0.at[k], self.s0, pos.xn),
            self.copy(k, self.mine(k, pos.px).at[h0], self.bx.at[k].at[h0], self.dx, pos.xn),
        ]
        if h1 is not None:
            copies += [
                self.copy(k, self.mine(k, pos.pd).at[h1], self.a1.at[k], self.s1, pos.yn),
                self.copy(k, self.mine(k, pos.py).at[h1], self.by.at[k].at[h1], self.dy, pos.yn),
            ]
        return copies

    def second_copies(self, k):
        pos = self.pos
        h0, h1 = self.halves
        copies = [
            self.copy(k, self.mine(k, pos.py).at[h0], self.by.at[k].at[h0], self.cy, pos.yn)
        ]
        if h1 is not None:
            copies.append(
                self.copy(k, self.mine(k, pos.px).at[h1], self.bx.at[k].at[h1], self.cx, pos.xn)
            )
        return copies

    def first(self, k):
        pos = self.pos
        z = pos.up(k)
        self.sibling_copy(k).wait_recv()
        for j in range(4):
            chip = pos.chip(3 - j)
            self.partial[z, chip, pos.c] = (
                self.partial[z, chip, pos.c].astype(F32) + self.theirs[z, chip].astype(F32)
            ).astype(self.partial.dtype)
        for copy in self.first_copies(k):
            copy.start()

    def landed(self, ref, sems, k):
        send(ref, ref, sems.at[0, k], sems.at[1, k], self.pos.xn).wait_recv()

    def second(self, k):
        pos = self.pos
        h0, h1 = self.halves
        copies = self.second_copies(k)
        self.landed(self.a0.at[k], self.s0, k)
        ref = self.mine(k, pos.py)
        ref[h0] = (ref[h0].astype(F32) + self.a0[k].astype(F32)).astype(ref.dtype)
        copies[0].start()
        if h1 is not None:
            self.landed(self.a1.at[k], self.s1, k)
            ref = self.mine(k, pos.px)
            ref[h1] = (ref[h1].astype(F32) + self.a1[k].astype(F32)).astype(ref.dtype)
            copies[1].start()

    def z_copy(self, k):
        pos = self.pos
        return send(
            self.bx.at[k], self.z.at[k], self.zs.at[0, k], self.zs.at[1, k], (pos.up(k), pos.s)
        )

    def third(self, k, total):
        pos = self.pos
        h0, h1 = self.halves
        self.landed(self.bx.at[k].at[h0], self.dx, k)
        self.landed(self.by.at[k].at[h0], self.cy, k)
        if h1 is not None:
            self.landed(self.by.at[k].at[h1], self.dy, k)
            self.landed(self.bx.at[k].at[h1], self.cx, k)
        total[...] = (
            self.mine(k, pos.p)[...].astype(F32)
            + self.bx[k].astype(F32)
            + self.by[k].astype(F32)
        )

        def on():
            self.bx[k] = total[...].astype(self.bx.dtype)
            self.z_copy(k).start()

        guarded(k != 0, on)

    def last(self, total):
        value = total[...]
        for k in range(1, self.pos.nb):
            self.landed(self.z.at[k], self.zs, k)
            value = value + self.z[k].astype(F32)
        total[...] = value

    def drain(self):
        def done(k, _):
            self.sibling_copy(k).wait_send()
            for copy in self.first_copies(k) + self.second_copies(k):
                copy.wait_send()
            guarded(k != 0, lambda: self.z_copy(k).wait_send())
            return 0

        lax.fori_loop(0, self.pos.nb, done, 0)


def half_shapes(shape, halves):
    def cut(half):
        return tuple(n if h == slice(None) else h.size for n, h in zip(shape, half))

    first = cut(halves[0])
    return first, (first if halves[1] is None else cut(halves[1]))


class RowScatter:
    def __init__(self, pos, out, bufs, sems):
        self.pos, self.out = pos, out
        self.mine, self.a0, self.a1, self.bx, self.by, self.far, self.near = bufs
        (self.sm,) = sems

    @staticmethod
    def scratch(rows, columns):
        return [
            pltpu.VMEM((rows, columns), BF16),
            pltpu.VMEM((rows, columns), BF16),
            pltpu.VMEM((2, rows, columns), BF16),
            pltpu.VMEM((2, rows, columns), BF16),
            pltpu.VMEM((rows, columns), F32),
            pltpu.VMEM((rows, columns), F32),
            DMA((2, 7)),
        ]

    def copy(self, i):
        pos, mine = self.pos, self.mine
        src, dst, there = (
            (mine.at[pos.pd, 0], self.a0, pos.xn),
            (mine.at[pos.pd, 1], self.a1, pos.yn),
            (mine.at[pos.px, 0], self.bx.at[0], pos.xn),
            (mine.at[pos.py, 1], self.by.at[1], pos.yn),
            (mine.at[pos.py, 0], self.by.at[0], pos.yn),
            (mine.at[pos.px, 1], self.bx.at[1], pos.xn),
            (self.far, self.near, pos.sib),
        )[i]
        return send(src, dst, self.sm.at[0, i], self.sm.at[1, i], there)

    def landed(self, i, ref):
        send(ref, ref, self.sm.at[0, i], self.sm.at[1, i], self.pos.xn).wait_recv()

    def first(self):
        for i in range(4):
            self.copy(i).start()

    def second(self):
        pos, mine = self.pos, self.mine
        self.landed(0, self.a0)
        mine[pos.py, 0] = (mine[pos.py, 0].astype(F32) + self.a0[...].astype(F32)).astype(BF16)
        self.copy(4).start()
        self.landed(1, self.a1)
        mine[pos.px, 1] = (mine[pos.px, 1].astype(F32) + self.a1[...].astype(F32)).astype(BF16)
        self.copy(5).start()

    def third(self):
        pos = self.pos
        self.landed(2, self.bx.at[0])
        self.landed(3, self.by.at[1])
        self.landed(4, self.by.at[0])
        self.landed(5, self.bx.at[1])

        def total(core):
            return (
                self.mine[pos.p, core].astype(F32)
                + self.bx[core].astype(F32)
                + self.by[core].astype(F32)
            )

        self.far[...] = total(1 - pos.c)
        self.copy(6).start()
        self.out[pos.c] += total(pos.c)

    def last(self):
        pos = self.pos
        self.landed(6, self.near)
        self.out[1 - pos.c] += self.near[...]
        for i in range(7):
            self.copy(i).wait_send()


class JointScatter:
    def __init__(self, pos, bufs, sems):
        self.pos = pos
        self.partial, self.theirs, self.zbuf, self.sums, self.got = bufs
        self.sb, self.zs, self.ps = sems

    @staticmethod
    def scratch(nb, shape):
        return [
            pltpu.VMEM((nb, 4, 2) + shape, BF16),
            pltpu.VMEM((nb, 4) + shape, BF16),
            pltpu.VMEM((nb, 4) + shape, BF16),
            pltpu.VMEM((4,) + shape, BF16),
            pltpu.VMEM((4,) + shape, BF16),
        ]

    @staticmethod
    def sem_scratch(nb):
        return [DMA((2,)), DMA((2, nb)), DMA((2, 4))]

    def sibling_copy(self):
        pos = self.pos
        return send(
            self.partial.at[:, :, 1 - pos.c], self.theirs, self.sb.at[0], self.sb.at[1], pos.sib
        )

    def z_copy(self, d):
        pos = self.pos
        return send(
            self.partial.at[pos.up(d), :, pos.c],
            self.zbuf.at[d],
            self.zs.at[0, d],
            self.zs.at[1, d],
            (pos.up(d), pos.s),
        )

    def plane_copy(self, k):
        pos = self.pos
        chip = pos.chip(k)
        return send(
            self.sums.at[chip],
            self.got.at[pos.p],
            self.ps.at[0, k],
            self.ps.at[1, k],
            (pos.b, 2 * chip + pos.c),
        )

    def begin(self):
        self.sibling_copy().start()

    def first(self):
        pos = self.pos
        self.sibling_copy().wait_recv()
        for d in (*range(1, pos.nb), 0):
            z = pos.up(d)
            self.partial[z, :, pos.c] = (
                self.partial[z, :, pos.c].astype(F32) + self.theirs[z].astype(F32)
            ).astype(BF16)
            if d:
                self.z_copy(d).start()

    def second(self):
        pos = self.pos
        value = self.partial[pos.b, :, pos.c].astype(F32)
        for d in range(1, pos.nb):
            self.z_copy(d).wait_recv()
            value = value + self.zbuf[d].astype(F32)
        self.sums[...] = value.astype(BF16)
        for k in range(1, 4):
            self.plane_copy(k).start()

    def last(self, out, vec):
        pos = self.pos
        width = out.shape[1] // 12
        self.got[pos.p] = self.sums[pos.p]
        for k in range(1, 4):
            ref = self.got.at[pos.chip(k)]
            send(ref, ref, self.ps.at[0, k], self.ps.at[1, k], pos.sib).wait_recv()
        extra = 0.0
        for chip in range(4):
            value = self.got[chip].astype(F32)
            for n in range(3):
                out[:, (4 * n + chip) * width : (4 * n + chip + 1) * width] = value[
                    :, n * width : (n + 1) * width
                ]
            extra = extra + value[:8, 3 * width : 3 * width + vec]
        self.sibling_copy().wait_send()
        for d in range(1, pos.nb):
            self.z_copy(d).wait_send()
        for k in range(1, 4):
            self.plane_copy(k).wait_send()
        return extra


def normed_rows(residual):
    centered = residual - jnp.mean(residual, axis=-1, keepdims=True)
    inverse = lax.rsqrt(jnp.mean(centered * centered, axis=-1, keepdims=True) + EPSILON)
    return centered * inverse, inverse


def transposed_dot(left, right):
    return lax.dot_general(left, right, (((0,), (0,)), ((), ())), preferred_element_type=F32)


def dot_transposed(left, right):
    return lax.dot_general(left, right, (((1,), (1,)), ((), ())), preferred_element_type=F32)


def feed_and_back(
    lengths, inputs, cotangent, mixed, vectors, hidden_bias,
    output_weight, expand_weight, reduce_weight, rows, weight, qkv, logs, nb, heads,
):
    _, count, model_width = inputs.shape
    hidden = hidden_bias.shape[1]
    block = hidden // nb
    width = heads * HEAD_DIM
    size, tokens = 8 * count, 2 * count
    owners = 8 * nb
    shard = vec = model_width // owners
    per = hidden // owners
    joint_shape = (shard, 3 * width + 64)
    shapes = [(16, 128), (shard, model_width), (shard, hidden), (per, model_width)]
    dtypes = [F32, BF16, BF16, BF16]

    def body(
        lengths_ref, inputs_ref, cotangent_ref, mixed_ref, vectors_ref, bias_ref,
        output_ref, expand_ref, reduce_ref, rows_any, weight_any, qkv_any, log_any,
        result_out, rows_out, joint_out, vectors_out, hidden_out,
        output_out, expand_out, reduce_out,
        output_w, expand_w, reduce_w, rows_ref, weight_ref, qkv_ref, log_ref, loads,
        context, first_normed, first_low, hidden_low, slope, feed, grad_low,
        grad_vectors, grad_bias, parts, small_total,
        grad_context, grad_qkv, grad_key, grad_value,
        *scratch,
    ):
        pos = Place(nb)
        scratch = list(scratch)

        def take(n):
            got = scratch[:n]
            del scratch[:n]
            return got

        mixing = ContextExchange(pos, parts, grad_context, take(2))
        row_sums = RowScatter(pos, rows_out, [hidden_low] + take(6), take(1))
        joints = JointScatter(pos, take(5), take(3))
        smalls, outputs, expands, reduces = (
            Scatter(pos, halves_of(shape), take(7), take(8)) for shape in shapes
        )

        def turn(i):
            return jnp.where(i < 2, 2 - i, 3 * (3 - i))

        def expand_load(z):
            at = pl.ds(z * block if isinstance(z, int) else pl.multiple_of(z * block, block), block)
            return pltpu.make_async_copy(expand_ref.at[:, at], expand_w.at[z], loads.at[z])

        def reduce_load(z):
            at = pl.ds(z * block if isinstance(z, int) else pl.multiple_of(z * block, block), block)
            return pltpu.make_async_copy(reduce_ref.at[at, :], reduce_w.at[z], loads.at[nb + z])

        output_load = pltpu.make_async_copy(output_ref, output_w, loads.at[2 * nb])
        later = [
            pltpu.make_async_copy(src, dst, loads.at[2 * nb + 1 + n])
            for n, (src, dst) in enumerate(
                ((rows_any, rows_ref), (weight_any, weight_ref), (qkv_any, qkv_ref), (log_any, log_ref))
            )
        ]
        output_load.start()
        for z in range(nb):
            expand_load(z).start()
            reduce_load(z).start()
        for copy in later:
            copy.start()
        barrier = pltpu.get_barrier_semaphore()
        partners = [(pos.up(d), pos.s) for d in range(1, nb)] + plane_others(pos)
        for device in partners:
            pl.semaphore_signal(barrier, inc=1, device_id=device, device_id_type=MESH)

        def vector(n):
            return vectors_ref[n : n + 1, :]

        for chip in range(4):
            context[:, chip * width : (chip + 1) * width] = mixed_ref[chip].reshape(tokens, width)
        output_load.wait()
        branch = jnp.dot(context[...], output_w[...], preferred_element_type=F32) + vector(4)
        normed, first_inverse = normed_rows(
            inputs_ref[...].reshape(tokens, model_width) + branch
        )
        first_normed[...] = normed
        first = normed * vector(0) + vector(1)
        rows_out[...] = first.reshape(2, count, model_width)
        first_low[...] = first.astype(BF16)
        feed[...] = jnp.broadcast_to(vector(7), feed.shape)

        def forward(z, _):
            at = pl.ds(pl.multiple_of(z * block, block), block)
            expand_load(z).wait()
            before = (
                jnp.dot(first_low[...], expand_w[z], preferred_element_type=F32)
                + bias_ref[:, at]
            )
            half = 0.5 * (1.0 + lax.erf(before * HALF_ROOT))
            low = (before * half).astype(BF16)
            hidden_low[z] = low.reshape(2, count, block)
            slope[z] = half + before * jnp.exp(-0.5 * before * before) * INV_ROOT_TAU
            reduce_load(z).wait()
            feed[...] += jnp.dot(low, reduce_w[z], preferred_element_type=F32)
            return 0

        lax.fori_loop(0, nb, forward, 0)
        normed, inverse = normed_rows(
            rows_out[...].reshape(tokens, model_width) + feed[...]
        )
        result_out[...] = (normed * vector(5) + vector(6)).reshape(2, count, model_width)

        places = pos.s * count + lax.broadcasted_iota(jnp.int32, (count, 1), 0)
        grad_res = jnp.concatenate(
            [jnp.where(places < lengths_ref[j], cotangent_ref[j], 0.0) for j in range(2)]
        )
        grad_second, gain, shift = norm_back(grad_res, normed, inverse, vector(5))
        grad_low[...] = grad_second.astype(BF16)
        grad_vectors[...] = jnp.zeros_like(grad_vectors)
        grad_vectors[5:6, :] = gain[None]
        grad_vectors[6:7, :] = shift[None]
        grad_vectors[7:8, :] = jnp.sum(grad_low[...].astype(F32), axis=0, keepdims=True)
        feed[...] = grad_second

        def backward(i, _):
            z = pos.up(turn(i))
            at = pl.ds(pl.multiple_of(z * block, block), block)
            for n in range(2):
                cut = slice(n * (block // 2), (n + 1) * (block // 2))
                reduces.partial[z, 2 * n : 2 * n + 2] = (
                    transposed_dot(
                        hidden_low[z, :, :, cut].reshape(tokens, block // 2), grad_low[...]
                    )
                    .reshape(2, 2, per, model_width)
                    .astype(BF16)
                )
            reduces.begin(turn(i))
            low = (dot_transposed(grad_low[...], reduce_w[z]) * slope[z]).astype(BF16)
            grad_bias[:, at] = jnp.sum(low.astype(F32), axis=0, keepdims=True)
            for n in range(2):
                cut = slice(n * (model_width // 2), (n + 1) * (model_width // 2))
                expands.partial[n * nb // 2 : (n + 1) * nb // 2, :, :, :, at] = (
                    transposed_dot(first_low[:, cut], low)
                    .reshape(nb // 2, 4, 2, shard, block)
                    .astype(BF16)
                )
            feed[...] += dot_transposed(low, expand_w[z])
            reduces.first(turn(i))
            return 0

        pl.semaphore_wait(barrier, len(partners))
        lax.fori_loop(0, nb, backward, 0)
        for k in range(nb):
            expands.begin(turn(k))
        grads, gain, shift = norm_back(feed[...], first_normed[...], first_inverse, vector(0))
        rows_out[...] = grads.reshape(2, count, model_width)
        low = grads.astype(BF16)
        grad_low[...] = low
        grad_vectors[0:1, :] = gain[None]
        grad_vectors[1:2, :] = shift[None]
        grad_vectors[4:5, :] = jnp.sum(low.astype(F32), axis=0, keepdims=True)
        low = dot_transposed(low, output_w[...]).astype(BF16)
        for chip in range(4):
            parts[chip] = low[:, chip * width : (chip + 1) * width].reshape(2, count, width)
        mixing.start()
        for n in range(2):
            cut = slice(n * (model_width // 2), (n + 1) * (model_width // 2))
            outputs.partial[n * nb // 2 : (n + 1) * nb // 2] = (
                transposed_dot(context[:, cut], grad_low[...])
                .reshape(nb // 2, 4, 2, shard, model_width)
                .astype(BF16)
            )
        for owner in range(owners):
            here = (owner // 8, owner % 8 // 2, owner % 2)
            smalls.partial[here] = jnp.concatenate(
                [
                    jnp.pad(
                        grad_vectors[:, owner * vec : (owner + 1) * vec], ((0, 0), (0, 128 - vec))
                    ),
                    jnp.broadcast_to(
                        jnp.pad(
                            grad_bias[:, owner * per : (owner + 1) * per], ((0, 0), (0, 128 - per))
                        ),
                        (8, 128),
                    ),
                ]
            )
        for k in range(nb):
            outputs.begin(turn(k))
            smalls.begin(turn(k))

        grad_key[...] = jnp.zeros_like(grad_key)
        grad_value[...] = jnp.zeros_like(grad_value)
        for copy in later:
            copy.wait()
        back = attend_back_block(
            lengths_ref[pos.c], qkv_ref, log_ref, grad_context, grad_qkv, grad_key, grad_value,
            heads, count,
        )

        def middle(i, _):
            k = turn(i)
            reduces.second(k)
            expands.first(k)
            guarded(i > 0, lambda: reduces.third(turn(i - 1), reduce_out))
            guarded(i == 0, mixing.arrive)
            back(i)
            return 0

        lax.fori_loop(0, nb, middle, 0)

        def late(i, _):
            k = turn(i)
            expands.second(k)
            outputs.first(k)
            smalls.first(k)
            return 0

        lax.fori_loop(0, 2, late, 0)
        grad_qkv[:, width : 2 * width] = (grad_key[...] * SCORE_SCALE).astype(BF16)
        grad_qkv[:, 2 * width :] = grad_value[...].astype(BF16)

        def spread(i, _):
            at = pl.ds(pl.multiple_of(i * tokens, tokens), tokens)
            row_sums.mine[i] = (
                dot_transposed(grad_qkv[at, :], weight_ref[...])
                .astype(BF16)
                .reshape(2, count, model_width)
            )
            return 0

        lax.fori_loop(0, 4, spread, 0)
        row_sums.first()
        for z in range(nb):
            grad_joint = transposed_dot(
                rows_ref[:, :, :, z * 8 * shard : (z + 1) * 8 * shard].reshape(size, 8 * shard),
                grad_qkv[...],
            )
            joints.partial[z, :, :, :, : 3 * width] = grad_joint.reshape(
                4, 2, shard, 3 * width
            ).astype(BF16)
        sums = jnp.sum(grad_qkv[...].astype(F32), axis=0, keepdims=True)
        joints.partial[:, :, :, :, 3 * width :] = jnp.zeros((nb, 4, 2, shard, 64), BF16)
        for s in range(8):
            at = slice(s * vec, (s + 1) * vec)
            value = jnp.concatenate([sums[:, :width][:, at], sums[:, 2 * width :][:, at]])
            joints.partial[pos.p, s // 2, s % 2, :, 3 * width :] = jnp.pad(
                value, ((0, shard - 2), (0, 64 - vec))
            ).astype(BF16)
        joints.begin()
        lax.fori_loop(2, nb, late, 0)
        joints.first()

        def summed(i, _):
            expands.third(turn(i), expand_out)
            return 0

        lax.fori_loop(0, nb - 1, summed, 0)
        reduces.third(turn(nb - 1), reduce_out)
        reduces.last(reduce_out)
        reduces.drain()
        row_sums.second()

        def final(i, _):
            k = turn(i)
            outputs.second(k)
            smalls.second(k)
            return 0

        lax.fori_loop(0, nb, final, 0)
        expands.third(turn(nb - 1), expand_out)
        joints.second()
        row_sums.third()
        expands.last(expand_out)
        expands.drain()
        mixing.drain()

        def end(i, _):
            k = turn(i)
            outputs.third(k, output_out)
            smalls.third(k, small_total)
            return 0

        lax.fori_loop(0, nb, end, 0)
        extra = joints.last(joint_out, vec)
        row_sums.last()
        for scatter, out in ((outputs, output_out), (smalls, small_total)):
            scatter.last(out)
            scatter.drain()
        lines = lax.broadcasted_iota(jnp.int32, (8, vec), 0)
        value = jnp.where(lines == 2, extra[0:1], small_total[:8, :vec])
        vectors_out[...] = jnp.where(lines == 3, extra[1:2], value)
        hidden_out[...] = small_total[8:9, :per]

    def vmem(shape, dtype):
        return pltpu.VMEM(shape, dtype)

    scratch = [
        vmem((model_width, model_width), BF16),
        vmem((nb, model_width, block), BF16),
        vmem((nb, block, model_width), BF16),
        vmem(rows.shape, BF16),
        vmem(weight.shape, BF16),
        vmem(qkv.shape, BF16),
        vmem(logs.shape, F32),
        DMA((2 * nb + 5,)),
        vmem((tokens, model_width), BF16),
        vmem((tokens, model_width), F32),
        vmem((tokens, model_width), BF16),
        vmem((nb, 2, count, block), BF16),
        vmem((nb, tokens, block), F32),
        vmem((tokens, model_width), F32),
        vmem((tokens, model_width), BF16),
        vmem((8, model_width), F32),
        vmem((1, hidden), F32),
        vmem((4, 2, count, width), BF16),
        vmem((16, 128), F32),
        vmem((4, 2, count, width), BF16),
        vmem((size, 3 * width), BF16),
        vmem((size, width), F32),
        vmem((size, width), F32),
    ]
    scratch += ContextExchange.scratch() + RowScatter.scratch(count, model_width)
    scratch += JointScatter.scratch(nb, joint_shape) + JointScatter.sem_scratch(nb)
    for shape, dtype in zip(shapes, dtypes):
        scratch += Scatter.scratch(nb, shape, dtype, halves_of(shape)) + Scatter.sem_scratch(nb)
    return pl.pallas_call(
        body,
        out_shape=tuple(
            jax.ShapeDtypeStruct(shape, F32)
            for shape in (
                inputs.shape,
                inputs.shape,
                (shard, 3 * model_width),
                (8, vec),
                (1, per),
                shapes[1],
                shapes[2],
                shapes[3],
            )
        ),
        in_specs=[SM] + [VM] * 5 + [ANY] * 7,
        out_specs=(VM,) * 8,
        scratch_shapes=scratch,
        name="feed_and_back",
        compiler_params=pltpu.CompilerParams(
            collective_id=4, has_side_effects=True, vmem_limit_bytes=VMEM_LIMIT
        ),
    )(
        lengths, inputs, cotangent, mixed, vectors, hidden_bias,
        output_weight, expand_weight, reduce_weight, rows, weight, qkv, logs,
    )


def hand_over(*arrays):
    count = len(arrays)

    def body(*refs):
        came, out, held = refs[:count], refs[count : 2 * count], refs[2 * count : 3 * count]
        sems = refs[3 * count]
        loads = [pltpu.make_async_copy(came[n], held[n], sems.at[0, n]) for n in range(count)]
        stores = [pltpu.make_async_copy(held[n], out[n], sems.at[1, n]) for n in range(count)]
        for copy in loads:
            copy.start()
        for load, store in zip(loads, stores):
            load.wait()
            store.start()
        for copy in stores:
            copy.wait()

    return pl.pallas_call(
        body,
        out_shape=tuple(jax.ShapeDtypeStruct(a.shape, a.dtype) for a in arrays),
        in_specs=[ANY] * count,
        out_specs=(ANY,) * count,
        scratch_shapes=[pltpu.VMEM(a.shape, a.dtype) for a in arrays] + [DMA((2, count))],
        name="hand_over",
        compiler_params=pltpu.CompilerParams(vmem_limit_bytes=VMEM_LIMIT),
    )(*arrays)


def plane_on_device(
    inputs,
    cotangent,
    lengths,
    joint_weight,
    output_weight,
    vectors,
    expand_weight,
    expand_bias,
    reduce_weight,
):
    nb = lax.axis_size("batch")
    _, _, model_width = inputs.shape
    hidden_width = expand_weight.shape[1]
    heads = model_width // (4 * HEAD_DIM)
    per = expand_bias.shape[0]
    (
        vector_rows, full_bias, rows_all, joint_all, qkv, logs,
        mixed, output_all, expand_all, reduce_all,
    ) = gather_attend(
        lengths,
        inputs,
        joint_weight,
        vectors,
        expand_bias.reshape(1, per),
        output_weight,
        expand_weight,
        reduce_weight,
        nb,
        heads,
    )
    full_output = output_all.reshape(model_width, model_width)
    full_expand = expand_all.reshape(model_width, hidden_width)
    full_reduce = reduce_all.reshape(hidden_width, model_width)

    result, grad_inputs, joint_sum, vectors_sum, bias_sum, output_sum, expand_sum, reduce_sum = (
        feed_and_back(
            lengths,
            inputs,
            cotangent,
            mixed,
            vector_rows,
            full_bias,
            full_output,
            full_expand,
            full_reduce,
            rows_all,
            joint_all,
            qkv,
            logs,
            nb,
            heads,
        )
    )
    (
        result, grad_inputs, joint_sum, output_sum, vectors_sum, expand_sum, bias_sum, reduce_sum,
    ) = hand_over(
        result, grad_inputs, joint_sum, output_sum, vectors_sum, expand_sum, bias_sum, reduce_sum
    )
    return (
        result,
        grad_inputs,
        joint_sum,
        output_sum,
        vectors_sum,
        expand_sum,
        bias_sum.reshape(per),
        reduce_sum,
    )


def plane_fits(mesh, inputs, expand_bias, expand_weight):
    return (
        mesh.shape["seq"] == 8
        and mesh.shape["batch"] == 4
        and inputs[0] == 2 * mesh.shape["batch"]
        and HEADS % 4 == 0
        and inputs[2] == HEADS * HEAD_DIM
        and inputs[1] % (8 * 16) == 0
        and inputs[2] % 256 == 0
        and expand_weight[0] % (8 * 32) == 0
        and expand_weight[1] % (16 * 32) == 0
        and expand_bias[0] <= 128 * 32
        and expand_weight[1] == 4 * inputs[2]
    )


def solution(mesh):
    def program(*args):
        fits = plane_fits(mesh, args[0].shape, args[7].shape, args[6].shape)
        return jax.shard_map(
            plane_on_device if fits else general_on_device,
            mesh=mesh,
            in_specs=(
                P("batch", "seq", None),
                P("batch", "seq", None),
                P("batch"),
                P(("batch", "seq"), None),
                P(("batch", "seq"), None),
                P(None, ("batch", "seq")),
                P(("batch", "seq"), None),
                P(("batch", "seq")),
                P(("batch", "seq"), None),
            ),
            out_specs=(
                P("batch", "seq", None),
                P("batch", "seq", None),
                P(("batch", "seq"), None),
                P(("batch", "seq"), None),
                P(None, ("batch", "seq")),
                P(("batch", "seq"), None),
                P(("batch", "seq")),
                P(("batch", "seq"), None),
            ),
            check_vma=False,
        )(*args)

    return program
```

```python
import functools
import math

import jax
import jax.numpy as jnp
from jax import lax
from jax.experimental import pallas as pl
from jax.experimental.pallas import tpu as pltpu
from jax.sharding import PartitionSpec as P

HEADS = 12
HEAD_DIM = 64


EPSILON = 1e-12
SCORE_SCALE = 0.125
NEG_FILL = -1e30
HALF_ROOT = 0.7071067811865476
INV_ROOT_TAU = 0.3989422804014327
block_limit = 256


def layer_norm(residual, norm_gain, norm_shift):
    centered = residual - jnp.mean(residual, axis=-1, keepdims=True)
    inverse = lax.rsqrt(jnp.mean(centered * centered, axis=-1, keepdims=True) + EPSILON)
    normed = centered * inverse
    return (normed * norm_gain + norm_shift, normed, inverse)


def norm_back(grad_out, normed, inverse, norm_gain):
    grad_normed = grad_out * norm_gain
    mean_grad = jnp.mean(grad_normed, axis=-1, keepdims=True)
    mean_proj = jnp.mean(grad_normed * normed, axis=-1, keepdims=True)
    grad_in = inverse * (grad_normed - mean_grad - normed * mean_proj)
    return (grad_in, jnp.sum(grad_out * normed, axis=0), jnp.sum(grad_out, axis=0))


def gelu_value(before_gelu):
    return 0.5 * before_gelu * (1.0 + lax.erf(before_gelu * HALF_ROOT))


def gelu_slope(before_gelu):
    return (
        0.5 * (1.0 + lax.erf(before_gelu * HALF_ROOT))
        + before_gelu * jnp.exp(-0.5 * before_gelu * before_gelu) * INV_ROOT_TAU
    )


def over_blocks(piece_rows, block_fn, carried):
    block_size = math.gcd(piece_rows, block_limit)

    def run_block(block_index, current):
        return block_fn(current, block_index * block_size, block_size)

    return lax.fori_loop(0, piece_rows // block_size, run_block, carried)


def head_scores(left_heads, right_heads, right_places, lengths):
    scores = (
        jnp.einsum("sqhd,skhd->shqk", left_heads, right_heads, preferred_element_type=jnp.float32)
        * SCORE_SCALE
    )
    allowed = right_places[None, :] < lengths[:, None]
    return jnp.where(allowed[:, None, None, :], scores, NEG_FILL)


def cut_heads(gathered_piece, offset, block_size, head_count):
    sliced = lax.dynamic_slice_in_dim(gathered_piece, offset, block_size, 1)
    return sliced.reshape(sliced.shape[0], block_size, head_count, -1)


def gather_attention(joint_weight, output_weight, vectors):
    return (
        lax.all_gather(joint_weight, ("batch", "seq"), axis=0, tiled=True),
        lax.all_gather(output_weight, ("batch", "seq"), axis=0, tiled=True),
        lax.all_gather(vectors, ("batch", "seq"), axis=1, tiled=True),
    )


def gather_feed(expand_weight, reduce_weight, expand_bias):
    return (
        lax.all_gather(expand_weight, ("batch", "seq"), axis=0, tiled=True),
        lax.all_gather(reduce_weight, ("batch", "seq"), axis=0, tiled=True),
        lax.all_gather(expand_bias, ("batch", "seq"), axis=0, tiled=True),
    )


def general_on_device(
    inputs,
    cotangent,
    lengths,
    joint_weight,
    output_weight,
    vectors,
    expand_weight,
    expand_bias,
    reduce_weight,
):
    seq_count, row_count, model_width = inputs.shape
    head_count = HEADS
    head_size = HEAD_DIM
    tokens = seq_count * row_count
    head_shape = (seq_count, row_count, head_count, head_size)
    own_places = lax.axis_index("seq") * row_count + jnp.arange(row_count, dtype=jnp.int32)
    row_valid = own_places[None, :] < lengths[:, None]
    row_mask = row_valid.reshape(tokens, 1).astype(jnp.float32)
    full_joint, full_output, full_vectors = gather_attention(joint_weight, output_weight, vectors)
    vector_rows = full_vectors.astype(jnp.float32)
    flat_inputs = inputs.reshape(tokens, model_width)
    input_low = flat_inputs.astype(jnp.bfloat16)
    projected = jnp.dot(input_low, full_joint, preferred_element_type=jnp.float32)
    query_low = (projected[:, :model_width] + vector_rows[2]).astype(jnp.bfloat16)
    key_low = projected[:, model_width : 2 * model_width].astype(jnp.bfloat16)
    value_low = (projected[:, 2 * model_width :] + vector_rows[3]).astype(jnp.bfloat16)
    query_heads = query_low.reshape(head_shape)
    key_rows = key_low.reshape(seq_count, row_count, model_width)
    value_rows = value_low.reshape(seq_count, row_count, model_width)
    start_state = (
        jnp.full((seq_count, head_count, row_count), NEG_FILL, jnp.float32),
        jnp.zeros((seq_count, head_count, row_count), jnp.float32),
        jnp.zeros(head_shape, jnp.float32),
    )
    key_piece = lax.all_gather(key_rows, "seq", axis=1, tiled=True)
    value_piece = lax.all_gather(value_rows, "seq", axis=1, tiled=True)

    def forward_score_block(current, offset, block_size):
        running_max, running_sum, summed = current
        key_heads = cut_heads(key_piece, offset, block_size, head_count)
        value_heads = cut_heads(value_piece, offset, block_size, head_count)
        key_places = offset + jnp.arange(block_size, dtype=jnp.int32)
        scores = head_scores(query_heads, key_heads, key_places, lengths)
        new_max = jnp.maximum(running_max, jnp.max(scores, axis=-1))
        factor = jnp.exp(running_max - new_max)
        exp_scores = jnp.exp(scores - new_max[..., None])
        running_sum = running_sum * factor + jnp.sum(exp_scores, axis=-1)
        update = jnp.einsum(
            "shqk,skhd->sqhd",
            exp_scores.astype(jnp.bfloat16),
            value_heads,
            preferred_element_type=jnp.float32,
        )
        summed = summed * jnp.transpose(factor, (0, 2, 1))[..., None] + update
        return (new_max, running_sum, summed)

    running_max, running_sum, summed = over_blocks(
        key_piece.shape[1], forward_score_block, start_state
    )
    attended = summed / jnp.transpose(running_sum, (0, 2, 1))[..., None]
    log_total = jnp.transpose(running_max + jnp.log(running_sum), (0, 2, 1))
    context_low = attended.reshape(tokens, model_width).astype(jnp.bfloat16)
    branch = jnp.dot(context_low, full_output, preferred_element_type=jnp.float32) + vector_rows[4]
    first, first_normed, first_inverse = layer_norm(
        flat_inputs + branch, vector_rows[0], vector_rows[1]
    )
    first_low = first.astype(jnp.bfloat16)
    full_expand, full_reduce, full_bias = gather_feed(expand_weight, reduce_weight, expand_bias)
    before_gelu = jnp.dot(
        first_low, full_expand, preferred_element_type=jnp.float32
    ) + full_bias.astype(jnp.float32)
    hidden_low = gelu_value(before_gelu).astype(jnp.bfloat16)
    feed = jnp.dot(hidden_low, full_reduce, preferred_element_type=jnp.float32) + vector_rows[7]
    result, second_normed, second_inverse = layer_norm(first + feed, vector_rows[5], vector_rows[6])
    full_expand, full_reduce, full_bias = gather_feed(expand_weight, reduce_weight, expand_bias)
    full_joint, full_output, full_vectors = gather_attention(joint_weight, output_weight, vectors)
    grad_res = cotangent.reshape(tokens, model_width) * row_mask
    grad_second, grad_gain_two, grad_shift_two = norm_back(
        grad_res, second_normed, second_inverse, vector_rows[5]
    )
    grad_feed_low = grad_second.astype(jnp.bfloat16)
    grad_reduce_local = jnp.dot(hidden_low.T, grad_feed_low, preferred_element_type=jnp.float32)
    grad_hidden = jnp.dot(
        grad_feed_low, full_reduce.T, preferred_element_type=jnp.float32
    ) * gelu_slope(before_gelu)
    grad_hidden_low = grad_hidden.astype(jnp.bfloat16)
    grad_expand_local = jnp.dot(first_low.T, grad_hidden_low, preferred_element_type=jnp.float32)
    grad_bias_local = jnp.sum(grad_hidden_low.astype(jnp.float32), axis=0)
    grad_first = grad_second + jnp.dot(
        grad_hidden_low, full_expand.T, preferred_element_type=jnp.float32
    )
    grad_resid, grad_gain_one, grad_shift_one = norm_back(
        grad_first, first_normed, first_inverse, vector_rows[0]
    )
    grad_branch_low = grad_resid.astype(jnp.bfloat16)
    grad_output_local = jnp.dot(context_low.T, grad_branch_low, preferred_element_type=jnp.float32)
    grad_context_low = jnp.dot(
        grad_branch_low, full_output.T, preferred_element_type=jnp.float32
    ).astype(jnp.bfloat16)
    grad_context_heads = grad_context_low.reshape(head_shape)
    row_delta = jnp.sum(grad_context_heads.astype(jnp.float32) * attended, axis=-1)
    log_heads = jnp.transpose(log_total, (0, 2, 1))
    delta_heads = jnp.transpose(row_delta, (0, 2, 1))
    query_key_piece = lax.all_gather(key_rows, "seq", axis=1, tiled=True)
    query_value_piece = lax.all_gather(value_rows, "seq", axis=1, tiled=True)

    def query_score_block(current, offset, block_size):
        key_heads = cut_heads(query_key_piece, offset, block_size, head_count)
        value_heads = cut_heads(query_value_piece, offset, block_size, head_count)
        key_places = offset + jnp.arange(block_size, dtype=jnp.int32)
        scores = head_scores(query_heads, key_heads, key_places, lengths)
        softmax_rows = jnp.exp(scores - log_heads[..., None])
        grad_probs = jnp.einsum(
            "sqhd,skhd->shqk", grad_context_heads, value_heads, preferred_element_type=jnp.float32
        )
        grad_scores = (softmax_rows * (grad_probs - delta_heads[..., None])).astype(jnp.bfloat16)
        return (
            current
            + jnp.einsum(
                "shqk,skhd->sqhd", grad_scores, key_heads, preferred_element_type=jnp.float32
            )
            * SCORE_SCALE
        )

    grad_query = over_blocks(
        query_key_piece.shape[1], query_score_block, jnp.zeros(head_shape, jnp.float32)
    )
    own_keys = key_low.reshape(head_shape)
    own_values = value_low.reshape(head_shape)
    query_rows = query_low.reshape(seq_count, row_count, model_width)
    grad_context_rows = grad_context_low.reshape(seq_count, row_count, model_width)
    zero_heads = jnp.zeros(head_shape, jnp.float32)
    query_piece = lax.all_gather(query_rows.astype(jnp.float32), "seq", axis=1, tiled=True).astype(
        jnp.bfloat16
    )
    grad_piece = lax.all_gather(
        grad_context_rows.astype(jnp.float32), "seq", axis=1, tiled=True
    ).astype(jnp.bfloat16)
    log_piece = lax.all_gather(log_total, "seq", axis=1, tiled=True)
    delta_piece = lax.all_gather(row_delta, "seq", axis=1, tiled=True)

    def key_score_block(current, offset, block_size):
        grad_key, grad_value = current
        query_block = cut_heads(query_piece, offset, block_size, head_count)
        grad_block = cut_heads(grad_piece, offset, block_size, head_count)
        log_block = jnp.transpose(
            lax.dynamic_slice_in_dim(log_piece, offset, block_size, 1), (0, 2, 1)
        )
        delta_block = jnp.transpose(
            lax.dynamic_slice_in_dim(delta_piece, offset, block_size, 1), (0, 2, 1)
        )
        scores = head_scores(query_block, own_keys, own_places, lengths)
        softmax_rows = jnp.exp(scores - log_block[..., None])
        grad_value = grad_value + jnp.einsum(
            "shqk,sqhd->skhd",
            softmax_rows.astype(jnp.bfloat16),
            grad_block,
            preferred_element_type=jnp.float32,
        )
        grad_probs = jnp.einsum(
            "sqhd,skhd->shqk", grad_block, own_values, preferred_element_type=jnp.float32
        )
        grad_scores = (softmax_rows * (grad_probs - delta_block[..., None])).astype(jnp.bfloat16)
        grad_key = (
            grad_key
            + jnp.einsum(
                "shqk,sqhd->skhd", grad_scores, query_block, preferred_element_type=jnp.float32
            )
            * SCORE_SCALE
        )
        return (grad_key, grad_value)

    grad_key, grad_value = over_blocks(
        query_piece.shape[1], key_score_block, (zero_heads, zero_heads)
    )
    grad_query_low = grad_query.reshape(tokens, model_width).astype(jnp.bfloat16)
    grad_key_low = grad_key.reshape(tokens, model_width).astype(jnp.bfloat16)
    grad_value_low = grad_value.reshape(tokens, model_width).astype(jnp.bfloat16)
    grad_projected = jnp.concatenate([grad_query_low, grad_key_low, grad_value_low], axis=1)
    grad_joint_local = jnp.dot(input_low.T, grad_projected, preferred_element_type=jnp.float32)
    grad_inputs = grad_resid + jnp.dot(
        grad_projected, full_joint.T, preferred_element_type=jnp.float32
    )
    grad_vector_local = jnp.stack(
        [
            grad_gain_one,
            grad_shift_one,
            jnp.sum(grad_query_low.astype(jnp.float32), axis=0),
            jnp.sum(grad_value_low.astype(jnp.float32), axis=0),
            jnp.sum(grad_branch_low.astype(jnp.float32), axis=0),
            grad_gain_two,
            grad_shift_two,
            jnp.sum(grad_feed_low.astype(jnp.float32), axis=0),
        ],
        axis=0,
    )
    every_grad = (
        lax.psum_scatter(grad_joint_local, ("batch", "seq"), scatter_dimension=0, tiled=True),
        lax.psum_scatter(grad_output_local, ("batch", "seq"), scatter_dimension=0, tiled=True),
        lax.psum_scatter(grad_vector_local, ("batch", "seq"), scatter_dimension=1, tiled=True),
        lax.psum_scatter(grad_expand_local, ("batch", "seq"), scatter_dimension=0, tiled=True),
        lax.psum_scatter(grad_reduce_local, ("batch", "seq"), scatter_dimension=0, tiled=True),
        lax.psum_scatter(grad_bias_local, ("batch", "seq"), scatter_dimension=0, tiled=True),
    )
    summed_grads = (
        every_grad[0],
        every_grad[1],
        every_grad[2],
        every_grad[3],
        every_grad[5],
        every_grad[4],
    )
    return (
        result.reshape(seq_count, row_count, model_width),
        grad_inputs.reshape(seq_count, row_count, model_width),
        summed_grads[0],
        summed_grads[1],
        summed_grads[2],
        summed_grads[3],
        summed_grads[4],
        summed_grads[5],
    )


MESH = pl.DeviceIdType.MESH
ANY = pl.BlockSpec(memory_space=pl.ANY)
VM = pl.BlockSpec(memory_space=pltpu.VMEM)
SM = pl.BlockSpec(memory_space=pltpu.SMEM)
DMA = pltpu.SemaphoreType.DMA
VMEM_LIMIT = 60 << 20
F32 = jnp.float32
BF16 = jnp.bfloat16


def send(src, dst, send_sem, recv_sem, device):
    return pltpu.make_async_remote_copy(
        src_ref=src,
        dst_ref=dst,
        send_sem=send_sem,
        recv_sem=recv_sem,
        device_id=device,
        device_id_type=MESH,
    )


class Place:
    def __init__(self, nb):
        self.nb = nb
        self.b = lax.axis_index("batch")
        self.s = lax.axis_index("seq")
        self.c = self.s % 2
        self.p = self.s // 2
        x, y = self.p % 2, self.p // 2
        self.px = 2 * y + (1 - x)
        self.py = 2 * (1 - y) + x
        self.pd = 2 * (1 - y) + (1 - x)
        self.sib = (self.b, 2 * self.p + 1 - self.c)
        self.xn = (self.b, 2 * self.px + self.c)
        self.yn = (self.b, 2 * self.py + self.c)

    def chip(self, step):
        return (self.p, self.px, self.py, self.pd)[step]

    def up(self, step):
        return (self.b + step) % self.nb

    def down(self, step):
        return (self.b + self.nb - step) % self.nb


def greet_near(pos):
    barrier = pltpu.get_barrier_semaphore()

    def signal(device):
        pl.semaphore_signal(barrier, inc=1, device_id=device, device_id_type=MESH)

    for device in plane_others(pos):
        signal(device)
    last = pos.nb - 1
    guarded(pos.b < last, lambda: signal(((pos.b + 1) % pos.nb, pos.s)))
    guarded(pos.b > 0, lambda: signal(((pos.b + last) % pos.nb, pos.s)))
    beside = jnp.where(pos.b < last, 1, 0) + jnp.where(pos.b > 0, 1, 0)
    pl.semaphore_wait(barrier, 7 + beside)


def same_core(pos):
    return [
        (pos.up(d), 2 * pos.chip(k) + pos.c)
        for d in range(pos.nb)
        for k in range(4)
        if d or k
    ]


def plane_others(pos):
    return [
        (pos.b, 2 * pos.chip(k) + (pos.c if j == 0 else 1 - pos.c))
        for k in range(4)
        for j in range(2)
        if k or j
    ]


def guarded(condition, action):
    if isinstance(condition, bool):
        if condition:
            action()
    else:

        @pl.when(condition)
        def _():
            action()


class Chain:
    def __init__(self, pos, mine, spot, sems):
        self.pos, self.mine, self.spot = pos, mine, spot
        self.up, self.down = sems

    @staticmethod
    def scratch(nb):
        return [DMA((2, nb)), DMA((2, nb))]

    def copy(self, src, z, sems, hop, there):
        pos = self.pos
        return send(src, self.spot(z), sems.at[0, hop], sems.at[1, hop], (there, pos.s))

    def moves(self, hop):
        pos = self.pos
        last = pos.nb - 1
        low, high = (pos.b - hop + 1 + pos.nb) % pos.nb, (pos.b + hop - 1) % pos.nb
        above, below = (pos.b + 1) % pos.nb, (pos.b + last) % pos.nb
        own = isinstance(hop, int) and hop == 1
        return (
            (
                (pos.b >= hop - 1) & (pos.b < last),
                self.copy(self.mine if own else self.spot(low), low, self.up, hop, above),
            ),
            (
                (pos.b + hop - 1 < pos.nb) & (pos.b > 0),
                self.copy(self.mine if own else self.spot(high), high, self.down, hop, below),
            ),
        )

    def start(self, hop=1):
        for made, copy in self.moves(hop):
            guarded(made, copy.start)

    def hop(self, hop):
        pos = self.pos
        low, high = (pos.b - hop + pos.nb) % pos.nb, (pos.b + hop) % pos.nb
        for made, z, sems in (
            (pos.b >= hop, low, self.up),
            (pos.b + hop < pos.nb, high, self.down),
        ):
            guarded(made, self.copy(self.spot(z), z, sems, hop, pos.b).wait_recv)
        guarded(hop < pos.nb - 1, lambda: self.start(hop + 1))

    def drain(self):
        for hop in range(1, self.pos.nb):
            for made, copy in self.moves(hop):
                guarded(made, copy.wait_send)


class Gather:
    def __init__(self, pos, shard, out, halves, sems):
        self.pos, self.shard, self.out, self.halves = pos, shard, out, halves
        self.xs, self.ys, self.f0, self.f1, self.sb, self.local_sem = sems[:6]
        self.chain = Chain(pos, shard, lambda z: out.at[z, pos.p, pos.c], sems[6:8])
        self.across = Chain(
            pos, out.at[pos.b, pos.pd, pos.c], lambda z: out.at[z, pos.pd, pos.c], sems[8:]
        )

    @staticmethod
    def scratch(nb):
        return [DMA((2, nb))] * 2 + [DMA((2,))] * 2 + [DMA((2, nb + 3)), DMA] + Chain.scratch(nb) * 2

    def z(self, k):
        return jnp.where(k <= self.pos.b, self.pos.b - k, k)

    def own(self):
        pos = self.pos
        self.local = pltpu.make_async_copy(
            self.shard, self.out.at[pos.b, pos.p, pos.c], self.local_sem
        )
        self.local.start()

    def x_copy(self, k, src=None):
        pos = self.pos
        there = self.out.at[self.z(k), pos.p, pos.c]
        src = there if src is None else src
        return send(src, there, self.xs.at[0, k], self.xs.at[1, k], pos.xn)

    def y_copy(self, k, src=None):
        pos = self.pos
        there = self.out.at[self.z(k), pos.p, pos.c]
        src = there if src is None else src
        return send(src, there, self.ys.at[0, k], self.ys.at[1, k], pos.yn)

    def plane(self, k, src=None):
        self.x_copy(k, src).start()
        self.y_copy(k, src).start()

    def landed(self, sems, k, chip):
        pos = self.pos
        ref = self.out.at[self.z(k), chip, pos.c]
        send(ref, ref, sems.at[0, k], sems.at[1, k], pos.xn).wait_recv()

    def y_forward(self):
        pos = self.pos
        ref = self.out.at[pos.b, pos.px, pos.c].at[self.halves[0]]
        return send(ref, ref, self.f0.at[0], self.f0.at[1], pos.yn)

    def x_forward(self):
        pos = self.pos
        ref = self.out.at[pos.b, pos.py, pos.c].at[self.halves[1]]
        return send(ref, ref, self.f1.at[0], self.f1.at[1], pos.xn)

    def forward(self):
        pos = self.pos
        self.landed(self.xs, 0, pos.px)
        self.y_forward().start()
        self.landed(self.ys, 0, pos.py)
        if self.halves[1] is not None:
            self.x_forward().start()

    def cross(self):
        pos = self.pos
        across = self.out.at[pos.b, pos.pd, pos.c]
        for half, sems in zip(self.halves, (self.f0, self.f1)):
            if half is not None:
                ref = across.at[half]
                send(ref, ref, sems.at[0], sems.at[1], pos.xn).wait_recv()

    def beside(self, k):
        pos = self.pos
        self.landed(self.xs, k, pos.px)
        self.landed(self.ys, k, pos.py)

    def sibling_copy(self, k, core=None):
        pos = self.pos
        ref = self.out.at[self.z(k), :, pos.c if core is None else core]
        return send(ref, ref, self.sb.at[0, k], self.sb.at[1, k], pos.sib)

    def sibling(self, k):
        self.sibling_copy(k).start()

    def part_copy(self, n, core=None):
        pos = self.pos
        k = pos.nb - 1
        ref = self.out.at[self.z(k), pos.chip(n), pos.c if core is None else core]
        return send(ref, ref, self.sb.at[0, k + n], self.sb.at[1, k + n], pos.sib)

    def finish(self, k):
        self.sibling_copy(k, 1 - self.pos.c).wait_recv()
        self.x_copy(k).wait_send()
        self.y_copy(k).wait_send()
        self.sibling_copy(k).wait_send()

    def end(self):
        k = self.pos.nb - 1
        for n in range(4):
            self.part_copy(n, 1 - self.pos.c).wait_recv()
        for n in range(4):
            self.part_copy(n).wait_send()
        self.x_copy(k).wait_send()
        self.y_copy(k).wait_send()

    def drain(self):
        self.y_forward().wait_send()
        if self.halves[1] is not None:
            self.x_forward().wait_send()
        self.chain.drain()
        self.across.drain()


class InputExchange:
    def __init__(self, pos, rows, out, sems):
        self.pos, self.rows, self.out, self.sems = pos, rows, out, sems
        self.started = []

    @staticmethod
    def scratch():
        return [DMA((2, 2)), DMA((2, 2)), DMA((2, 2)), DMA((2,)), DMA]

    def go(self, copy):
        copy.start()
        self.started.append(copy)

    def start(self):
        pos, (xs, ys, _, sb, local) = self.pos, self.sems
        there = self.out.at[pos.p, pos.c]
        for sems, chip in ((xs, pos.px), (ys, pos.py)):
            for j in range(2):
                self.go(
                    send(
                        self.rows.at[j],
                        there,
                        sems.at[0, j],
                        sems.at[1, pos.c],
                        (pos.b, 2 * chip + j),
                    )
                )
        self.go(send(self.rows.at[1 - pos.c], there, sb.at[0], sb.at[1], pos.sib))
        self.local = pltpu.make_async_copy(self.rows.at[pos.c], there, local)
        self.local.start()

    def landed(self, sems, j, chip):
        ref = self.out.at[chip, j]
        send(ref, ref, sems.at[0, j], sems.at[1, j], self.pos.xn).wait_recv()

    def forward(self):
        pos, (xs, ys, fs, _, _) = self.pos, self.sems
        self.landed(xs, 0, pos.px)
        ref = self.out.at[pos.px, 0]
        self.go(send(ref, ref, fs.at[0, 0], fs.at[1, 0], pos.yn))
        self.landed(ys, 1, pos.py)
        ref = self.out.at[pos.py, 1]
        self.go(send(ref, ref, fs.at[0, 1], fs.at[1, 1], pos.xn))

    def finish(self):
        pos, (xs, ys, fs, sb, _) = self.pos, self.sems
        self.landed(xs, 1, pos.px)
        self.landed(ys, 0, pos.py)
        self.landed(fs, 0, pos.pd)
        self.landed(fs, 1, pos.pd)
        ref = self.out.at[pos.p, 1 - pos.c]
        send(ref, ref, sb.at[0], sb.at[1], pos.sib).wait_recv()
        self.local.wait()

    def drain(self):
        for copy in self.started:
            copy.wait_send()


class JointGather:
    def __init__(self, pos, parts, out, sems):
        self.pos, self.parts, self.out = pos, parts, out
        self.direct, self.sb, self.local_sem = sems[:3]
        self.chain = Chain(
            pos, out.at[pos.b, :, pos.c], lambda z: out.at[z, :, pos.c], sems[3:]
        )

    @staticmethod
    def scratch(nb):
        return [DMA((2, 4)), DMA((2,)), DMA] + Chain.scratch(nb)

    def start(self):
        pos = self.pos
        there = self.out.at[pos.b, pos.p, pos.c]
        self.started = [
            send(
                self.parts.at[pos.chip(k)],
                there,
                self.direct.at[0, k],
                self.direct.at[1, k],
                (pos.b, 2 * pos.chip(k) + pos.c),
            )
            for k in range(1, 4)
        ]
        for copy in self.started:
            copy.start()
        self.local = pltpu.make_async_copy(self.parts.at[pos.p], there, self.local_sem)
        self.local.start()

    def own(self):
        pos = self.pos
        for k in range(1, 4):
            ref = self.out.at[pos.b, pos.chip(k), pos.c]
            send(ref, ref, self.direct.at[0, k], self.direct.at[1, k], pos.sib).wait_recv()
        self.local.wait()
        self.chain.start()

    def sibling(self):
        pos = self.pos
        ref = self.out.at[:, :, pos.c]
        send(ref, ref, self.sb.at[0], self.sb.at[1], pos.sib).start()

    def finish(self):
        pos = self.pos
        ref = self.out.at[:, :, 1 - pos.c]
        send(ref, ref, self.sb.at[0], self.sb.at[1], pos.sib).wait_recv()

    def drain(self):
        for copy in self.started:
            copy.wait_send()
        ref = self.out.at[:, :, self.pos.c]
        send(ref, ref, self.sb.at[0], self.sb.at[1], self.pos.sib).wait_send()
        self.chain.drain()


class ContextExchange:
    def __init__(self, pos, parts, out, sems):
        self.pos, self.parts, self.out = pos, parts, out
        self.sems, self.local_sem = sems

    @staticmethod
    def scratch():
        return [DMA((2, 8)), DMA]

    def pairs(self):
        pos = self.pos
        for k in range(4):
            for j in range(2):
                if k or j:
                    yield 2 * k + j, pos.chip(k), pos.c if j == 0 else 1 - pos.c

    def copies(self):
        pos, sems = self.pos, self.sems
        there = self.out.at[pos.p, pos.c]
        return [
            send(
                self.parts.at[chip, core],
                there,
                sems.at[0, i],
                sems.at[1, i],
                (pos.b, 2 * chip + core),
            )
            for i, chip, core in self.pairs()
        ]

    def local(self):
        pos = self.pos
        return pltpu.make_async_copy(
            self.parts.at[pos.p, pos.c], self.out.at[pos.p, pos.c], self.local_sem
        )

    def start(self):
        for copy in self.copies():
            copy.start()
        self.local().start()

    def arrive(self):
        for i, chip, core in self.pairs():
            ref = self.out.at[chip, core]
            send(ref, ref, self.sems.at[0, i], self.sems.at[1, i], self.pos.sib).wait_recv()
        self.local().wait()

    def drain(self):
        for copy in self.copies():
            copy.wait_send()


def gather_attend(
    lengths, inputs, joint, vectors, hidden_bias, output, expand, reduce, nb, heads
):
    _, count, model_width = inputs.shape
    shard = vec = model_width // (8 * nb)
    per = reduce.shape[0]
    width = heads * HEAD_DIM
    size = 8 * count
    joint_shape = (4, shard, 3 * width + 64)
    small_shape = (16, 128)

    def body(
        lengths_ref, inputs_ref, joint_weight_ref, own_vectors_ref, own_bias_ref,
        output_ref, expand_ref, reduce_ref,
        vectors_out, hidden_out, rows_any, weight_any, qkv_any, log_any,
        context_out, output_out, expand_out, reduce_out,
        rows_out, weight_out, qkv_out, log_out, stores,
        joint_all, context, small_all, bias_ref, rows_ref, joint_ref, small_ref,
        *scratch,
    ):
        pos = Place(nb)
        scratch = list(scratch)

        def take(n):
            got = scratch[:n]
            del scratch[:n]
            return got

        exchange = InputExchange(pos, rows_ref, rows_out, take(5))
        joints = JointGather(pos, joint_ref, joint_all, take(5))
        mixing = ContextExchange(pos, context, context_out, take(2))
        outputs, expands, reduces, smalls = (
            Gather(pos, part, out, halves_of(part.shape), take(10))
            for part, out in (
                (output_ref, output_out),
                (expand_ref, expand_out),
                (reduce_ref, reduce_out),
                (small_ref, small_all),
            )
        )
        gathers = (expands, smalls, reduces, outputs)
        units = ((expands, smalls), (reduces,), (outputs,))

        saves = [
            pltpu.make_async_copy(src, dst, stores.at[n])
            for n, (src, dst) in enumerate(
                (
                    (rows_out, rows_any),
                    (weight_out, weight_any),
                    (qkv_out, qkv_any),
                    (log_out, log_any),
                )
            )
        ]

        def project(i, _):
            at = pl.ds(pl.multiple_of(i * 2 * count, 2 * count), 2 * count)
            qkv_out[at, :] = (
                jnp.dot(
                    rows_out[i].reshape(2 * count, model_width),
                    weight_out[...],
                    preferred_element_type=F32,
                )
                + bias_ref[...]
            ).astype(BF16)
            return 0

        def prepare():
            joints.finish()
            for z in range(nb):
                weight_out[z * 8 * shard : (z + 1) * 8 * shard, :] = joint_all[
                    z, :, :, :, : 3 * width
                ].reshape(8 * shard, 3 * width)
            bias_ref[...] = jnp.zeros_like(bias_ref)
            for s in range(8):
                spot = joint_all[pos.p, s // 2, s % 2, :, 3 * width :].astype(F32)
                bias_ref[:, s * vec : (s + 1) * vec] = spot[0:1, :vec]
                bias_ref[:, 2 * width + s * vec : 2 * width + (s + 1) * vec] = spot[1:2, :vec]
            lax.fori_loop(0, 4, project, 0)
            for copy in saves[:3]:
                copy.start()

        def hop(k):
            for gather in gathers:
                gather.chain.hop(k)

        def relay(k, some):
            for gather in some:
                gather.across.hop(k)

        def share(k):
            for gather in gathers:
                gather.beside(k)
                gather.sibling(k)

        attend = attend_block(lengths_ref[pos.c], qkv_out, log_out, context, heads, count)

        def spread(k):
            for gather in gathers:
                gather.plane(k)

        weight = joint_weight_ref[...]
        spot = jnp.pad(
            own_vectors_ref[2:4, :].astype(F32), ((0, shard - 2), (0, 64 - vec))
        ).astype(BF16)
        for chip in range(4):
            at = slice(chip * width, (chip + 1) * width)
            joint_ref[chip] = jnp.concatenate(
                [weight[:, n * model_width :][:, at] for n in range(3)] + [spot], axis=1
            )
        small_ref[...] = jnp.concatenate(
            [
                jnp.pad(own_vectors_ref[...].astype(F32), ((0, 0), (0, 128 - vec))),
                jnp.pad(own_bias_ref[...].astype(F32), ((0, 7), (0, 128 - per))),
            ]
        ).astype(BF16)
        rows_ref[...] = inputs_ref[...].astype(BF16)
        greet_near(pos)
        joints.start()
        for gather in gathers:
            gather.own()
            gather.chain.start()
            gather.plane(0, gather.shard)
        joints.own()
        for n, gather in enumerate(gathers):
            gather.forward()
            if n == 1:
                exchange.start()
        hop(1)
        joints.chain.hop(1)
        for gather in gathers:
            gather.local.wait()
            gather.cross()
            gather.sibling(0)
        joints.chain.hop(2)
        hop(2)
        for gather in gathers:
            gather.across.start()
        exchange.forward()
        spread(1)
        joints.chain.hop(3)
        joints.sibling()
        exchange.finish()
        spread(2)
        prepare()
        hop(3)
        spread(3)
        attend(0)
        relay(1, gathers)
        attend(1)
        attend(2)
        relay(2, gathers)
        attend(3)
        mixing.start()
        saves[3].start()
        share(1)
        relay(nb - 1, (smalls,))
        share(2)
        for gather in gathers:
            gather.beside(nb - 1)
            for n in range(3):
                gather.part_copy(n).start()
        smalls.part_copy(3).start()

        def finish(k, _):
            for gather in gathers:
                gather.finish(k)
            return 0

        lax.fori_loop(0, nb - 1, finish, 0)
        smalls.end()
        for owner in range(8 * nb):
            part = small_all[owner // 8, owner % 8 // 2, owner % 2].astype(F32)
            vectors_out[:, owner * vec : (owner + 1) * vec] = part[:8, :vec]
            hidden_out[:, owner * per : (owner + 1) * per] = part[8:9, :per]
        smalls.drain()
        exchange.drain()
        joints.drain()
        for gather in (expands, reduces, outputs):
            gather.across.hop(nb - 1)
            gather.part_copy(3).start()
        for gather in (expands, reduces, outputs):
            gather.drain()
        mixing.arrive()
        mixing.drain()
        for gather in (expands, reduces, outputs):
            gather.end()
        for copy in saves:
            copy.wait()

    kept = (
        ((4, 2) + inputs.shape[1:], BF16),
        ((model_width, 3 * width), BF16),
        ((size, 3 * width), BF16),
        ((size, 128), F32),
    )

    def shape(part):
        return jax.ShapeDtypeStruct((nb, 4, 2) + part.shape, part.dtype)

    return pl.pallas_call(
        body,
        out_shape=(
            jax.ShapeDtypeStruct((8, model_width), F32),
            jax.ShapeDtypeStruct((1, 8 * nb * per), F32),
            *(jax.ShapeDtypeStruct(shape, dtype) for shape, dtype in kept),
            jax.ShapeDtypeStruct((4, 2, count, width), BF16),
            shape(output),
            shape(expand),
            shape(reduce),
        ),
        in_specs=[SM] + [VM] * 7,
        out_specs=(VM,) * 2 + (ANY,) * 8,
        scratch_shapes=[pltpu.VMEM(shape, dtype) for shape, dtype in kept]
        + [DMA((4,))]
        + [
            pltpu.VMEM((nb, 4, 2) + joint_shape[1:], BF16),
            pltpu.VMEM((4, 2, count, width), BF16),
            pltpu.VMEM((nb, 4, 2) + small_shape, BF16),
            pltpu.VMEM((1, 3 * width), F32),
            pltpu.VMEM(inputs.shape, BF16),
            pltpu.VMEM(joint_shape, BF16),
            pltpu.VMEM(small_shape, BF16),
        ]
        + InputExchange.scratch()
        + JointGather.scratch(nb)
        + ContextExchange.scratch()
        + Gather.scratch(nb) * 4,
        name="gather_attend",
        compiler_params=pltpu.CompilerParams(
            collective_id=1, has_side_effects=True, vmem_limit_bytes=VMEM_LIMIT
        ),
    )(lengths, inputs, joint, vectors, hidden_bias, output, expand, reduce)


def halves_of(shape):
    rows, columns = shape
    if columns % 256 == 0 and columns >= 1024:
        return (
            (slice(None), pl.ds(0, columns // 2)),
            (slice(None), pl.ds(columns // 2, columns // 2)),
        )
    if rows % 32 == 0:
        return (
            (pl.ds(0, rows // 2), slice(None)),
            (pl.ds(rows // 2, rows // 2), slice(None)),
        )
    if columns % 256 == 0:
        return (
            (slice(None), pl.ds(0, columns // 2)),
            (slice(None), pl.ds(columns // 2, columns // 2)),
        )
    return ((slice(None), slice(None)), None)


def attend_block(limit, qkv_ref, log_ref, context_ref, heads, count):
    width = heads * HEAD_DIM
    size = 8 * count

    def part(n, _):
        at = pl.ds(pl.multiple_of(n * count, count), count)
        allowed = lax.broadcasted_iota(jnp.int32, (1, size), 1) < limit
        lanes = lax.broadcasted_iota(jnp.int32, (count, 128), 1)
        parts, logs = [], jnp.zeros((count, 128), F32)
        for h in range(heads):
            query = qkv_ref[at, h * HEAD_DIM : (h + 1) * HEAD_DIM]
            key = qkv_ref[:, width + h * HEAD_DIM : width + (h + 1) * HEAD_DIM]
            value = qkv_ref[:, 2 * width + h * HEAD_DIM : 2 * width + (h + 1) * HEAD_DIM]
            scores = (
                lax.dot_general(
                    query, key, (((1,), (1,)), ((), ())), preferred_element_type=F32
                )
                * SCORE_SCALE
            )
            scores = jnp.where(allowed, scores, NEG_FILL)
            top = jnp.max(scores, axis=-1, keepdims=True)
            exps = jnp.exp(scores - top)
            total = jnp.sum(exps, axis=-1, keepdims=True)
            mixed = jnp.dot(exps.astype(BF16), value, preferred_element_type=F32)
            parts.append(mixed / total)
            logs = jnp.where(lanes == h, top + jnp.log(total), logs)
        context_ref[n // 2, n % 2] = jnp.concatenate(parts, axis=1).astype(BF16)
        log_ref[at, :] = logs
        return 0

    def block(i):
        lax.fori_loop(2 * i, 2 * i + 2, part, 0)

    return block


def attend_back_block(limit, qkv_ref, log_ref, grad_ref, grad_qkv, grad_key, grad_value, heads, count):
    width = heads * HEAD_DIM
    size = 8 * count
    along_keys = (((1,), (1,)), ((), ()))
    along_rows = (((0,), (0,)), ((), ()))

    def part(n, _):
        at = pl.ds(pl.multiple_of(n * count, count), count)
        allowed = lax.broadcasted_iota(jnp.int32, (1, size), 1) < limit
        grads = grad_ref[n // 2, n % 2]
        parts = []
        for h in range(heads):
            query = qkv_ref[at, h * HEAD_DIM : (h + 1) * HEAD_DIM]
            key = qkv_ref[:, width + h * HEAD_DIM : width + (h + 1) * HEAD_DIM]
            value = qkv_ref[:, 2 * width + h * HEAD_DIM : 2 * width + (h + 1) * HEAD_DIM]
            grad_out = grads[:, h * HEAD_DIM : (h + 1) * HEAD_DIM]
            scores = (
                lax.dot_general(query, key, along_keys, preferred_element_type=F32)
                * SCORE_SCALE
            )
            probs = jnp.where(allowed, jnp.exp(scores - log_ref[at, h : h + 1]), 0.0)
            grad_probs = lax.dot_general(
                grad_out, value, along_keys, preferred_element_type=F32
            )
            delta = jnp.sum(probs * grad_probs, axis=-1, keepdims=True)
            grad_scores = (probs * (grad_probs - delta)).astype(BF16)
            parts.append(
                jnp.dot(grad_scores, key, preferred_element_type=F32) * SCORE_SCALE
            )
            key_part = lax.dot_general(
                grad_scores, query, along_rows, preferred_element_type=F32
            )
            value_part = lax.dot_general(
                probs.astype(BF16), grad_out, along_rows, preferred_element_type=F32
            )
            own = slice(h * HEAD_DIM, (h + 1) * HEAD_DIM)
            grad_key[:, own] += key_part
            grad_value[:, own] += value_part
        grad_qkv[at, :width] = jnp.concatenate(parts, axis=1).astype(BF16)
        return 0

    def block(i):
        lax.fori_loop(2 * i, 2 * i + 2, part, 0)

    return block


class Scatter:
    def __init__(self, pos, halves, bufs, sems):
        self.pos, self.halves = pos, halves
        (self.partial, self.theirs, self.a0, self.a1, self.bx, self.by, self.z) = bufs
        (self.sb, self.s0, self.s1, self.dx, self.dy, self.cx, self.cy, self.zs) = sems

    @staticmethod
    def scratch(nb, shape, dtype, halves):
        first, second = half_shapes(shape, halves)
        return [
            pltpu.VMEM((nb, 4, 2) + shape, dtype),
            pltpu.VMEM((nb, 4) + shape, dtype),
            pltpu.VMEM((nb,) + first, dtype),
            pltpu.VMEM((nb,) + second, dtype),
            pltpu.VMEM((nb,) + shape, dtype),
            pltpu.VMEM((nb,) + shape, dtype),
            pltpu.VMEM((nb,) + shape, dtype),
        ]

    @staticmethod
    def sem_scratch(nb):
        return [DMA((2, nb)) for _ in range(8)]

    def mine(self, k, chip):
        return self.partial.at[self.pos.up(k), chip, self.pos.c]

    def sibling_copy(self, k):
        pos = self.pos
        z = pos.up(k)
        return send(
            self.partial.at[z, :, 1 - pos.c],
            self.theirs.at[z],
            self.sb.at[0, k],
            self.sb.at[1, k],
            pos.sib,
        )

    def begin(self, k):
        self.sibling_copy(k).start()

    def copy(self, k, src, dst, sems, there):
        return send(src, dst, sems.at[0, k], sems.at[1, k], there)

    def first_copies(self, k):
        pos = self.pos
        h0, h1 = self.halves
        copies = [
            self.copy(k, self.mine(k, pos.pd).at[h0], self.a0.at[k], self.s0, pos.xn),
            self.copy(k, self.mine(k, pos.px).at[h0], self.bx.at[k].at[h0], self.dx, pos.xn),
        ]
        if h1 is not None:
            copies += [
                self.copy(k, self.mine(k, pos.pd).at[h1], self.a1.at[k], self.s1, pos.yn),
                self.copy(k, self.mine(k, pos.py).at[h1], self.by.at[k].at[h1], self.dy, pos.yn),
            ]
        return copies

    def second_copies(self, k):
        pos = self.pos
        h0, h1 = self.halves
        copies = [
            self.copy(k, self.mine(k, pos.py).at[h0], self.by.at[k].at[h0], self.cy, pos.yn)
        ]
        if h1 is not None:
            copies.append(
                self.copy(k, self.mine(k, pos.px).at[h1], self.bx.at[k].at[h1], self.cx, pos.xn)
            )
        return copies

    def first(self, k):
        pos = self.pos
        z = pos.up(k)
        self.sibling_copy(k).wait_recv()
        for j in range(4):
            chip = pos.chip(3 - j)
            self.partial[z, chip, pos.c] = (
                self.partial[z, chip, pos.c].astype(F32) + self.theirs[z, chip].astype(F32)
            ).astype(self.partial.dtype)
        for copy in self.first_copies(k):
            copy.start()

    def landed(self, ref, sems, k):
        send(ref, ref, sems.at[0, k], sems.at[1, k], self.pos.xn).wait_recv()

    def second(self, k):
        pos = self.pos
        h0, h1 = self.halves
        copies = self.second_copies(k)
        self.landed(self.a0.at[k], self.s0, k)
        ref = self.mine(k, pos.py)
        ref[h0] = (ref[h0].astype(F32) + self.a0[k].astype(F32)).astype(ref.dtype)
        copies[0].start()
        if h1 is not None:
            self.landed(self.a1.at[k], self.s1, k)
            ref = self.mine(k, pos.px)
            ref[h1] = (ref[h1].astype(F32) + self.a1[k].astype(F32)).astype(ref.dtype)
            copies[1].start()

    def z_copy(self, k):
        pos = self.pos
        return send(
            self.bx.at[k], self.z.at[k], self.zs.at[0, k], self.zs.at[1, k], (pos.up(k), pos.s)
        )

    def third(self, k, total):
        pos = self.pos
        h0, h1 = self.halves
        self.landed(self.bx.at[k].at[h0], self.dx, k)
        self.landed(self.by.at[k].at[h0], self.cy, k)
        if h1 is not None:
            self.landed(self.by.at[k].at[h1], self.dy, k)
            self.landed(self.bx.at[k].at[h1], self.cx, k)
        total[...] = (
            self.mine(k, pos.p)[...].astype(F32)
            + self.bx[k].astype(F32)
            + self.by[k].astype(F32)
        )

        def on():
            self.bx[k] = total[...].astype(self.bx.dtype)
            self.z_copy(k).start()

        guarded(k != 0, on)

    def last(self, total):
        value = total[...]
        for k in range(1, self.pos.nb):
            self.landed(self.z.at[k], self.zs, k)
            value = value + self.z[k].astype(F32)
        total[...] = value

    def drain(self):
        def done(k, _):
            self.sibling_copy(k).wait_send()
            for copy in self.first_copies(k) + self.second_copies(k):
                copy.wait_send()
            guarded(k != 0, lambda: self.z_copy(k).wait_send())
            return 0

        lax.fori_loop(0, self.pos.nb, done, 0)


def half_shapes(shape, halves):
    def cut(half):
        return tuple(n if h == slice(None) else h.size for n, h in zip(shape, half))

    first = cut(halves[0])
    return first, (first if halves[1] is None else cut(halves[1]))


class RowScatter:
    def __init__(self, pos, out, bufs, sems):
        self.pos, self.out = pos, out
        self.mine, self.a0, self.a1, self.bx, self.by, self.far, self.near = bufs
        (self.sm,) = sems

    @staticmethod
    def scratch(rows, columns):
        return [
            pltpu.VMEM((rows, columns), BF16),
            pltpu.VMEM((rows, columns), BF16),
            pltpu.VMEM((2, rows, columns), BF16),
            pltpu.VMEM((2, rows, columns), BF16),
            pltpu.VMEM((rows, columns), F32),
            pltpu.VMEM((rows, columns), F32),
            DMA((2, 7)),
        ]

    def copy(self, i):
        pos, mine = self.pos, self.mine
        src, dst, there = (
            (mine.at[pos.pd, 0], self.a0, pos.xn),
            (mine.at[pos.pd, 1], self.a1, pos.yn),
            (mine.at[pos.px, 0], self.bx.at[0], pos.xn),
            (mine.at[pos.py, 1], self.by.at[1], pos.yn),
            (mine.at[pos.py, 0], self.by.at[0], pos.yn),
            (mine.at[pos.px, 1], self.bx.at[1], pos.xn),
            (self.far, self.near, pos.sib),
        )[i]
        return send(src, dst, self.sm.at[0, i], self.sm.at[1, i], there)

    def landed(self, i, ref):
        send(ref, ref, self.sm.at[0, i], self.sm.at[1, i], self.pos.xn).wait_recv()

    def first(self):
        for i in range(4):
            self.copy(i).start()

    def second(self):
        pos, mine = self.pos, self.mine
        self.landed(0, self.a0)
        mine[pos.py, 0] = (mine[pos.py, 0].astype(F32) + self.a0[...].astype(F32)).astype(BF16)
        self.copy(4).start()
        self.landed(1, self.a1)
        mine[pos.px, 1] = (mine[pos.px, 1].astype(F32) + self.a1[...].astype(F32)).astype(BF16)
        self.copy(5).start()

    def third(self):
        pos = self.pos
        self.landed(2, self.bx.at[0])
        self.landed(3, self.by.at[1])
        self.landed(4, self.by.at[0])
        self.landed(5, self.bx.at[1])

        def total(core):
            return (
                self.mine[pos.p, core].astype(F32)
                + self.bx[core].astype(F32)
                + self.by[core].astype(F32)
            )

        self.far[...] = total(1 - pos.c)
        self.copy(6).start()
        self.out[pos.c] += total(pos.c)

    def last(self):
        pos = self.pos
        self.landed(6, self.near)
        self.out[1 - pos.c] += self.near[...]
        for i in range(7):
            self.copy(i).wait_send()


class JointScatter:
    def __init__(self, pos, bufs, sems):
        self.pos = pos
        self.partial, self.theirs, self.zbuf, self.sums, self.got = bufs
        self.sb, self.zs, self.ps = sems

    @staticmethod
    def scratch(nb, shape):
        return [
            pltpu.VMEM((nb, 4, 2) + shape, BF16),
            pltpu.VMEM((nb, 4) + shape, BF16),
            pltpu.VMEM((nb, 4) + shape, BF16),
            pltpu.VMEM((4,) + shape, BF16),
            pltpu.VMEM((4,) + shape, BF16),
        ]

    @staticmethod
    def sem_scratch(nb):
        return [DMA((2,)), DMA((2, nb)), DMA((2, 4))]

    def sibling_copy(self):
        pos = self.pos
        return send(
            self.partial.at[:, :, 1 - pos.c], self.theirs, self.sb.at[0], self.sb.at[1], pos.sib
        )

    def z_copy(self, d):
        pos = self.pos
        return send(
            self.partial.at[pos.up(d), :, pos.c],
            self.zbuf.at[d],
            self.zs.at[0, d],
            self.zs.at[1, d],
            (pos.up(d), pos.s),
        )

    def plane_copy(self, k):
        pos = self.pos
        chip = pos.chip(k)
        return send(
            self.sums.at[chip],
            self.got.at[pos.p],
            self.ps.at[0, k],
            self.ps.at[1, k],
            (pos.b, 2 * chip + pos.c),
        )

    def begin(self):
        self.sibling_copy().start()

    def first(self):
        pos = self.pos
        self.sibling_copy().wait_recv()
        for d in (*range(1, pos.nb), 0):
            z = pos.up(d)
            self.partial[z, :, pos.c] = (
                self.partial[z, :, pos.c].astype(F32) + self.theirs[z].astype(F32)
            ).astype(BF16)
            if d:
                self.z_copy(d).start()

    def second(self):
        pos = self.pos
        value = self.partial[pos.b, :, pos.c].astype(F32)
        for d in range(1, pos.nb):
            self.z_copy(d).wait_recv()
            value = value + self.zbuf[d].astype(F32)
        self.sums[...] = value.astype(BF16)
        for k in range(1, 4):
            self.plane_copy(k).start()

    def last(self, out, vec):
        pos = self.pos
        width = out.shape[1] // 12
        self.got[pos.p] = self.sums[pos.p]
        for k in range(1, 4):
            ref = self.got.at[pos.chip(k)]
            send(ref, ref, self.ps.at[0, k], self.ps.at[1, k], pos.sib).wait_recv()
        extra = 0.0
        for chip in range(4):
            value = self.got[chip].astype(F32)
            for n in range(3):
                out[:, (4 * n + chip) * width : (4 * n + chip + 1) * width] = value[
                    :, n * width : (n + 1) * width
                ]
            extra = extra + value[:8, 3 * width : 3 * width + vec]
        self.sibling_copy().wait_send()
        for d in range(1, pos.nb):
            self.z_copy(d).wait_send()
        for k in range(1, 4):
            self.plane_copy(k).wait_send()
        return extra


def normed_rows(residual):
    centered = residual - jnp.mean(residual, axis=-1, keepdims=True)
    inverse = lax.rsqrt(jnp.mean(centered * centered, axis=-1, keepdims=True) + EPSILON)
    return centered * inverse, inverse


def transposed_dot(left, right):
    return lax.dot_general(left, right, (((0,), (0,)), ((), ())), preferred_element_type=F32)


def dot_transposed(left, right):
    return lax.dot_general(left, right, (((1,), (1,)), ((), ())), preferred_element_type=F32)


def feed_and_back(
    lengths, inputs, cotangent, mixed, vectors, hidden_bias,
    output_weight, expand_weight, reduce_weight, rows, weight, qkv, logs, nb, heads,
):
    _, count, model_width = inputs.shape
    hidden = hidden_bias.shape[1]
    block = hidden // nb
    width = heads * HEAD_DIM
    size, tokens = 8 * count, 2 * count
    owners = 8 * nb
    shard = vec = model_width // owners
    per = hidden // owners
    joint_shape = (shard, 3 * width + 64)
    shapes = [(16, 128), (shard, model_width), (shard, hidden), (per, model_width)]
    dtypes = [F32, BF16, BF16, BF16]

    def body(
        lengths_ref, inputs_ref, cotangent_ref, mixed_ref, vectors_ref, bias_ref,
        output_ref, expand_ref, reduce_ref, rows_any, weight_any, qkv_any, log_any,
        result_out, rows_out, joint_out, vectors_out, hidden_out,
        output_out, expand_out, reduce_out,
        output_w, expand_w, reduce_w, rows_ref, weight_ref, qkv_ref, log_ref, loads,
        context, first_normed, first_low, hidden_low, slope, feed, grad_low,
        grad_vectors, grad_bias, parts, small_total,
        grad_context, grad_qkv, grad_key, grad_value,
        *scratch,
    ):
        pos = Place(nb)
        scratch = list(scratch)

        def take(n):
            got = scratch[:n]
            del scratch[:n]
            return got

        mixing = ContextExchange(pos, parts, grad_context, take(2))
        row_sums = RowScatter(pos, rows_out, [hidden_low] + take(6), take(1))
        joints = JointScatter(pos, take(5), take(3))
        smalls, outputs, expands, reduces = (
            Scatter(pos, halves_of(shape), take(7), take(8)) for shape in shapes
        )

        def turn(i):
            return jnp.where(i < 2, 2 - i, 3 * (3 - i))

        def expand_load(z):
            at = pl.ds(z * block if isinstance(z, int) else pl.multiple_of(z * block, block), block)
            return pltpu.make_async_copy(expand_ref.at[:, at], expand_w.at[z], loads.at[z])

        def reduce_load(z):
            at = pl.ds(z * block if isinstance(z, int) else pl.multiple_of(z * block, block), block)
            return pltpu.make_async_copy(reduce_ref.at[at, :], reduce_w.at[z], loads.at[nb + z])

        output_load = pltpu.make_async_copy(output_ref, output_w, loads.at[2 * nb])
        later = [
            pltpu.make_async_copy(src, dst, loads.at[2 * nb + 1 + n])
            for n, (src, dst) in enumerate(
                ((rows_any, rows_ref), (weight_any, weight_ref), (qkv_any, qkv_ref), (log_any, log_ref))
            )
        ]
        output_load.start()
        for z in range(nb):
            expand_load(z).start()
            reduce_load(z).start()
        for copy in later:
            copy.start()
        barrier = pltpu.get_barrier_semaphore()
        partners = [(pos.up(d), pos.s) for d in range(1, nb)] + plane_others(pos)
        for device in partners:
            pl.semaphore_signal(barrier, inc=1, device_id=device, device_id_type=MESH)

        def vector(n):
            return vectors_ref[n : n + 1, :]

        for chip in range(4):
            context[:, chip * width : (chip + 1) * width] = mixed_ref[chip].reshape(tokens, width)
        output_load.wait()
        branch = jnp.dot(context[...], output_w[...], preferred_element_type=F32) + vector(4)
        normed, first_inverse = normed_rows(
            inputs_ref[...].reshape(tokens, model_width) + branch
        )
        first_normed[...] = normed
        first = normed * vector(0) + vector(1)
        rows_out[...] = first.reshape(2, count, model_width)
        first_low[...] = first.astype(BF16)
        feed[...] = jnp.broadcast_to(vector(7), feed.shape)

        def forward(z, _):
            at = pl.ds(pl.multiple_of(z * block, block), block)
            expand_load(z).wait()
            before = (
                jnp.dot(first_low[...], expand_w[z], preferred_element_type=F32)
                + bias_ref[:, at]
            )
            half = 0.5 * (1.0 + lax.erf(before * HALF_ROOT))
            low = (before * half).astype(BF16)
            hidden_low[z] = low.reshape(2, count, block)
            slope[z] = half + before * jnp.exp(-0.5 * before * before) * INV_ROOT_TAU
            reduce_load(z).wait()
            feed[...] += jnp.dot(low, reduce_w[z], preferred_element_type=F32)
            return 0

        lax.fori_loop(0, nb, forward, 0)
        normed, inverse = normed_rows(
            rows_out[...].reshape(tokens, model_width) + feed[...]
        )
        result_out[...] = (normed * vector(5) + vector(6)).reshape(2, count, model_width)

        places = pos.s * count + lax.broadcasted_iota(jnp.int32, (count, 1), 0)
        grad_res = jnp.concatenate(
            [jnp.where(places < lengths_ref[j], cotangent_ref[j], 0.0) for j in range(2)]
        )
        grad_second, gain, shift = norm_back(grad_res, normed, inverse, vector(5))
        grad_low[...] = grad_second.astype(BF16)
        grad_vectors[...] = jnp.zeros_like(grad_vectors)
        grad_vectors[5:6, :] = gain[None]
        grad_vectors[6:7, :] = shift[None]
        grad_vectors[7:8, :] = jnp.sum(grad_low[...].astype(F32), axis=0, keepdims=True)
        feed[...] = grad_second

        def backward(i, _):
            z = pos.up(turn(i))
            at = pl.ds(pl.multiple_of(z * block, block), block)
            for n in range(2):
                cut = slice(n * (block // 2), (n + 1) * (block // 2))
                reduces.partial[z, 2 * n : 2 * n + 2] = (
                    transposed_dot(
                        hidden_low[z, :, :, cut].reshape(tokens, block // 2), grad_low[...]
                    )
                    .reshape(2, 2, per, model_width)
                    .astype(BF16)
                )
            reduces.begin(turn(i))
            low = (dot_transposed(grad_low[...], reduce_w[z]) * slope[z]).astype(BF16)
            grad_bias[:, at] = jnp.sum(low.astype(F32), axis=0, keepdims=True)
            for n in range(2):
                cut = slice(n * (model_width // 2), (n + 1) * (model_width // 2))
                expands.partial[n * nb // 2 : (n + 1) * nb // 2, :, :, :, at] = (
                    transposed_dot(first_low[:, cut], low)
                    .reshape(nb // 2, 4, 2, shard, block)
                    .astype(BF16)
                )
            feed[...] += dot_transposed(low, expand_w[z])
            reduces.first(turn(i))
            return 0

        pl.semaphore_wait(barrier, len(partners))
        lax.fori_loop(0, nb, backward, 0)
        for k in range(nb):
            expands.begin(turn(k))
        grads, gain, shift = norm_back(feed[...], first_normed[...], first_inverse, vector(0))
        rows_out[...] = grads.reshape(2, count, model_width)
        low = grads.astype(BF16)
        grad_low[...] = low
        grad_vectors[0:1, :] = gain[None]
        grad_vectors[1:2, :] = shift[None]
        grad_vectors[4:5, :] = jnp.sum(low.astype(F32), axis=0, keepdims=True)
        low = dot_transposed(low, output_w[...]).astype(BF16)
        for chip in range(4):
            parts[chip] = low[:, chip * width : (chip + 1) * width].reshape(2, count, width)
        mixing.start()
        for n in range(2):
            cut = slice(n * (model_width // 2), (n + 1) * (model_width // 2))
            outputs.partial[n * nb // 2 : (n + 1) * nb // 2] = (
                transposed_dot(context[:, cut], grad_low[...])
                .reshape(nb // 2, 4, 2, shard, model_width)
                .astype(BF16)
            )
        for owner in range(owners):
            here = (owner // 8, owner % 8 // 2, owner % 2)
            smalls.partial[here] = jnp.concatenate(
                [
                    jnp.pad(
                        grad_vectors[:, owner * vec : (owner + 1) * vec], ((0, 0), (0, 128 - vec))
                    ),
                    jnp.broadcast_to(
                        jnp.pad(
                            grad_bias[:, owner * per : (owner + 1) * per], ((0, 0), (0, 128 - per))
                        ),
                        (8, 128),
                    ),
                ]
            )
        for k in range(nb):
            outputs.begin(turn(k))
            smalls.begin(turn(k))

        grad_key[...] = jnp.zeros_like(grad_key)
        grad_value[...] = jnp.zeros_like(grad_value)
        for copy in later:
            copy.wait()
        back = attend_back_block(
            lengths_ref[pos.c], qkv_ref, log_ref, grad_context, grad_qkv, grad_key, grad_value,
            heads, count,
        )

        def middle(i, _):
            k = turn(i)
            reduces.second(k)
            expands.first(k)
            guarded(i > 0, lambda: reduces.third(turn(i - 1), reduce_out))
            guarded(i == 0, mixing.arrive)
            back(i)
            return 0

        lax.fori_loop(0, nb, middle, 0)

        def late(i, _):
            k = turn(i)
            expands.second(k)
            outputs.first(k)
            smalls.first(k)
            return 0

        lax.fori_loop(0, 2, late, 0)
        grad_qkv[:, width : 2 * width] = (grad_key[...] * SCORE_SCALE).astype(BF16)
        grad_qkv[:, 2 * width :] = grad_value[...].astype(BF16)

        def spread(i, _):
            at = pl.ds(pl.multiple_of(i * tokens, tokens), tokens)
            row_sums.mine[i] = (
                dot_transposed(grad_qkv[at, :], weight_ref[...])
                .astype(BF16)
                .reshape(2, count, model_width)
            )
            return 0

        lax.fori_loop(0, 4, spread, 0)
        row_sums.first()
        for z in range(nb):
            grad_joint = transposed_dot(
                rows_ref[:, :, :, z * 8 * shard : (z + 1) * 8 * shard].reshape(size, 8 * shard),
                grad_qkv[...],
            )
            joints.partial[z, :, :, :, : 3 * width] = grad_joint.reshape(
                4, 2, shard, 3 * width
            ).astype(BF16)
        sums = jnp.sum(grad_qkv[...].astype(F32), axis=0, keepdims=True)
        joints.partial[:, :, :, :, 3 * width :] = jnp.zeros((nb, 4, 2, shard, 64), BF16)
        for s in range(8):
            at = slice(s * vec, (s + 1) * vec)
            value = jnp.concatenate([sums[:, :width][:, at], sums[:, 2 * width :][:, at]])
            joints.partial[pos.p, s // 2, s % 2, :, 3 * width :] = jnp.pad(
                value, ((0, shard - 2), (0, 64 - vec))
            ).astype(BF16)
        joints.begin()
        lax.fori_loop(2, nb, late, 0)
        joints.first()

        def summed(i, _):
            expands.third(turn(i), expand_out)
            return 0

        lax.fori_loop(0, nb - 1, summed, 0)
        reduces.third(turn(nb - 1), reduce_out)
        reduces.last(reduce_out)
        reduces.drain()
        row_sums.second()

        def final(i, _):
            k = turn(i)
            outputs.second(k)
            smalls.second(k)
            return 0

        lax.fori_loop(0, nb, final, 0)
        expands.third(turn(nb - 1), expand_out)
        joints.second()
        row_sums.third()
        expands.last(expand_out)
        expands.drain()
        mixing.drain()

        def end(i, _):
            k = turn(i)
            outputs.third(k, output_out)
            smalls.third(k, small_total)
            return 0

        lax.fori_loop(0, nb, end, 0)
        extra = joints.last(joint_out, vec)
        row_sums.last()
        for scatter, out in ((outputs, output_out), (smalls, small_total)):
            scatter.last(out)
            scatter.drain()
        lines = lax.broadcasted_iota(jnp.int32, (8, vec), 0)
        value = jnp.where(lines == 2, extra[0:1], small_total[:8, :vec])
        vectors_out[...] = jnp.where(lines == 3, extra[1:2], value)
        hidden_out[...] = small_total[8:9, :per]

    def vmem(shape, dtype):
        return pltpu.VMEM(shape, dtype)

    scratch = [
        vmem((model_width, model_width), BF16),
        vmem((nb, model_width, block), BF16),
        vmem((nb, block, model_width), BF16),
        vmem(rows.shape, BF16),
        vmem(weight.shape, BF16),
        vmem(qkv.shape, BF16),
        vmem(logs.shape, F32),
        DMA((2 * nb + 5,)),
        vmem((tokens, model_width), BF16),
        vmem((tokens, model_width), F32),
        vmem((tokens, model_width), BF16),
        vmem((nb, 2, count, block), BF16),
        vmem((nb, tokens, block), F32),
        vmem((tokens, model_width), F32),
        vmem((tokens, model_width), BF16),
        vmem((8, model_width), F32),
        vmem((1, hidden), F32),
        vmem((4, 2, count, width), BF16),
        vmem((16, 128), F32),
        vmem((4, 2, count, width), BF16),
        vmem((size, 3 * width), BF16),
        vmem((size, width), F32),
        vmem((size, width), F32),
    ]
    scratch += ContextExchange.scratch() + RowScatter.scratch(count, model_width)
    scratch += JointScatter.scratch(nb, joint_shape) + JointScatter.sem_scratch(nb)
    for shape, dtype in zip(shapes, dtypes):
        scratch += Scatter.scratch(nb, shape, dtype, halves_of(shape)) + Scatter.sem_scratch(nb)
    return pl.pallas_call(
        body,
        out_shape=tuple(
            jax.ShapeDtypeStruct(shape, F32)
            for shape in (
                inputs.shape,
                inputs.shape,
                (shard, 3 * model_width),
                (8, vec),
                (1, per),
                shapes[1],
                shapes[2],
                shapes[3],
            )
        ),
        in_specs=[SM] + [VM] * 5 + [ANY] * 7,
        out_specs=(VM,) * 8,
        scratch_shapes=scratch,
        name="feed_and_back",
        compiler_params=pltpu.CompilerParams(
            collective_id=4, has_side_effects=True, vmem_limit_bytes=VMEM_LIMIT
        ),
    )(
        lengths, inputs, cotangent, mixed, vectors, hidden_bias,
        output_weight, expand_weight, reduce_weight, rows, weight, qkv, logs,
    )


def hand_over(*arrays):
    count = len(arrays)

    def body(*refs):
        came, out, held = refs[:count], refs[count : 2 * count], refs[2 * count : 3 * count]
        sems = refs[3 * count]
        loads = [pltpu.make_async_copy(came[n], held[n], sems.at[0, n]) for n in range(count)]
        stores = [pltpu.make_async_copy(held[n], out[n], sems.at[1, n]) for n in range(count)]
        for copy in loads:
            copy.start()
        for load, store in zip(loads, stores):
            load.wait()
            store.start()
        for copy in stores:
            copy.wait()

    return pl.pallas_call(
        body,
        out_shape=tuple(jax.ShapeDtypeStruct(a.shape, a.dtype) for a in arrays),
        in_specs=[ANY] * count,
        out_specs=(ANY,) * count,
        scratch_shapes=[pltpu.VMEM(a.shape, a.dtype) for a in arrays] + [DMA((2, count))],
        name="hand_over",
        compiler_params=pltpu.CompilerParams(vmem_limit_bytes=VMEM_LIMIT),
    )(*arrays)


def plane_on_device(
    inputs,
    cotangent,
    lengths,
    joint_weight,
    output_weight,
    vectors,
    expand_weight,
    expand_bias,
    reduce_weight,
):
    nb = lax.axis_size("batch")
    _, _, model_width = inputs.shape
    hidden_width = expand_weight.shape[1]
    heads = model_width // (4 * HEAD_DIM)
    per = expand_bias.shape[0]
    (
        vector_rows, full_bias, rows_all, joint_all, qkv, logs,
        mixed, output_all, expand_all, reduce_all,
    ) = gather_attend(
        lengths,
        inputs,
        joint_weight,
        vectors,
        expand_bias.reshape(1, per),
        output_weight,
        expand_weight,
        reduce_weight,
        nb,
        heads,
    )
    full_output = output_all.reshape(model_width, model_width)
    full_expand = expand_all.reshape(model_width, hidden_width)
    full_reduce = reduce_all.reshape(hidden_width, model_width)

    result, grad_inputs, joint_sum, vectors_sum, bias_sum, output_sum, expand_sum, reduce_sum = (
        feed_and_back(
            lengths,
            inputs,
            cotangent,
            mixed,
            vector_rows,
            full_bias,
            full_output,
            full_expand,
            full_reduce,
            rows_all,
            joint_all,
            qkv,
            logs,
            nb,
            heads,
        )
    )
    (
        result, grad_inputs, joint_sum, output_sum, vectors_sum, expand_sum, bias_sum, reduce_sum,
    ) = hand_over(
        result, grad_inputs, joint_sum, output_sum, vectors_sum, expand_sum, bias_sum, reduce_sum
    )
    return (
        result,
        grad_inputs,
        joint_sum,
        output_sum,
        vectors_sum,
        expand_sum,
        bias_sum.reshape(per),
        reduce_sum,
    )


def plane_fits(mesh, inputs, expand_bias, expand_weight):
    return (
        mesh.shape["seq"] == 8
        and mesh.shape["batch"] == 4
        and inputs[0] == 2 * mesh.shape["batch"]
        and HEADS % 4 == 0
        and inputs[2] == HEADS * HEAD_DIM
        and inputs[1] % (8 * 16) == 0
        and inputs[2] % 256 == 0
        and expand_weight[0] % (8 * 32) == 0
        and expand_weight[1] % (16 * 32) == 0
        and expand_bias[0] <= 128 * 32
        and expand_weight[1] == 4 * inputs[2]
    )


def solution(mesh):
    def program(*args):
        fits = plane_fits(mesh, args[0].shape, args[7].shape, args[6].shape)
        return jax.shard_map(
            plane_on_device if fits else general_on_device,
            mesh=mesh,
            in_specs=(
                P("batch", "seq", None),
                P("batch", "seq", None),
                P("batch"),
                P(("batch", "seq"), None),
                P(("batch", "seq"), None),
                P(None, ("batch", "seq")),
                P(("batch", "seq"), None),
                P(("batch", "seq")),
                P(("batch", "seq"), None),
            ),
            out_specs=(
                P("batch", "seq", None),
                P("batch", "seq", None),
                P(("batch", "seq"), None),
                P(("batch", "seq"), None),
                P(None, ("batch", "seq")),
                P(("batch", "seq"), None),
                P(("batch", "seq")),
                P(("batch", "seq"), None),
            ),
            check_vma=False,
        )(*args)

    return program
```

```python
import functools
import math

import jax
import jax.numpy as jnp
from jax import lax
from jax.experimental import pallas as pl
from jax.experimental.pallas import tpu as pltpu
from jax.sharding import PartitionSpec as P

HEADS = 12
HEAD_DIM = 64


EPSILON = 1e-12
SCORE_SCALE = 0.125
NEG_FILL = -1e30
HALF_ROOT = 0.7071067811865476
INV_ROOT_TAU = 0.3989422804014327
block_limit = 256


def layer_norm(residual, norm_gain, norm_shift):
    centered = residual - jnp.mean(residual, axis=-1, keepdims=True)
    inverse = lax.rsqrt(jnp.mean(centered * centered, axis=-1, keepdims=True) + EPSILON)
    normed = centered * inverse
    return (normed * norm_gain + norm_shift, normed, inverse)


def norm_back(grad_out, normed, inverse, norm_gain):
    grad_normed = grad_out * norm_gain
    mean_grad = jnp.mean(grad_normed, axis=-1, keepdims=True)
    mean_proj = jnp.mean(grad_normed * normed, axis=-1, keepdims=True)
    grad_in = inverse * (grad_normed - mean_grad - normed * mean_proj)
    return (grad_in, jnp.sum(grad_out * normed, axis=0), jnp.sum(grad_out, axis=0))


def gelu_value(before_gelu):
    return 0.5 * before_gelu * (1.0 + lax.erf(before_gelu * HALF_ROOT))


def gelu_slope(before_gelu):
    return (
        0.5 * (1.0 + lax.erf(before_gelu * HALF_ROOT))
        + before_gelu * jnp.exp(-0.5 * before_gelu * before_gelu) * INV_ROOT_TAU
    )


def over_blocks(piece_rows, block_fn, carried):
    block_size = math.gcd(piece_rows, block_limit)

    def run_block(block_index, current):
        return block_fn(current, block_index * block_size, block_size)

    return lax.fori_loop(0, piece_rows // block_size, run_block, carried)


def head_scores(left_heads, right_heads, right_places, lengths):
    scores = (
        jnp.einsum("sqhd,skhd->shqk", left_heads, right_heads, preferred_element_type=jnp.float32)
        * SCORE_SCALE
    )
    allowed = right_places[None, :] < lengths[:, None]
    return jnp.where(allowed[:, None, None, :], scores, NEG_FILL)


def cut_heads(gathered_piece, offset, block_size, head_count):
    sliced = lax.dynamic_slice_in_dim(gathered_piece, offset, block_size, 1)
    return sliced.reshape(sliced.shape[0], block_size, head_count, -1)


def gather_attention(joint_weight, output_weight, vectors):
    return (
        lax.all_gather(joint_weight, ("batch", "seq"), axis=0, tiled=True),
        lax.all_gather(output_weight, ("batch", "seq"), axis=0, tiled=True),
        lax.all_gather(vectors, ("batch", "seq"), axis=1, tiled=True),
    )


def gather_feed(expand_weight, reduce_weight, expand_bias):
    return (
        lax.all_gather(expand_weight, ("batch", "seq"), axis=0, tiled=True),
        lax.all_gather(reduce_weight, ("batch", "seq"), axis=0, tiled=True),
        lax.all_gather(expand_bias, ("batch", "seq"), axis=0, tiled=True),
    )


def general_on_device(
    inputs,
    cotangent,
    lengths,
    joint_weight,
    output_weight,
    vectors,
    expand_weight,
    expand_bias,
    reduce_weight,
):
    seq_count, row_count, model_width = inputs.shape
    head_count = HEADS
    head_size = HEAD_DIM
    tokens = seq_count * row_count
    head_shape = (seq_count, row_count, head_count, head_size)
    own_places = lax.axis_index("seq") * row_count + jnp.arange(row_count, dtype=jnp.int32)
    row_valid = own_places[None, :] < lengths[:, None]
    row_mask = row_valid.reshape(tokens, 1).astype(jnp.float32)
    full_joint, full_output, full_vectors = gather_attention(joint_weight, output_weight, vectors)
    vector_rows = full_vectors.astype(jnp.float32)
    flat_inputs = inputs.reshape(tokens, model_width)
    input_low = flat_inputs.astype(jnp.bfloat16)
    projected = jnp.dot(input_low, full_joint, preferred_element_type=jnp.float32)
    query_low = (projected[:, :model_width] + vector_rows[2]).astype(jnp.bfloat16)
    key_low = projected[:, model_width : 2 * model_width].astype(jnp.bfloat16)
    value_low = (projected[:, 2 * model_width :] + vector_rows[3]).astype(jnp.bfloat16)
    query_heads = query_low.reshape(head_shape)
    key_rows = key_low.reshape(seq_count, row_count, model_width)
    value_rows = value_low.reshape(seq_count, row_count, model_width)
    start_state = (
        jnp.full((seq_count, head_count, row_count), NEG_FILL, jnp.float32),
        jnp.zeros((seq_count, head_count, row_count), jnp.float32),
        jnp.zeros(head_shape, jnp.float32),
    )
    key_piece = lax.all_gather(key_rows, "seq", axis=1, tiled=True)
    value_piece = lax.all_gather(value_rows, "seq", axis=1, tiled=True)

    def forward_score_block(current, offset, block_size):
        running_max, running_sum, summed = current
        key_heads = cut_heads(key_piece, offset, block_size, head_count)
        value_heads = cut_heads(value_piece, offset, block_size, head_count)
        key_places = offset + jnp.arange(block_size, dtype=jnp.int32)
        scores = head_scores(query_heads, key_heads, key_places, lengths)
        new_max = jnp.maximum(running_max, jnp.max(scores, axis=-1))
        factor = jnp.exp(running_max - new_max)
        exp_scores = jnp.exp(scores - new_max[..., None])
        running_sum = running_sum * factor + jnp.sum(exp_scores, axis=-1)
        update = jnp.einsum(
            "shqk,skhd->sqhd",
            exp_scores.astype(jnp.bfloat16),
            value_heads,
            preferred_element_type=jnp.float32,
        )
        summed = summed * jnp.transpose(factor, (0, 2, 1))[..., None] + update
        return (new_max, running_sum, summed)

    running_max, running_sum, summed = over_blocks(
        key_piece.shape[1], forward_score_block, start_state
    )
    attended = summed / jnp.transpose(running_sum, (0, 2, 1))[..., None]
    log_total = jnp.transpose(running_max + jnp.log(running_sum), (0, 2, 1))
    context_low = attended.reshape(tokens, model_width).astype(jnp.bfloat16)
    branch = jnp.dot(context_low, full_output, preferred_element_type=jnp.float32) + vector_rows[4]
    first, first_normed, first_inverse = layer_norm(
        flat_inputs + branch, vector_rows[0], vector_rows[1]
    )
    first_low = first.astype(jnp.bfloat16)
    full_expand, full_reduce, full_bias = gather_feed(expand_weight, reduce_weight, expand_bias)
    before_gelu = jnp.dot(
        first_low, full_expand, preferred_element_type=jnp.float32
    ) + full_bias.astype(jnp.float32)
    hidden_low = gelu_value(before_gelu).astype(jnp.bfloat16)
    feed = jnp.dot(hidden_low, full_reduce, preferred_element_type=jnp.float32) + vector_rows[7]
    result, second_normed, second_inverse = layer_norm(first + feed, vector_rows[5], vector_rows[6])
    full_expand, full_reduce, full_bias = gather_feed(expand_weight, reduce_weight, expand_bias)
    full_joint, full_output, full_vectors = gather_attention(joint_weight, output_weight, vectors)
    grad_res = cotangent.reshape(tokens, model_width) * row_mask
    grad_second, grad_gain_two, grad_shift_two = norm_back(
        grad_res, second_normed, second_inverse, vector_rows[5]
    )
    grad_feed_low = grad_second.astype(jnp.bfloat16)
    grad_reduce_local = jnp.dot(hidden_low.T, grad_feed_low, preferred_element_type=jnp.float32)
    grad_hidden = jnp.dot(
        grad_feed_low, full_reduce.T, preferred_element_type=jnp.float32
    ) * gelu_slope(before_gelu)
    grad_hidden_low = grad_hidden.astype(jnp.bfloat16)
    grad_expand_local = jnp.dot(first_low.T, grad_hidden_low, preferred_element_type=jnp.float32)
    grad_bias_local = jnp.sum(grad_hidden_low.astype(jnp.float32), axis=0)
    grad_first = grad_second + jnp.dot(
        grad_hidden_low, full_expand.T, preferred_element_type=jnp.float32
    )
    grad_resid, grad_gain_one, grad_shift_one = norm_back(
        grad_first, first_normed, first_inverse, vector_rows[0]
    )
    grad_branch_low = grad_resid.astype(jnp.bfloat16)
    grad_output_local = jnp.dot(context_low.T, grad_branch_low, preferred_element_type=jnp.float32)
    grad_context_low = jnp.dot(
        grad_branch_low, full_output.T, preferred_element_type=jnp.float32
    ).astype(jnp.bfloat16)
    grad_context_heads = grad_context_low.reshape(head_shape)
    row_delta = jnp.sum(grad_context_heads.astype(jnp.float32) * attended, axis=-1)
    log_heads = jnp.transpose(log_total, (0, 2, 1))
    delta_heads = jnp.transpose(row_delta, (0, 2, 1))
    query_key_piece = lax.all_gather(key_rows, "seq", axis=1, tiled=True)
    query_value_piece = lax.all_gather(value_rows, "seq", axis=1, tiled=True)

    def query_score_block(current, offset, block_size):
        key_heads = cut_heads(query_key_piece, offset, block_size, head_count)
        value_heads = cut_heads(query_value_piece, offset, block_size, head_count)
        key_places = offset + jnp.arange(block_size, dtype=jnp.int32)
        scores = head_scores(query_heads, key_heads, key_places, lengths)
        softmax_rows = jnp.exp(scores - log_heads[..., None])
        grad_probs = jnp.einsum(
            "sqhd,skhd->shqk", grad_context_heads, value_heads, preferred_element_type=jnp.float32
        )
        grad_scores = (softmax_rows * (grad_probs - delta_heads[..., None])).astype(jnp.bfloat16)
        return (
            current
            + jnp.einsum(
                "shqk,skhd->sqhd", grad_scores, key_heads, preferred_element_type=jnp.float32
            )
            * SCORE_SCALE
        )

    grad_query = over_blocks(
        query_key_piece.shape[1], query_score_block, jnp.zeros(head_shape, jnp.float32)
    )
    own_keys = key_low.reshape(head_shape)
    own_values = value_low.reshape(head_shape)
    query_rows = query_low.reshape(seq_count, row_count, model_width)
    grad_context_rows = grad_context_low.reshape(seq_count, row_count, model_width)
    zero_heads = jnp.zeros(head_shape, jnp.float32)
    query_piece = lax.all_gather(query_rows.astype(jnp.float32), "seq", axis=1, tiled=True).astype(
        jnp.bfloat16
    )
    grad_piece = lax.all_gather(
        grad_context_rows.astype(jnp.float32), "seq", axis=1, tiled=True
    ).astype(jnp.bfloat16)
    log_piece = lax.all_gather(log_total, "seq", axis=1, tiled=True)
    delta_piece = lax.all_gather(row_delta, "seq", axis=1, tiled=True)

    def key_score_block(current, offset, block_size):
        grad_key, grad_value = current
        query_block = cut_heads(query_piece, offset, block_size, head_count)
        grad_block = cut_heads(grad_piece, offset, block_size, head_count)
        log_block = jnp.transpose(
            lax.dynamic_slice_in_dim(log_piece, offset, block_size, 1), (0, 2, 1)
        )
        delta_block = jnp.transpose(
            lax.dynamic_slice_in_dim(delta_piece, offset, block_size, 1), (0, 2, 1)
        )
        scores = head_scores(query_block, own_keys, own_places, lengths)
        softmax_rows = jnp.exp(scores - log_block[..., None])
        grad_value = grad_value + jnp.einsum(
            "shqk,sqhd->skhd",
            softmax_rows.astype(jnp.bfloat16),
            grad_block,
            preferred_element_type=jnp.float32,
        )
        grad_probs = jnp.einsum(
            "sqhd,skhd->shqk", grad_block, own_values, preferred_element_type=jnp.float32
        )
        grad_scores = (softmax_rows * (grad_probs - delta_block[..., None])).astype(jnp.bfloat16)
        grad_key = (
            grad_key
            + jnp.einsum(
                "shqk,sqhd->skhd", grad_scores, query_block, preferred_element_type=jnp.float32
            )
            * SCORE_SCALE
        )
        return (grad_key, grad_value)

    grad_key, grad_value = over_blocks(
        query_piece.shape[1], key_score_block, (zero_heads, zero_heads)
    )
    grad_query_low = grad_query.reshape(tokens, model_width).astype(jnp.bfloat16)
    grad_key_low = grad_key.reshape(tokens, model_width).astype(jnp.bfloat16)
    grad_value_low = grad_value.reshape(tokens, model_width).astype(jnp.bfloat16)
    grad_projected = jnp.concatenate([grad_query_low, grad_key_low, grad_value_low], axis=1)
    grad_joint_local = jnp.dot(input_low.T, grad_projected, preferred_element_type=jnp.float32)
    grad_inputs = grad_resid + jnp.dot(
        grad_projected, full_joint.T, preferred_element_type=jnp.float32
    )
    grad_vector_local = jnp.stack(
        [
            grad_gain_one,
            grad_shift_one,
            jnp.sum(grad_query_low.astype(jnp.float32), axis=0),
            jnp.sum(grad_value_low.astype(jnp.float32), axis=0),
            jnp.sum(grad_branch_low.astype(jnp.float32), axis=0),
            grad_gain_two,
            grad_shift_two,
            jnp.sum(grad_feed_low.astype(jnp.float32), axis=0),
        ],
        axis=0,
    )
    every_grad = (
        lax.psum_scatter(grad_joint_local, ("batch", "seq"), scatter_dimension=0, tiled=True),
        lax.psum_scatter(grad_output_local, ("batch", "seq"), scatter_dimension=0, tiled=True),
        lax.psum_scatter(grad_vector_local, ("batch", "seq"), scatter_dimension=1, tiled=True),
        lax.psum_scatter(grad_expand_local, ("batch", "seq"), scatter_dimension=0, tiled=True),
        lax.psum_scatter(grad_reduce_local, ("batch", "seq"), scatter_dimension=0, tiled=True),
        lax.psum_scatter(grad_bias_local, ("batch", "seq"), scatter_dimension=0, tiled=True),
    )
    summed_grads = (
        every_grad[0],
        every_grad[1],
        every_grad[2],
        every_grad[3],
        every_grad[5],
        every_grad[4],
    )
    return (
        result.reshape(seq_count, row_count, model_width),
        grad_inputs.reshape(seq_count, row_count, model_width),
        summed_grads[0],
        summed_grads[1],
        summed_grads[2],
        summed_grads[3],
        summed_grads[4],
        summed_grads[5],
    )


MESH = pl.DeviceIdType.MESH
ANY = pl.BlockSpec(memory_space=pl.ANY)
VM = pl.BlockSpec(memory_space=pltpu.VMEM)
SM = pl.BlockSpec(memory_space=pltpu.SMEM)
DMA = pltpu.SemaphoreType.DMA
VMEM_LIMIT = 60 << 20
F32 = jnp.float32
BF16 = jnp.bfloat16


def send(src, dst, send_sem, recv_sem, device):
    return pltpu.make_async_remote_copy(
        src_ref=src,
        dst_ref=dst,
        send_sem=send_sem,
        recv_sem=recv_sem,
        device_id=device,
        device_id_type=MESH,
    )


class Place:
    def __init__(self, nb):
        self.nb = nb
        self.b = lax.axis_index("batch")
        self.s = lax.axis_index("seq")
        self.c = self.s % 2
        self.p = self.s // 2
        x, y = self.p % 2, self.p // 2
        self.px = 2 * y + (1 - x)
        self.py = 2 * (1 - y) + x
        self.pd = 2 * (1 - y) + (1 - x)
        self.sib = (self.b, 2 * self.p + 1 - self.c)
        self.xn = (self.b, 2 * self.px + self.c)
        self.yn = (self.b, 2 * self.py + self.c)

    def chip(self, step):
        return (self.p, self.px, self.py, self.pd)[step]

    def up(self, step):
        return (self.b + step) % self.nb

    def down(self, step):
        return (self.b + self.nb - step) % self.nb


def greet_near(pos):
    barrier = pltpu.get_barrier_semaphore()

    def signal(device):
        pl.semaphore_signal(barrier, inc=1, device_id=device, device_id_type=MESH)

    for device in plane_others(pos):
        signal(device)
    last = pos.nb - 1
    guarded(pos.b < last, lambda: signal(((pos.b + 1) % pos.nb, pos.s)))
    guarded(pos.b > 0, lambda: signal(((pos.b + last) % pos.nb, pos.s)))


def meet_near(pos):
    beside = jnp.where(pos.b < pos.nb - 1, 1, 0) + jnp.where(pos.b > 0, 1, 0)
    pl.semaphore_wait(pltpu.get_barrier_semaphore(), 7 + beside)


def same_core(pos):
    return [
        (pos.up(d), 2 * pos.chip(k) + pos.c)
        for d in range(pos.nb)
        for k in range(4)
        if d or k
    ]


def plane_others(pos):
    return [
        (pos.b, 2 * pos.chip(k) + (pos.c if j == 0 else 1 - pos.c))
        for k in range(4)
        for j in range(2)
        if k or j
    ]


def guarded(condition, action):
    if isinstance(condition, bool):
        if condition:
            action()
    else:

        @pl.when(condition)
        def _():
            action()


class Chain:
    def __init__(self, pos, mine, spot, sems):
        self.pos, self.mine, self.spot = pos, mine, spot
        self.up, self.down = sems

    @staticmethod
    def scratch(nb):
        return [DMA((2, nb)), DMA((2, nb))]

    def copy(self, src, z, sems, hop, there):
        pos = self.pos
        return send(src, self.spot(z), sems.at[0, hop], sems.at[1, hop], (there, pos.s))

    def moves(self, hop):
        pos = self.pos
        last = pos.nb - 1
        low, high = (pos.b - hop + 1 + pos.nb) % pos.nb, (pos.b + hop - 1) % pos.nb
        above, below = (pos.b + 1) % pos.nb, (pos.b + last) % pos.nb
        own = isinstance(hop, int) and hop == 1
        return (
            (
                (pos.b >= hop - 1) & (pos.b < last),
                self.copy(self.mine if own else self.spot(low), low, self.up, hop, above),
            ),
            (
                (pos.b + hop - 1 < pos.nb) & (pos.b > 0),
                self.copy(self.mine if own else self.spot(high), high, self.down, hop, below),
            ),
        )

    def start(self, hop=1):
        for made, copy in self.moves(hop):
            guarded(made, copy.start)

    def hop(self, hop):
        pos = self.pos
        low, high = (pos.b - hop + pos.nb) % pos.nb, (pos.b + hop) % pos.nb
        for made, z, sems in (
            (pos.b >= hop, low, self.up),
            (pos.b + hop < pos.nb, high, self.down),
        ):
            guarded(made, self.copy(self.spot(z), z, sems, hop, pos.b).wait_recv)
        guarded(hop < pos.nb - 1, lambda: self.start(hop + 1))

    def drain(self):
        for hop in range(1, self.pos.nb):
            for made, copy in self.moves(hop):
                guarded(made, copy.wait_send)


class Gather:
    def __init__(self, pos, shard, out, halves, sems):
        self.pos, self.shard, self.out, self.halves = pos, shard, out, halves
        self.xs, self.ys, self.f0, self.f1, self.sb, self.local_sem = sems[:6]
        self.chain = Chain(pos, shard, lambda z: out.at[z, pos.p, pos.c], sems[6:8])
        self.across = Chain(
            pos, out.at[pos.b, pos.pd, pos.c], lambda z: out.at[z, pos.pd, pos.c], sems[8:]
        )

    @staticmethod
    def scratch(nb):
        return [DMA((2, nb))] * 2 + [DMA((2,))] * 2 + [DMA((2, nb + 3)), DMA] + Chain.scratch(nb) * 2

    def z(self, k):
        return jnp.where(k <= self.pos.b, self.pos.b - k, k)

    def own(self):
        pos = self.pos
        self.local = pltpu.make_async_copy(
            self.shard, self.out.at[pos.b, pos.p, pos.c], self.local_sem
        )
        self.local.start()

    def x_copy(self, k, src=None):
        pos = self.pos
        there = self.out.at[self.z(k), pos.p, pos.c]
        src = there if src is None else src
        return send(src, there, self.xs.at[0, k], self.xs.at[1, k], pos.xn)

    def y_copy(self, k, src=None):
        pos = self.pos
        there = self.out.at[self.z(k), pos.p, pos.c]
        src = there if src is None else src
        return send(src, there, self.ys.at[0, k], self.ys.at[1, k], pos.yn)

    def plane(self, k, src=None):
        self.x_copy(k, src).start()
        self.y_copy(k, src).start()

    def landed(self, sems, k, chip):
        pos = self.pos
        ref = self.out.at[self.z(k), chip, pos.c]
        send(ref, ref, sems.at[0, k], sems.at[1, k], pos.xn).wait_recv()

    def y_forward(self):
        pos = self.pos
        ref = self.out.at[pos.b, pos.px, pos.c].at[self.halves[0]]
        return send(ref, ref, self.f0.at[0], self.f0.at[1], pos.yn)

    def x_forward(self):
        pos = self.pos
        ref = self.out.at[pos.b, pos.py, pos.c].at[self.halves[1]]
        return send(ref, ref, self.f1.at[0], self.f1.at[1], pos.xn)

    def forward(self):
        pos = self.pos
        self.landed(self.xs, 0, pos.px)
        self.y_forward().start()
        self.landed(self.ys, 0, pos.py)
        if self.halves[1] is not None:
            self.x_forward().start()

    def cross(self):
        pos = self.pos
        across = self.out.at[pos.b, pos.pd, pos.c]
        for half, sems in zip(self.halves, (self.f0, self.f1)):
            if half is not None:
                ref = across.at[half]
                send(ref, ref, sems.at[0], sems.at[1], pos.xn).wait_recv()

    def beside(self, k):
        pos = self.pos
        self.landed(self.xs, k, pos.px)
        self.landed(self.ys, k, pos.py)

    def sibling_copy(self, k, core=None):
        pos = self.pos
        ref = self.out.at[self.z(k), :, pos.c if core is None else core]
        return send(ref, ref, self.sb.at[0, k], self.sb.at[1, k], pos.sib)

    def sibling(self, k):
        self.sibling_copy(k).start()

    def part_copy(self, n, core=None):
        pos = self.pos
        k = pos.nb - 1
        ref = self.out.at[self.z(k), pos.chip(n), pos.c if core is None else core]
        return send(ref, ref, self.sb.at[0, k + n], self.sb.at[1, k + n], pos.sib)

    def finish(self, k):
        self.sibling_copy(k, 1 - self.pos.c).wait_recv()
        self.x_copy(k).wait_send()
        self.y_copy(k).wait_send()
        self.sibling_copy(k).wait_send()

    def end(self):
        k = self.pos.nb - 1
        for n in range(4):
            self.part_copy(n, 1 - self.pos.c).wait_recv()
        for n in range(4):
            self.part_copy(n).wait_send()
        self.x_copy(k).wait_send()
        self.y_copy(k).wait_send()

    def drain(self):
        self.y_forward().wait_send()
        if self.halves[1] is not None:
            self.x_forward().wait_send()
        self.chain.drain()
        self.across.drain()


class InputExchange:
    def __init__(self, pos, rows, out, sems):
        self.pos, self.rows, self.out, self.sems = pos, rows, out, sems
        self.started = []

    @staticmethod
    def scratch():
        return [DMA((2, 2)), DMA((2, 2)), DMA((2, 2)), DMA((2,)), DMA]

    def go(self, copy):
        copy.start()
        self.started.append(copy)

    def start(self):
        pos, (xs, ys, _, sb, local) = self.pos, self.sems
        there = self.out.at[pos.p, pos.c]
        for sems, chip in ((xs, pos.px), (ys, pos.py)):
            for j in range(2):
                self.go(
                    send(
                        self.rows.at[j],
                        there,
                        sems.at[0, j],
                        sems.at[1, pos.c],
                        (pos.b, 2 * chip + j),
                    )
                )
        self.go(send(self.rows.at[1 - pos.c], there, sb.at[0], sb.at[1], pos.sib))
        self.local = pltpu.make_async_copy(self.rows.at[pos.c], there, local)
        self.local.start()

    def landed(self, sems, j, chip):
        ref = self.out.at[chip, j]
        send(ref, ref, sems.at[0, j], sems.at[1, j], self.pos.xn).wait_recv()

    def forward(self):
        pos, (xs, ys, fs, _, _) = self.pos, self.sems
        self.landed(xs, 0, pos.px)
        ref = self.out.at[pos.px, 0]
        self.go(send(ref, ref, fs.at[0, 0], fs.at[1, 0], pos.yn))
        self.landed(ys, 1, pos.py)
        ref = self.out.at[pos.py, 1]
        self.go(send(ref, ref, fs.at[0, 1], fs.at[1, 1], pos.xn))

    def finish(self):
        pos, (xs, ys, fs, sb, _) = self.pos, self.sems
        self.landed(xs, 1, pos.px)
        self.landed(ys, 0, pos.py)
        self.landed(fs, 0, pos.pd)
        self.landed(fs, 1, pos.pd)
        ref = self.out.at[pos.p, 1 - pos.c]
        send(ref, ref, sb.at[0], sb.at[1], pos.sib).wait_recv()
        self.local.wait()

    def drain(self):
        for copy in self.started:
            copy.wait_send()


class JointGather:
    def __init__(self, pos, parts, out, sems):
        self.pos, self.parts, self.out = pos, parts, out
        self.direct, self.sb, self.local_sem = sems[:3]
        self.chain = Chain(
            pos, out.at[pos.b, :, pos.c], lambda z: out.at[z, :, pos.c], sems[3:]
        )

    @staticmethod
    def scratch(nb):
        return [DMA((2, 4)), DMA((2,)), DMA] + Chain.scratch(nb)

    def start(self):
        pos = self.pos
        there = self.out.at[pos.b, pos.p, pos.c]
        self.started = [
            send(
                self.parts.at[pos.chip(k)],
                there,
                self.direct.at[0, k],
                self.direct.at[1, k],
                (pos.b, 2 * pos.chip(k) + pos.c),
            )
            for k in range(1, 4)
        ]
        for copy in self.started:
            copy.start()
        self.local = pltpu.make_async_copy(self.parts.at[pos.p], there, self.local_sem)
        self.local.start()

    def own(self):
        pos = self.pos
        for k in range(1, 4):
            ref = self.out.at[pos.b, pos.chip(k), pos.c]
            send(ref, ref, self.direct.at[0, k], self.direct.at[1, k], pos.sib).wait_recv()
        self.local.wait()
        self.chain.start()

    def sibling(self):
        pos = self.pos
        ref = self.out.at[:, :, pos.c]
        send(ref, ref, self.sb.at[0], self.sb.at[1], pos.sib).start()

    def finish(self):
        pos = self.pos
        ref = self.out.at[:, :, 1 - pos.c]
        send(ref, ref, self.sb.at[0], self.sb.at[1], pos.sib).wait_recv()

    def drain(self):
        for copy in self.started:
            copy.wait_send()
        ref = self.out.at[:, :, self.pos.c]
        send(ref, ref, self.sb.at[0], self.sb.at[1], self.pos.sib).wait_send()
        self.chain.drain()


class ContextExchange:
    def __init__(self, pos, parts, out, sems):
        self.pos, self.parts, self.out = pos, parts, out
        self.sems, self.local_sem = sems

    @staticmethod
    def scratch():
        return [DMA((2, 8)), DMA]

    def pairs(self):
        pos = self.pos
        for k in range(4):
            for j in range(2):
                if k or j:
                    yield 2 * k + j, pos.chip(k), pos.c if j == 0 else 1 - pos.c

    def copies(self):
        pos, sems = self.pos, self.sems
        there = self.out.at[pos.p, pos.c]
        return [
            send(
                self.parts.at[chip, core],
                there,
                sems.at[0, i],
                sems.at[1, i],
                (pos.b, 2 * chip + core),
            )
            for i, chip, core in self.pairs()
        ]

    def local(self):
        pos = self.pos
        return pltpu.make_async_copy(
            self.parts.at[pos.p, pos.c], self.out.at[pos.p, pos.c], self.local_sem
        )

    def start(self):
        for copy in self.copies():
            copy.start()
        self.local().start()

    def arrive(self):
        for i, chip, core in self.pairs():
            ref = self.out.at[chip, core]
            send(ref, ref, self.sems.at[0, i], self.sems.at[1, i], self.pos.sib).wait_recv()
        self.local().wait()

    def drain(self):
        for copy in self.copies():
            copy.wait_send()


def gather_attend(
    lengths, inputs, joint, vectors, hidden_bias, output, expand, reduce, nb, heads
):
    _, count, model_width = inputs.shape
    shard = vec = model_width // (8 * nb)
    per = reduce.shape[0]
    width = heads * HEAD_DIM
    size = 8 * count
    joint_shape = (4, shard, 3 * width + 64)
    small_shape = (16, 128)

    def body(
        lengths_ref, inputs_ref, joint_weight_ref, own_vectors_ref, own_bias_ref,
        output_ref, expand_ref, reduce_ref,
        vectors_out, hidden_out, rows_any, weight_any, qkv_any, log_any,
        context_out, output_out, expand_out, reduce_out,
        rows_out, weight_out, qkv_out, log_out, stores,
        joint_all, context, small_all, bias_ref, rows_ref, joint_ref, small_ref,
        *scratch,
    ):
        pos = Place(nb)
        scratch = list(scratch)

        def take(n):
            got = scratch[:n]
            del scratch[:n]
            return got

        exchange = InputExchange(pos, rows_ref, rows_out, take(5))
        joints = JointGather(pos, joint_ref, joint_all, take(5))
        mixing = ContextExchange(pos, context, context_out, take(2))
        outputs, expands, reduces, smalls = (
            Gather(pos, part, out, halves_of(part.shape), take(10))
            for part, out in (
                (output_ref, output_out),
                (expand_ref, expand_out),
                (reduce_ref, reduce_out),
                (small_ref, small_all),
            )
        )
        gathers = (expands, smalls, reduces, outputs)
        units = ((expands, smalls), (reduces,), (outputs,))

        saves = [
            pltpu.make_async_copy(src, dst, stores.at[n])
            for n, (src, dst) in enumerate(
                (
                    (rows_out, rows_any),
                    (weight_out, weight_any),
                    (qkv_out, qkv_any),
                    (log_out, log_any),
                )
            )
        ]

        def project(i, _):
            at = pl.ds(pl.multiple_of(i * 2 * count, 2 * count), 2 * count)
            qkv_out[at, :] = (
                jnp.dot(
                    rows_out[i].reshape(2 * count, model_width),
                    weight_out[...],
                    preferred_element_type=F32,
                )
                + bias_ref[...]
            ).astype(BF16)
            return 0

        def prepare():
            joints.finish()
            for z in range(nb):
                weight_out[z * 8 * shard : (z + 1) * 8 * shard, :] = joint_all[
                    z, :, :, :, : 3 * width
                ].reshape(8 * shard, 3 * width)
            bias_ref[...] = jnp.zeros_like(bias_ref)
            for s in range(8):
                spot = joint_all[pos.p, s // 2, s % 2, :, 3 * width :].astype(F32)
                bias_ref[:, s * vec : (s + 1) * vec] = spot[0:1, :vec]
                bias_ref[:, 2 * width + s * vec : 2 * width + (s + 1) * vec] = spot[1:2, :vec]
            lax.fori_loop(0, 4, project, 0)
            for copy in saves[:3]:
                copy.start()

        def hop(k):
            for gather in gathers:
                gather.chain.hop(k)

        def relay(k, some):
            for gather in some:
                gather.across.hop(k)

        def share(k):
            for gather in gathers:
                gather.beside(k)
                gather.sibling(k)

        attend = attend_block(lengths_ref[pos.c], qkv_out, log_out, context, heads, count)

        def spread(k):
            for gather in gathers:
                gather.plane(k)

        greet_near(pos)
        weight = joint_weight_ref[...]
        spot = jnp.pad(
            own_vectors_ref[2:4, :].astype(F32), ((0, shard - 2), (0, 64 - vec))
        ).astype(BF16)
        for chip in range(4):
            at = slice(chip * width, (chip + 1) * width)
            joint_ref[chip] = jnp.concatenate(
                [weight[:, n * model_width :][:, at] for n in range(3)] + [spot], axis=1
            )
        small_ref[...] = jnp.concatenate(
            [
                jnp.pad(own_vectors_ref[...].astype(F32), ((0, 0), (0, 128 - vec))),
                jnp.pad(own_bias_ref[...].astype(F32), ((0, 7), (0, 128 - per))),
            ]
        ).astype(BF16)
        meet_near(pos)
        joints.start()
        for gather in gathers:
            gather.own()
            gather.chain.start()
            gather.plane(0, gather.shard)
        rows_ref[...] = inputs_ref[...].astype(BF16)
        joints.own()
        for n, gather in enumerate(gathers):
            gather.forward()
            if n == 1:
                exchange.start()
        hop(1)
        joints.chain.hop(1)
        for gather in gathers:
            gather.local.wait()
            gather.cross()
            gather.sibling(0)
        joints.chain.hop(2)
        hop(2)
        for gather in gathers:
            gather.across.start()
        exchange.forward()
        spread(1)
        joints.chain.hop(3)
        joints.sibling()
        exchange.finish()
        spread(2)
        prepare()
        hop(3)
        spread(3)
        attend(0)
        relay(1, gathers)
        attend(1)
        attend(2)
        relay(2, gathers)
        attend(3)
        mixing.start()
        saves[3].start()
        share(1)
        relay(nb - 1, (smalls,))
        share(2)
        for gather in gathers:
            gather.beside(nb - 1)
            for n in range(3):
                gather.part_copy(n).start()
        smalls.part_copy(3).start()

        def finish(k, _):
            for gather in gathers:
                gather.finish(k)
            return 0

        lax.fori_loop(0, nb - 1, finish, 0)
        smalls.end()
        for owner in range(8 * nb):
            part = small_all[owner // 8, owner % 8 // 2, owner % 2].astype(F32)
            vectors_out[:, owner * vec : (owner + 1) * vec] = part[:8, :vec]
            hidden_out[:, owner * per : (owner + 1) * per] = part[8:9, :per]
        smalls.drain()
        exchange.drain()
        joints.drain()
        for gather in (expands, reduces, outputs):
            gather.across.hop(nb - 1)
            gather.part_copy(3).start()
        for gather in (expands, reduces, outputs):
            gather.drain()
        mixing.arrive()
        mixing.drain()
        for gather in (expands, reduces, outputs):
            gather.end()
        for copy in saves:
            copy.wait()

    kept = (
        ((4, 2) + inputs.shape[1:], BF16),
        ((model_width, 3 * width), BF16),
        ((size, 3 * width), BF16),
        ((size, 128), F32),
    )

    def shape(part):
        return jax.ShapeDtypeStruct((nb, 4, 2) + part.shape, part.dtype)

    return pl.pallas_call(
        body,
        out_shape=(
            jax.ShapeDtypeStruct((8, model_width), F32),
            jax.ShapeDtypeStruct((1, 8 * nb * per), F32),
            *(jax.ShapeDtypeStruct(shape, dtype) for shape, dtype in kept),
            jax.ShapeDtypeStruct((4, 2, count // 2, 2 * width), BF16),
            shape(output),
            shape(expand),
            shape(reduce),
        ),
        in_specs=[SM] + [VM] * 7,
        out_specs=(VM,) * 2 + (ANY,) * 8,
        scratch_shapes=[pltpu.VMEM(shape, dtype) for shape, dtype in kept]
        + [DMA((4,))]
        + [
            pltpu.VMEM((nb, 4, 2) + joint_shape[1:], BF16),
            pltpu.VMEM((4, 2, count // 2, 2 * width), BF16),
            pltpu.VMEM((nb, 4, 2) + small_shape, BF16),
            pltpu.VMEM((1, 3 * width), F32),
            pltpu.VMEM(inputs.shape, BF16),
            pltpu.VMEM(joint_shape, BF16),
            pltpu.VMEM(small_shape, BF16),
        ]
        + InputExchange.scratch()
        + JointGather.scratch(nb)
        + ContextExchange.scratch()
        + Gather.scratch(nb) * 4,
        name="gather_attend",
        compiler_params=pltpu.CompilerParams(
            collective_id=1, has_side_effects=True, vmem_limit_bytes=VMEM_LIMIT
        ),
    )(lengths, inputs, joint, vectors, hidden_bias, output, expand, reduce)


def halves_of(shape):
    rows, columns = shape
    if columns % 256 == 0 and columns >= 1024:
        return (
            (slice(None), pl.ds(0, columns // 2)),
            (slice(None), pl.ds(columns // 2, columns // 2)),
        )
    if rows % 32 == 0:
        return (
            (pl.ds(0, rows // 2), slice(None)),
            (pl.ds(rows // 2, rows // 2), slice(None)),
        )
    if columns % 256 == 0:
        return (
            (slice(None), pl.ds(0, columns // 2)),
            (slice(None), pl.ds(columns // 2, columns // 2)),
        )
    return ((slice(None), slice(None)), None)


def attend_block(limit, qkv_ref, log_ref, context_ref, heads, count):
    width = heads * HEAD_DIM
    size = 8 * count

    def part(n, _):
        at = pl.ds(pl.multiple_of(n * count, count), count)
        allowed = lax.broadcasted_iota(jnp.int32, (1, size), 1) < limit
        lanes = lax.broadcasted_iota(jnp.int32, (count, 128), 1)
        parts, logs = [], jnp.zeros((count, 128), F32)
        for h in range(heads):
            query = qkv_ref[at, h * HEAD_DIM : (h + 1) * HEAD_DIM]
            key = qkv_ref[:, width + h * HEAD_DIM : width + (h + 1) * HEAD_DIM]
            value = qkv_ref[:, 2 * width + h * HEAD_DIM : 2 * width + (h + 1) * HEAD_DIM]
            scores = (
                lax.dot_general(
                    query, key, (((1,), (1,)), ((), ())), preferred_element_type=F32
                )
                * SCORE_SCALE
            )
            scores = jnp.where(allowed, scores, NEG_FILL)
            top = jnp.max(scores, axis=-1, keepdims=True)
            exps = jnp.exp(scores - top)
            total = jnp.sum(exps, axis=-1, keepdims=True)
            mixed = jnp.dot(exps.astype(BF16), value, preferred_element_type=F32)
            parts.append(mixed / total)
            logs = jnp.where(lanes == h, top + jnp.log(total), logs)
        context_ref[n // 2, n % 2] = packed(jnp.concatenate(parts, axis=1)).astype(BF16)
        log_ref[at, :] = logs
        return 0

    def block(i):
        lax.fori_loop(2 * i, 2 * i + 2, part, 0)

    return block


def packed(rows):
    half = rows.shape[0] // 2
    return jnp.concatenate([rows[:half], rows[half:]], axis=1)


def unpacked(rows):
    half = rows.shape[1] // 2
    return jnp.concatenate([rows[:, :half], rows[:, half:]], axis=0)


def attend_back_block(limit, qkv_ref, log_ref, grad_ref, grad_qkv, grad_key, grad_value, heads, count):
    width = heads * HEAD_DIM
    size = 8 * count
    along_keys = (((1,), (1,)), ((), ()))
    along_rows = (((0,), (0,)), ((), ()))

    def part(n, _):
        at = pl.ds(pl.multiple_of(n * count, count), count)
        allowed = lax.broadcasted_iota(jnp.int32, (1, size), 1) < limit
        grads = unpacked(grad_ref[n // 2, n % 2])
        parts = []
        for h in range(heads):
            query = qkv_ref[at, h * HEAD_DIM : (h + 1) * HEAD_DIM]
            key = qkv_ref[:, width + h * HEAD_DIM : width + (h + 1) * HEAD_DIM]
            value = qkv_ref[:, 2 * width + h * HEAD_DIM : 2 * width + (h + 1) * HEAD_DIM]
            grad_out = grads[:, h * HEAD_DIM : (h + 1) * HEAD_DIM]
            scores = (
                lax.dot_general(query, key, along_keys, preferred_element_type=F32)
                * SCORE_SCALE
            )
            probs = jnp.where(allowed, jnp.exp(scores - log_ref[at, h : h + 1]), 0.0)
            grad_probs = lax.dot_general(
                grad_out, value, along_keys, preferred_element_type=F32
            )
            delta = jnp.sum(probs * grad_probs, axis=-1, keepdims=True)
            grad_scores = (probs * (grad_probs - delta)).astype(BF16)
            parts.append(
                jnp.dot(grad_scores, key, preferred_element_type=F32) * SCORE_SCALE
            )
            key_part = lax.dot_general(
                grad_scores, query, along_rows, preferred_element_type=F32
            )
            value_part = lax.dot_general(
                probs.astype(BF16), grad_out, along_rows, preferred_element_type=F32
            )
            own = slice(h * HEAD_DIM, (h + 1) * HEAD_DIM)
            grad_key[:, own] += key_part
            grad_value[:, own] += value_part
        grad_qkv[at, :width] = jnp.concatenate(parts, axis=1).astype(BF16)
        return 0

    def block(i):
        lax.fori_loop(2 * i, 2 * i + 2, part, 0)

    return block


class Scatter:
    def __init__(self, pos, halves, bufs, sems):
        self.pos, self.halves = pos, halves
        (self.partial, self.theirs, self.a0, self.a1, self.bx, self.by, self.z) = bufs
        (self.sb, self.s0, self.s1, self.dx, self.dy, self.cx, self.cy, self.zs) = sems

    @staticmethod
    def scratch(nb, shape, dtype, halves):
        first, second = half_shapes(shape, halves)
        return [
            pltpu.VMEM((nb, 4, 2) + shape, dtype),
            pltpu.VMEM((nb, 4) + shape, dtype),
            pltpu.VMEM((nb,) + first, dtype),
            pltpu.VMEM((nb,) + second, dtype),
            pltpu.VMEM((nb,) + shape, dtype),
            pltpu.VMEM((nb,) + shape, dtype),
            pltpu.VMEM((nb - 1,) + shape, dtype),
        ]

    @staticmethod
    def sem_scratch(nb):
        return [DMA((2, nb)) for _ in range(8)]

    def mine(self, k, chip):
        return self.partial.at[self.pos.up(k), chip, self.pos.c]

    def sibling_copy(self, k):
        pos = self.pos
        z = pos.up(k)
        return send(
            self.partial.at[z, :, 1 - pos.c],
            self.theirs.at[z],
            self.sb.at[0, k],
            self.sb.at[1, k],
            pos.sib,
        )

    def begin(self, k):
        self.sibling_copy(k).start()

    def copy(self, k, src, dst, sems, there):
        return send(src, dst, sems.at[0, k], sems.at[1, k], there)

    def first_copies(self, k):
        pos = self.pos
        h0, h1 = self.halves
        copies = [
            self.copy(k, self.mine(k, pos.pd).at[h0], self.a0.at[k], self.s0, pos.xn),
            self.copy(k, self.mine(k, pos.px).at[h0], self.bx.at[k].at[h0], self.dx, pos.xn),
        ]
        if h1 is not None:
            copies += [
                self.copy(k, self.mine(k, pos.pd).at[h1], self.a1.at[k], self.s1, pos.yn),
                self.copy(k, self.mine(k, pos.py).at[h1], self.by.at[k].at[h1], self.dy, pos.yn),
            ]
        return copies

    def second_copies(self, k):
        pos = self.pos
        h0, h1 = self.halves
        copies = [
            self.copy(k, self.mine(k, pos.py).at[h0], self.by.at[k].at[h0], self.cy, pos.yn)
        ]
        if h1 is not None:
            copies.append(
                self.copy(k, self.mine(k, pos.px).at[h1], self.bx.at[k].at[h1], self.cx, pos.xn)
            )
        return copies

    def first(self, k):
        pos = self.pos
        z = pos.up(k)
        self.sibling_copy(k).wait_recv()
        for j in range(4):
            chip = pos.chip(3 - j)
            self.partial[z, chip, pos.c] = (
                self.partial[z, chip, pos.c].astype(F32) + self.theirs[z, chip].astype(F32)
            ).astype(self.partial.dtype)
        for copy in self.first_copies(k):
            copy.start()

    def landed(self, ref, sems, k):
        send(ref, ref, sems.at[0, k], sems.at[1, k], self.pos.xn).wait_recv()

    def second(self, k):
        pos = self.pos
        h0, h1 = self.halves
        copies = self.second_copies(k)
        self.landed(self.a0.at[k], self.s0, k)
        ref = self.mine(k, pos.py)
        ref[h0] = (ref[h0].astype(F32) + self.a0[k].astype(F32)).astype(ref.dtype)
        copies[0].start()
        if h1 is not None:
            self.landed(self.a1.at[k], self.s1, k)
            ref = self.mine(k, pos.px)
            ref[h1] = (ref[h1].astype(F32) + self.a1[k].astype(F32)).astype(ref.dtype)
            copies[1].start()

    def z_copy(self, k):
        pos = self.pos
        return send(
            self.bx.at[k], self.z.at[k - 1], self.zs.at[0, k], self.zs.at[1, k], (pos.up(k), pos.s)
        )

    def third(self, k, total):
        pos = self.pos
        h0, h1 = self.halves
        self.landed(self.bx.at[k].at[h0], self.dx, k)
        self.landed(self.by.at[k].at[h0], self.cy, k)
        if h1 is not None:
            self.landed(self.by.at[k].at[h1], self.dy, k)
            self.landed(self.bx.at[k].at[h1], self.cx, k)
        total[...] = (
            self.mine(k, pos.p)[...].astype(F32)
            + self.bx[k].astype(F32)
            + self.by[k].astype(F32)
        )

        def on():
            self.bx[k] = total[...].astype(self.bx.dtype)
            self.z_copy(k).start()

        guarded(k != 0, on)

    def last(self, total):
        value = total[...]
        for k in range(1, self.pos.nb):
            self.landed(self.z.at[k - 1], self.zs, k)
            value = value + self.z[k - 1].astype(F32)
        total[...] = value

    def drain(self):
        def done(k, _):
            self.sibling_copy(k).wait_send()
            for copy in self.first_copies(k) + self.second_copies(k):
                copy.wait_send()
            guarded(k != 0, lambda: self.z_copy(k).wait_send())
            return 0

        lax.fori_loop(0, self.pos.nb, done, 0)


def half_shapes(shape, halves):
    def cut(half):
        return tuple(n if h == slice(None) else h.size for n, h in zip(shape, half))

    first = cut(halves[0])
    return first, (first if halves[1] is None else cut(halves[1]))


class RowScatter:
    def __init__(self, pos, out, bufs, sems):
        self.pos, self.out = pos, out
        self.mine, self.a0, self.a1, self.bx, self.by, self.far, self.near = bufs
        (self.sm,) = sems

    @staticmethod
    def scratch(rows, columns):
        return [
            pltpu.VMEM((rows, columns), BF16),
            pltpu.VMEM((rows, columns), BF16),
            pltpu.VMEM((2, rows, columns), BF16),
            pltpu.VMEM((2, rows, columns), BF16),
            pltpu.VMEM((rows, columns), F32),
            pltpu.VMEM((rows, columns), F32),
            DMA((2, 7)),
        ]

    def copy(self, i):
        pos, mine = self.pos, self.mine
        src, dst, there = (
            (mine.at[pos.pd, 0], self.a0, pos.xn),
            (mine.at[pos.pd, 1], self.a1, pos.yn),
            (mine.at[pos.px, 0], self.bx.at[0], pos.xn),
            (mine.at[pos.py, 1], self.by.at[1], pos.yn),
            (mine.at[pos.py, 0], self.by.at[0], pos.yn),
            (mine.at[pos.px, 1], self.bx.at[1], pos.xn),
            (self.far, self.near, pos.sib),
        )[i]
        return send(src, dst, self.sm.at[0, i], self.sm.at[1, i], there)

    def landed(self, i, ref):
        send(ref, ref, self.sm.at[0, i], self.sm.at[1, i], self.pos.xn).wait_recv()

    def first(self):
        for i in range(4):
            self.copy(i).start()

    def second(self):
        pos, mine = self.pos, self.mine
        self.landed(0, self.a0)
        mine[pos.py, 0] = (mine[pos.py, 0].astype(F32) + self.a0[...].astype(F32)).astype(BF16)
        self.copy(4).start()
        self.landed(1, self.a1)
        mine[pos.px, 1] = (mine[pos.px, 1].astype(F32) + self.a1[...].astype(F32)).astype(BF16)
        self.copy(5).start()

    def third(self):
        pos = self.pos
        self.landed(2, self.bx.at[0])
        self.landed(3, self.by.at[1])
        self.landed(4, self.by.at[0])
        self.landed(5, self.bx.at[1])

        def total(core):
            return (
                self.mine[pos.p, core].astype(F32)
                + self.bx[core].astype(F32)
                + self.by[core].astype(F32)
            )

        self.far[...] = total(1 - pos.c)
        self.copy(6).start()
        self.out[pos.c] += total(pos.c)

    def last(self):
        pos = self.pos
        self.landed(6, self.near)
        self.out[1 - pos.c] += self.near[...]
        for i in range(7):
            self.copy(i).wait_send()


class JointScatter:
    def __init__(self, pos, bufs, sems):
        self.pos = pos
        self.partial, self.theirs, self.zbuf, self.sums, self.got = bufs
        self.sb, self.zs, self.ps = sems

    @staticmethod
    def scratch(nb, shape):
        return [
            pltpu.VMEM((nb, 4, 2) + shape, BF16),
            pltpu.VMEM((nb, 4) + shape, BF16),
            pltpu.VMEM((nb - 1, 4) + shape, BF16),
            pltpu.VMEM((4,) + shape, BF16),
            pltpu.VMEM((4,) + shape, BF16),
        ]

    @staticmethod
    def sem_scratch(nb):
        return [DMA((2,)), DMA((2, nb)), DMA((2, 4))]

    def sibling_copy(self):
        pos = self.pos
        return send(
            self.partial.at[:, :, 1 - pos.c], self.theirs, self.sb.at[0], self.sb.at[1], pos.sib
        )

    def z_copy(self, d):
        pos = self.pos
        return send(
            self.partial.at[pos.up(d), :, pos.c],
            self.zbuf.at[d - 1],
            self.zs.at[0, d],
            self.zs.at[1, d],
            (pos.up(d), pos.s),
        )

    def plane_copy(self, k):
        pos = self.pos
        chip = pos.chip(k)
        return send(
            self.sums.at[chip],
            self.got.at[pos.p],
            self.ps.at[0, k],
            self.ps.at[1, k],
            (pos.b, 2 * chip + pos.c),
        )

    def begin(self):
        self.sibling_copy().start()

    def first(self):
        pos = self.pos
        self.sibling_copy().wait_recv()
        for d in (*range(1, pos.nb), 0):
            z = pos.up(d)
            self.partial[z, :, pos.c] = (
                self.partial[z, :, pos.c].astype(F32) + self.theirs[z].astype(F32)
            ).astype(BF16)
            if d:
                self.z_copy(d).start()

    def second(self):
        pos = self.pos
        value = self.partial[pos.b, :, pos.c].astype(F32)
        for d in range(1, pos.nb):
            self.z_copy(d).wait_recv()
            value = value + self.zbuf[d - 1].astype(F32)
        self.sums[...] = value.astype(BF16)
        for k in range(1, 4):
            self.plane_copy(k).start()

    def last(self, out, vec):
        pos = self.pos
        width = out.shape[1] // 12
        self.got[pos.p] = self.sums[pos.p]
        for k in range(1, 4):
            ref = self.got.at[pos.chip(k)]
            send(ref, ref, self.ps.at[0, k], self.ps.at[1, k], pos.sib).wait_recv()
        extra = 0.0
        for chip in range(4):
            value = self.got[chip].astype(F32)
            for n in range(3):
                out[:, (4 * n + chip) * width : (4 * n + chip + 1) * width] = value[
                    :, n * width : (n + 1) * width
                ]
            extra = extra + value[:8, 3 * width : 3 * width + vec]
        self.sibling_copy().wait_send()
        for d in range(1, pos.nb):
            self.z_copy(d).wait_send()
        for k in range(1, 4):
            self.plane_copy(k).wait_send()
        return extra


def normed_rows(residual):
    centered = residual - jnp.mean(residual, axis=-1, keepdims=True)
    inverse = lax.rsqrt(jnp.mean(centered * centered, axis=-1, keepdims=True) + EPSILON)
    return centered * inverse, inverse


def transposed_dot(left, right):
    return lax.dot_general(left, right, (((0,), (0,)), ((), ())), preferred_element_type=F32)


def dot_transposed(left, right):
    return lax.dot_general(left, right, (((1,), (1,)), ((), ())), preferred_element_type=F32)


def feed_and_back(
    lengths, inputs, cotangent, mixed, vectors, hidden_bias,
    output_weight, expand_weight, reduce_weight, rows, weight, qkv, logs, nb, heads,
):
    _, count, model_width = inputs.shape
    hidden = hidden_bias.shape[1]
    block = hidden // nb
    width = heads * HEAD_DIM
    size, tokens = 8 * count, 2 * count
    owners = 8 * nb
    shard = vec = model_width // owners
    per = hidden // owners
    joint_shape = (shard, 3 * width + 64)
    shapes = [(16, 128), (shard, model_width), (shard, hidden), (per, model_width)]
    dtypes = [F32, BF16, BF16, BF16]

    def body(
        lengths_ref, inputs_ref, cotangent_ref, mixed_ref, vectors_ref, bias_ref,
        output_ref, expand_ref, reduce_ref, rows_any, weight_any, qkv_any, log_any,
        result_out, rows_out, joint_out, vectors_out, hidden_out,
        output_out, expand_out, reduce_out,
        output_w, expand_w, reduce_w, rows_ref, weight_ref, qkv_ref, log_ref, loads,
        context, first_normed, first_low, hidden_low, slope, feed, grad_low,
        grad_vectors, grad_bias, parts, small_total,
        grad_context, grad_qkv, grad_key, grad_value,
        *scratch,
    ):
        pos = Place(nb)
        scratch = list(scratch)

        def take(n):
            got = scratch[:n]
            del scratch[:n]
            return got

        mixing = ContextExchange(pos, parts, grad_context, take(2))
        row_sums = RowScatter(pos, rows_out, [hidden_low] + take(6), take(1))
        joints = JointScatter(pos, take(5), take(3))
        smalls, outputs, expands, reduces = (
            Scatter(pos, halves_of(shape), take(7), take(8)) for shape in shapes
        )

        def turn(i):
            return jnp.where(i < 2, 2 - i, 3 * (3 - i))

        def expand_load(z):
            at = pl.ds(z * block if isinstance(z, int) else pl.multiple_of(z * block, block), block)
            return pltpu.make_async_copy(expand_ref.at[:, at], expand_w.at[z], loads.at[z])

        def reduce_load(z):
            at = pl.ds(z * block if isinstance(z, int) else pl.multiple_of(z * block, block), block)
            return pltpu.make_async_copy(reduce_ref.at[at, :], reduce_w.at[z], loads.at[nb + z])

        output_load = pltpu.make_async_copy(output_ref, output_w, loads.at[2 * nb])
        later = [
            pltpu.make_async_copy(src, dst, loads.at[2 * nb + 1 + n])
            for n, (src, dst) in enumerate(
                ((rows_any, rows_ref), (weight_any, weight_ref), (qkv_any, qkv_ref), (log_any, log_ref))
            )
        ]
        output_load.start()
        for z in range(nb):
            expand_load(z).start()
            reduce_load(z).start()
        for copy in later:
            copy.start()
        barrier = pltpu.get_barrier_semaphore()
        partners = [(pos.up(d), pos.s) for d in range(1, nb)] + plane_others(pos)
        for device in partners:
            pl.semaphore_signal(barrier, inc=1, device_id=device, device_id_type=MESH)

        def vector(n):
            return vectors_ref[n : n + 1, :]

        for chip in range(4):
            for j in range(2):
                context[j * count : (j + 1) * count, chip * width : (chip + 1) * width] = unpacked(
                    mixed_ref[chip, j]
                )
        output_load.wait()
        branch = jnp.dot(context[...], output_w[...], preferred_element_type=F32) + vector(4)
        normed, first_inverse = normed_rows(
            inputs_ref[...].reshape(tokens, model_width) + branch
        )
        first_normed[...] = normed
        first = normed * vector(0) + vector(1)
        rows_out[...] = first.reshape(2, count, model_width)
        first_low[...] = first.astype(BF16)
        feed[...] = jnp.broadcast_to(vector(7), feed.shape)

        def forward(z, _):
            at = pl.ds(pl.multiple_of(z * block, block), block)
            expand_load(z).wait()
            before = (
                jnp.dot(first_low[...], expand_w[z], preferred_element_type=F32)
                + bias_ref[:, at]
            )
            half = 0.5 * (1.0 + lax.erf(before * HALF_ROOT))
            low = (before * half).astype(BF16)
            hidden_low[z] = low.reshape(2, count, block)
            slope[z] = half + before * jnp.exp(-0.5 * before * before) * INV_ROOT_TAU
            reduce_load(z).wait()
            feed[...] += jnp.dot(low, reduce_w[z], preferred_element_type=F32)
            return 0

        lax.fori_loop(0, nb, forward, 0)
        normed, inverse = normed_rows(
            rows_out[...].reshape(tokens, model_width) + feed[...]
        )
        result_out[...] = (normed * vector(5) + vector(6)).reshape(2, count, model_width)

        places = pos.s * count + lax.broadcasted_iota(jnp.int32, (count, 1), 0)
        grad_res = jnp.concatenate(
            [jnp.where(places < lengths_ref[j], cotangent_ref[j], 0.0) for j in range(2)]
        )
        grad_second, gain, shift = norm_back(grad_res, normed, inverse, vector(5))
        grad_low[...] = grad_second.astype(BF16)
        grad_vectors[...] = jnp.zeros_like(grad_vectors)
        grad_vectors[5:6, :] = gain[None]
        grad_vectors[6:7, :] = shift[None]
        grad_vectors[7:8, :] = jnp.sum(grad_low[...].astype(F32), axis=0, keepdims=True)
        feed[...] = grad_second

        def backward(i, _):
            z = pos.up(turn(i))
            at = pl.ds(pl.multiple_of(z * block, block), block)
            for n in range(2):
                cut = slice(n * (block // 2), (n + 1) * (block // 2))
                reduces.partial[z, 2 * n : 2 * n + 2] = (
                    transposed_dot(
                        hidden_low[z, :, :, cut].reshape(tokens, block // 2), grad_low[...]
                    )
                    .reshape(2, 2, per, model_width)
                    .astype(BF16)
                )
            reduces.begin(turn(i))
            low = (dot_transposed(grad_low[...], reduce_w[z]) * slope[z]).astype(BF16)
            grad_bias[:, at] = jnp.sum(low.astype(F32), axis=0, keepdims=True)
            for n in range(2):
                cut = slice(n * (model_width // 2), (n + 1) * (model_width // 2))
                expands.partial[n * nb // 2 : (n + 1) * nb // 2, :, :, :, at] = (
                    transposed_dot(first_low[:, cut], low)
                    .reshape(nb // 2, 4, 2, shard, block)
                    .astype(BF16)
                )
            feed[...] += dot_transposed(low, expand_w[z])
            reduces.first(turn(i))
            return 0

        pl.semaphore_wait(barrier, len(partners))
        lax.fori_loop(0, nb, backward, 0)
        for k in range(nb):
            expands.begin(turn(k))
        grads, gain, shift = norm_back(feed[...], first_normed[...], first_inverse, vector(0))
        rows_out[...] = grads.reshape(2, count, model_width)
        low = grads.astype(BF16)
        grad_low[...] = low
        grad_vectors[0:1, :] = gain[None]
        grad_vectors[1:2, :] = shift[None]
        grad_vectors[4:5, :] = jnp.sum(low.astype(F32), axis=0, keepdims=True)
        low = dot_transposed(low, output_w[...]).astype(BF16)
        for chip in range(4):
            for j in range(2):
                parts[chip, j] = packed(
                    low[j * count : (j + 1) * count, chip * width : (chip + 1) * width]
                )
        mixing.start()
        for n in range(2):
            cut = slice(n * (model_width // 2), (n + 1) * (model_width // 2))
            outputs.partial[n * nb // 2 : (n + 1) * nb // 2] = (
                transposed_dot(context[:, cut], grad_low[...])
                .reshape(nb // 2, 4, 2, shard, model_width)
                .astype(BF16)
            )
        for owner in range(owners):
            here = (owner // 8, owner % 8 // 2, owner % 2)
            smalls.partial[here] = jnp.concatenate(
                [
                    jnp.pad(
                        grad_vectors[:, owner * vec : (owner + 1) * vec], ((0, 0), (0, 128 - vec))
                    ),
                    jnp.broadcast_to(
                        jnp.pad(
                            grad_bias[:, owner * per : (owner + 1) * per], ((0, 0), (0, 128 - per))
                        ),
                        (8, 128),
                    ),
                ]
            )
        for k in range(nb):
            outputs.begin(turn(k))
            smalls.begin(turn(k))

        grad_key[...] = jnp.zeros_like(grad_key)
        grad_value[...] = jnp.zeros_like(grad_value)
        for copy in later:
            copy.wait()
        back = attend_back_block(
            lengths_ref[pos.c], qkv_ref, log_ref, grad_context, grad_qkv, grad_key, grad_value,
            heads, count,
        )

        def middle(i, _):
            k = turn(i)
            reduces.second(k)
            expands.first(k)
            guarded(i > 0, lambda: reduces.third(turn(i - 1), reduce_out))
            guarded(i == 0, mixing.arrive)
            back(i)
            guarded(i > 0, lambda: expands.second(turn(i - 1)))
            guarded(i > 1, lambda: expands.third(turn(i - 2), expand_out))
            return 0

        lax.fori_loop(0, nb, middle, 0)

        def late(i, _):
            k = turn(i)
            outputs.first(k)
            smalls.first(k)
            return 0

        grad_qkv[:, width : 2 * width] = (grad_key[...] * SCORE_SCALE).astype(BF16)
        grad_qkv[:, 2 * width :] = grad_value[...].astype(BF16)

        def spread(i, _):
            at = pl.ds(pl.multiple_of(i * tokens, tokens), tokens)
            row_sums.mine[i] = (
                dot_transposed(grad_qkv[at, :], weight_ref[...])
                .astype(BF16)
                .reshape(2, count, model_width)
            )
            return 0

        for z in range(nb):
            grad_joint = transposed_dot(
                rows_ref[:, :, :, z * 8 * shard : (z + 1) * 8 * shard].reshape(size, 8 * shard),
                grad_qkv[...],
            )
            joints.partial[z, :, :, :, : 3 * width] = grad_joint.reshape(
                4, 2, shard, 3 * width
            ).astype(BF16)
        sums = jnp.sum(grad_qkv[...].astype(F32), axis=0, keepdims=True)
        joints.partial[:, :, :, :, 3 * width :] = jnp.zeros((nb, 4, 2, shard, 64), BF16)
        for s in range(8):
            at = slice(s * vec, (s + 1) * vec)
            value = jnp.concatenate([sums[:, :width][:, at], sums[:, 2 * width :][:, at]])
            joints.partial[pos.p, s // 2, s % 2, :, 3 * width :] = jnp.pad(
                value, ((0, shard - 2), (0, 64 - vec))
            ).astype(BF16)
        joints.begin()
        lax.fori_loop(0, 4, spread, 0)
        row_sums.first()
        joints.first()
        expands.second(turn(3))
        lax.fori_loop(0, nb, late, 0)

        expands.third(turn(2), expand_out)
        reduces.third(turn(nb - 1), reduce_out)
        reduces.last(reduce_out)
        reduces.drain()
        row_sums.second()

        def final(i, _):
            k = turn(i)
            outputs.second(k)
            smalls.second(k)
            return 0

        lax.fori_loop(0, nb, final, 0)
        expands.third(turn(nb - 1), expand_out)
        joints.second()
        row_sums.third()
        expands.last(expand_out)
        expands.drain()
        mixing.drain()

        def end(i, _):
            k = turn(i)
            outputs.third(k, output_out)
            smalls.third(k, small_total)
            return 0

        lax.fori_loop(0, nb, end, 0)
        extra = joints.last(joint_out, vec)
        row_sums.last()
        for scatter, out in ((outputs, output_out), (smalls, small_total)):
            scatter.last(out)
            scatter.drain()
        lines = lax.broadcasted_iota(jnp.int32, (8, vec), 0)
        value = jnp.where(lines == 2, extra[0:1], small_total[:8, :vec])
        vectors_out[...] = jnp.where(lines == 3, extra[1:2], value)
        hidden_out[...] = small_total[8:9, :per]

    def vmem(shape, dtype):
        return pltpu.VMEM(shape, dtype)

    scratch = [
        vmem((model_width, model_width), BF16),
        vmem((nb, model_width, block), BF16),
        vmem((nb, block, model_width), BF16),
        vmem(rows.shape, BF16),
        vmem(weight.shape, BF16),
        vmem(qkv.shape, BF16),
        vmem(logs.shape, F32),
        DMA((2 * nb + 5,)),
        vmem((tokens, model_width), BF16),
        vmem((tokens, model_width), F32),
        vmem((tokens, model_width), BF16),
        vmem((nb, 2, count, block), BF16),
        vmem((nb, tokens, block), F32),
        vmem((tokens, model_width), F32),
        vmem((tokens, model_width), BF16),
        vmem((8, model_width), F32),
        vmem((1, hidden), F32),
        vmem((4, 2, count // 2, 2 * width), BF16),
        vmem((16, 128), F32),
        vmem((4, 2, count // 2, 2 * width), BF16),
        vmem((size, 3 * width), BF16),
        vmem((size, width), F32),
        vmem((size, width), F32),
    ]
    scratch += ContextExchange.scratch() + RowScatter.scratch(count, model_width)
    scratch += JointScatter.scratch(nb, joint_shape) + JointScatter.sem_scratch(nb)
    for shape, dtype in zip(shapes, dtypes):
        scratch += Scatter.scratch(nb, shape, dtype, halves_of(shape)) + Scatter.sem_scratch(nb)
    return pl.pallas_call(
        body,
        out_shape=tuple(
            jax.ShapeDtypeStruct(shape, F32)
            for shape in (
                inputs.shape,
                inputs.shape,
                (shard, 3 * model_width),
                (8, vec),
                (1, per),
                shapes[1],
                shapes[2],
                shapes[3],
            )
        ),
        in_specs=[SM] + [VM] * 5 + [ANY] * 7,
        out_specs=(VM,) * 8,
        scratch_shapes=scratch,
        name="feed_and_back",
        compiler_params=pltpu.CompilerParams(
            collective_id=4, has_side_effects=True, vmem_limit_bytes=VMEM_LIMIT
        ),
    )(
        lengths, inputs, cotangent, mixed, vectors, hidden_bias,
        output_weight, expand_weight, reduce_weight, rows, weight, qkv, logs,
    )


def hand_over(*arrays):
    count = len(arrays)

    def body(*refs):
        came, out, held = refs[:count], refs[count : 2 * count], refs[2 * count : 3 * count]
        sems = refs[3 * count]
        loads = [pltpu.make_async_copy(came[n], held[n], sems.at[0, n]) for n in range(count)]
        stores = [pltpu.make_async_copy(held[n], out[n], sems.at[1, n]) for n in range(count)]
        for copy in loads:
            copy.start()
        for load, store in zip(loads, stores):
            load.wait()
            store.start()
        for copy in stores:
            copy.wait()

    return pl.pallas_call(
        body,
        out_shape=tuple(jax.ShapeDtypeStruct(a.shape, a.dtype) for a in arrays),
        in_specs=[ANY] * count,
        out_specs=(ANY,) * count,
        scratch_shapes=[pltpu.VMEM(a.shape, a.dtype) for a in arrays] + [DMA((2, count))],
        name="hand_over",
        compiler_params=pltpu.CompilerParams(vmem_limit_bytes=VMEM_LIMIT),
    )(*arrays)


def plane_on_device(
    inputs,
    cotangent,
    lengths,
    joint_weight,
    output_weight,
    vectors,
    expand_weight,
    expand_bias,
    reduce_weight,
):
    nb = lax.axis_size("batch")
    _, _, model_width = inputs.shape
    hidden_width = expand_weight.shape[1]
    heads = model_width // (4 * HEAD_DIM)
    per = expand_bias.shape[0]
    (
        vector_rows, full_bias, rows_all, joint_all, qkv, logs,
        mixed, output_all, expand_all, reduce_all,
    ) = gather_attend(
        lengths,
        inputs,
        joint_weight,
        vectors,
        expand_bias.reshape(1, per),
        output_weight,
        expand_weight,
        reduce_weight,
        nb,
        heads,
    )
    full_output = output_all.reshape(model_width, model_width)
    full_expand = expand_all.reshape(model_width, hidden_width)
    full_reduce = reduce_all.reshape(hidden_width, model_width)

    result, grad_inputs, joint_sum, vectors_sum, bias_sum, output_sum, expand_sum, reduce_sum = (
        feed_and_back(
            lengths,
            inputs,
            cotangent,
            mixed,
            vector_rows,
            full_bias,
            full_output,
            full_expand,
            full_reduce,
            rows_all,
            joint_all,
            qkv,
            logs,
            nb,
            heads,
        )
    )
    (
        result, grad_inputs, joint_sum, output_sum, vectors_sum, expand_sum, bias_sum, reduce_sum,
    ) = hand_over(
        result, grad_inputs, joint_sum, output_sum, vectors_sum, expand_sum, bias_sum, reduce_sum
    )
    return (
        result,
        grad_inputs,
        joint_sum,
        output_sum,
        vectors_sum,
        expand_sum,
        bias_sum.reshape(per),
        reduce_sum,
    )


def plane_fits(mesh, inputs, expand_bias, expand_weight):
    return (
        mesh.shape["seq"] == 8
        and mesh.shape["batch"] == 4
        and inputs[0] == 2 * mesh.shape["batch"]
        and HEADS % 4 == 0
        and inputs[2] == HEADS * HEAD_DIM
        and inputs[1] % (8 * 16) == 0
        and inputs[2] % 256 == 0
        and expand_weight[0] % (8 * 32) == 0
        and expand_weight[1] % (16 * 32) == 0
        and expand_bias[0] <= 128 * 32
        and expand_weight[1] == 4 * inputs[2]
    )


def solution(mesh):
    def program(*args):
        fits = plane_fits(mesh, args[0].shape, args[7].shape, args[6].shape)
        return jax.shard_map(
            plane_on_device if fits else general_on_device,
            mesh=mesh,
            in_specs=(
                P("batch", "seq", None),
                P("batch", "seq", None),
                P("batch"),
                P(("batch", "seq"), None),
                P(("batch", "seq"), None),
                P(None, ("batch", "seq")),
                P(("batch", "seq"), None),
                P(("batch", "seq")),
                P(("batch", "seq"), None),
            ),
            out_specs=(
                P("batch", "seq", None),
                P("batch", "seq", None),
                P(("batch", "seq"), None),
                P(("batch", "seq"), None),
                P(None, ("batch", "seq")),
                P(("batch", "seq"), None),
                P(("batch", "seq")),
                P(("batch", "seq"), None),
            ),
            check_vma=False,
        )(*args)

    return program
```

```python
import functools
import math

import jax
import jax.numpy as jnp
from jax import lax
from jax.experimental import pallas as pl
from jax.experimental.pallas import tpu as pltpu
from jax.sharding import PartitionSpec as P

HEADS = 12
HEAD_DIM = 64


EPSILON = 1e-12
SCORE_SCALE = 0.125
NEG_FILL = -1e30
HALF_ROOT = 0.7071067811865476
INV_ROOT_TAU = 0.3989422804014327
block_limit = 256


def layer_norm(residual, norm_gain, norm_shift):
    centered = residual - jnp.mean(residual, axis=-1, keepdims=True)
    inverse = lax.rsqrt(jnp.mean(centered * centered, axis=-1, keepdims=True) + EPSILON)
    normed = centered * inverse
    return (normed * norm_gain + norm_shift, normed, inverse)


def norm_back(grad_out, normed, inverse, norm_gain):
    grad_normed = grad_out * norm_gain
    mean_grad = jnp.mean(grad_normed, axis=-1, keepdims=True)
    mean_proj = jnp.mean(grad_normed * normed, axis=-1, keepdims=True)
    grad_in = inverse * (grad_normed - mean_grad - normed * mean_proj)
    return (grad_in, jnp.sum(grad_out * normed, axis=0), jnp.sum(grad_out, axis=0))


def gelu_value(before_gelu):
    return 0.5 * before_gelu * (1.0 + lax.erf(before_gelu * HALF_ROOT))


def gelu_slope(before_gelu):
    return (
        0.5 * (1.0 + lax.erf(before_gelu * HALF_ROOT))
        + before_gelu * jnp.exp(-0.5 * before_gelu * before_gelu) * INV_ROOT_TAU
    )


def over_blocks(piece_rows, block_fn, carried):
    block_size = math.gcd(piece_rows, block_limit)

    def run_block(block_index, current):
        return block_fn(current, block_index * block_size, block_size)

    return lax.fori_loop(0, piece_rows // block_size, run_block, carried)


def head_scores(left_heads, right_heads, right_places, lengths):
    scores = (
        jnp.einsum("sqhd,skhd->shqk", left_heads, right_heads, preferred_element_type=jnp.float32)
        * SCORE_SCALE
    )
    allowed = right_places[None, :] < lengths[:, None]
    return jnp.where(allowed[:, None, None, :], scores, NEG_FILL)


def cut_heads(gathered_piece, offset, block_size, head_count):
    sliced = lax.dynamic_slice_in_dim(gathered_piece, offset, block_size, 1)
    return sliced.reshape(sliced.shape[0], block_size, head_count, -1)


def gather_attention(joint_weight, output_weight, vectors):
    return (
        lax.all_gather(joint_weight, ("batch", "seq"), axis=0, tiled=True),
        lax.all_gather(output_weight, ("batch", "seq"), axis=0, tiled=True),
        lax.all_gather(vectors, ("batch", "seq"), axis=1, tiled=True),
    )


def gather_feed(expand_weight, reduce_weight, expand_bias):
    return (
        lax.all_gather(expand_weight, ("batch", "seq"), axis=0, tiled=True),
        lax.all_gather(reduce_weight, ("batch", "seq"), axis=0, tiled=True),
        lax.all_gather(expand_bias, ("batch", "seq"), axis=0, tiled=True),
    )


def general_on_device(
    inputs,
    cotangent,
    lengths,
    joint_weight,
    output_weight,
    vectors,
    expand_weight,
    expand_bias,
    reduce_weight,
):
    seq_count, row_count, model_width = inputs.shape
    head_count = HEADS
    head_size = HEAD_DIM
    tokens = seq_count * row_count
    head_shape = (seq_count, row_count, head_count, head_size)
    own_places = lax.axis_index("seq") * row_count + jnp.arange(row_count, dtype=jnp.int32)
    row_valid = own_places[None, :] < lengths[:, None]
    row_mask = row_valid.reshape(tokens, 1).astype(jnp.float32)
    full_joint, full_output, full_vectors = gather_attention(joint_weight, output_weight, vectors)
    vector_rows = full_vectors.astype(jnp.float32)
    flat_inputs = inputs.reshape(tokens, model_width)
    input_low = flat_inputs.astype(jnp.bfloat16)
    projected = jnp.dot(input_low, full_joint, preferred_element_type=jnp.float32)
    query_low = (projected[:, :model_width] + vector_rows[2]).astype(jnp.bfloat16)
    key_low = projected[:, model_width : 2 * model_width].astype(jnp.bfloat16)
    value_low = (projected[:, 2 * model_width :] + vector_rows[3]).astype(jnp.bfloat16)
    query_heads = query_low.reshape(head_shape)
    key_rows = key_low.reshape(seq_count, row_count, model_width)
    value_rows = value_low.reshape(seq_count, row_count, model_width)
    start_state = (
        jnp.full((seq_count, head_count, row_count), NEG_FILL, jnp.float32),
        jnp.zeros((seq_count, head_count, row_count), jnp.float32),
        jnp.zeros(head_shape, jnp.float32),
    )
    key_piece = lax.all_gather(key_rows, "seq", axis=1, tiled=True)
    value_piece = lax.all_gather(value_rows, "seq", axis=1, tiled=True)

    def forward_score_block(current, offset, block_size):
        running_max, running_sum, summed = current
        key_heads = cut_heads(key_piece, offset, block_size, head_count)
        value_heads = cut_heads(value_piece, offset, block_size, head_count)
        key_places = offset + jnp.arange(block_size, dtype=jnp.int32)
        scores = head_scores(query_heads, key_heads, key_places, lengths)
        new_max = jnp.maximum(running_max, jnp.max(scores, axis=-1))
        factor = jnp.exp(running_max - new_max)
        exp_scores = jnp.exp(scores - new_max[..., None])
        running_sum = running_sum * factor + jnp.sum(exp_scores, axis=-1)
        update = jnp.einsum(
            "shqk,skhd->sqhd",
            exp_scores.astype(jnp.bfloat16),
            value_heads,
            preferred_element_type=jnp.float32,
        )
        summed = summed * jnp.transpose(factor, (0, 2, 1))[..., None] + update
        return (new_max, running_sum, summed)

    running_max, running_sum, summed = over_blocks(
        key_piece.shape[1], forward_score_block, start_state
    )
    attended = summed / jnp.transpose(running_sum, (0, 2, 1))[..., None]
    log_total = jnp.transpose(running_max + jnp.log(running_sum), (0, 2, 1))
    context_low = attended.reshape(tokens, model_width).astype(jnp.bfloat16)
    branch = jnp.dot(context_low, full_output, preferred_element_type=jnp.float32) + vector_rows[4]
    first, first_normed, first_inverse = layer_norm(
        flat_inputs + branch, vector_rows[0], vector_rows[1]
    )
    first_low = first.astype(jnp.bfloat16)
    full_expand, full_reduce, full_bias = gather_feed(expand_weight, reduce_weight, expand_bias)
    before_gelu = jnp.dot(
        first_low, full_expand, preferred_element_type=jnp.float32
    ) + full_bias.astype(jnp.float32)
    hidden_low = gelu_value(before_gelu).astype(jnp.bfloat16)
    feed = jnp.dot(hidden_low, full_reduce, preferred_element_type=jnp.float32) + vector_rows[7]
    result, second_normed, second_inverse = layer_norm(first + feed, vector_rows[5], vector_rows[6])
    full_expand, full_reduce, full_bias = gather_feed(expand_weight, reduce_weight, expand_bias)
    full_joint, full_output, full_vectors = gather_attention(joint_weight, output_weight, vectors)
    grad_res = cotangent.reshape(tokens, model_width) * row_mask
    grad_second, grad_gain_two, grad_shift_two = norm_back(
        grad_res, second_normed, second_inverse, vector_rows[5]
    )
    grad_feed_low = grad_second.astype(jnp.bfloat16)
    grad_reduce_local = jnp.dot(hidden_low.T, grad_feed_low, preferred_element_type=jnp.float32)
    grad_hidden = jnp.dot(
        grad_feed_low, full_reduce.T, preferred_element_type=jnp.float32
    ) * gelu_slope(before_gelu)
    grad_hidden_low = grad_hidden.astype(jnp.bfloat16)
    grad_expand_local = jnp.dot(first_low.T, grad_hidden_low, preferred_element_type=jnp.float32)
    grad_bias_local = jnp.sum(grad_hidden_low.astype(jnp.float32), axis=0)
    grad_first = grad_second + jnp.dot(
        grad_hidden_low, full_expand.T, preferred_element_type=jnp.float32
    )
    grad_resid, grad_gain_one, grad_shift_one = norm_back(
        grad_first, first_normed, first_inverse, vector_rows[0]
    )
    grad_branch_low = grad_resid.astype(jnp.bfloat16)
    grad_output_local = jnp.dot(context_low.T, grad_branch_low, preferred_element_type=jnp.float32)
    grad_context_low = jnp.dot(
        grad_branch_low, full_output.T, preferred_element_type=jnp.float32
    ).astype(jnp.bfloat16)
    grad_context_heads = grad_context_low.reshape(head_shape)
    row_delta = jnp.sum(grad_context_heads.astype(jnp.float32) * attended, axis=-1)
    log_heads = jnp.transpose(log_total, (0, 2, 1))
    delta_heads = jnp.transpose(row_delta, (0, 2, 1))
    query_key_piece = lax.all_gather(key_rows, "seq", axis=1, tiled=True)
    query_value_piece = lax.all_gather(value_rows, "seq", axis=1, tiled=True)

    def query_score_block(current, offset, block_size):
        key_heads = cut_heads(query_key_piece, offset, block_size, head_count)
        value_heads = cut_heads(query_value_piece, offset, block_size, head_count)
        key_places = offset + jnp.arange(block_size, dtype=jnp.int32)
        scores = head_scores(query_heads, key_heads, key_places, lengths)
        softmax_rows = jnp.exp(scores - log_heads[..., None])
        grad_probs = jnp.einsum(
            "sqhd,skhd->shqk", grad_context_heads, value_heads, preferred_element_type=jnp.float32
        )
        grad_scores = (softmax_rows * (grad_probs - delta_heads[..., None])).astype(jnp.bfloat16)
        return (
            current
            + jnp.einsum(
                "shqk,skhd->sqhd", grad_scores, key_heads, preferred_element_type=jnp.float32
            )
            * SCORE_SCALE
        )

    grad_query = over_blocks(
        query_key_piece.shape[1], query_score_block, jnp.zeros(head_shape, jnp.float32)
    )
    own_keys = key_low.reshape(head_shape)
    own_values = value_low.reshape(head_shape)
    query_rows = query_low.reshape(seq_count, row_count, model_width)
    grad_context_rows = grad_context_low.reshape(seq_count, row_count, model_width)
    zero_heads = jnp.zeros(head_shape, jnp.float32)
    query_piece = lax.all_gather(query_rows.astype(jnp.float32), "seq", axis=1, tiled=True).astype(
        jnp.bfloat16
    )
    grad_piece = lax.all_gather(
        grad_context_rows.astype(jnp.float32), "seq", axis=1, tiled=True
    ).astype(jnp.bfloat16)
    log_piece = lax.all_gather(log_total, "seq", axis=1, tiled=True)
    delta_piece = lax.all_gather(row_delta, "seq", axis=1, tiled=True)

    def key_score_block(current, offset, block_size):
        grad_key, grad_value = current
        query_block = cut_heads(query_piece, offset, block_size, head_count)
        grad_block = cut_heads(grad_piece, offset, block_size, head_count)
        log_block = jnp.transpose(
            lax.dynamic_slice_in_dim(log_piece, offset, block_size, 1), (0, 2, 1)
        )
        delta_block = jnp.transpose(
            lax.dynamic_slice_in_dim(delta_piece, offset, block_size, 1), (0, 2, 1)
        )
        scores = head_scores(query_block, own_keys, own_places, lengths)
        softmax_rows = jnp.exp(scores - log_block[..., None])
        grad_value = grad_value + jnp.einsum(
            "shqk,sqhd->skhd",
            softmax_rows.astype(jnp.bfloat16),
            grad_block,
            preferred_element_type=jnp.float32,
        )
        grad_probs = jnp.einsum(
            "sqhd,skhd->shqk", grad_block, own_values, preferred_element_type=jnp.float32
        )
        grad_scores = (softmax_rows * (grad_probs - delta_block[..., None])).astype(jnp.bfloat16)
        grad_key = (
            grad_key
            + jnp.einsum(
                "shqk,sqhd->skhd", grad_scores, query_block, preferred_element_type=jnp.float32
            )
            * SCORE_SCALE
        )
        return (grad_key, grad_value)

    grad_key, grad_value = over_blocks(
        query_piece.shape[1], key_score_block, (zero_heads, zero_heads)
    )
    grad_query_low = grad_query.reshape(tokens, model_width).astype(jnp.bfloat16)
    grad_key_low = grad_key.reshape(tokens, model_width).astype(jnp.bfloat16)
    grad_value_low = grad_value.reshape(tokens, model_width).astype(jnp.bfloat16)
    grad_projected = jnp.concatenate([grad_query_low, grad_key_low, grad_value_low], axis=1)
    grad_joint_local = jnp.dot(input_low.T, grad_projected, preferred_element_type=jnp.float32)
    grad_inputs = grad_resid + jnp.dot(
        grad_projected, full_joint.T, preferred_element_type=jnp.float32
    )
    grad_vector_local = jnp.stack(
        [
            grad_gain_one,
            grad_shift_one,
            jnp.sum(grad_query_low.astype(jnp.float32), axis=0),
            jnp.sum(grad_value_low.astype(jnp.float32), axis=0),
            jnp.sum(grad_branch_low.astype(jnp.float32), axis=0),
            grad_gain_two,
            grad_shift_two,
            jnp.sum(grad_feed_low.astype(jnp.float32), axis=0),
        ],
        axis=0,
    )
    every_grad = (
        lax.psum_scatter(grad_joint_local, ("batch", "seq"), scatter_dimension=0, tiled=True),
        lax.psum_scatter(grad_output_local, ("batch", "seq"), scatter_dimension=0, tiled=True),
        lax.psum_scatter(grad_vector_local, ("batch", "seq"), scatter_dimension=1, tiled=True),
        lax.psum_scatter(grad_expand_local, ("batch", "seq"), scatter_dimension=0, tiled=True),
        lax.psum_scatter(grad_reduce_local, ("batch", "seq"), scatter_dimension=0, tiled=True),
        lax.psum_scatter(grad_bias_local, ("batch", "seq"), scatter_dimension=0, tiled=True),
    )
    summed_grads = (
        every_grad[0],
        every_grad[1],
        every_grad[2],
        every_grad[3],
        every_grad[5],
        every_grad[4],
    )
    return (
        result.reshape(seq_count, row_count, model_width),
        grad_inputs.reshape(seq_count, row_count, model_width),
        summed_grads[0],
        summed_grads[1],
        summed_grads[2],
        summed_grads[3],
        summed_grads[4],
        summed_grads[5],
    )


MESH = pl.DeviceIdType.MESH
ANY = pl.BlockSpec(memory_space=pl.ANY)
VM = pl.BlockSpec(memory_space=pltpu.VMEM)
SM = pl.BlockSpec(memory_space=pltpu.SMEM)
DMA = pltpu.SemaphoreType.DMA
VMEM_LIMIT = 60 << 20
F32 = jnp.float32
BF16 = jnp.bfloat16


def send(src, dst, send_sem, recv_sem, device):
    return pltpu.make_async_remote_copy(
        src_ref=src,
        dst_ref=dst,
        send_sem=send_sem,
        recv_sem=recv_sem,
        device_id=device,
        device_id_type=MESH,
    )


class Place:
    def __init__(self, nb):
        self.nb = nb
        self.b = lax.axis_index("batch")
        self.s = lax.axis_index("seq")
        self.c = self.s % 2
        self.p = self.s // 2
        x, y = self.p % 2, self.p // 2
        self.px = 2 * y + (1 - x)
        self.py = 2 * (1 - y) + x
        self.pd = 2 * (1 - y) + (1 - x)
        self.sib = (self.b, 2 * self.p + 1 - self.c)
        self.xn = (self.b, 2 * self.px + self.c)
        self.yn = (self.b, 2 * self.py + self.c)

    def chip(self, step):
        return (self.p, self.px, self.py, self.pd)[step]

    def up(self, step):
        return (self.b + step) % self.nb

    def down(self, step):
        return (self.b + self.nb - step) % self.nb


def greet_near(pos):
    barrier = pltpu.get_barrier_semaphore()

    def signal(device):
        pl.semaphore_signal(barrier, inc=1, device_id=device, device_id_type=MESH)

    for device in plane_others(pos):
        signal(device)
    last = pos.nb - 1
    guarded(pos.b < last, lambda: signal(((pos.b + 1) % pos.nb, pos.s)))
    guarded(pos.b > 0, lambda: signal(((pos.b + last) % pos.nb, pos.s)))


def meet_near(pos):
    beside = jnp.where(pos.b < pos.nb - 1, 1, 0) + jnp.where(pos.b > 0, 1, 0)
    pl.semaphore_wait(pltpu.get_barrier_semaphore(), 7 + beside)


def same_core(pos):
    return [
        (pos.up(d), 2 * pos.chip(k) + pos.c)
        for d in range(pos.nb)
        for k in range(4)
        if d or k
    ]


def plane_others(pos):
    return [
        (pos.b, 2 * pos.chip(k) + (pos.c if j == 0 else 1 - pos.c))
        for k in range(4)
        for j in range(2)
        if k or j
    ]


def guarded(condition, action):
    if isinstance(condition, bool):
        if condition:
            action()
    else:

        @pl.when(condition)
        def _():
            action()


class Chain:
    def __init__(self, pos, mine, spot, sems):
        self.pos, self.mine, self.spot = pos, mine, spot
        self.up, self.down = sems

    @staticmethod
    def scratch(nb):
        return [DMA((2, nb)), DMA((2, nb))]

    def copy(self, src, z, sems, hop, there):
        pos = self.pos
        return send(src, self.spot(z), sems.at[0, hop], sems.at[1, hop], (there, pos.s))

    def moves(self, hop):
        pos = self.pos
        last = pos.nb - 1
        low, high = (pos.b - hop + 1 + pos.nb) % pos.nb, (pos.b + hop - 1) % pos.nb
        above, below = (pos.b + 1) % pos.nb, (pos.b + last) % pos.nb
        own = isinstance(hop, int) and hop == 1
        return (
            (
                (pos.b >= hop - 1) & (pos.b < last),
                self.copy(self.mine if own else self.spot(low), low, self.up, hop, above),
            ),
            (
                (pos.b + hop - 1 < pos.nb) & (pos.b > 0),
                self.copy(self.mine if own else self.spot(high), high, self.down, hop, below),
            ),
        )

    def start(self, hop=1):
        for made, copy in self.moves(hop):
            guarded(made, copy.start)

    def hop(self, hop):
        pos = self.pos
        low, high = (pos.b - hop + pos.nb) % pos.nb, (pos.b + hop) % pos.nb
        for made, z, sems in (
            (pos.b >= hop, low, self.up),
            (pos.b + hop < pos.nb, high, self.down),
        ):
            guarded(made, self.copy(self.spot(z), z, sems, hop, pos.b).wait_recv)
        guarded(hop < pos.nb - 1, lambda: self.start(hop + 1))

    def drain(self):
        for hop in range(1, self.pos.nb):
            for made, copy in self.moves(hop):
                guarded(made, copy.wait_send)


class Gather:
    def __init__(self, pos, shard, out, halves, sems):
        self.pos, self.shard, self.out, self.halves = pos, shard, out, halves
        self.xs, self.ys, self.f0, self.f1, self.sb, self.local_sem = sems[:6]
        self.chain = Chain(pos, shard, lambda z: out.at[z, pos.p, pos.c], sems[6:8])
        self.across = Chain(
            pos, out.at[pos.b, pos.pd, pos.c], lambda z: out.at[z, pos.pd, pos.c], sems[8:]
        )

    @staticmethod
    def scratch(nb):
        return [DMA((2, nb))] * 2 + [DMA((2,))] * 2 + [DMA((2, nb + 3)), DMA] + Chain.scratch(nb) * 2

    def z(self, k):
        return jnp.where(k <= self.pos.b, self.pos.b - k, k)

    def own(self):
        pos = self.pos
        self.local = pltpu.make_async_copy(
            self.shard, self.out.at[pos.b, pos.p, pos.c], self.local_sem
        )
        self.local.start()

    def x_copy(self, k, src=None):
        pos = self.pos
        there = self.out.at[self.z(k), pos.p, pos.c]
        src = there if src is None else src
        return send(src, there, self.xs.at[0, k], self.xs.at[1, k], pos.xn)

    def y_copy(self, k, src=None):
        pos = self.pos
        there = self.out.at[self.z(k), pos.p, pos.c]
        src = there if src is None else src
        return send(src, there, self.ys.at[0, k], self.ys.at[1, k], pos.yn)

    def plane(self, k, src=None):
        self.x_copy(k, src).start()
        self.y_copy(k, src).start()

    def landed(self, sems, k, chip):
        pos = self.pos
        ref = self.out.at[self.z(k), chip, pos.c]
        send(ref, ref, sems.at[0, k], sems.at[1, k], pos.xn).wait_recv()

    def y_forward(self):
        pos = self.pos
        ref = self.out.at[pos.b, pos.px, pos.c].at[self.halves[0]]
        return send(ref, ref, self.f0.at[0], self.f0.at[1], pos.yn)

    def x_forward(self):
        pos = self.pos
        ref = self.out.at[pos.b, pos.py, pos.c].at[self.halves[1]]
        return send(ref, ref, self.f1.at[0], self.f1.at[1], pos.xn)

    def forward(self):
        pos = self.pos
        self.landed(self.xs, 0, pos.px)
        self.y_forward().start()
        self.landed(self.ys, 0, pos.py)
        if self.halves[1] is not None:
            self.x_forward().start()

    def cross(self):
        pos = self.pos
        across = self.out.at[pos.b, pos.pd, pos.c]
        for half, sems in zip(self.halves, (self.f0, self.f1)):
            if half is not None:
                ref = across.at[half]
                send(ref, ref, sems.at[0], sems.at[1], pos.xn).wait_recv()

    def beside(self, k):
        pos = self.pos
        self.landed(self.xs, k, pos.px)
        self.landed(self.ys, k, pos.py)

    def sibling_copy(self, k, core=None):
        pos = self.pos
        ref = self.out.at[self.z(k), :, pos.c if core is None else core]
        return send(ref, ref, self.sb.at[0, k], self.sb.at[1, k], pos.sib)

    def sibling(self, k):
        self.sibling_copy(k).start()

    def part_copy(self, n, core=None):
        pos = self.pos
        k = pos.nb - 1
        ref = self.out.at[self.z(k), pos.chip(n), pos.c if core is None else core]
        return send(ref, ref, self.sb.at[0, k + n], self.sb.at[1, k + n], pos.sib)

    def finish(self, k):
        self.sibling_copy(k, 1 - self.pos.c).wait_recv()
        self.x_copy(k).wait_send()
        self.y_copy(k).wait_send()
        self.sibling_copy(k).wait_send()

    def end(self):
        k = self.pos.nb - 1
        for n in range(4):
            self.part_copy(n, 1 - self.pos.c).wait_recv()
        for n in range(4):
            self.part_copy(n).wait_send()
        self.x_copy(k).wait_send()
        self.y_copy(k).wait_send()

    def drain(self):
        self.y_forward().wait_send()
        if self.halves[1] is not None:
            self.x_forward().wait_send()
        self.chain.drain()
        self.across.drain()


class InputExchange:
    def __init__(self, pos, rows, out, sems):
        self.pos, self.rows, self.out, self.sems = pos, rows, out, sems
        self.started = []

    @staticmethod
    def scratch():
        return [DMA((2, 2)), DMA((2, 2)), DMA((2, 2)), DMA((2,)), DMA]

    def go(self, copy):
        copy.start()
        self.started.append(copy)

    def start(self):
        pos, (xs, ys, _, sb, local) = self.pos, self.sems
        there = self.out.at[pos.p, pos.c]
        for sems, chip in ((xs, pos.px), (ys, pos.py)):
            for j in range(2):
                self.go(
                    send(
                        self.rows.at[j],
                        there,
                        sems.at[0, j],
                        sems.at[1, pos.c],
                        (pos.b, 2 * chip + j),
                    )
                )
        self.go(send(self.rows.at[1 - pos.c], there, sb.at[0], sb.at[1], pos.sib))
        self.local = pltpu.make_async_copy(self.rows.at[pos.c], there, local)
        self.local.start()

    def landed(self, sems, j, chip):
        ref = self.out.at[chip, j]
        send(ref, ref, sems.at[0, j], sems.at[1, j], self.pos.xn).wait_recv()

    def forward(self):
        pos, (xs, ys, fs, _, _) = self.pos, self.sems
        self.landed(xs, 0, pos.px)
        ref = self.out.at[pos.px, 0]
        self.go(send(ref, ref, fs.at[0, 0], fs.at[1, 0], pos.yn))
        self.landed(ys, 1, pos.py)
        ref = self.out.at[pos.py, 1]
        self.go(send(ref, ref, fs.at[0, 1], fs.at[1, 1], pos.xn))

    def finish(self):
        pos, (xs, ys, fs, sb, _) = self.pos, self.sems
        self.landed(xs, 1, pos.px)
        self.landed(ys, 0, pos.py)
        self.landed(fs, 0, pos.pd)
        self.landed(fs, 1, pos.pd)
        ref = self.out.at[pos.p, 1 - pos.c]
        send(ref, ref, sb.at[0], sb.at[1], pos.sib).wait_recv()
        self.local.wait()

    def drain(self):
        for copy in self.started:
            copy.wait_send()


class JointGather:
    def __init__(self, pos, parts, out, sems):
        self.pos, self.parts, self.out = pos, parts, out
        self.direct, self.sb, self.local_sem = sems[:3]
        self.chain = Chain(
            pos, out.at[pos.b, :, pos.c], lambda z: out.at[z, :, pos.c], sems[3:]
        )

    @staticmethod
    def scratch(nb):
        return [DMA((2, 4)), DMA((2,)), DMA] + Chain.scratch(nb)

    def start(self):
        pos = self.pos
        there = self.out.at[pos.b, pos.p, pos.c]
        self.started = [
            send(
                self.parts.at[pos.chip(k)],
                there,
                self.direct.at[0, k],
                self.direct.at[1, k],
                (pos.b, 2 * pos.chip(k) + pos.c),
            )
            for k in range(1, 4)
        ]
        for copy in self.started:
            copy.start()
        self.local = pltpu.make_async_copy(self.parts.at[pos.p], there, self.local_sem)
        self.local.start()

    def own(self):
        pos = self.pos
        for k in range(1, 4):
            ref = self.out.at[pos.b, pos.chip(k), pos.c]
            send(ref, ref, self.direct.at[0, k], self.direct.at[1, k], pos.sib).wait_recv()
        self.local.wait()
        self.chain.start()

    def sibling(self):
        pos = self.pos
        ref = self.out.at[:, :, pos.c]
        send(ref, ref, self.sb.at[0], self.sb.at[1], pos.sib).start()

    def finish(self):
        pos = self.pos
        ref = self.out.at[:, :, 1 - pos.c]
        send(ref, ref, self.sb.at[0], self.sb.at[1], pos.sib).wait_recv()

    def drain(self):
        for copy in self.started:
            copy.wait_send()
        ref = self.out.at[:, :, self.pos.c]
        send(ref, ref, self.sb.at[0], self.sb.at[1], self.pos.sib).wait_send()
        self.chain.drain()


class ContextExchange:
    def __init__(self, pos, parts, out, sems):
        self.pos, self.parts, self.out = pos, parts, out
        self.sems, self.local_sem = sems

    @staticmethod
    def scratch():
        return [DMA((2, 8)), DMA]

    def pairs(self):
        pos = self.pos
        for k in range(4):
            for j in range(2):
                if k or j:
                    yield 2 * k + j, pos.chip(k), pos.c if j == 0 else 1 - pos.c

    def copies(self):
        pos, sems = self.pos, self.sems
        there = self.out.at[pos.p, pos.c]
        return [
            send(
                self.parts.at[chip, core],
                there,
                sems.at[0, i],
                sems.at[1, i],
                (pos.b, 2 * chip + core),
            )
            for i, chip, core in self.pairs()
        ]

    def local(self):
        pos = self.pos
        return pltpu.make_async_copy(
            self.parts.at[pos.p, pos.c], self.out.at[pos.p, pos.c], self.local_sem
        )

    def start(self):
        for copy in self.copies():
            copy.start()
        self.local().start()

    def arrive(self):
        for i, chip, core in self.pairs():
            ref = self.out.at[chip, core]
            send(ref, ref, self.sems.at[0, i], self.sems.at[1, i], self.pos.sib).wait_recv()
        self.local().wait()

    def drain(self):
        for copy in self.copies():
            copy.wait_send()


def gather_attend(
    lengths, inputs, joint, vectors, hidden_bias, output, expand, reduce, nb, heads
):
    _, count, model_width = inputs.shape
    shard = vec = model_width // (8 * nb)
    per = reduce.shape[0]
    width = heads * HEAD_DIM
    size = 8 * count
    joint_shape = (4, shard, 3 * width + 64)
    small_shape = (16, 128)

    def body(
        lengths_ref, inputs_ref, joint_weight_ref, own_vectors_ref, own_bias_ref,
        output_ref, expand_ref, reduce_ref,
        vectors_out, hidden_out, rows_any, weight_any, qkv_any, log_any,
        context_out, output_out, expand_out, reduce_out,
        rows_out, weight_out, qkv_out, log_out, stores,
        joint_all, context, small_all, bias_ref, rows_ref, joint_ref, small_ref,
        *scratch,
    ):
        pos = Place(nb)
        scratch = list(scratch)

        def take(n):
            got = scratch[:n]
            del scratch[:n]
            return got

        exchange = InputExchange(pos, rows_ref, rows_out, take(5))
        joints = JointGather(pos, joint_ref, joint_all, take(5))
        mixing = ContextExchange(pos, context, context_out, take(2))
        outputs, expands, reduces, smalls = (
            Gather(pos, part, out, halves_of(part.shape), take(10))
            for part, out in (
                (output_ref, output_out),
                (expand_ref, expand_out),
                (reduce_ref, reduce_out),
                (small_ref, small_all),
            )
        )
        gathers = (expands, smalls, reduces, outputs)
        units = ((expands, smalls), (reduces,), (outputs,))

        saves = [
            pltpu.make_async_copy(src, dst, stores.at[n])
            for n, (src, dst) in enumerate(
                (
                    (rows_out, rows_any),
                    (weight_out, weight_any),
                    (qkv_out, qkv_any),
                    (log_out, log_any),
                )
            )
        ]

        def project(i, _):
            at = pl.ds(pl.multiple_of(i * 2 * count, 2 * count), 2 * count)
            qkv_out[at, :] = (
                jnp.dot(
                    rows_out[i].reshape(2 * count, model_width),
                    weight_out[...],
                    preferred_element_type=F32,
                )
                + bias_ref[...]
            ).astype(BF16)
            return 0

        def prepare():
            joints.finish()
            for z in range(nb):
                weight_out[z * 8 * shard : (z + 1) * 8 * shard, :] = joint_all[
                    z, :, :, :, : 3 * width
                ].reshape(8 * shard, 3 * width)
            bias_ref[...] = jnp.zeros_like(bias_ref)
            for s in range(8):
                spot = joint_all[pos.p, s // 2, s % 2, :, 3 * width :].astype(F32)
                bias_ref[:, s * vec : (s + 1) * vec] = spot[0:1, :vec]
                bias_ref[:, 2 * width + s * vec : 2 * width + (s + 1) * vec] = spot[1:2, :vec]
            lax.fori_loop(0, 4, project, 0)
            for copy in saves[:3]:
                copy.start()

        def hop(k):
            for gather in gathers:
                gather.chain.hop(k)

        def relay(k, some):
            for gather in some:
                gather.across.hop(k)

        def share(k):
            for gather in gathers:
                gather.beside(k)
                gather.sibling(k)

        attend = attend_block(lengths_ref[pos.c], qkv_out, log_out, context, heads, count)

        def spread(k):
            for gather in gathers:
                gather.plane(k)

        greet_near(pos)
        weight = joint_weight_ref[...]
        spot = jnp.pad(
            own_vectors_ref[2:4, :].astype(F32), ((0, shard - 2), (0, 64 - vec))
        ).astype(BF16)
        for chip in range(4):
            at = slice(chip * width, (chip + 1) * width)
            joint_ref[chip] = jnp.concatenate(
                [weight[:, n * model_width :][:, at] for n in range(3)] + [spot], axis=1
            )
        small_ref[...] = jnp.concatenate(
            [
                jnp.pad(own_vectors_ref[...].astype(F32), ((0, 0), (0, 128 - vec))),
                jnp.pad(own_bias_ref[...].astype(F32), ((0, 7), (0, 128 - per))),
            ]
        ).astype(BF16)
        meet_near(pos)
        joints.start()
        for gather in gathers:
            gather.own()
            gather.chain.start()
            gather.plane(0, gather.shard)
        rows_ref[...] = inputs_ref[...].astype(BF16)
        joints.own()
        for n, gather in enumerate(gathers):
            gather.forward()
            if n == 1:
                exchange.start()
        hop(1)
        joints.chain.hop(1)
        for gather in gathers:
            gather.local.wait()
            gather.cross()
            gather.sibling(0)
        joints.chain.hop(2)
        hop(2)
        for gather in gathers:
            gather.across.start()
        exchange.forward()
        spread(1)
        joints.chain.hop(3)
        joints.sibling()
        exchange.finish()
        spread(2)
        prepare()
        hop(3)
        spread(3)
        attend(0)
        relay(1, gathers)
        attend(1)
        attend(2)
        relay(2, gathers)
        attend(3)
        mixing.start()
        saves[3].start()
        share(1)
        relay(nb - 1, (smalls,))
        share(2)
        for gather in gathers:
            gather.beside(nb - 1)
            for n in range(3):
                gather.part_copy(n).start()
        smalls.part_copy(3).start()

        def finish(k, _):
            for gather in gathers:
                gather.finish(k)
            return 0

        lax.fori_loop(0, nb - 1, finish, 0)
        smalls.end()
        for owner in range(8 * nb):
            part = small_all[owner // 8, owner % 8 // 2, owner % 2].astype(F32)
            vectors_out[:, owner * vec : (owner + 1) * vec] = part[:8, :vec]
            hidden_out[:, owner * per : (owner + 1) * per] = part[8:9, :per]
        smalls.drain()
        exchange.drain()
        joints.drain()
        for gather in (expands, reduces, outputs):
            gather.across.hop(nb - 1)
            gather.part_copy(3).start()
        for gather in (expands, reduces, outputs):
            gather.drain()
        mixing.arrive()
        mixing.drain()
        for gather in (expands, reduces, outputs):
            gather.end()
        for copy in saves:
            copy.wait()

    kept = (
        ((4, 2) + inputs.shape[1:], BF16),
        ((model_width, 3 * width), BF16),
        ((size, 3 * width), BF16),
        ((size, 128), F32),
    )

    def shape(part):
        return jax.ShapeDtypeStruct((nb, 4, 2) + part.shape, part.dtype)

    return pl.pallas_call(
        body,
        out_shape=(
            jax.ShapeDtypeStruct((8, model_width), F32),
            jax.ShapeDtypeStruct((1, 8 * nb * per), F32),
            *(jax.ShapeDtypeStruct(shape, dtype) for shape, dtype in kept),
            jax.ShapeDtypeStruct((4, 2, count // 2, 2 * width), BF16),
            shape(output),
            shape(expand),
            shape(reduce),
        ),
        in_specs=[SM] + [VM] * 7,
        out_specs=(VM,) * 2 + (ANY,) * 8,
        scratch_shapes=[pltpu.VMEM(shape, dtype) for shape, dtype in kept]
        + [DMA((4,))]
        + [
            pltpu.VMEM((nb, 4, 2) + joint_shape[1:], BF16),
            pltpu.VMEM((4, 2, count // 2, 2 * width), BF16),
            pltpu.VMEM((nb, 4, 2) + small_shape, BF16),
            pltpu.VMEM((1, 3 * width), F32),
            pltpu.VMEM(inputs.shape, BF16),
            pltpu.VMEM(joint_shape, BF16),
            pltpu.VMEM(small_shape, BF16),
        ]
        + InputExchange.scratch()
        + JointGather.scratch(nb)
        + ContextExchange.scratch()
        + Gather.scratch(nb) * 4,
        name="gather_attend",
        compiler_params=pltpu.CompilerParams(
            collective_id=1, has_side_effects=True, vmem_limit_bytes=VMEM_LIMIT
        ),
    )(lengths, inputs, joint, vectors, hidden_bias, output, expand, reduce)


def halves_of(shape):
    rows, columns = shape
    if columns % 256 == 0 and columns >= 1024:
        return (
            (slice(None), pl.ds(0, columns // 2)),
            (slice(None), pl.ds(columns // 2, columns // 2)),
        )
    if rows % 32 == 0:
        return (
            (pl.ds(0, rows // 2), slice(None)),
            (pl.ds(rows // 2, rows // 2), slice(None)),
        )
    if columns % 256 == 0:
        return (
            (slice(None), pl.ds(0, columns // 2)),
            (slice(None), pl.ds(columns // 2, columns // 2)),
        )
    return ((slice(None), slice(None)), None)


def attend_block(limit, qkv_ref, log_ref, context_ref, heads, count):
    width = heads * HEAD_DIM
    size = 8 * count

    def part(n, _):
        at = pl.ds(pl.multiple_of(n * count, count), count)
        allowed = lax.broadcasted_iota(jnp.int32, (1, size), 1) < limit
        lanes = lax.broadcasted_iota(jnp.int32, (count, 128), 1)
        parts, logs = [], jnp.zeros((count, 128), F32)
        for h in range(heads):
            query = qkv_ref[at, h * HEAD_DIM : (h + 1) * HEAD_DIM]
            key = qkv_ref[:, width + h * HEAD_DIM : width + (h + 1) * HEAD_DIM]
            value = qkv_ref[:, 2 * width + h * HEAD_DIM : 2 * width + (h + 1) * HEAD_DIM]
            scores = (
                lax.dot_general(
                    query, key, (((1,), (1,)), ((), ())), preferred_element_type=F32
                )
                * SCORE_SCALE
            )
            scores = jnp.where(allowed, scores, NEG_FILL)
            top = jnp.max(scores, axis=-1, keepdims=True)
            exps = jnp.exp(scores - top)
            total = jnp.sum(exps, axis=-1, keepdims=True)
            mixed = jnp.dot(exps.astype(BF16), value, preferred_element_type=F32)
            parts.append(mixed / total)
            logs = jnp.where(lanes == h, top + jnp.log(total), logs)
        context_ref[n // 2, n % 2] = packed(jnp.concatenate(parts, axis=1)).astype(BF16)
        log_ref[at, :] = logs
        return 0

    def block(i):
        lax.fori_loop(2 * i, 2 * i + 2, part, 0)

    return block


def packed(rows):
    half = rows.shape[0] // 2
    return jnp.concatenate([rows[:half], rows[half:]], axis=1)


def unpacked(rows):
    half = rows.shape[1] // 2
    return jnp.concatenate([rows[:, :half], rows[:, half:]], axis=0)


def attend_back_block(limit, qkv_ref, log_ref, grad_ref, grad_qkv, grad_key, grad_value, heads, count):
    width = heads * HEAD_DIM
    size = 8 * count
    along_keys = (((1,), (1,)), ((), ()))
    along_rows = (((0,), (0,)), ((), ()))

    def part(n, _):
        at = pl.ds(pl.multiple_of(n * count, count), count)
        allowed = lax.broadcasted_iota(jnp.int32, (1, size), 1) < limit
        grads = unpacked(grad_ref[n // 2, n % 2])
        parts = []
        for h in range(heads):
            query = qkv_ref[at, h * HEAD_DIM : (h + 1) * HEAD_DIM]
            key = qkv_ref[:, width + h * HEAD_DIM : width + (h + 1) * HEAD_DIM]
            value = qkv_ref[:, 2 * width + h * HEAD_DIM : 2 * width + (h + 1) * HEAD_DIM]
            grad_out = grads[:, h * HEAD_DIM : (h + 1) * HEAD_DIM]
            scores = (
                lax.dot_general(query, key, along_keys, preferred_element_type=F32)
                * SCORE_SCALE
            )
            probs = jnp.where(allowed, jnp.exp(scores - log_ref[at, h : h + 1]), 0.0)
            grad_probs = lax.dot_general(
                grad_out, value, along_keys, preferred_element_type=F32
            )
            delta = jnp.sum(probs * grad_probs, axis=-1, keepdims=True)
            grad_scores = (probs * (grad_probs - delta)).astype(BF16)
            parts.append(
                jnp.dot(grad_scores, key, preferred_element_type=F32) * SCORE_SCALE
            )
            key_part = lax.dot_general(
                grad_scores, query, along_rows, preferred_element_type=F32
            )
            value_part = lax.dot_general(
                probs.astype(BF16), grad_out, along_rows, preferred_element_type=F32
            )
            own = slice(h * HEAD_DIM, (h + 1) * HEAD_DIM)
            grad_key[:, own] += key_part
            grad_value[:, own] += value_part
        grad_qkv[at, :width] = jnp.concatenate(parts, axis=1).astype(BF16)
        return 0

    def block(i):
        lax.fori_loop(2 * i, 2 * i + 2, part, 0)

    return block


class Scatter:
    def __init__(self, pos, halves, bufs, sems):
        self.pos, self.halves = pos, halves
        (self.partial, self.theirs, self.a0, self.a1, self.bx, self.by, self.z) = bufs
        (self.sb, self.s0, self.s1, self.dx, self.dy, self.cx, self.cy, self.zs) = sems

    @staticmethod
    def scratch(nb, shape, dtype, halves):
        first, second = half_shapes(shape, halves)
        return [
            pltpu.VMEM((nb, 4, 2) + shape, dtype),
            pltpu.VMEM((nb, 4) + shape, dtype),
            pltpu.VMEM((nb,) + first, dtype),
            pltpu.VMEM((nb,) + second, dtype),
            pltpu.VMEM((nb,) + shape, dtype),
            pltpu.VMEM((nb,) + shape, dtype),
            pltpu.VMEM((nb - 1,) + shape, dtype),
        ]

    @staticmethod
    def sem_scratch(nb):
        return [DMA((2, nb)) for _ in range(8)]

    def mine(self, k, chip):
        return self.partial.at[self.pos.up(k), chip, self.pos.c]

    def sibling_copy(self, k):
        pos = self.pos
        z = pos.up(k)
        return send(
            self.partial.at[z, :, 1 - pos.c],
            self.theirs.at[z],
            self.sb.at[0, k],
            self.sb.at[1, k],
            pos.sib,
        )

    def begin(self, k):
        self.sibling_copy(k).start()

    def copy(self, k, src, dst, sems, there):
        return send(src, dst, sems.at[0, k], sems.at[1, k], there)

    def first_copies(self, k):
        pos = self.pos
        h0, h1 = self.halves
        copies = [
            self.copy(k, self.mine(k, pos.pd).at[h0], self.a0.at[k], self.s0, pos.xn),
            self.copy(k, self.mine(k, pos.px).at[h0], self.bx.at[k].at[h0], self.dx, pos.xn),
        ]
        if h1 is not None:
            copies += [
                self.copy(k, self.mine(k, pos.pd).at[h1], self.a1.at[k], self.s1, pos.yn),
                self.copy(k, self.mine(k, pos.py).at[h1], self.by.at[k].at[h1], self.dy, pos.yn),
            ]
        return copies

    def second_copies(self, k):
        pos = self.pos
        h0, h1 = self.halves
        copies = [
            self.copy(k, self.mine(k, pos.py).at[h0], self.by.at[k].at[h0], self.cy, pos.yn)
        ]
        if h1 is not None:
            copies.append(
                self.copy(k, self.mine(k, pos.px).at[h1], self.bx.at[k].at[h1], self.cx, pos.xn)
            )
        return copies

    def first(self, k):
        pos = self.pos
        z = pos.up(k)
        self.sibling_copy(k).wait_recv()
        for j in range(4):
            chip = pos.chip(3 - j)
            self.partial[z, chip, pos.c] = (
                self.partial[z, chip, pos.c].astype(F32) + self.theirs[z, chip].astype(F32)
            ).astype(self.partial.dtype)
        for copy in self.first_copies(k):
            copy.start()

    def landed(self, ref, sems, k):
        send(ref, ref, sems.at[0, k], sems.at[1, k], self.pos.xn).wait_recv()

    def second(self, k):
        pos = self.pos
        h0, h1 = self.halves
        copies = self.second_copies(k)
        self.landed(self.a0.at[k], self.s0, k)
        ref = self.mine(k, pos.py)
        ref[h0] = (ref[h0].astype(F32) + self.a0[k].astype(F32)).astype(ref.dtype)
        copies[0].start()
        if h1 is not None:
            self.landed(self.a1.at[k], self.s1, k)
            ref = self.mine(k, pos.px)
            ref[h1] = (ref[h1].astype(F32) + self.a1[k].astype(F32)).astype(ref.dtype)
            copies[1].start()

    def z_copy(self, k):
        pos = self.pos
        return send(
            self.bx.at[k], self.z.at[k - 1], self.zs.at[0, k], self.zs.at[1, k], (pos.up(k), pos.s)
        )

    def third(self, k, total):
        pos = self.pos
        h0, h1 = self.halves
        self.landed(self.bx.at[k].at[h0], self.dx, k)
        self.landed(self.by.at[k].at[h0], self.cy, k)
        if h1 is not None:
            self.landed(self.by.at[k].at[h1], self.dy, k)
            self.landed(self.bx.at[k].at[h1], self.cx, k)
        total[...] = (
            self.mine(k, pos.p)[...].astype(F32)
            + self.bx[k].astype(F32)
            + self.by[k].astype(F32)
        )

        def on():
            self.bx[k] = total[...].astype(self.bx.dtype)
            self.z_copy(k).start()

        guarded(k != 0, on)

    def last(self, total):
        value = total[...]
        for k in range(1, self.pos.nb):
            self.landed(self.z.at[k - 1], self.zs, k)
            value = value + self.z[k - 1].astype(F32)
        total[...] = value

    def drain(self):
        def done(k, _):
            self.sibling_copy(k).wait_send()
            for copy in self.first_copies(k) + self.second_copies(k):
                copy.wait_send()
            guarded(k != 0, lambda: self.z_copy(k).wait_send())
            return 0

        lax.fori_loop(0, self.pos.nb, done, 0)


def half_shapes(shape, halves):
    def cut(half):
        return tuple(n if h == slice(None) else h.size for n, h in zip(shape, half))

    first = cut(halves[0])
    return first, (first if halves[1] is None else cut(halves[1]))


class RowScatter:
    def __init__(self, pos, out, bufs, sems):
        self.pos, self.out = pos, out
        self.mine, self.a0, self.a1, self.bx, self.by, self.far, self.near = bufs
        (self.sm,) = sems

    @staticmethod
    def scratch(rows, columns):
        return [
            pltpu.VMEM((rows, columns), BF16),
            pltpu.VMEM((rows, columns), BF16),
            pltpu.VMEM((2, rows, columns), BF16),
            pltpu.VMEM((2, rows, columns), BF16),
            pltpu.VMEM((rows, columns), F32),
            pltpu.VMEM((rows, columns), F32),
            DMA((2, 7)),
        ]

    def copy(self, i):
        pos, mine = self.pos, self.mine
        src, dst, there = (
            (mine.at[pos.pd, 0], self.a0, pos.xn),
            (mine.at[pos.pd, 1], self.a1, pos.yn),
            (mine.at[pos.px, 0], self.bx.at[0], pos.xn),
            (mine.at[pos.py, 1], self.by.at[1], pos.yn),
            (mine.at[pos.py, 0], self.by.at[0], pos.yn),
            (mine.at[pos.px, 1], self.bx.at[1], pos.xn),
            (self.far, self.near, pos.sib),
        )[i]
        return send(src, dst, self.sm.at[0, i], self.sm.at[1, i], there)

    def landed(self, i, ref):
        send(ref, ref, self.sm.at[0, i], self.sm.at[1, i], self.pos.xn).wait_recv()

    def first(self):
        for i in range(4):
            self.copy(i).start()

    def second(self):
        pos, mine = self.pos, self.mine
        self.landed(0, self.a0)
        mine[pos.py, 0] = (mine[pos.py, 0].astype(F32) + self.a0[...].astype(F32)).astype(BF16)
        self.copy(4).start()
        self.landed(1, self.a1)
        mine[pos.px, 1] = (mine[pos.px, 1].astype(F32) + self.a1[...].astype(F32)).astype(BF16)
        self.copy(5).start()

    def third(self):
        pos = self.pos
        self.landed(2, self.bx.at[0])
        self.landed(3, self.by.at[1])
        self.landed(4, self.by.at[0])
        self.landed(5, self.bx.at[1])

        def total(core):
            return (
                self.mine[pos.p, core].astype(F32)
                + self.bx[core].astype(F32)
                + self.by[core].astype(F32)
            )

        self.far[...] = total(1 - pos.c)
        self.copy(6).start()
        self.out[pos.c] += total(pos.c)

    def last(self):
        pos = self.pos
        self.landed(6, self.near)
        self.out[1 - pos.c] += self.near[...]
        for i in range(7):
            self.copy(i).wait_send()


class JointScatter:
    def __init__(self, pos, bufs, sems):
        self.pos = pos
        self.partial, self.theirs, self.zbuf, self.sums, self.got = bufs
        self.sb, self.zs, self.ps = sems

    @staticmethod
    def scratch(nb, shape):
        return [
            pltpu.VMEM((nb, 4, 2) + shape, BF16),
            pltpu.VMEM((nb, 4) + shape, BF16),
            pltpu.VMEM((nb - 1, 4) + shape, BF16),
            pltpu.VMEM((4,) + shape, BF16),
            pltpu.VMEM((4,) + shape, BF16),
        ]

    @staticmethod
    def sem_scratch(nb):
        return [DMA((2,)), DMA((2, nb)), DMA((2, 4))]

    def sibling_copy(self):
        pos = self.pos
        return send(
            self.partial.at[:, :, 1 - pos.c], self.theirs, self.sb.at[0], self.sb.at[1], pos.sib
        )

    def z_copy(self, d):
        pos = self.pos
        return send(
            self.partial.at[pos.up(d), :, pos.c],
            self.zbuf.at[d - 1],
            self.zs.at[0, d],
            self.zs.at[1, d],
            (pos.up(d), pos.s),
        )

    def plane_copy(self, k):
        pos = self.pos
        chip = pos.chip(k)
        return send(
            self.sums.at[chip],
            self.got.at[pos.p],
            self.ps.at[0, k],
            self.ps.at[1, k],
            (pos.b, 2 * chip + pos.c),
        )

    def begin(self):
        self.sibling_copy().start()

    def first(self):
        pos = self.pos
        self.sibling_copy().wait_recv()
        for d in (*range(1, pos.nb), 0):
            z = pos.up(d)
            self.partial[z, :, pos.c] = (
                self.partial[z, :, pos.c].astype(F32) + self.theirs[z].astype(F32)
            ).astype(BF16)
            if d:
                self.z_copy(d).start()

    def second(self):
        pos = self.pos
        value = self.partial[pos.b, :, pos.c].astype(F32)
        for d in range(1, pos.nb):
            self.z_copy(d).wait_recv()
            value = value + self.zbuf[d - 1].astype(F32)
        self.sums[...] = value.astype(BF16)
        for k in range(1, 4):
            self.plane_copy(k).start()

    def last(self, out, vec):
        pos = self.pos
        width = out.shape[1] // 12
        self.got[pos.p] = self.sums[pos.p]
        for k in range(1, 4):
            ref = self.got.at[pos.chip(k)]
            send(ref, ref, self.ps.at[0, k], self.ps.at[1, k], pos.sib).wait_recv()
        extra = 0.0
        for chip in range(4):
            value = self.got[chip].astype(F32)
            for n in range(3):
                out[:, (4 * n + chip) * width : (4 * n + chip + 1) * width] = value[
                    :, n * width : (n + 1) * width
                ]
            extra = extra + value[:8, 3 * width : 3 * width + vec]
        self.sibling_copy().wait_send()
        for d in range(1, pos.nb):
            self.z_copy(d).wait_send()
        for k in range(1, 4):
            self.plane_copy(k).wait_send()
        return extra


def normed_rows(residual):
    centered = residual - jnp.mean(residual, axis=-1, keepdims=True)
    inverse = lax.rsqrt(jnp.mean(centered * centered, axis=-1, keepdims=True) + EPSILON)
    return centered * inverse, inverse


def transposed_dot(left, right):
    return lax.dot_general(left, right, (((0,), (0,)), ((), ())), preferred_element_type=F32)


def dot_transposed(left, right):
    return lax.dot_general(left, right, (((1,), (1,)), ((), ())), preferred_element_type=F32)


def feed_and_back(
    lengths, inputs, cotangent, mixed, vectors, hidden_bias,
    output_weight, expand_weight, reduce_weight, rows, weight, qkv, logs, nb, heads,
):
    _, count, model_width = inputs.shape
    hidden = hidden_bias.shape[1]
    block = hidden // nb
    width = heads * HEAD_DIM
    size, tokens = 8 * count, 2 * count
    owners = 8 * nb
    shard = vec = model_width // owners
    per = hidden // owners
    joint_shape = (shard, 3 * width + 64)
    shapes = [(16, 128), (shard, model_width), (shard, hidden), (per, model_width)]
    dtypes = [F32, BF16, BF16, BF16]

    def body(
        lengths_ref, inputs_ref, cotangent_ref, mixed_ref, vectors_ref, bias_ref,
        output_ref, expand_ref, reduce_ref, rows_any, weight_any, qkv_any, log_any,
        result_out, rows_out, joint_out, vectors_out, hidden_out,
        output_out, expand_out, reduce_out,
        output_w, expand_w, reduce_w, rows_ref, weight_ref, qkv_ref, log_ref, loads,
        context, first_normed, first_low, hidden_low, slope, feed, grad_low,
        grad_vectors, grad_bias, parts, small_total,
        grad_context, grad_qkv, grad_key, grad_value,
        *scratch,
    ):
        pos = Place(nb)
        scratch = list(scratch)

        def take(n):
            got = scratch[:n]
            del scratch[:n]
            return got

        mixing = ContextExchange(pos, parts, grad_context, take(2))
        row_sums = RowScatter(pos, rows_out, [hidden_low] + take(6), take(1))
        joints = JointScatter(pos, take(5), take(3))
        smalls, outputs, expands, reduces = (
            Scatter(pos, halves_of(shape), take(7), take(8)) for shape in shapes
        )

        def turn(i):
            return jnp.where(i < 2, 2 - i, 3 * (3 - i))

        def expand_load(z):
            at = pl.ds(z * block if isinstance(z, int) else pl.multiple_of(z * block, block), block)
            return pltpu.make_async_copy(expand_ref.at[:, at], expand_w.at[z], loads.at[z])

        def reduce_load(z):
            at = pl.ds(z * block if isinstance(z, int) else pl.multiple_of(z * block, block), block)
            return pltpu.make_async_copy(reduce_ref.at[at, :], reduce_w.at[z], loads.at[nb + z])

        output_load = pltpu.make_async_copy(output_ref, output_w, loads.at[2 * nb])
        later = [
            pltpu.make_async_copy(src, dst, loads.at[2 * nb + 1 + n])
            for n, (src, dst) in enumerate(
                ((rows_any, rows_ref), (weight_any, weight_ref), (qkv_any, qkv_ref), (log_any, log_ref))
            )
        ]
        output_load.start()
        for z in range(nb):
            expand_load(z).start()
            reduce_load(z).start()
        for copy in later:
            copy.start()
        barrier = pltpu.get_barrier_semaphore()
        partners = [(pos.up(d), pos.s) for d in range(1, nb)] + plane_others(pos)
        for device in partners:
            pl.semaphore_signal(barrier, inc=1, device_id=device, device_id_type=MESH)

        def vector(n):
            return vectors_ref[n : n + 1, :]

        for chip in range(4):
            for j in range(2):
                context[j * count : (j + 1) * count, chip * width : (chip + 1) * width] = unpacked(
                    mixed_ref[chip, j]
                )
        output_load.wait()
        branch = jnp.dot(context[...], output_w[...], preferred_element_type=F32) + vector(4)
        normed, first_inverse = normed_rows(
            inputs_ref[...].reshape(tokens, model_width) + branch
        )
        first_normed[...] = normed
        first = normed * vector(0) + vector(1)
        rows_out[...] = first.reshape(2, count, model_width)
        first_low[...] = first.astype(BF16)
        feed[...] = jnp.broadcast_to(vector(7), feed.shape)

        def forward(z, _):
            at = pl.ds(pl.multiple_of(z * block, block), block)
            expand_load(z).wait()
            before = (
                jnp.dot(first_low[...], expand_w[z], preferred_element_type=F32)
                + bias_ref[:, at]
            )
            half = 0.5 * (1.0 + lax.erf(before * HALF_ROOT))
            low = (before * half).astype(BF16)
            hidden_low[z] = low.reshape(2, count, block)
            slope[z] = half + before * jnp.exp(-0.5 * before * before) * INV_ROOT_TAU
            reduce_load(z).wait()
            feed[...] += jnp.dot(low, reduce_w[z], preferred_element_type=F32)
            return 0

        lax.fori_loop(0, nb, forward, 0)
        normed, inverse = normed_rows(
            rows_out[...].reshape(tokens, model_width) + feed[...]
        )
        result_out[...] = (normed * vector(5) + vector(6)).reshape(2, count, model_width)

        places = pos.s * count + lax.broadcasted_iota(jnp.int32, (count, 1), 0)
        grad_res = jnp.concatenate(
            [jnp.where(places < lengths_ref[j], cotangent_ref[j], 0.0) for j in range(2)]
        )
        grad_second, gain, shift = norm_back(grad_res, normed, inverse, vector(5))
        grad_low[...] = grad_second.astype(BF16)
        grad_vectors[...] = jnp.zeros_like(grad_vectors)
        grad_vectors[5:6, :] = gain[None]
        grad_vectors[6:7, :] = shift[None]
        grad_vectors[7:8, :] = jnp.sum(grad_low[...].astype(F32), axis=0, keepdims=True)
        feed[...] = grad_second

        def backward(i, _):
            z = pos.up(turn(i))
            at = pl.ds(pl.multiple_of(z * block, block), block)
            for n in range(2):
                cut = slice(n * (block // 2), (n + 1) * (block // 2))
                reduces.partial[z, 2 * n : 2 * n + 2] = (
                    transposed_dot(
                        hidden_low[z, :, :, cut].reshape(tokens, block // 2), grad_low[...]
                    )
                    .reshape(2, 2, per, model_width)
                    .astype(BF16)
                )
            reduces.begin(turn(i))
            low = (dot_transposed(grad_low[...], reduce_w[z]) * slope[z]).astype(BF16)
            grad_bias[:, at] = jnp.sum(low.astype(F32), axis=0, keepdims=True)
            for n in range(2):
                cut = slice(n * (model_width // 2), (n + 1) * (model_width // 2))
                expands.partial[n * nb // 2 : (n + 1) * nb // 2, :, :, :, at] = (
                    transposed_dot(first_low[:, cut], low)
                    .reshape(nb // 2, 4, 2, shard, block)
                    .astype(BF16)
                )
            feed[...] += dot_transposed(low, expand_w[z])
            reduces.first(turn(i))
            return 0

        pl.semaphore_wait(barrier, len(partners))
        lax.fori_loop(0, nb, backward, 0)
        for k in range(nb):
            expands.begin(turn(k))
        grads, gain, shift = norm_back(feed[...], first_normed[...], first_inverse, vector(0))
        rows_out[...] = grads.reshape(2, count, model_width)
        low = grads.astype(BF16)
        grad_low[...] = low
        grad_vectors[0:1, :] = gain[None]
        grad_vectors[1:2, :] = shift[None]
        grad_vectors[4:5, :] = jnp.sum(low.astype(F32), axis=0, keepdims=True)
        low = dot_transposed(low, output_w[...]).astype(BF16)
        for chip in range(4):
            for j in range(2):
                parts[chip, j] = packed(
                    low[j * count : (j + 1) * count, chip * width : (chip + 1) * width]
                )
        mixing.start()
        for n in range(2):
            cut = slice(n * (model_width // 2), (n + 1) * (model_width // 2))
            outputs.partial[n * nb // 2 : (n + 1) * nb // 2] = (
                transposed_dot(context[:, cut], grad_low[...])
                .reshape(nb // 2, 4, 2, shard, model_width)
                .astype(BF16)
            )
        for owner in range(owners):
            here = (owner // 8, owner % 8 // 2, owner % 2)
            smalls.partial[here] = jnp.concatenate(
                [
                    jnp.pad(
                        grad_vectors[:, owner * vec : (owner + 1) * vec], ((0, 0), (0, 128 - vec))
                    ),
                    jnp.broadcast_to(
                        jnp.pad(
                            grad_bias[:, owner * per : (owner + 1) * per], ((0, 0), (0, 128 - per))
                        ),
                        (8, 128),
                    ),
                ]
            )
        for k in range(nb):
            outputs.begin(turn(k))
            smalls.begin(turn(k))

        grad_key[...] = jnp.zeros_like(grad_key)
        grad_value[...] = jnp.zeros_like(grad_value)
        for copy in later:
            copy.wait()
        back = attend_back_block(
            lengths_ref[pos.c], qkv_ref, log_ref, grad_context, grad_qkv, grad_key, grad_value,
            heads, count,
        )

        def middle(i, _):
            k = turn(i)
            reduces.second(k)
            expands.first(k)
            guarded(i > 0, lambda: reduces.third(turn(i - 1), reduce_out))
            guarded(i == 0, mixing.arrive)
            back(i)
            guarded(i > 0, lambda: expands.second(turn(i - 1)))
            guarded(i > 1, lambda: expands.third(turn(i - 2), expand_out))
            return 0

        lax.fori_loop(0, nb, middle, 0)

        def late(i, _):
            k = turn(i)
            outputs.first(k)
            smalls.first(k)
            return 0

        grad_qkv[:, width : 2 * width] = (grad_key[...] * SCORE_SCALE).astype(BF16)
        grad_qkv[:, 2 * width :] = grad_value[...].astype(BF16)

        def spread(i, _):
            at = pl.ds(pl.multiple_of(i * tokens, tokens), tokens)
            row_sums.mine[i] = (
                dot_transposed(grad_qkv[at, :], weight_ref[...])
                .astype(BF16)
                .reshape(2, count, model_width)
            )
            return 0

        for z in range(nb):
            grad_joint = transposed_dot(
                rows_ref[:, :, :, z * 8 * shard : (z + 1) * 8 * shard].reshape(size, 8 * shard),
                grad_qkv[...],
            )
            joints.partial[z, :, :, :, : 3 * width] = grad_joint.reshape(
                4, 2, shard, 3 * width
            ).astype(BF16)
        sums = jnp.sum(grad_qkv[...].astype(F32), axis=0, keepdims=True)
        joints.partial[:, :, :, :, 3 * width :] = jnp.zeros((nb, 4, 2, shard, 64), BF16)
        for s in range(8):
            at = slice(s * vec, (s + 1) * vec)
            value = jnp.concatenate([sums[:, :width][:, at], sums[:, 2 * width :][:, at]])
            joints.partial[pos.p, s // 2, s % 2, :, 3 * width :] = jnp.pad(
                value, ((0, shard - 2), (0, 64 - vec))
            ).astype(BF16)
        joints.begin()
        lax.fori_loop(0, 4, spread, 0)
        row_sums.first()
        joints.first()
        expands.second(turn(3))
        lax.fori_loop(0, nb, late, 0)

        expands.third(turn(2), expand_out)
        reduces.third(turn(nb - 1), reduce_out)
        reduces.last(reduce_out)
        reduces.drain()
        row_sums.second()

        def final(i, _):
            k = turn(i)
            outputs.second(k)
            smalls.second(k)
            return 0

        lax.fori_loop(0, nb, final, 0)
        expands.third(turn(nb - 1), expand_out)
        joints.second()
        row_sums.third()
        expands.last(expand_out)
        expands.drain()
        mixing.drain()

        def end(i, _):
            k = turn(i)
            outputs.third(k, output_out)
            smalls.third(k, small_total)
            return 0

        lax.fori_loop(0, nb, end, 0)
        extra = joints.last(joint_out, vec)
        row_sums.last()
        for scatter, out in ((outputs, output_out), (smalls, small_total)):
            scatter.last(out)
            scatter.drain()
        lines = lax.broadcasted_iota(jnp.int32, (8, vec), 0)
        value = jnp.where(lines == 2, extra[0:1], small_total[:8, :vec])
        vectors_out[...] = jnp.where(lines == 3, extra[1:2], value)
        hidden_out[...] = small_total[8:9, :per]

    def vmem(shape, dtype):
        return pltpu.VMEM(shape, dtype)

    scratch = [
        vmem((model_width, model_width), BF16),
        vmem((nb, model_width, block), BF16),
        vmem((nb, block, model_width), BF16),
        vmem(rows.shape, BF16),
        vmem(weight.shape, BF16),
        vmem(qkv.shape, BF16),
        vmem(logs.shape, F32),
        DMA((2 * nb + 5,)),
        vmem((tokens, model_width), BF16),
        vmem((tokens, model_width), F32),
        vmem((tokens, model_width), BF16),
        vmem((nb, 2, count, block), BF16),
        vmem((nb, tokens, block), F32),
        vmem((tokens, model_width), F32),
        vmem((tokens, model_width), BF16),
        vmem((8, model_width), F32),
        vmem((1, hidden), F32),
        vmem((4, 2, count // 2, 2 * width), BF16),
        vmem((16, 128), F32),
        vmem((4, 2, count // 2, 2 * width), BF16),
        vmem((size, 3 * width), BF16),
        vmem((size, width), F32),
        vmem((size, width), F32),
    ]
    scratch += ContextExchange.scratch() + RowScatter.scratch(count, model_width)
    scratch += JointScatter.scratch(nb, joint_shape) + JointScatter.sem_scratch(nb)
    for shape, dtype in zip(shapes, dtypes):
        scratch += Scatter.scratch(nb, shape, dtype, halves_of(shape)) + Scatter.sem_scratch(nb)
    return pl.pallas_call(
        body,
        out_shape=tuple(
            jax.ShapeDtypeStruct(shape, F32)
            for shape in (
                inputs.shape,
                inputs.shape,
                (shard, 3 * model_width),
                (8, vec),
                (1, per),
                shapes[1],
                shapes[2],
                shapes[3],
            )
        ),
        in_specs=[SM] + [VM] * 5 + [ANY] * 7,
        out_specs=(VM,) * 8,
        scratch_shapes=scratch,
        name="feed_and_back",
        compiler_params=pltpu.CompilerParams(
            collective_id=4, has_side_effects=True, vmem_limit_bytes=VMEM_LIMIT
        ),
    )(
        lengths, inputs, cotangent, mixed, vectors, hidden_bias,
        output_weight, expand_weight, reduce_weight, rows, weight, qkv, logs,
    )


def hand_over(*arrays):
    count = len(arrays)
    pieces = []
    for n, array in enumerate(arrays):
        if array.ndim == 3:
            half = array.shape[1] // 2
            pieces += [
                (n, (i, pl.ds(j * half, half))) for i in range(array.shape[0]) for j in range(2)
            ]
        else:
            pieces.append((n, slice(None)))

    def body(*refs):
        came, out, held = refs[:count], refs[count : 2 * count], refs[2 * count : 3 * count]
        sems = refs[3 * count]
        loads = [
            pltpu.make_async_copy(came[n].at[cut], held[n].at[cut], sems.at[0, i])
            for i, (n, cut) in enumerate(pieces)
        ]
        stores = [
            pltpu.make_async_copy(held[n].at[cut], out[n].at[cut], sems.at[1, i])
            for i, (n, cut) in enumerate(pieces)
        ]
        for copy in loads:
            copy.start()
        for load, store in zip(loads, stores):
            load.wait()
            store.start()
        for copy in stores:
            copy.wait()

    return pl.pallas_call(
        body,
        out_shape=tuple(jax.ShapeDtypeStruct(a.shape, a.dtype) for a in arrays),
        in_specs=[ANY] * count,
        out_specs=(ANY,) * count,
        scratch_shapes=[pltpu.VMEM(a.shape, a.dtype) for a in arrays] + [DMA((2, len(pieces)))],
        name="hand_over",
        compiler_params=pltpu.CompilerParams(vmem_limit_bytes=VMEM_LIMIT),
    )(*arrays)


def plane_on_device(
    inputs,
    cotangent,
    lengths,
    joint_weight,
    output_weight,
    vectors,
    expand_weight,
    expand_bias,
    reduce_weight,
):
    nb = lax.axis_size("batch")
    _, _, model_width = inputs.shape
    hidden_width = expand_weight.shape[1]
    heads = model_width // (4 * HEAD_DIM)
    per = expand_bias.shape[0]
    (
        vector_rows, full_bias, rows_all, joint_all, qkv, logs,
        mixed, output_all, expand_all, reduce_all,
    ) = gather_attend(
        lengths,
        inputs,
        joint_weight,
        vectors,
        expand_bias.reshape(1, per),
        output_weight,
        expand_weight,
        reduce_weight,
        nb,
        heads,
    )
    full_output = output_all.reshape(model_width, model_width)
    full_expand = expand_all.reshape(model_width, hidden_width)
    full_reduce = reduce_all.reshape(hidden_width, model_width)

    result, grad_inputs, joint_sum, vectors_sum, bias_sum, output_sum, expand_sum, reduce_sum = (
        feed_and_back(
            lengths,
            inputs,
            cotangent,
            mixed,
            vector_rows,
            full_bias,
            full_output,
            full_expand,
            full_reduce,
            rows_all,
            joint_all,
            qkv,
            logs,
            nb,
            heads,
        )
    )
    (
        result, grad_inputs, joint_sum, output_sum, vectors_sum, expand_sum, bias_sum, reduce_sum,
    ) = hand_over(
        result, grad_inputs, joint_sum, output_sum, vectors_sum, expand_sum, bias_sum, reduce_sum
    )
    return (
        result,
        grad_inputs,
        joint_sum,
        output_sum,
        vectors_sum,
        expand_sum,
        bias_sum.reshape(per),
        reduce_sum,
    )


def plane_fits(mesh, inputs, expand_bias, expand_weight):
    return (
        mesh.shape["seq"] == 8
        and mesh.shape["batch"] == 4
        and inputs[0] == 2 * mesh.shape["batch"]
        and HEADS % 4 == 0
        and inputs[2] == HEADS * HEAD_DIM
        and inputs[1] % (8 * 16) == 0
        and inputs[2] % 256 == 0
        and expand_weight[0] % (8 * 32) == 0
        and expand_weight[1] % (16 * 32) == 0
        and expand_bias[0] <= 128 * 32
        and expand_weight[1] == 4 * inputs[2]
    )


def solution(mesh):
    def program(*args):
        fits = plane_fits(mesh, args[0].shape, args[7].shape, args[6].shape)
        return jax.shard_map(
            plane_on_device if fits else general_on_device,
            mesh=mesh,
            in_specs=(
                P("batch", "seq", None),
                P("batch", "seq", None),
                P("batch"),
                P(("batch", "seq"), None),
                P(("batch", "seq"), None),
                P(None, ("batch", "seq")),
                P(("batch", "seq"), None),
                P(("batch", "seq")),
                P(("batch", "seq"), None),
            ),
            out_specs=(
                P("batch", "seq", None),
                P("batch", "seq", None),
                P(("batch", "seq"), None),
                P(("batch", "seq"), None),
                P(None, ("batch", "seq")),
                P(("batch", "seq"), None),
                P(("batch", "seq")),
                P(("batch", "seq"), None),
            ),
            check_vma=False,
        )(*args)

    return program
```

```python
import functools
import math

import jax
import jax.numpy as jnp
from jax import lax
from jax.experimental import pallas as pl
from jax.experimental.pallas import tpu as pltpu
from jax.sharding import PartitionSpec as P

HEADS = 12
HEAD_DIM = 64


EPSILON = 1e-12
SCORE_SCALE = 0.125
NEG_FILL = -1e30
HALF_ROOT = 0.7071067811865476
INV_ROOT_TAU = 0.3989422804014327
block_limit = 256


def layer_norm(residual, norm_gain, norm_shift):
    centered = residual - jnp.mean(residual, axis=-1, keepdims=True)
    inverse = lax.rsqrt(jnp.mean(centered * centered, axis=-1, keepdims=True) + EPSILON)
    normed = centered * inverse
    return (normed * norm_gain + norm_shift, normed, inverse)


def norm_back(grad_out, normed, inverse, norm_gain):
    grad_normed = grad_out * norm_gain
    mean_grad = jnp.mean(grad_normed, axis=-1, keepdims=True)
    mean_proj = jnp.mean(grad_normed * normed, axis=-1, keepdims=True)
    grad_in = inverse * (grad_normed - mean_grad - normed * mean_proj)
    return (grad_in, jnp.sum(grad_out * normed, axis=0), jnp.sum(grad_out, axis=0))


def gelu_value(before_gelu):
    return 0.5 * before_gelu * (1.0 + lax.erf(before_gelu * HALF_ROOT))


def gelu_slope(before_gelu):
    return (
        0.5 * (1.0 + lax.erf(before_gelu * HALF_ROOT))
        + before_gelu * jnp.exp(-0.5 * before_gelu * before_gelu) * INV_ROOT_TAU
    )


def over_blocks(piece_rows, block_fn, carried):
    block_size = math.gcd(piece_rows, block_limit)

    def run_block(block_index, current):
        return block_fn(current, block_index * block_size, block_size)

    return lax.fori_loop(0, piece_rows // block_size, run_block, carried)


def head_scores(left_heads, right_heads, right_places, lengths):
    scores = (
        jnp.einsum("sqhd,skhd->shqk", left_heads, right_heads, preferred_element_type=jnp.float32)
        * SCORE_SCALE
    )
    allowed = right_places[None, :] < lengths[:, None]
    return jnp.where(allowed[:, None, None, :], scores, NEG_FILL)


def cut_heads(gathered_piece, offset, block_size, head_count):
    sliced = lax.dynamic_slice_in_dim(gathered_piece, offset, block_size, 1)
    return sliced.reshape(sliced.shape[0], block_size, head_count, -1)


def gather_attention(joint_weight, output_weight, vectors):
    return (
        lax.all_gather(joint_weight, ("batch", "seq"), axis=0, tiled=True),
        lax.all_gather(output_weight, ("batch", "seq"), axis=0, tiled=True),
        lax.all_gather(vectors, ("batch", "seq"), axis=1, tiled=True),
    )


def gather_feed(expand_weight, reduce_weight, expand_bias):
    return (
        lax.all_gather(expand_weight, ("batch", "seq"), axis=0, tiled=True),
        lax.all_gather(reduce_weight, ("batch", "seq"), axis=0, tiled=True),
        lax.all_gather(expand_bias, ("batch", "seq"), axis=0, tiled=True),
    )


def general_on_device(
    inputs,
    cotangent,
    lengths,
    joint_weight,
    output_weight,
    vectors,
    expand_weight,
    expand_bias,
    reduce_weight,
):
    seq_count, row_count, model_width = inputs.shape
    head_count = HEADS
    head_size = HEAD_DIM
    tokens = seq_count * row_count
    head_shape = (seq_count, row_count, head_count, head_size)
    own_places = lax.axis_index("seq") * row_count + jnp.arange(row_count, dtype=jnp.int32)
    row_valid = own_places[None, :] < lengths[:, None]
    row_mask = row_valid.reshape(tokens, 1).astype(jnp.float32)
    full_joint, full_output, full_vectors = gather_attention(joint_weight, output_weight, vectors)
    vector_rows = full_vectors.astype(jnp.float32)
    flat_inputs = inputs.reshape(tokens, model_width)
    input_low = flat_inputs.astype(jnp.bfloat16)
    projected = jnp.dot(input_low, full_joint, preferred_element_type=jnp.float32)
    query_low = (projected[:, :model_width] + vector_rows[2]).astype(jnp.bfloat16)
    key_low = projected[:, model_width : 2 * model_width].astype(jnp.bfloat16)
    value_low = (projected[:, 2 * model_width :] + vector_rows[3]).astype(jnp.bfloat16)
    query_heads = query_low.reshape(head_shape)
    key_rows = key_low.reshape(seq_count, row_count, model_width)
    value_rows = value_low.reshape(seq_count, row_count, model_width)
    start_state = (
        jnp.full((seq_count, head_count, row_count), NEG_FILL, jnp.float32),
        jnp.zeros((seq_count, head_count, row_count), jnp.float32),
        jnp.zeros(head_shape, jnp.float32),
    )
    key_piece = lax.all_gather(key_rows, "seq", axis=1, tiled=True)
    value_piece = lax.all_gather(value_rows, "seq", axis=1, tiled=True)

    def forward_score_block(current, offset, block_size):
        running_max, running_sum, summed = current
        key_heads = cut_heads(key_piece, offset, block_size, head_count)
        value_heads = cut_heads(value_piece, offset, block_size, head_count)
        key_places = offset + jnp.arange(block_size, dtype=jnp.int32)
        scores = head_scores(query_heads, key_heads, key_places, lengths)
        new_max = jnp.maximum(running_max, jnp.max(scores, axis=-1))
        factor = jnp.exp(running_max - new_max)
        exp_scores = jnp.exp(scores - new_max[..., None])
        running_sum = running_sum * factor + jnp.sum(exp_scores, axis=-1)
        update = jnp.einsum(
            "shqk,skhd->sqhd",
            exp_scores.astype(jnp.bfloat16),
            value_heads,
            preferred_element_type=jnp.float32,
        )
        summed = summed * jnp.transpose(factor, (0, 2, 1))[..., None] + update
        return (new_max, running_sum, summed)

    running_max, running_sum, summed = over_blocks(
        key_piece.shape[1], forward_score_block, start_state
    )
    attended = summed / jnp.transpose(running_sum, (0, 2, 1))[..., None]
    log_total = jnp.transpose(running_max + jnp.log(running_sum), (0, 2, 1))
    context_low = attended.reshape(tokens, model_width).astype(jnp.bfloat16)
    branch = jnp.dot(context_low, full_output, preferred_element_type=jnp.float32) + vector_rows[4]
    first, first_normed, first_inverse = layer_norm(
        flat_inputs + branch, vector_rows[0], vector_rows[1]
    )
    first_low = first.astype(jnp.bfloat16)
    full_expand, full_reduce, full_bias = gather_feed(expand_weight, reduce_weight, expand_bias)
    before_gelu = jnp.dot(
        first_low, full_expand, preferred_element_type=jnp.float32
    ) + full_bias.astype(jnp.float32)
    hidden_low = gelu_value(before_gelu).astype(jnp.bfloat16)
    feed = jnp.dot(hidden_low, full_reduce, preferred_element_type=jnp.float32) + vector_rows[7]
    result, second_normed, second_inverse = layer_norm(first + feed, vector_rows[5], vector_rows[6])
    full_expand, full_reduce, full_bias = gather_feed(expand_weight, reduce_weight, expand_bias)
    full_joint, full_output, full_vectors = gather_attention(joint_weight, output_weight, vectors)
    grad_res = cotangent.reshape(tokens, model_width) * row_mask
    grad_second, grad_gain_two, grad_shift_two = norm_back(
        grad_res, second_normed, second_inverse, vector_rows[5]
    )
    grad_feed_low = grad_second.astype(jnp.bfloat16)
    grad_reduce_local = jnp.dot(hidden_low.T, grad_feed_low, preferred_element_type=jnp.float32)
    grad_hidden = jnp.dot(
        grad_feed_low, full_reduce.T, preferred_element_type=jnp.float32
    ) * gelu_slope(before_gelu)
    grad_hidden_low = grad_hidden.astype(jnp.bfloat16)
    grad_expand_local = jnp.dot(first_low.T, grad_hidden_low, preferred_element_type=jnp.float32)
    grad_bias_local = jnp.sum(grad_hidden_low.astype(jnp.float32), axis=0)
    grad_first = grad_second + jnp.dot(
        grad_hidden_low, full_expand.T, preferred_element_type=jnp.float32
    )
    grad_resid, grad_gain_one, grad_shift_one = norm_back(
        grad_first, first_normed, first_inverse, vector_rows[0]
    )
    grad_branch_low = grad_resid.astype(jnp.bfloat16)
    grad_output_local = jnp.dot(context_low.T, grad_branch_low, preferred_element_type=jnp.float32)
    grad_context_low = jnp.dot(
        grad_branch_low, full_output.T, preferred_element_type=jnp.float32
    ).astype(jnp.bfloat16)
    grad_context_heads = grad_context_low.reshape(head_shape)
    row_delta = jnp.sum(grad_context_heads.astype(jnp.float32) * attended, axis=-1)
    log_heads = jnp.transpose(log_total, (0, 2, 1))
    delta_heads = jnp.transpose(row_delta, (0, 2, 1))
    query_key_piece = lax.all_gather(key_rows, "seq", axis=1, tiled=True)
    query_value_piece = lax.all_gather(value_rows, "seq", axis=1, tiled=True)

    def query_score_block(current, offset, block_size):
        key_heads = cut_heads(query_key_piece, offset, block_size, head_count)
        value_heads = cut_heads(query_value_piece, offset, block_size, head_count)
        key_places = offset + jnp.arange(block_size, dtype=jnp.int32)
        scores = head_scores(query_heads, key_heads, key_places, lengths)
        softmax_rows = jnp.exp(scores - log_heads[..., None])
        grad_probs = jnp.einsum(
            "sqhd,skhd->shqk", grad_context_heads, value_heads, preferred_element_type=jnp.float32
        )
        grad_scores = (softmax_rows * (grad_probs - delta_heads[..., None])).astype(jnp.bfloat16)
        return (
            current
            + jnp.einsum(
                "shqk,skhd->sqhd", grad_scores, key_heads, preferred_element_type=jnp.float32
            )
            * SCORE_SCALE
        )

    grad_query = over_blocks(
        query_key_piece.shape[1], query_score_block, jnp.zeros(head_shape, jnp.float32)
    )
    own_keys = key_low.reshape(head_shape)
    own_values = value_low.reshape(head_shape)
    query_rows = query_low.reshape(seq_count, row_count, model_width)
    grad_context_rows = grad_context_low.reshape(seq_count, row_count, model_width)
    zero_heads = jnp.zeros(head_shape, jnp.float32)
    query_piece = lax.all_gather(query_rows.astype(jnp.float32), "seq", axis=1, tiled=True).astype(
        jnp.bfloat16
    )
    grad_piece = lax.all_gather(
        grad_context_rows.astype(jnp.float32), "seq", axis=1, tiled=True
    ).astype(jnp.bfloat16)
    log_piece = lax.all_gather(log_total, "seq", axis=1, tiled=True)
    delta_piece = lax.all_gather(row_delta, "seq", axis=1, tiled=True)

    def key_score_block(current, offset, block_size):
        grad_key, grad_value = current
        query_block = cut_heads(query_piece, offset, block_size, head_count)
        grad_block = cut_heads(grad_piece, offset, block_size, head_count)
        log_block = jnp.transpose(
            lax.dynamic_slice_in_dim(log_piece, offset, block_size, 1), (0, 2, 1)
        )
        delta_block = jnp.transpose(
            lax.dynamic_slice_in_dim(delta_piece, offset, block_size, 1), (0, 2, 1)
        )
        scores = head_scores(query_block, own_keys, own_places, lengths)
        softmax_rows = jnp.exp(scores - log_block[..., None])
        grad_value = grad_value + jnp.einsum(
            "shqk,sqhd->skhd",
            softmax_rows.astype(jnp.bfloat16),
            grad_block,
            preferred_element_type=jnp.float32,
        )
        grad_probs = jnp.einsum(
            "sqhd,skhd->shqk", grad_block, own_values, preferred_element_type=jnp.float32
        )
        grad_scores = (softmax_rows * (grad_probs - delta_block[..., None])).astype(jnp.bfloat16)
        grad_key = (
            grad_key
            + jnp.einsum(
                "shqk,sqhd->skhd", grad_scores, query_block, preferred_element_type=jnp.float32
            )
            * SCORE_SCALE
        )
        return (grad_key, grad_value)

    grad_key, grad_value = over_blocks(
        query_piece.shape[1], key_score_block, (zero_heads, zero_heads)
    )
    grad_query_low = grad_query.reshape(tokens, model_width).astype(jnp.bfloat16)
    grad_key_low = grad_key.reshape(tokens, model_width).astype(jnp.bfloat16)
    grad_value_low = grad_value.reshape(tokens, model_width).astype(jnp.bfloat16)
    grad_projected = jnp.concatenate([grad_query_low, grad_key_low, grad_value_low], axis=1)
    grad_joint_local = jnp.dot(input_low.T, grad_projected, preferred_element_type=jnp.float32)
    grad_inputs = grad_resid + jnp.dot(
        grad_projected, full_joint.T, preferred_element_type=jnp.float32
    )
    grad_vector_local = jnp.stack(
        [
            grad_gain_one,
            grad_shift_one,
            jnp.sum(grad_query_low.astype(jnp.float32), axis=0),
            jnp.sum(grad_value_low.astype(jnp.float32), axis=0),
            jnp.sum(grad_branch_low.astype(jnp.float32), axis=0),
            grad_gain_two,
            grad_shift_two,
            jnp.sum(grad_feed_low.astype(jnp.float32), axis=0),
        ],
        axis=0,
    )
    every_grad = (
        lax.psum_scatter(grad_joint_local, ("batch", "seq"), scatter_dimension=0, tiled=True),
        lax.psum_scatter(grad_output_local, ("batch", "seq"), scatter_dimension=0, tiled=True),
        lax.psum_scatter(grad_vector_local, ("batch", "seq"), scatter_dimension=1, tiled=True),
        lax.psum_scatter(grad_expand_local, ("batch", "seq"), scatter_dimension=0, tiled=True),
        lax.psum_scatter(grad_reduce_local, ("batch", "seq"), scatter_dimension=0, tiled=True),
        lax.psum_scatter(grad_bias_local, ("batch", "seq"), scatter_dimension=0, tiled=True),
    )
    summed_grads = (
        every_grad[0],
        every_grad[1],
        every_grad[2],
        every_grad[3],
        every_grad[5],
        every_grad[4],
    )
    return (
        result.reshape(seq_count, row_count, model_width),
        grad_inputs.reshape(seq_count, row_count, model_width),
        summed_grads[0],
        summed_grads[1],
        summed_grads[2],
        summed_grads[3],
        summed_grads[4],
        summed_grads[5],
    )


MESH = pl.DeviceIdType.MESH
ANY = pl.BlockSpec(memory_space=pl.ANY)
VM = pl.BlockSpec(memory_space=pltpu.VMEM)
SM = pl.BlockSpec(memory_space=pltpu.SMEM)
DMA = pltpu.SemaphoreType.DMA
VMEM_LIMIT = 60 << 20
F32 = jnp.float32
BF16 = jnp.bfloat16


def send(src, dst, send_sem, recv_sem, device):
    return pltpu.make_async_remote_copy(
        src_ref=src,
        dst_ref=dst,
        send_sem=send_sem,
        recv_sem=recv_sem,
        device_id=device,
        device_id_type=MESH,
    )


class Place:
    def __init__(self, nb):
        self.nb = nb
        self.b = lax.axis_index("batch")
        self.s = lax.axis_index("seq")
        self.c = self.s % 2
        self.p = self.s // 2
        x, y = self.p % 2, self.p // 2
        self.px = 2 * y + (1 - x)
        self.py = 2 * (1 - y) + x
        self.pd = 2 * (1 - y) + (1 - x)
        self.sib = (self.b, 2 * self.p + 1 - self.c)
        self.xn = (self.b, 2 * self.px + self.c)
        self.yn = (self.b, 2 * self.py + self.c)

    def chip(self, step):
        return (self.p, self.px, self.py, self.pd)[step]

    def up(self, step):
        return (self.b + step) % self.nb

    def down(self, step):
        return (self.b + self.nb - step) % self.nb


def greet_near(pos):
    barrier = pltpu.get_barrier_semaphore()

    def signal(device):
        pl.semaphore_signal(barrier, inc=1, device_id=device, device_id_type=MESH)

    for device in plane_others(pos):
        signal(device)
    last = pos.nb - 1
    guarded(pos.b < last, lambda: signal(((pos.b + 1) % pos.nb, pos.s)))
    guarded(pos.b > 0, lambda: signal(((pos.b + last) % pos.nb, pos.s)))


def meet_near(pos):
    beside = jnp.where(pos.b < pos.nb - 1, 1, 0) + jnp.where(pos.b > 0, 1, 0)
    pl.semaphore_wait(pltpu.get_barrier_semaphore(), 7 + beside)


def same_core(pos):
    return [
        (pos.up(d), 2 * pos.chip(k) + pos.c)
        for d in range(pos.nb)
        for k in range(4)
        if d or k
    ]


def plane_others(pos):
    return [
        (pos.b, 2 * pos.chip(k) + (pos.c if j == 0 else 1 - pos.c))
        for k in range(4)
        for j in range(2)
        if k or j
    ]


def guarded(condition, action):
    if isinstance(condition, bool):
        if condition:
            action()
    else:

        @pl.when(condition)
        def _():
            action()


class Chain:
    def __init__(self, pos, mine, spot, sems):
        self.pos, self.mine, self.spot = pos, mine, spot
        self.up, self.down = sems

    @staticmethod
    def scratch(nb):
        return [DMA((2, nb)), DMA((2, nb))]

    def copy(self, src, z, sems, hop, there):
        pos = self.pos
        return send(src, self.spot(z), sems.at[0, hop], sems.at[1, hop], (there, pos.s))

    def moves(self, hop):
        pos = self.pos
        last = pos.nb - 1
        low, high = (pos.b - hop + 1 + pos.nb) % pos.nb, (pos.b + hop - 1) % pos.nb
        above, below = (pos.b + 1) % pos.nb, (pos.b + last) % pos.nb
        own = isinstance(hop, int) and hop == 1
        return (
            (
                (pos.b >= hop - 1) & (pos.b < last),
                self.copy(self.mine if own else self.spot(low), low, self.up, hop, above),
            ),
            (
                (pos.b + hop - 1 < pos.nb) & (pos.b > 0),
                self.copy(self.mine if own else self.spot(high), high, self.down, hop, below),
            ),
        )

    def start(self, hop=1):
        for made, copy in self.moves(hop):
            guarded(made, copy.start)

    def hop(self, hop):
        pos = self.pos
        low, high = (pos.b - hop + pos.nb) % pos.nb, (pos.b + hop) % pos.nb
        for made, z, sems in (
            (pos.b >= hop, low, self.up),
            (pos.b + hop < pos.nb, high, self.down),
        ):
            guarded(made, self.copy(self.spot(z), z, sems, hop, pos.b).wait_recv)
        guarded(hop < pos.nb - 1, lambda: self.start(hop + 1))

    def drain(self):
        for hop in range(1, self.pos.nb):
            for made, copy in self.moves(hop):
                guarded(made, copy.wait_send)


class Gather:
    def __init__(self, pos, shard, out, halves, sems):
        self.pos, self.shard, self.out, self.halves = pos, shard, out, halves
        self.xs, self.ys, self.f0, self.f1, self.sb, self.local_sem = sems[:6]
        self.chain = Chain(pos, shard, lambda z: out.at[z, pos.p, pos.c], sems[6:8])
        self.across = Chain(
            pos, out.at[pos.b, pos.pd, pos.c], lambda z: out.at[z, pos.pd, pos.c], sems[8:]
        )

    @staticmethod
    def scratch(nb):
        return [DMA((2, nb))] * 2 + [DMA((2,))] * 2 + [DMA((2, nb + 3)), DMA] + Chain.scratch(nb) * 2

    def z(self, k):
        return jnp.where(k <= self.pos.b, self.pos.b - k, k)

    def own(self):
        pos = self.pos
        self.local = pltpu.make_async_copy(
            self.shard, self.out.at[pos.b, pos.p, pos.c], self.local_sem
        )
        self.local.start()

    def x_copy(self, k, src=None):
        pos = self.pos
        there = self.out.at[self.z(k), pos.p, pos.c]
        src = there if src is None else src
        return send(src, there, self.xs.at[0, k], self.xs.at[1, k], pos.xn)

    def y_copy(self, k, src=None):
        pos = self.pos
        there = self.out.at[self.z(k), pos.p, pos.c]
        src = there if src is None else src
        return send(src, there, self.ys.at[0, k], self.ys.at[1, k], pos.yn)

    def plane(self, k, src=None):
        self.x_copy(k, src).start()
        self.y_copy(k, src).start()

    def landed(self, sems, k, chip):
        pos = self.pos
        ref = self.out.at[self.z(k), chip, pos.c]
        send(ref, ref, sems.at[0, k], sems.at[1, k], pos.xn).wait_recv()

    def y_forward(self):
        pos = self.pos
        ref = self.out.at[pos.b, pos.px, pos.c].at[self.halves[0]]
        return send(ref, ref, self.f0.at[0], self.f0.at[1], pos.yn)

    def x_forward(self):
        pos = self.pos
        ref = self.out.at[pos.b, pos.py, pos.c].at[self.halves[1]]
        return send(ref, ref, self.f1.at[0], self.f1.at[1], pos.xn)

    def forward(self):
        pos = self.pos
        self.landed(self.xs, 0, pos.px)
        self.y_forward().start()
        self.landed(self.ys, 0, pos.py)
        if self.halves[1] is not None:
            self.x_forward().start()

    def cross(self):
        pos = self.pos
        across = self.out.at[pos.b, pos.pd, pos.c]
        for half, sems in zip(self.halves, (self.f0, self.f1)):
            if half is not None:
                ref = across.at[half]
                send(ref, ref, sems.at[0], sems.at[1], pos.xn).wait_recv()

    def beside(self, k):
        pos = self.pos
        self.landed(self.xs, k, pos.px)
        self.landed(self.ys, k, pos.py)

    def sibling_copy(self, k, core=None):
        pos = self.pos
        ref = self.out.at[self.z(k), :, pos.c if core is None else core]
        return send(ref, ref, self.sb.at[0, k], self.sb.at[1, k], pos.sib)

    def sibling(self, k):
        self.sibling_copy(k).start()

    def part_copy(self, n, core=None):
        pos = self.pos
        k = pos.nb - 1
        ref = self.out.at[self.z(k), pos.chip(n), pos.c if core is None else core]
        return send(ref, ref, self.sb.at[0, k + n], self.sb.at[1, k + n], pos.sib)

    def finish(self, k):
        self.sibling_copy(k, 1 - self.pos.c).wait_recv()
        self.x_copy(k).wait_send()
        self.y_copy(k).wait_send()
        self.sibling_copy(k).wait_send()

    def end(self):
        k = self.pos.nb - 1
        for n in range(4):
            self.part_copy(n, 1 - self.pos.c).wait_recv()
        for n in range(4):
            self.part_copy(n).wait_send()
        self.x_copy(k).wait_send()
        self.y_copy(k).wait_send()

    def drain(self):
        self.y_forward().wait_send()
        if self.halves[1] is not None:
            self.x_forward().wait_send()
        self.chain.drain()
        self.across.drain()


class InputExchange:
    def __init__(self, pos, rows, out, sems):
        self.pos, self.rows, self.out, self.sems = pos, rows, out, sems
        self.started = []

    @staticmethod
    def scratch():
        return [DMA((2, 2)), DMA((2, 2)), DMA((2, 2)), DMA((2,)), DMA]

    def go(self, copy):
        copy.start()
        self.started.append(copy)

    def start(self):
        pos, (xs, ys, _, sb, local) = self.pos, self.sems
        there = self.out.at[pos.p, pos.c]
        for sems, chip in ((xs, pos.px), (ys, pos.py)):
            for j in range(2):
                self.go(
                    send(
                        self.rows.at[j],
                        there,
                        sems.at[0, j],
                        sems.at[1, pos.c],
                        (pos.b, 2 * chip + j),
                    )
                )
        self.go(send(self.rows.at[1 - pos.c], there, sb.at[0], sb.at[1], pos.sib))
        self.local = pltpu.make_async_copy(self.rows.at[pos.c], there, local)
        self.local.start()

    def landed(self, sems, j, chip):
        ref = self.out.at[chip, j]
        send(ref, ref, sems.at[0, j], sems.at[1, j], self.pos.xn).wait_recv()

    def forward(self):
        pos, (xs, ys, fs, _, _) = self.pos, self.sems
        self.landed(xs, 0, pos.px)
        ref = self.out.at[pos.px, 0]
        self.go(send(ref, ref, fs.at[0, 0], fs.at[1, 0], pos.yn))
        self.landed(ys, 1, pos.py)
        ref = self.out.at[pos.py, 1]
        self.go(send(ref, ref, fs.at[0, 1], fs.at[1, 1], pos.xn))

    def finish(self):
        pos, (xs, ys, fs, sb, _) = self.pos, self.sems
        self.landed(xs, 1, pos.px)
        self.landed(ys, 0, pos.py)
        self.landed(fs, 0, pos.pd)
        self.landed(fs, 1, pos.pd)
        ref = self.out.at[pos.p, 1 - pos.c]
        send(ref, ref, sb.at[0], sb.at[1], pos.sib).wait_recv()
        self.local.wait()

    def drain(self):
        for copy in self.started:
            copy.wait_send()


class JointGather:
    def __init__(self, pos, parts, out, sems):
        self.pos, self.parts, self.out = pos, parts, out
        self.direct, self.sb, self.local_sem = sems[:3]
        self.chain = Chain(
            pos, out.at[pos.b, :, pos.c], lambda z: out.at[z, :, pos.c], sems[3:]
        )

    @staticmethod
    def scratch(nb):
        return [DMA((2, 4)), DMA((2,)), DMA] + Chain.scratch(nb)

    def start(self):
        pos = self.pos
        there = self.out.at[pos.b, pos.p, pos.c]
        self.started = [
            send(
                self.parts.at[pos.chip(k)],
                there,
                self.direct.at[0, k],
                self.direct.at[1, k],
                (pos.b, 2 * pos.chip(k) + pos.c),
            )
            for k in range(1, 4)
        ]
        for copy in self.started:
            copy.start()
        self.local = pltpu.make_async_copy(self.parts.at[pos.p], there, self.local_sem)
        self.local.start()

    def own(self):
        pos = self.pos
        for k in range(1, 4):
            ref = self.out.at[pos.b, pos.chip(k), pos.c]
            send(ref, ref, self.direct.at[0, k], self.direct.at[1, k], pos.sib).wait_recv()
        self.local.wait()
        self.chain.start()

    def sibling(self):
        pos = self.pos
        ref = self.out.at[:, :, pos.c]
        send(ref, ref, self.sb.at[0], self.sb.at[1], pos.sib).start()

    def finish(self):
        pos = self.pos
        ref = self.out.at[:, :, 1 - pos.c]
        send(ref, ref, self.sb.at[0], self.sb.at[1], pos.sib).wait_recv()

    def drain(self):
        for copy in self.started:
            copy.wait_send()
        ref = self.out.at[:, :, self.pos.c]
        send(ref, ref, self.sb.at[0], self.sb.at[1], self.pos.sib).wait_send()
        self.chain.drain()


class ContextExchange:
    def __init__(self, pos, parts, out, sems):
        self.pos, self.parts, self.out = pos, parts, out
        self.sems, self.local_sem = sems

    @staticmethod
    def scratch():
        return [DMA((2, 8)), DMA]

    def pairs(self):
        pos = self.pos
        for k in range(4):
            for j in range(2):
                if k or j:
                    yield 2 * k + j, pos.chip(k), pos.c if j == 0 else 1 - pos.c

    def copies(self):
        pos, sems = self.pos, self.sems
        there = self.out.at[pos.p, pos.c]
        return [
            send(
                self.parts.at[chip, core],
                there,
                sems.at[0, i],
                sems.at[1, i],
                (pos.b, 2 * chip + core),
            )
            for i, chip, core in self.pairs()
        ]

    def local(self):
        pos = self.pos
        return pltpu.make_async_copy(
            self.parts.at[pos.p, pos.c], self.out.at[pos.p, pos.c], self.local_sem
        )

    def start(self):
        for copy in self.copies():
            copy.start()
        self.local().start()

    def arrive(self):
        for i, chip, core in self.pairs():
            ref = self.out.at[chip, core]
            send(ref, ref, self.sems.at[0, i], self.sems.at[1, i], self.pos.sib).wait_recv()
        self.local().wait()

    def drain(self):
        for copy in self.copies():
            copy.wait_send()


def gather_attend(
    lengths, inputs, joint, vectors, hidden_bias, output, expand, reduce, nb, heads
):
    _, count, model_width = inputs.shape
    shard = vec = model_width // (8 * nb)
    per = reduce.shape[0]
    width = heads * HEAD_DIM
    size = 8 * count
    joint_shape = (4, shard, 3 * width + 64)
    small_shape = (16, 128)

    def body(
        lengths_ref, inputs_ref, joint_weight_ref, own_vectors_ref, own_bias_ref,
        output_ref, expand_ref, reduce_ref,
        vectors_out, hidden_out, rows_any, weight_any, qkv_any, log_any,
        context_out, output_out, expand_out, reduce_out,
        rows_out, weight_out, qkv_out, log_out, stores,
        joint_all, context, small_all, bias_ref, rows_ref, joint_ref, small_ref,
        *scratch,
    ):
        pos = Place(nb)
        scratch = list(scratch)

        def take(n):
            got = scratch[:n]
            del scratch[:n]
            return got

        exchange = InputExchange(pos, rows_ref, rows_out, take(5))
        joints = JointGather(pos, joint_ref, joint_all, take(5))
        mixing = ContextExchange(pos, context, context_out, take(2))
        outputs, expands, reduces, smalls = (
            Gather(pos, part, out, halves_of(part.shape), take(10))
            for part, out in (
                (output_ref, output_out),
                (expand_ref, expand_out),
                (reduce_ref, reduce_out),
                (small_ref, small_all),
            )
        )
        gathers = (expands, smalls, reduces, outputs)
        units = ((expands, smalls), (reduces,), (outputs,))

        saves = [
            pltpu.make_async_copy(src, dst, stores.at[n])
            for n, (src, dst) in enumerate(
                (
                    (rows_out, rows_any),
                    (weight_out, weight_any),
                    (qkv_out, qkv_any),
                    (log_out, log_any),
                )
            )
        ]

        def project(i, _):
            at = pl.ds(pl.multiple_of(i * 2 * count, 2 * count), 2 * count)
            qkv_out[at, :] = (
                jnp.dot(
                    rows_out[i].reshape(2 * count, model_width),
                    weight_out[...],
                    preferred_element_type=F32,
                )
                + bias_ref[...]
            ).astype(BF16)
            return 0

        def prepare():
            joints.finish()
            for z in range(nb):
                weight_out[z * 8 * shard : (z + 1) * 8 * shard, :] = joint_all[
                    z, :, :, :, : 3 * width
                ].reshape(8 * shard, 3 * width)
            bias_ref[...] = jnp.zeros_like(bias_ref)
            for s in range(8):
                spot = joint_all[pos.p, s // 2, s % 2, :, 3 * width :].astype(F32)
                bias_ref[:, s * vec : (s + 1) * vec] = spot[0:1, :vec]
                bias_ref[:, 2 * width + s * vec : 2 * width + (s + 1) * vec] = spot[1:2, :vec]
            lax.fori_loop(0, 4, project, 0)
            for copy in saves[:3]:
                copy.start()

        def hop(k):
            for gather in gathers:
                gather.chain.hop(k)

        def relay(k, some):
            for gather in some:
                gather.across.hop(k)

        def share(k):
            for gather in gathers:
                gather.beside(k)
                gather.sibling(k)

        attend = attend_block(lengths_ref[pos.c], qkv_out, log_out, context, heads, count)

        def spread(k):
            for gather in gathers:
                gather.plane(k)

        greet_near(pos)
        weight = joint_weight_ref[...]
        spot = jnp.pad(
            own_vectors_ref[2:4, :].astype(F32), ((0, shard - 2), (0, 64 - vec))
        ).astype(BF16)
        for chip in range(4):
            at = slice(chip * width, (chip + 1) * width)
            joint_ref[chip] = jnp.concatenate(
                [weight[:, n * model_width :][:, at] for n in range(3)] + [spot], axis=1
            )
        small_ref[...] = jnp.concatenate(
            [
                jnp.pad(own_vectors_ref[...].astype(F32), ((0, 0), (0, 128 - vec))),
                jnp.pad(own_bias_ref[...].astype(F32), ((0, 7), (0, 128 - per))),
            ]
        ).astype(BF16)
        meet_near(pos)
        joints.start()
        for gather in gathers:
            gather.own()
            gather.chain.start()
            gather.plane(0, gather.shard)
        rows_ref[...] = inputs_ref[...].astype(BF16)
        joints.own()
        for n, gather in enumerate(gathers):
            gather.forward()
            if n == 1:
                exchange.start()
        hop(1)
        joints.chain.hop(1)
        for gather in gathers:
            gather.local.wait()
            gather.cross()
            gather.sibling(0)
        joints.chain.hop(2)
        hop(2)
        for gather in gathers:
            gather.across.start()
        exchange.forward()
        spread(1)
        joints.chain.hop(3)
        joints.sibling()
        exchange.finish()
        spread(2)
        prepare()
        hop(3)
        spread(3)
        attend(0)
        relay(1, gathers)
        attend(1)
        attend(2)
        relay(2, gathers)
        attend(3)
        mixing.start()
        saves[3].start()
        share(1)
        relay(nb - 1, (smalls,))
        share(2)
        for gather in gathers:
            gather.beside(nb - 1)
            for n in range(3):
                gather.part_copy(n).start()
        smalls.part_copy(3).start()

        def finish(k, _):
            for gather in gathers:
                gather.finish(k)
            return 0

        lax.fori_loop(0, nb - 1, finish, 0)
        smalls.end()
        for owner in range(8 * nb):
            part = small_all[owner // 8, owner % 8 // 2, owner % 2].astype(F32)
            vectors_out[:, owner * vec : (owner + 1) * vec] = part[:8, :vec]
            hidden_out[:, owner * per : (owner + 1) * per] = part[8:9, :per]
        smalls.drain()
        exchange.drain()
        joints.drain()
        for gather in (expands, reduces, outputs):
            gather.across.hop(nb - 1)
            gather.part_copy(3).start()
        for gather in (expands, reduces, outputs):
            gather.drain()
        mixing.arrive()
        mixing.drain()
        for gather in (expands, reduces, outputs):
            gather.end()
        for copy in saves:
            copy.wait()

    kept = (
        ((4, 2) + inputs.shape[1:], BF16),
        ((model_width, 3 * width), BF16),
        ((size, 3 * width), BF16),
        ((size, 128), F32),
    )

    def shape(part):
        return jax.ShapeDtypeStruct((nb, 4, 2) + part.shape, part.dtype)

    return pl.pallas_call(
        body,
        out_shape=(
            jax.ShapeDtypeStruct((8, model_width), F32),
            jax.ShapeDtypeStruct((1, 8 * nb * per), F32),
            *(jax.ShapeDtypeStruct(shape, dtype) for shape, dtype in kept),
            jax.ShapeDtypeStruct((4, 2, count // 2, 2 * width), BF16),
            shape(output),
            shape(expand),
            shape(reduce),
        ),
        in_specs=[SM] + [VM] * 7,
        out_specs=(VM,) * 2 + (ANY,) * 8,
        scratch_shapes=[pltpu.VMEM(shape, dtype) for shape, dtype in kept]
        + [DMA((4,))]
        + [
            pltpu.VMEM((nb, 4, 2) + joint_shape[1:], BF16),
            pltpu.VMEM((4, 2, count // 2, 2 * width), BF16),
            pltpu.VMEM((nb, 4, 2) + small_shape, BF16),
            pltpu.VMEM((1, 3 * width), F32),
            pltpu.VMEM(inputs.shape, BF16),
            pltpu.VMEM(joint_shape, BF16),
            pltpu.VMEM(small_shape, BF16),
        ]
        + InputExchange.scratch()
        + JointGather.scratch(nb)
        + ContextExchange.scratch()
        + Gather.scratch(nb) * 4,
        name="gather_attend",
        compiler_params=pltpu.CompilerParams(
            collective_id=1, has_side_effects=True, vmem_limit_bytes=VMEM_LIMIT
        ),
    )(lengths, inputs, joint, vectors, hidden_bias, output, expand, reduce)


def halves_of(shape):
    rows, columns = shape
    if columns % 256 == 0 and columns >= 1024:
        return (
            (slice(None), pl.ds(0, columns // 2)),
            (slice(None), pl.ds(columns // 2, columns // 2)),
        )
    if rows % 32 == 0:
        return (
            (pl.ds(0, rows // 2), slice(None)),
            (pl.ds(rows // 2, rows // 2), slice(None)),
        )
    if columns % 256 == 0:
        return (
            (slice(None), pl.ds(0, columns // 2)),
            (slice(None), pl.ds(columns // 2, columns // 2)),
        )
    return ((slice(None), slice(None)), None)


def attend_block(limit, qkv_ref, log_ref, context_ref, heads, count):
    width = heads * HEAD_DIM
    size = 8 * count

    def part(n, _):
        at = pl.ds(pl.multiple_of(n * count, count), count)
        allowed = lax.broadcasted_iota(jnp.int32, (1, size), 1) < limit
        lanes = lax.broadcasted_iota(jnp.int32, (count, 128), 1)
        parts, logs = [], jnp.zeros((count, 128), F32)
        for h in range(heads):
            query = qkv_ref[at, h * HEAD_DIM : (h + 1) * HEAD_DIM]
            key = qkv_ref[:, width + h * HEAD_DIM : width + (h + 1) * HEAD_DIM]
            value = qkv_ref[:, 2 * width + h * HEAD_DIM : 2 * width + (h + 1) * HEAD_DIM]
            scores = (
                lax.dot_general(
                    query, key, (((1,), (1,)), ((), ())), preferred_element_type=F32
                )
                * SCORE_SCALE
            )
            scores = jnp.where(allowed, scores, NEG_FILL)
            top = jnp.max(scores, axis=-1, keepdims=True)
            exps = jnp.exp(scores - top)
            total = jnp.sum(exps, axis=-1, keepdims=True)
            mixed = jnp.dot(exps.astype(BF16), value, preferred_element_type=F32)
            parts.append(mixed / total)
            logs = jnp.where(lanes == h, top + jnp.log(total), logs)
        context_ref[n // 2, n % 2] = packed(jnp.concatenate(parts, axis=1)).astype(BF16)
        log_ref[at, :] = logs
        return 0

    def block(i):
        lax.fori_loop(2 * i, 2 * i + 2, part, 0)

    return block


def packed(rows):
    half = rows.shape[0] // 2
    return jnp.concatenate([rows[:half], rows[half:]], axis=1)


def unpacked(rows):
    half = rows.shape[1] // 2
    return jnp.concatenate([rows[:, :half], rows[:, half:]], axis=0)


def attend_back_block(limit, qkv_ref, log_ref, grad_ref, grad_qkv, grad_key, grad_value, heads, count):
    width = heads * HEAD_DIM
    size = 8 * count
    along_keys = (((1,), (1,)), ((), ()))
    along_rows = (((0,), (0,)), ((), ()))

    def part(n, _):
        at = pl.ds(pl.multiple_of(n * count, count), count)
        allowed = lax.broadcasted_iota(jnp.int32, (1, size), 1) < limit
        grads = unpacked(grad_ref[n // 2, n % 2])
        parts = []
        for h in range(heads):
            query = qkv_ref[at, h * HEAD_DIM : (h + 1) * HEAD_DIM]
            key = qkv_ref[:, width + h * HEAD_DIM : width + (h + 1) * HEAD_DIM]
            value = qkv_ref[:, 2 * width + h * HEAD_DIM : 2 * width + (h + 1) * HEAD_DIM]
            grad_out = grads[:, h * HEAD_DIM : (h + 1) * HEAD_DIM]
            scores = (
                lax.dot_general(query, key, along_keys, preferred_element_type=F32)
                * SCORE_SCALE
            )
            probs = jnp.where(allowed, jnp.exp(scores - log_ref[at, h : h + 1]), 0.0)
            grad_probs = lax.dot_general(
                grad_out, value, along_keys, preferred_element_type=F32
            )
            delta = jnp.sum(probs * grad_probs, axis=-1, keepdims=True)
            grad_scores = (probs * (grad_probs - delta)).astype(BF16)
            parts.append(
                jnp.dot(grad_scores, key, preferred_element_type=F32) * SCORE_SCALE
            )
            key_part = lax.dot_general(
                grad_scores, query, along_rows, preferred_element_type=F32
            )
            value_part = lax.dot_general(
                probs.astype(BF16), grad_out, along_rows, preferred_element_type=F32
            )
            own = slice(h * HEAD_DIM, (h + 1) * HEAD_DIM)
            grad_key[:, own] += key_part
            grad_value[:, own] += value_part
        grad_qkv[at, :width] = jnp.concatenate(parts, axis=1).astype(BF16)
        return 0

    def block(i):
        lax.fori_loop(2 * i, 2 * i + 2, part, 0)

    return block


class Scatter:
    def __init__(self, pos, halves, bufs, sems):
        self.pos, self.halves = pos, halves
        (self.partial, self.theirs, self.a0, self.a1, self.bx, self.by, self.z) = bufs
        (self.sb, self.s0, self.s1, self.dx, self.dy, self.cx, self.cy, self.zs) = sems

    @staticmethod
    def scratch(nb, shape, dtype, halves):
        first, second = half_shapes(shape, halves)
        return [
            pltpu.VMEM((nb, 4, 2) + shape, dtype),
            pltpu.VMEM((nb, 4) + shape, dtype),
            pltpu.VMEM((nb,) + first, dtype),
            pltpu.VMEM((nb,) + second, dtype),
            pltpu.VMEM((nb,) + shape, dtype),
            pltpu.VMEM((nb,) + shape, dtype),
            pltpu.VMEM((nb - 1,) + shape, dtype),
        ]

    @staticmethod
    def sem_scratch(nb):
        return [DMA((2, nb)) for _ in range(8)]

    def mine(self, k, chip):
        return self.partial.at[self.pos.up(k), chip, self.pos.c]

    def sibling_copy(self, k):
        pos = self.pos
        z = pos.up(k)
        return send(
            self.partial.at[z, :, 1 - pos.c],
            self.theirs.at[z],
            self.sb.at[0, k],
            self.sb.at[1, k],
            pos.sib,
        )

    def begin(self, k):
        self.sibling_copy(k).start()

    def copy(self, k, src, dst, sems, there):
        return send(src, dst, sems.at[0, k], sems.at[1, k], there)

    def first_copies(self, k):
        pos = self.pos
        h0, h1 = self.halves
        copies = [
            self.copy(k, self.mine(k, pos.pd).at[h0], self.a0.at[k], self.s0, pos.xn),
            self.copy(k, self.mine(k, pos.px).at[h0], self.bx.at[k].at[h0], self.dx, pos.xn),
        ]
        if h1 is not None:
            copies += [
                self.copy(k, self.mine(k, pos.pd).at[h1], self.a1.at[k], self.s1, pos.yn),
                self.copy(k, self.mine(k, pos.py).at[h1], self.by.at[k].at[h1], self.dy, pos.yn),
            ]
        return copies

    def second_copies(self, k):
        pos = self.pos
        h0, h1 = self.halves
        copies = [
            self.copy(k, self.mine(k, pos.py).at[h0], self.by.at[k].at[h0], self.cy, pos.yn)
        ]
        if h1 is not None:
            copies.append(
                self.copy(k, self.mine(k, pos.px).at[h1], self.bx.at[k].at[h1], self.cx, pos.xn)
            )
        return copies

    def first(self, k):
        pos = self.pos
        z = pos.up(k)
        self.sibling_copy(k).wait_recv()
        for j in range(4):
            chip = pos.chip(3 - j)
            self.partial[z, chip, pos.c] = (
                self.partial[z, chip, pos.c].astype(F32) + self.theirs[z, chip].astype(F32)
            ).astype(self.partial.dtype)
        for copy in self.first_copies(k):
            copy.start()

    def landed(self, ref, sems, k):
        send(ref, ref, sems.at[0, k], sems.at[1, k], self.pos.xn).wait_recv()

    def second(self, k):
        pos = self.pos
        h0, h1 = self.halves
        copies = self.second_copies(k)
        self.landed(self.a0.at[k], self.s0, k)
        ref = self.mine(k, pos.py)
        ref[h0] = (ref[h0].astype(F32) + self.a0[k].astype(F32)).astype(ref.dtype)
        copies[0].start()
        if h1 is not None:
            self.landed(self.a1.at[k], self.s1, k)
            ref = self.mine(k, pos.px)
            ref[h1] = (ref[h1].astype(F32) + self.a1[k].astype(F32)).astype(ref.dtype)
            copies[1].start()

    def z_copy(self, k):
        pos = self.pos
        return send(
            self.bx.at[k], self.z.at[k - 1], self.zs.at[0, k], self.zs.at[1, k], (pos.up(k), pos.s)
        )

    def third(self, k, total):
        pos = self.pos
        h0, h1 = self.halves
        self.landed(self.bx.at[k].at[h0], self.dx, k)
        self.landed(self.by.at[k].at[h0], self.cy, k)
        if h1 is not None:
            self.landed(self.by.at[k].at[h1], self.dy, k)
            self.landed(self.bx.at[k].at[h1], self.cx, k)
        total[...] = (
            self.mine(k, pos.p)[...].astype(F32)
            + self.bx[k].astype(F32)
            + self.by[k].astype(F32)
        )

        def on():
            self.bx[k] = total[...].astype(self.bx.dtype)
            self.z_copy(k).start()

        guarded(k != 0, on)

    def last(self, total):
        value = total[...]
        for k in range(1, self.pos.nb):
            self.landed(self.z.at[k - 1], self.zs, k)
            value = value + self.z[k - 1].astype(F32)
        total[...] = value

    def drain(self):
        def done(k, _):
            self.sibling_copy(k).wait_send()
            for copy in self.first_copies(k) + self.second_copies(k):
                copy.wait_send()
            guarded(k != 0, lambda: self.z_copy(k).wait_send())
            return 0

        lax.fori_loop(0, self.pos.nb, done, 0)


def half_shapes(shape, halves):
    def cut(half):
        return tuple(n if h == slice(None) else h.size for n, h in zip(shape, half))

    first = cut(halves[0])
    return first, (first if halves[1] is None else cut(halves[1]))


class RowScatter:
    def __init__(self, pos, out, bufs, sems):
        self.pos, self.out = pos, out
        self.mine, self.a0, self.a1, self.bx, self.by, self.far, self.near = bufs
        (self.sm,) = sems

    @staticmethod
    def scratch(rows, columns):
        return [
            pltpu.VMEM((rows, columns), BF16),
            pltpu.VMEM((rows, columns), BF16),
            pltpu.VMEM((2, rows, columns), BF16),
            pltpu.VMEM((2, rows, columns), BF16),
            pltpu.VMEM((rows, columns), F32),
            pltpu.VMEM((rows, columns), F32),
            DMA((2, 7)),
        ]

    def copy(self, i):
        pos, mine = self.pos, self.mine
        src, dst, there = (
            (mine.at[pos.pd, 0], self.a0, pos.xn),
            (mine.at[pos.pd, 1], self.a1, pos.yn),
            (mine.at[pos.px, 0], self.bx.at[0], pos.xn),
            (mine.at[pos.py, 1], self.by.at[1], pos.yn),
            (mine.at[pos.py, 0], self.by.at[0], pos.yn),
            (mine.at[pos.px, 1], self.bx.at[1], pos.xn),
            (self.far, self.near, pos.sib),
        )[i]
        return send(src, dst, self.sm.at[0, i], self.sm.at[1, i], there)

    def landed(self, i, ref):
        send(ref, ref, self.sm.at[0, i], self.sm.at[1, i], self.pos.xn).wait_recv()

    def first(self):
        for i in range(4):
            self.copy(i).start()

    def second(self):
        pos, mine = self.pos, self.mine
        self.landed(0, self.a0)
        mine[pos.py, 0] = (mine[pos.py, 0].astype(F32) + self.a0[...].astype(F32)).astype(BF16)
        self.copy(4).start()
        self.landed(1, self.a1)
        mine[pos.px, 1] = (mine[pos.px, 1].astype(F32) + self.a1[...].astype(F32)).astype(BF16)
        self.copy(5).start()

    def third(self):
        pos = self.pos
        self.landed(2, self.bx.at[0])
        self.landed(3, self.by.at[1])
        self.landed(4, self.by.at[0])
        self.landed(5, self.bx.at[1])

        def total(core):
            return (
                self.mine[pos.p, core].astype(F32)
                + self.bx[core].astype(F32)
                + self.by[core].astype(F32)
            )

        self.far[...] = total(1 - pos.c)
        self.copy(6).start()
        self.out[pos.c] += total(pos.c)

    def last(self):
        pos = self.pos
        self.landed(6, self.near)
        self.out[1 - pos.c] += self.near[...]
        for i in range(7):
            self.copy(i).wait_send()


class JointScatter:
    def __init__(self, pos, bufs, sems):
        self.pos = pos
        self.partial, self.theirs, self.zbuf, self.sums, self.got = bufs
        self.sb, self.zs, self.ps = sems

    @staticmethod
    def scratch(nb, shape):
        return [
            pltpu.VMEM((nb, 4, 2) + shape, BF16),
            pltpu.VMEM((nb, 4) + shape, BF16),
            pltpu.VMEM((nb - 1, 4) + shape, BF16),
            pltpu.VMEM((4,) + shape, BF16),
            pltpu.VMEM((4,) + shape, BF16),
        ]

    @staticmethod
    def sem_scratch(nb):
        return [DMA((2,)), DMA((2, nb)), DMA((2, 4))]

    def sibling_copy(self):
        pos = self.pos
        return send(
            self.partial.at[:, :, 1 - pos.c], self.theirs, self.sb.at[0], self.sb.at[1], pos.sib
        )

    def z_copy(self, d):
        pos = self.pos
        return send(
            self.partial.at[pos.up(d), :, pos.c],
            self.zbuf.at[d - 1],
            self.zs.at[0, d],
            self.zs.at[1, d],
            (pos.up(d), pos.s),
        )

    def plane_copy(self, k):
        pos = self.pos
        chip = pos.chip(k)
        return send(
            self.sums.at[chip],
            self.got.at[pos.p],
            self.ps.at[0, k],
            self.ps.at[1, k],
            (pos.b, 2 * chip + pos.c),
        )

    def begin(self):
        self.sibling_copy().start()

    def first(self):
        pos = self.pos
        self.sibling_copy().wait_recv()
        for d in (2, *(n for n in range(1, pos.nb) if n != 2), 0):
            z = pos.up(d)
            self.partial[z, :, pos.c] = (
                self.partial[z, :, pos.c].astype(F32) + self.theirs[z].astype(F32)
            ).astype(BF16)
            if d:
                self.z_copy(d).start()

    def second(self):
        pos = self.pos
        value = self.partial[pos.b, :, pos.c].astype(F32)
        for d in range(1, pos.nb):
            self.z_copy(d).wait_recv()
            value = value + self.zbuf[d - 1].astype(F32)
        self.sums[...] = value.astype(BF16)
        for k in range(1, 4):
            self.plane_copy(k).start()

    def last(self, out, vec):
        pos = self.pos
        width = out.shape[1] // 12
        self.got[pos.p] = self.sums[pos.p]
        for k in range(1, 4):
            ref = self.got.at[pos.chip(k)]
            send(ref, ref, self.ps.at[0, k], self.ps.at[1, k], pos.sib).wait_recv()
        extra = 0.0
        for chip in range(4):
            value = self.got[chip].astype(F32)
            for n in range(3):
                out[:, (4 * n + chip) * width : (4 * n + chip + 1) * width] = value[
                    :, n * width : (n + 1) * width
                ]
            extra = extra + value[:8, 3 * width : 3 * width + vec]
        self.sibling_copy().wait_send()
        for d in range(1, pos.nb):
            self.z_copy(d).wait_send()
        for k in range(1, 4):
            self.plane_copy(k).wait_send()
        return extra


def normed_rows(residual):
    centered = residual - jnp.mean(residual, axis=-1, keepdims=True)
    inverse = lax.rsqrt(jnp.mean(centered * centered, axis=-1, keepdims=True) + EPSILON)
    return centered * inverse, inverse


def transposed_dot(left, right):
    return lax.dot_general(left, right, (((0,), (0,)), ((), ())), preferred_element_type=F32)


def dot_transposed(left, right):
    return lax.dot_general(left, right, (((1,), (1,)), ((), ())), preferred_element_type=F32)


def feed_and_back(
    lengths, inputs, cotangent, mixed, vectors, hidden_bias,
    output_weight, expand_weight, reduce_weight, rows, weight, qkv, logs, nb, heads,
):
    _, count, model_width = inputs.shape
    hidden = hidden_bias.shape[1]
    block = hidden // nb
    width = heads * HEAD_DIM
    size, tokens = 8 * count, 2 * count
    owners = 8 * nb
    shard = vec = model_width // owners
    per = hidden // owners
    joint_shape = (shard, 3 * width + 64)
    shapes = [(16, 128), (shard, model_width), (shard, hidden), (per, model_width)]
    dtypes = [F32, BF16, BF16, BF16]

    def body(
        lengths_ref, inputs_ref, cotangent_ref, mixed_ref, vectors_ref, bias_ref,
        output_ref, expand_ref, reduce_ref, rows_any, weight_any, qkv_any, log_any,
        result_out, rows_out, joint_out, vectors_out, hidden_out,
        output_out, expand_out, reduce_out,
        output_w, expand_w, reduce_w, rows_ref, weight_ref, qkv_ref, log_ref, loads,
        context, first_normed, first_low, hidden_low, slope, feed, grad_low,
        grad_vectors, grad_bias, parts, small_total,
        grad_context, grad_qkv, grad_key, grad_value,
        *scratch,
    ):
        pos = Place(nb)
        scratch = list(scratch)

        def take(n):
            got = scratch[:n]
            del scratch[:n]
            return got

        mixing = ContextExchange(pos, parts, grad_context, take(2))
        row_sums = RowScatter(pos, rows_out, [hidden_low] + take(6), take(1))
        joints = JointScatter(pos, take(5), take(3))
        smalls, outputs, expands, reduces = (
            Scatter(pos, halves_of(shape), take(7), take(8)) for shape in shapes
        )

        def turn(i):
            return jnp.where(i < 2, 2 - i, 3 * (3 - i))

        def expand_load(z):
            at = pl.ds(z * block if isinstance(z, int) else pl.multiple_of(z * block, block), block)
            return pltpu.make_async_copy(expand_ref.at[:, at], expand_w.at[z], loads.at[z])

        def reduce_load(z):
            at = pl.ds(z * block if isinstance(z, int) else pl.multiple_of(z * block, block), block)
            return pltpu.make_async_copy(reduce_ref.at[at, :], reduce_w.at[z], loads.at[nb + z])

        output_load = pltpu.make_async_copy(output_ref, output_w, loads.at[2 * nb])
        later = [
            pltpu.make_async_copy(src, dst, loads.at[2 * nb + 1 + n])
            for n, (src, dst) in enumerate(
                ((rows_any, rows_ref), (weight_any, weight_ref), (qkv_any, qkv_ref), (log_any, log_ref))
            )
        ]
        output_load.start()
        for z in range(nb):
            expand_load(z).start()
            reduce_load(z).start()
        for copy in later:
            copy.start()
        barrier = pltpu.get_barrier_semaphore()
        partners = [(pos.up(d), pos.s) for d in range(1, nb)] + plane_others(pos)
        for device in partners:
            pl.semaphore_signal(barrier, inc=1, device_id=device, device_id_type=MESH)

        def vector(n):
            return vectors_ref[n : n + 1, :]

        for chip in range(4):
            for j in range(2):
                context[j * count : (j + 1) * count, chip * width : (chip + 1) * width] = unpacked(
                    mixed_ref[chip, j]
                )
        output_load.wait()
        branch = jnp.dot(context[...], output_w[...], preferred_element_type=F32) + vector(4)
        normed, first_inverse = normed_rows(
            inputs_ref[...].reshape(tokens, model_width) + branch
        )
        first_normed[...] = normed
        first = normed * vector(0) + vector(1)
        rows_out[...] = first.reshape(2, count, model_width)
        first_low[...] = first.astype(BF16)
        feed[...] = jnp.broadcast_to(vector(7), feed.shape)

        def forward(z, _):
            at = pl.ds(pl.multiple_of(z * block, block), block)
            expand_load(z).wait()
            before = (
                jnp.dot(first_low[...], expand_w[z], preferred_element_type=F32)
                + bias_ref[:, at]
            )
            half = 0.5 * (1.0 + lax.erf(before * HALF_ROOT))
            low = (before * half).astype(BF16)
            hidden_low[z] = low.reshape(2, count, block)
            slope[z] = half + before * jnp.exp(-0.5 * before * before) * INV_ROOT_TAU
            reduce_load(z).wait()
            feed[...] += jnp.dot(low, reduce_w[z], preferred_element_type=F32)
            return 0

        lax.fori_loop(0, nb, forward, 0)
        normed, inverse = normed_rows(
            rows_out[...].reshape(tokens, model_width) + feed[...]
        )
        result_out[...] = (normed * vector(5) + vector(6)).reshape(2, count, model_width)

        places = pos.s * count + lax.broadcasted_iota(jnp.int32, (count, 1), 0)
        grad_res = jnp.concatenate(
            [jnp.where(places < lengths_ref[j], cotangent_ref[j], 0.0) for j in range(2)]
        )
        grad_second, gain, shift = norm_back(grad_res, normed, inverse, vector(5))
        grad_low[...] = grad_second.astype(BF16)
        grad_vectors[...] = jnp.zeros_like(grad_vectors)
        grad_vectors[5:6, :] = gain[None]
        grad_vectors[6:7, :] = shift[None]
        grad_vectors[7:8, :] = jnp.sum(grad_low[...].astype(F32), axis=0, keepdims=True)
        feed[...] = grad_second

        def backward(i, _):
            z = pos.up(turn(i))
            at = pl.ds(pl.multiple_of(z * block, block), block)
            for n in range(2):
                cut = slice(n * (block // 2), (n + 1) * (block // 2))
                reduces.partial[z, 2 * n : 2 * n + 2] = (
                    transposed_dot(
                        hidden_low[z, :, :, cut].reshape(tokens, block // 2), grad_low[...]
                    )
                    .reshape(2, 2, per, model_width)
                    .astype(BF16)
                )
            reduces.begin(turn(i))
            low = (dot_transposed(grad_low[...], reduce_w[z]) * slope[z]).astype(BF16)
            grad_bias[:, at] = jnp.sum(low.astype(F32), axis=0, keepdims=True)
            for n in range(2):
                cut = slice(n * (model_width // 2), (n + 1) * (model_width // 2))
                expands.partial[n * nb // 2 : (n + 1) * nb // 2, :, :, :, at] = (
                    transposed_dot(first_low[:, cut], low)
                    .reshape(nb // 2, 4, 2, shard, block)
                    .astype(BF16)
                )
            feed[...] += dot_transposed(low, expand_w[z])
            reduces.first(turn(i))
            return 0

        pl.semaphore_wait(barrier, len(partners))
        lax.fori_loop(0, nb, backward, 0)
        for k in range(nb):
            expands.begin(turn(k))
        grads, gain, shift = norm_back(feed[...], first_normed[...], first_inverse, vector(0))
        rows_out[...] = grads.reshape(2, count, model_width)
        low = grads.astype(BF16)
        grad_low[...] = low
        grad_vectors[0:1, :] = gain[None]
        grad_vectors[1:2, :] = shift[None]
        grad_vectors[4:5, :] = jnp.sum(low.astype(F32), axis=0, keepdims=True)
        low = dot_transposed(low, output_w[...]).astype(BF16)
        for chip in range(4):
            for j in range(2):
                parts[chip, j] = packed(
                    low[j * count : (j + 1) * count, chip * width : (chip + 1) * width]
                )
        mixing.start()
        for n in range(2):
            cut = slice(n * (model_width // 2), (n + 1) * (model_width // 2))
            outputs.partial[n * nb // 2 : (n + 1) * nb // 2] = (
                transposed_dot(context[:, cut], grad_low[...])
                .reshape(nb // 2, 4, 2, shard, model_width)
                .astype(BF16)
            )
        for owner in range(owners):
            here = (owner // 8, owner % 8 // 2, owner % 2)
            smalls.partial[here] = jnp.concatenate(
                [
                    jnp.pad(
                        grad_vectors[:, owner * vec : (owner + 1) * vec], ((0, 0), (0, 128 - vec))
                    ),
                    jnp.broadcast_to(
                        jnp.pad(
                            grad_bias[:, owner * per : (owner + 1) * per], ((0, 0), (0, 128 - per))
                        ),
                        (8, 128),
                    ),
                ]
            )
        for k in range(nb):
            outputs.begin(turn(k))
            smalls.begin(turn(k))

        grad_key[...] = jnp.zeros_like(grad_key)
        grad_value[...] = jnp.zeros_like(grad_value)
        for copy in later:
            copy.wait()
        back = attend_back_block(
            lengths_ref[pos.c], qkv_ref, log_ref, grad_context, grad_qkv, grad_key, grad_value,
            heads, count,
        )

        def middle(i, _):
            k = turn(i)
            reduces.second(k)
            expands.first(k)
            guarded(i > 0, lambda: reduces.third(turn(i - 1), reduce_out))
            guarded(i == 0, mixing.arrive)
            back(i)
            guarded(i > 0, lambda: expands.second(turn(i - 1)))
            guarded(i > 1, lambda: expands.third(turn(i - 2), expand_out))
            return 0

        lax.fori_loop(0, nb, middle, 0)

        def late(i, _):
            k = turn(i)
            outputs.first(k)
            smalls.first(k)
            return 0

        grad_qkv[:, width : 2 * width] = (grad_key[...] * SCORE_SCALE).astype(BF16)
        grad_qkv[:, 2 * width :] = grad_value[...].astype(BF16)

        def spread(i, _):
            at = pl.ds(pl.multiple_of(i * tokens, tokens), tokens)
            row_sums.mine[i] = (
                dot_transposed(grad_qkv[at, :], weight_ref[...])
                .astype(BF16)
                .reshape(2, count, model_width)
            )
            return 0

        for z in range(nb):
            grad_joint = transposed_dot(
                rows_ref[:, :, :, z * 8 * shard : (z + 1) * 8 * shard].reshape(size, 8 * shard),
                grad_qkv[...],
            )
            joints.partial[z, :, :, :, : 3 * width] = grad_joint.reshape(
                4, 2, shard, 3 * width
            ).astype(BF16)
        sums = jnp.sum(grad_qkv[...].astype(F32), axis=0, keepdims=True)
        joints.partial[:, :, :, :, 3 * width :] = jnp.zeros((nb, 4, 2, shard, 64), BF16)
        for s in range(8):
            at = slice(s * vec, (s + 1) * vec)
            value = jnp.concatenate([sums[:, :width][:, at], sums[:, 2 * width :][:, at]])
            joints.partial[pos.p, s // 2, s % 2, :, 3 * width :] = jnp.pad(
                value, ((0, shard - 2), (0, 64 - vec))
            ).astype(BF16)
        joints.begin()
        lax.fori_loop(0, 4, spread, 0)
        row_sums.first()
        joints.first()
        expands.second(turn(3))
        lax.fori_loop(0, nb, late, 0)

        expands.third(turn(2), expand_out)
        reduces.third(turn(nb - 1), reduce_out)
        reduces.last(reduce_out)
        reduces.drain()
        row_sums.second()

        def final(i, _):
            k = turn(i)
            outputs.second(k)
            smalls.second(k)
            return 0

        lax.fori_loop(0, nb, final, 0)
        expands.third(turn(nb - 1), expand_out)
        joints.second()
        row_sums.third()
        expands.last(expand_out)
        expands.drain()
        mixing.drain()

        def end(i, _):
            k = turn(i)
            outputs.third(k, output_out)
            smalls.third(k, small_total)
            return 0

        lax.fori_loop(0, nb, end, 0)
        extra = joints.last(joint_out, vec)
        row_sums.last()
        for scatter, out in ((outputs, output_out), (smalls, small_total)):
            scatter.last(out)
            scatter.drain()
        lines = lax.broadcasted_iota(jnp.int32, (8, vec), 0)
        value = jnp.where(lines == 2, extra[0:1], small_total[:8, :vec])
        vectors_out[...] = jnp.where(lines == 3, extra[1:2], value)
        hidden_out[...] = small_total[8:9, :per]

    def vmem(shape, dtype):
        return pltpu.VMEM(shape, dtype)

    scratch = [
        vmem((model_width, model_width), BF16),
        vmem((nb, model_width, block), BF16),
        vmem((nb, block, model_width), BF16),
        vmem(rows.shape, BF16),
        vmem(weight.shape, BF16),
        vmem(qkv.shape, BF16),
        vmem(logs.shape, F32),
        DMA((2 * nb + 5,)),
        vmem((tokens, model_width), BF16),
        vmem((tokens, model_width), F32),
        vmem((tokens, model_width), BF16),
        vmem((nb, 2, count, block), BF16),
        vmem((nb, tokens, block), F32),
        vmem((tokens, model_width), F32),
        vmem((tokens, model_width), BF16),
        vmem((8, model_width), F32),
        vmem((1, hidden), F32),
        vmem((4, 2, count // 2, 2 * width), BF16),
        vmem((16, 128), F32),
        vmem((4, 2, count // 2, 2 * width), BF16),
        vmem((size, 3 * width), BF16),
        vmem((size, width), F32),
        vmem((size, width), F32),
    ]
    scratch += ContextExchange.scratch() + RowScatter.scratch(count, model_width)
    scratch += JointScatter.scratch(nb, joint_shape) + JointScatter.sem_scratch(nb)
    for shape, dtype in zip(shapes, dtypes):
        scratch += Scatter.scratch(nb, shape, dtype, halves_of(shape)) + Scatter.sem_scratch(nb)
    return pl.pallas_call(
        body,
        out_shape=tuple(
            jax.ShapeDtypeStruct(shape, F32)
            for shape in (
                inputs.shape,
                inputs.shape,
                (shard, 3 * model_width),
                (8, vec),
                (1, per),
                shapes[1],
                shapes[2],
                shapes[3],
            )
        ),
        in_specs=[SM] + [VM] * 5 + [ANY] * 7,
        out_specs=(VM,) * 8,
        scratch_shapes=scratch,
        name="feed_and_back",
        compiler_params=pltpu.CompilerParams(
            collective_id=4, has_side_effects=True, vmem_limit_bytes=VMEM_LIMIT
        ),
    )(
        lengths, inputs, cotangent, mixed, vectors, hidden_bias,
        output_weight, expand_weight, reduce_weight, rows, weight, qkv, logs,
    )


def hand_over(*arrays):
    count = len(arrays)

    def body(*refs):
        came, out, held = refs[:count], refs[count : 2 * count], refs[2 * count : 3 * count]
        sems = refs[3 * count]
        loads = [pltpu.make_async_copy(came[n], held[n], sems.at[0, n]) for n in range(count)]
        stores = [pltpu.make_async_copy(held[n], out[n], sems.at[1, n]) for n in range(count)]
        for copy in loads:
            copy.start()
        for load, store in zip(loads, stores):
            load.wait()
            store.start()
        for copy in stores:
            copy.wait()

    return pl.pallas_call(
        body,
        out_shape=tuple(jax.ShapeDtypeStruct(a.shape, a.dtype) for a in arrays),
        in_specs=[ANY] * count,
        out_specs=(ANY,) * count,
        scratch_shapes=[pltpu.VMEM(a.shape, a.dtype) for a in arrays] + [DMA((2, count))],
        name="hand_over",
        compiler_params=pltpu.CompilerParams(vmem_limit_bytes=VMEM_LIMIT),
    )(*arrays)


def plane_on_device(
    inputs,
    cotangent,
    lengths,
    joint_weight,
    output_weight,
    vectors,
    expand_weight,
    expand_bias,
    reduce_weight,
):
    nb = lax.axis_size("batch")
    _, _, model_width = inputs.shape
    hidden_width = expand_weight.shape[1]
    heads = model_width // (4 * HEAD_DIM)
    per = expand_bias.shape[0]
    (
        vector_rows, full_bias, rows_all, joint_all, qkv, logs,
        mixed, output_all, expand_all, reduce_all,
    ) = gather_attend(
        lengths,
        inputs,
        joint_weight,
        vectors,
        expand_bias.reshape(1, per),
        output_weight,
        expand_weight,
        reduce_weight,
        nb,
        heads,
    )
    full_output = output_all.reshape(model_width, model_width)
    full_expand = expand_all.reshape(model_width, hidden_width)
    full_reduce = reduce_all.reshape(hidden_width, model_width)

    result, grad_inputs, joint_sum, vectors_sum, bias_sum, output_sum, expand_sum, reduce_sum = (
        feed_and_back(
            lengths,
            inputs,
            cotangent,
            mixed,
            vector_rows,
            full_bias,
            full_output,
            full_expand,
            full_reduce,
            rows_all,
            joint_all,
            qkv,
            logs,
            nb,
            heads,
        )
    )
    (
        result, grad_inputs, joint_sum, output_sum, vectors_sum, expand_sum, bias_sum, reduce_sum,
    ) = hand_over(
        result, grad_inputs, joint_sum, output_sum, vectors_sum, expand_sum, bias_sum, reduce_sum
    )
    return (
        result,
        grad_inputs,
        joint_sum,
        output_sum,
        vectors_sum,
        expand_sum,
        bias_sum.reshape(per),
        reduce_sum,
    )


def plane_fits(mesh, inputs, expand_bias, expand_weight):
    return (
        mesh.shape["seq"] == 8
        and mesh.shape["batch"] == 4
        and inputs[0] == 2 * mesh.shape["batch"]
        and HEADS % 4 == 0
        and inputs[2] == HEADS * HEAD_DIM
        and inputs[1] % (8 * 16) == 0
        and inputs[2] % 256 == 0
        and expand_weight[0] % (8 * 32) == 0
        and expand_weight[1] % (16 * 32) == 0
        and expand_bias[0] <= 128 * 32
        and expand_weight[1] == 4 * inputs[2]
    )


def solution(mesh):
    def program(*args):
        fits = plane_fits(mesh, args[0].shape, args[7].shape, args[6].shape)
        return jax.shard_map(
            plane_on_device if fits else general_on_device,
            mesh=mesh,
            in_specs=(
                P("batch", "seq", None),
                P("batch", "seq", None),
                P("batch"),
                P(("batch", "seq"), None),
                P(("batch", "seq"), None),
                P(None, ("batch", "seq")),
                P(("batch", "seq"), None),
                P(("batch", "seq")),
                P(("batch", "seq"), None),
            ),
            out_specs=(
                P("batch", "seq", None),
                P("batch", "seq", None),
                P(("batch", "seq"), None),
                P(("batch", "seq"), None),
                P(None, ("batch", "seq")),
                P(("batch", "seq"), None),
                P(("batch", "seq")),
                P(("batch", "seq"), None),
            ),
            check_vma=False,
        )(*args)

    return program
```
